32 devices in a mesh: rep: 16 (over z, y, core), grp: 2 (over x).
Axes of the slice: x: 2, y: 2, z: 4, core: 2. Of those that a mesh axis runs over, the one named last changes fastest.
Arguments:
- tokens: bfloat16 [16, 1568, 1024], P('rep', 'grp'), may hold values from -6 to 6
- query_weight: bfloat16 [1024, 1024], P('grp'), may hold values from -0.1875 to 0.1875
- key_weight: bfloat16 [1024, 1024], P('grp'), may hold values from -0.1875 to 0.1875
- value_weight: bfloat16 [1024, 1024], P('grp'), may hold values from -0.1875 to 0.1875
- query_bias: float32 [1024], P('grp'), may hold values from -4 to 4
- value_bias: float32 [1024], P('grp'), may hold values from -0.75 to 0.75
- out_weight: bfloat16 [1024, 1024], P('grp'), may hold values from -4 to 4
- out_bias: float32 [1024], P('grp'), may hold values from -4 to 4
- first_gain: float32 [1024], P('grp'), may hold values from 0.5 to 1.5
- first_shift: float32 [1024], P('grp'), may hold values from -4 to 4
- second_gain: float32 [1024], P('grp'), may hold values from 0.5 to 1.5
- second_shift: float32 [1024], P('grp'), may hold values from -4 to 4
- up_weight: bfloat16 [1024, 4096], P('grp'), may hold values from -0.1875 to 0.1875
- up_bias: float32 [4096], P('grp'), may hold values from -4 to 4
- down_weight: bfloat16 [4096, 1024], P('grp'), may hold values from -0.09375 to 0.09375
- down_bias: float32 [1024], P('grp'), may hold values from -4 to 4
- cotangent: bfloat16 [16, 1568, 1024], P('rep', 'grp'), may hold values from -6 to 6
Outputs:
- layer_out: bfloat16 [16, 1568, 1024], P('rep', 'grp')
- tokens_grad: bfloat16 [16, 1568, 1024], P('rep', 'grp')
- query_weight_grad: float32 [1024, 1024], P('grp')
- key_weight_grad: float32 [1024, 1024], P('grp')
- value_weight_grad: float32 [1024, 1024], P('grp')
- query_bias_grad: float32 [1024], P('grp')
- value_bias_grad: float32 [1024], P('grp')
- out_weight_grad: float32 [1024, 1024], P('grp')
- out_bias_grad: float32 [1024], P('grp')
- first_gain_grad: float32 [1024], P('grp')
- first_shift_grad: float32 [1024], P('grp')
- second_gain_grad: float32 [1024], P('grp')
- second_shift_grad: float32 [1024], P('grp')
- up_weight_grad: float32 [1024, 4096], P('grp')
- up_bias_grad: float32 [4096], P('grp')
- down_weight_grad: float32 [4096, 1024], P('grp')
- down_bias_grad: float32 [1024], P('grp')
The draws below stay inside these ranges and needn't reach their ends.
All inputs are finite; a program needn't handle non-finite values.
Results may differ from the reference program's by a relative error of at most 0.033.
Values may be sent and summed in bfloat16 or wider, within the bound.
No kernel may reach another device: no remote copies, remote signals or barrier semaphores. Data moves between devices by JAX's collectives and lax.ppermute only.
A program may use at most 448 MiB of HBM per device.

```python
import jax
import jax.numpy as jnp
from jax import lax

D = 1024
HEADS = 16
HEAD_DIM = 64
FF = 4096
LEN = 1568
CLIPS = 16


def level_of(key, shape, shards, low, high):
    loudness, own = 1.0, jax.random.fold_in(key, 6)
    for axis_at, blocks in shards:
        steps = jnp.exp(jax.random.uniform(jax.random.fold_in(own, axis_at), (blocks,), jnp.float32, low / len(shards), high / len(shards)))
        loudness = loudness * jnp.repeat(steps, shape[axis_at] // blocks).reshape([-1 if axis == axis_at else 1 for axis in range(len(shape))])
    return loudness


def normal_values(own_key, shape, width, limit, cuts=(), kind=jnp.bfloat16):
    loudness = level_of(own_key, shape, cuts, -0.22, 0.18) if cuts else 1.0
    array = jax.random.normal(own_key, shape, jnp.float32) * width * loudness
    return jnp.minimum(jnp.maximum(array, -limit), limit).astype(kind)


def setup_inputs(seed: int = 0) -> dict:
    splits = jax.random.split(jax.random.key(seed), 18)
    tokens = normal_values(splits[0], (CLIPS, LEN, D), 1.0, 6.0, ((0, 16), (1, 2)))
    query_weight = normal_values(splits[1], (D, D), D ** -0.5, 0.1875, ((0, 2),))
    key_weight = normal_values(splits[2], (D, D), D ** -0.5, 0.1875, ((0, 2),))
    value_weight = normal_values(splits[3], (D, D), D ** -0.5, 0.1875, ((0, 2),))
    query_bias = normal_values(splits[4], (D,), 1.0, 4.0, ((0, 2),), jnp.float32)
    value_bias = normal_values(splits[5], (D,), 0.05, 0.75, ((0, 2),), jnp.float32)
    out_weight = normal_values(splits[6], (D, D), (max(D // 512, 1)) ** -0.5, 4.0, ((0, 2),))
    out_bias = normal_values(splits[7], (D,), 0.5, 4.0, ((0, 2),), jnp.float32)
    first_gain = jnp.clip(1.0 + 0.1 * jax.random.normal(splits[8], (D,), jnp.float32), 0.5, 1.5)
    first_shift = normal_values(splits[9], (D,), 0.3, 4.0, ((0, 2),), jnp.float32)
    second_gain = jnp.clip(1.0 + 0.1 * jax.random.normal(splits[10], (D,), jnp.float32), 0.5, 1.5)
    second_shift = normal_values(splits[11], (D,), 0.3, 4.0, ((0, 2),), jnp.float32)
    up_weight = normal_values(splits[12], (D, FF), D ** -0.5, 0.1875, ((0, 2),))
    up_bias = normal_values(splits[13], (FF,), 0.5, 4.0, ((0, 2),), jnp.float32)
    down_weight = normal_values(splits[14], (FF, D), FF ** -0.5, 0.09375, ((0, 2),))
    down_bias = normal_values(splits[15], (D,), 0.5, 4.0, ((0, 2),), jnp.float32)
    cotangent = normal_values(splits[16], (CLIPS, LEN, D), 1.0, 6.0, ((0, 16), (1, 2)))
    return dict(tokens=tokens, query_weight=query_weight, key_weight=key_weight, value_weight=value_weight, query_bias=query_bias, value_bias=value_bias, out_weight=out_weight, out_bias=out_bias, first_gain=first_gain, first_shift=first_shift, second_gain=second_gain, second_shift=second_shift, up_weight=up_weight, up_bias=up_bias, down_weight=down_weight, down_bias=down_bias, cotangent=cotangent)


@jax.custom_vjp
def low(v):
    return lax.optimization_barrier(v.astype(jnp.bfloat16)).astype(jnp.float32)

@jax.custom_vjp
def low_back(v):
    return v

def low_keep(v):
    return (low(v), None)

def low_pass(kept, grad):
    return (grad,)

def back_keep(v):
    return (v, None)

def back_low(kept, grad):
    return (low(grad),)
low.defvjp(low_keep, low_pass)
low_back.defvjp(back_keep, back_low)
EPS = 1e-06
HIGH = lax.Precision.HIGHEST

def norm_rows(values, gain, shift):
    average = lax.optimization_barrier(jnp.mean(values, axis=-1, keepdims=True))
    centred = values - average
    spread = lax.optimization_barrier(jnp.mean(centred * centred, axis=-1, keepdims=True))
    return centred * lax.rsqrt(spread + EPS) * gain + shift

def product(left, right):
    return jnp.dot(left, right, precision=HIGH)

def clip_layer(params, clip):
    query_weight, key_weight, value_weight, query_bias, value_bias, out_weight, out_bias, first_gain, first_shift, second_gain, second_shift, up_weight, up_bias, down_weight, down_bias = params
    length = clip.shape[0]
    first = low(norm_rows(clip, first_gain, first_shift))
    query = low(low_back(product(first, query_weight) + query_bias)).reshape(length, HEADS, HEAD_DIM)
    key = low(low_back(product(first, key_weight))).reshape(length, HEADS, HEAD_DIM)
    value = low(low_back(product(first, value_weight) + value_bias)).reshape(length, HEADS, HEAD_DIM)
    scale = HEAD_DIM ** (-0.5)
    scores = low_back(jnp.einsum('qhd,khd->hqk', query, key, precision=HIGH) * scale)
    probs = low(jax.nn.softmax(scores, axis=-1))
    mixed = jnp.einsum('hqk,khd->qhd', probs, value, precision=HIGH).reshape(length, D)
    mixed = low(low_back(mixed))
    middle = clip + low_back(product(mixed, out_weight) + out_bias)
    second = low(norm_rows(middle, second_gain, second_shift))
    pre = low_back(product(second, up_weight) + up_bias)
    hidden = low(jax.nn.gelu(pre, approximate=False))
    return middle + product(hidden, down_weight) + down_bias

def reference(tokens, query_weight, key_weight, value_weight, query_bias, value_bias, out_weight, out_bias, first_gain, first_shift, second_gain, second_shift, up_weight, up_bias, down_weight, down_bias, cotangent):
    params = tuple((item.astype(jnp.float32) for item in (query_weight, key_weight, value_weight, query_bias, value_bias, out_weight, out_bias, first_gain, first_shift, second_gain, second_shift, up_weight, up_bias, down_weight, down_bias)))
    inputs = tokens.astype(jnp.float32)

    def forward(weights, clips):

        def one_clip(clip):
            return clip_layer(weights, clip)
        return lax.map(jax.checkpoint(one_clip), clips)
    result, pullback = jax.vjp(forward, params, inputs)
    grads, input_grad = pullback(cotangent.astype(jnp.float32))
    return (result.astype(jnp.bfloat16), input_grad.astype(jnp.bfloat16), grads[0], grads[1], grads[2], grads[3], grads[4], grads[5], grads[6], grads[7], grads[8], grads[9], grads[10], grads[11], grads[12], grads[13], grads[14])
```

```python
import functools

import jax
import jax.numpy as jnp
from jax import lax
from jax.experimental import pallas as pl
from jax.experimental.pallas import tpu as pltpu
from jax.sharding import Mesh
from jax.sharding import PartitionSpec as P

HEAD_DIM = 64
PAIR = 2 * HEAD_DIM
EPS = 1e-06
LOG2E = 1.4426950408889634
F32 = jnp.float32
BF16 = jnp.bfloat16
SWAP = [(0, 1), (1, 0)]
VMEM_LIMIT = 62 << 20


def contract(left, right, left_dim, right_dim):
    return lax.dot_general(
        left, right, (((left_dim,), (right_dim,)), ((), ())), preferred_element_type=F32
    )


def attend_kernel(tile, rows, padded, qkv_ref, out_ref, lse_ref, q_t, v_t, out_t):
    scale = HEAD_DIM**-0.5 * LOG2E
    ones = jnp.ones((16, rows), BF16)
    q_t[:, :rows] = qkv_ref[:, :PAIR].T
    if padded > rows:
        q_t[:, rows:] = jnp.zeros((PAIR, padded - rows), BF16)
    values_t = qkv_ref[:, 2 * PAIR :].T
    step = HEAD_DIM + 16
    for head in range(2):
        v_t[head * step : head * step + HEAD_DIM, :] = values_t[
            head * HEAD_DIM : (head + 1) * HEAD_DIM, :
        ]
        v_t[head * step + HEAD_DIM : (head + 1) * step, :] = ones

    def block(index, carry):
        columns = pl.ds(pl.multiple_of(index * tile, tile), tile)
        empty = jnp.zeros((HEAD_DIM, tile), BF16)
        for head in range(2):
            lanes = slice(head * HEAD_DIM, (head + 1) * HEAD_DIM)
            query = q_t[lanes, columns]
            query = jnp.concatenate([query, empty] if head == 0 else [empty, query], axis=0)
            scores = contract(qkv_ref[:, PAIR : 2 * PAIR], query, 1, 0)
            highest = jnp.max(scores, axis=0, keepdims=True) * scale
            expon = jnp.exp2(scores * scale - highest).astype(BF16)
            mixed = contract(v_t[head * step : (head + 1) * step, :], expon, 1, 0)
            total = mixed[HEAD_DIM : HEAD_DIM + 1, :]
            out_t[lanes, columns] = mixed[:HEAD_DIM, :] / total
            lse_ref[head : head + 1, columns] = highest + jnp.log2(total)
        return carry

    lax.fori_loop(0, padded // tile, block, 0)
    out_ref[...] = out_t[...].T[:rows, :].astype(BF16)


def attend(qkv, tile=512):
    rows, width = qkv.shape
    pairs = width // (3 * PAIR)
    padded = -(-rows // tile) * tile
    return pl.pallas_call(
        functools.partial(attend_kernel, tile, rows, padded),
        grid=(pairs,),
        in_specs=[pl.BlockSpec((rows, 3 * PAIR), lambda i: (0, i))],
        out_specs=[
            pl.BlockSpec((rows, PAIR), lambda i: (0, i)),
            pl.BlockSpec((None, 2, padded), lambda i: (i, 0, 0)),
        ],
        out_shape=[
            jax.ShapeDtypeStruct((rows, pairs * PAIR), BF16),
            jax.ShapeDtypeStruct((pairs, 2, padded), F32),
        ],
        scratch_shapes=[
            pltpu.VMEM((PAIR, padded), BF16),
            pltpu.VMEM((PAIR + 32, rows), BF16),
            pltpu.VMEM((PAIR, padded), F32),
        ],
        compiler_params=pltpu.CompilerParams(vmem_limit_bytes=VMEM_LIMIT),
        cost_estimate=pl.CostEstimate(
            flops=16 * rows * rows * PAIR * pairs,
            bytes_accessed=8 * rows * PAIR * pairs,
            transcendentals=2 * rows * rows * pairs,
        ),
        name="attend",
    )(qkv)


def attend_back_kernel(
    tile, rows, padded, qkv_ref, grad_ref, out_ref, lse_ref, dqkv_ref, q_t, g_t, k_t, delta,
    dq_t, dk_t, dv_t,
):
    scale = HEAD_DIM**-0.5
    q_t[:, :rows] = qkv_ref[:, :PAIR].T
    g_t[:, :rows] = grad_ref[...].T
    if padded > rows:
        q_t[:, rows:] = jnp.zeros((PAIR, padded - rows), BF16)
        g_t[:, rows:] = jnp.zeros((PAIR, padded - rows), BF16)
        delta[:, rows:] = jnp.zeros((2, padded - rows), F32)
    k_t[...] = qkv_ref[:, PAIR : 2 * PAIR].T
    product = (grad_ref[...].astype(F32) * out_ref[...].astype(F32)).T
    delta[0:1, :rows] = jnp.sum(product[:HEAD_DIM, :], axis=0, keepdims=True)
    delta[1:2, :rows] = jnp.sum(product[HEAD_DIM:, :], axis=0, keepdims=True)
    dk_t[...] = jnp.zeros_like(dk_t)
    dv_t[...] = jnp.zeros_like(dv_t)

    def block(index, carry):
        columns = pl.ds(pl.multiple_of(index * tile, tile), tile)
        empty = jnp.zeros((HEAD_DIM, tile), BF16)
        for head in range(2):
            lanes = slice(head * HEAD_DIM, (head + 1) * HEAD_DIM)
            query = q_t[lanes, columns]
            grad = g_t[lanes, columns]
            query_pad = jnp.concatenate([query, empty] if head == 0 else [empty, query], axis=0)
            grad_pad = jnp.concatenate([grad, empty] if head == 0 else [empty, grad], axis=0)
            scores = contract(qkv_ref[:, PAIR : 2 * PAIR], query_pad, 1, 0)
            grad_probs = contract(qkv_ref[:, 2 * PAIR :], grad_pad, 1, 0)
            weights = jnp.exp2(scores * (scale * LOG2E) - lse_ref[head : head + 1, columns])
            grad_scores = (weights * (grad_probs - delta[head : head + 1, columns])).astype(BF16)
            dv_t[lanes, :] += contract(grad, weights.astype(BF16), 1, 1)
            dq_t[lanes, columns] = contract(k_t[lanes, :], grad_scores, 1, 0)
            dk_t[lanes, :] += contract(query, grad_scores, 1, 1)
        return carry

    lax.fori_loop(0, padded // tile, block, 0)
    dqkv_ref[:, :PAIR] = (dq_t[...].T[:rows, :] * scale).astype(BF16)
    dqkv_ref[:, PAIR : 2 * PAIR] = (dk_t[...].T * scale).astype(BF16)
    dqkv_ref[:, 2 * PAIR :] = dv_t[...].T.astype(BF16)


def attend_back(qkv, grad, out, lse, tile=256):
    rows, width = qkv.shape
    pairs = width // (3 * PAIR)
    padded = -(-rows // tile) * tile
    return pl.pallas_call(
        functools.partial(attend_back_kernel, tile, rows, padded),
        grid=(pairs,),
        in_specs=[
            pl.BlockSpec((rows, 3 * PAIR), lambda i: (0, i)),
            pl.BlockSpec((rows, PAIR), lambda i: (0, i)),
            pl.BlockSpec((rows, PAIR), lambda i: (0, i)),
            pl.BlockSpec((None, 2, lse.shape[2]), lambda i: (i, 0, 0)),
        ],
        out_specs=pl.BlockSpec((rows, 3 * PAIR), lambda i: (0, i)),
        out_shape=jax.ShapeDtypeStruct((rows, width), BF16),
        scratch_shapes=[
            pltpu.VMEM((PAIR, padded), BF16),
            pltpu.VMEM((PAIR, padded), BF16),
            pltpu.VMEM((PAIR, rows), BF16),
            pltpu.VMEM((2, padded), F32),
            pltpu.VMEM((PAIR, padded), F32),
            pltpu.VMEM((PAIR, rows), F32),
            pltpu.VMEM((PAIR, rows), F32),
        ],
        compiler_params=pltpu.CompilerParams(vmem_limit_bytes=VMEM_LIMIT),
        cost_estimate=pl.CostEstimate(
            flops=40 * rows * rows * PAIR * pairs,
            bytes_accessed=16 * rows * PAIR * pairs,
            transcendentals=2 * rows * rows * pairs,
        ),
        name="attend_back",
    )(qkv, grad, out, lse)


def feed_kernel(
    x_ref, dy_ref, up_ref, bias_ref, down_ref, out_ref, dx_ref, up_grad_ref, bias_grad_ref,
    down_grad_ref, x_t, out_sum, dx_sum, hidden, d_pre, *, chunk,
):
    index = pl.program_id(0)
    rows = x_ref.shape[0]

    @pl.when(index == 0)
    def _():
        x_t[...] = x_ref[...].T
        out_sum[...] = jnp.zeros_like(out_sum)
        dx_sum[...] = jnp.zeros_like(dx_sum)

    bias_grad = jnp.zeros(bias_grad_ref.shape, F32)
    for start in range(0, rows, chunk):
        part = slice(start, start + chunk)
        pre = contract(x_ref[part, :], up_ref[...], 1, 0) + bias_ref[...]
        d_hidden = contract(dy_ref[part, :], down_ref[...], 1, 1)
        share = 0.5 * (1.0 + lax.erf(pre * 0.7071067811865476))
        hidden[part, :] = (pre * share).astype(BF16)
        slope = share + pre * (jnp.exp(-0.5 * pre * pre) * 0.3989422804014327)
        d_low = (d_hidden * slope).astype(BF16)
        d_pre[part, :] = d_low
        bias_grad = bias_grad + jnp.sum(d_low.astype(F32), axis=0, keepdims=True)
        out_sum[part, :] += contract(hidden[part, :], down_ref[...], 1, 0)
        dx_sum[part, :] += contract(d_pre[part, :], up_ref[...], 1, 1)
    bias_grad_ref[...] = bias_grad
    up_grad_ref[...] = contract(x_t[...], d_pre[...], 1, 0).astype(BF16)
    down_grad_ref[...] = contract(hidden[...], dy_ref[...], 0, 0).astype(BF16)

    @pl.when(index == pl.num_programs(0) - 1)
    def _():
        out_ref[...] = out_sum[...].astype(BF16)
        dx_ref[...] = dx_sum[...].astype(BF16)


def feed(x, dy, up, bias, down, tile=512):
    rows, width = x.shape
    hidden = up.shape[1]
    chunk = rows // 2 if rows % 32 == 0 else rows
    whole = pl.BlockSpec((rows, width), lambda j: (0, 0), pipeline_mode=pl.Buffered(1))
    up_spec = pl.BlockSpec((width, tile), lambda j: (0, j))
    bias_spec = pl.BlockSpec((1, tile), lambda j: (0, j))
    down_spec = pl.BlockSpec((tile, width), lambda j: (j, 0))
    return pl.pallas_call(
        functools.partial(feed_kernel, chunk=chunk),
        grid=(hidden // tile,),
        in_specs=[whole, whole, up_spec, bias_spec, down_spec],
        out_specs=[whole, whole, up_spec, bias_spec, down_spec],
        out_shape=[
            jax.ShapeDtypeStruct((rows, width), BF16),
            jax.ShapeDtypeStruct((rows, width), BF16),
            jax.ShapeDtypeStruct((width, hidden), BF16),
            jax.ShapeDtypeStruct((1, hidden), F32),
            jax.ShapeDtypeStruct((hidden, width), BF16),
        ],
        scratch_shapes=[
            pltpu.VMEM((width, rows), BF16),
            pltpu.VMEM((rows, width), F32),
            pltpu.VMEM((rows, width), F32),
            pltpu.VMEM((rows, tile), BF16),
            pltpu.VMEM((rows, tile), BF16),
        ],
        compiler_params=pltpu.CompilerParams(vmem_limit_bytes=VMEM_LIMIT),
        cost_estimate=pl.CostEstimate(
            flops=12 * rows * width * hidden,
            bytes_accessed=8 * rows * width + 8 * width * hidden,
            transcendentals=2 * rows * hidden,
        ),
        name="feed",
    )(x, dy, up, bias, down)


def norm_parts(values, gain, shift):
    average = jnp.mean(values, axis=-1, keepdims=True)
    centred = values - average
    spread = jnp.mean(centred * centred, axis=-1, keepdims=True)
    inverse = lax.rsqrt(spread + EPS)
    normed = centred * inverse
    return (normed * gain + shift, normed, inverse)


def norm_back(grad, normed, inverse, gain):
    scaled = grad * gain
    first_term = jnp.mean(scaled, axis=-1, keepdims=True)
    second_term = jnp.mean(scaled * normed, axis=-1, keepdims=True)
    result = inverse * (scaled - first_term - normed * second_term)
    return (result, jnp.sum(grad * normed, axis=0), jnp.sum(grad, axis=0))


def pick(values, index, axis):
    return lax.dynamic_index_in_dim(values, index, axis, keepdims=False)


def join(own, other, index):
    return jnp.where(index == 0, jnp.stack([own, other]), jnp.stack([other, own]))


def body(
    grp, tokens, query_weight, key_weight, value_weight, query_bias, value_bias, out_weight,
    out_bias, first_gain, first_shift, second_gain, second_shift, up_weight, up_bias,
    down_weight, down_bias, cotangent,
):
    clips, local, width = tokens.shape
    assert clips == 1
    quarter = grp // 2
    core = lax.axis_index("core")
    half = lax.axis_index("half")
    own_rows = width // grp
    set_width = width // grp
    pairs = set_width // PAIR
    hidden = up_weight.shape[1]
    set_hidden = hidden // grp

    there = []
    for b in range(2):
        for h in range(2):
            for q in range(quarter):
                g = h * quarter + q
                source = (b * 2 + h) * quarter + q
                target = ((g % 2) * 2 + b) * quarter + g // 2
                there.append((source, target))
    back = [(target, source) for source, target in there]
    axes = ("core", "half", "gq")

    def swap_half(values):
        return lax.ppermute(values, "half", SWAP)

    def both_halves(values):
        return join(values, swap_half(values), half)

    def spread(values):
        if grp == 2:
            return jnp.concatenate([values, lax.ppermute(values, "core", SWAP)], axis=0)
        return lax.all_gather(values, ("gq", "core"), axis=0, tiled=True)

    def collect(values):
        if grp == 2:
            other = lax.ppermute(values[local:], "core", SWAP)
            return values[:local].astype(F32) + other.astype(F32)
        return lax.psum_scatter(
            values, ("gq", "core"), scatter_dimension=0, tiled=True
        ).astype(F32)

    def set_columns(values):
        parts = values.reshape(values.shape[0], 2, quarter, 2, -1)
        parts = pick(parts, core, 3)
        return parts.transpose(0, 2, 1, 3).reshape(values.shape[0], quarter, -1)

    def all_rows(values):
        if quarter > 1:
            values = lax.all_to_all(values, "gq", split_axis=1, concat_axis=0, tiled=True)
        values = both_halves(values.reshape(-1, values.shape[-1]))
        return values.reshape(-1, values.shape[-1])

    def set_rows(values):
        values = pick(values.reshape(2, -1, values.shape[-1]), core, 0)
        return both_halves(values).reshape(-1, values.shape[-1])

    def set_entries(values):
        parts = values.reshape(2, quarter, 2, -1)
        parts = pick(pick(parts, core, 2), lax.axis_index("gq"), 1)
        return parts.reshape(1, -1)

    vectors = jnp.concatenate(
        [query_bias, value_bias, out_bias, first_gain, first_shift, second_gain, second_shift,
         down_bias, up_bias]
    )
    if quarter > 1:
        vectors = lax.all_gather(vectors, "gq", axis=0)
    vectors = both_halves(vectors).reshape(grp, -1)
    (full_qbias, full_vbias, full_obias, gain_one, shift_one, gain_two, shift_two, full_dbias) = [
        vectors[:, i * own_rows : (i + 1) * own_rows].reshape(-1) for i in range(8)
    ]
    full_ubias = vectors[:, 8 * own_rows :].reshape(-1)

    clip_tokens = lax.ppermute(tokens.reshape(local, width), axes, there)

    parts = [
        set_columns(w).reshape(own_rows, quarter, pairs, PAIR)
        for w in (query_weight, key_weight, value_weight)
    ]
    qkv_weight = all_rows(jnp.stack(parts, axis=3).reshape(own_rows, quarter, 3 * set_width))
    out_set = set_rows(out_weight)
    up_set = all_rows(set_columns(up_weight))
    down_set = set_rows(down_weight)
    grad_out = lax.ppermute(cotangent.reshape(local, width), axes, there)

    zeros = jnp.zeros((1, set_width), F32)
    qkv_bias = jnp.stack(
        [b.reshape(pairs, PAIR) for b in (set_entries(full_qbias), zeros, set_entries(full_vbias))],
        axis=1,
    ).reshape(1, 3 * set_width)

    inputs = clip_tokens.astype(F32)
    first_norm, first_normed, first_inverse = norm_parts(inputs, gain_one, shift_one)
    first = spread(first_norm.astype(BF16))
    qkv = (contract(first, qkv_weight, 1, 0) + qkv_bias).astype(BF16)
    mixed, lse = attend(qkv)
    if grp == 2:
        other = contract(mixed[local:], out_set, 1, 0).astype(BF16)
        other = lax.ppermute(other, "core", SWAP)
        middle = inputs + contract(mixed[:local], out_set, 1, 0) + full_obias
        middle = middle + other.astype(F32)
    else:
        middle = inputs + collect(contract(mixed, out_set, 1, 0).astype(BF16)) + full_obias
    second_norm, second_normed, second_inverse = norm_parts(middle, gain_two, shift_two)
    second = spread(second_norm.astype(BF16))
    grad_all = spread(grad_out)
    feed_out, feed_back, up_grad, up_bias_grad, down_grad = feed(
        second, grad_all, up_set, set_entries(full_ubias), down_set
    )
    result = (middle + collect(feed_out) + full_dbias).astype(BF16)
    layer_out = lax.ppermute(result, axes, back).reshape(1, local, width)

    grad_wide = grad_out.astype(F32)
    grad_second, grad_gain_two, grad_shift_two = norm_back(
        collect(feed_back), second_normed, second_inverse, gain_two
    )
    grad_middle = grad_wide + grad_second
    grad_middle_low = grad_middle.astype(BF16)
    grad_middle_all = spread(grad_middle_low)
    grad_mixed = contract(grad_middle_all, out_set, 1, 1).astype(BF16)
    out_grad = contract(mixed, grad_middle_all, 0, 0).astype(BF16)
    dqkv = attend_back(qkv, grad_mixed, mixed, lse)
    qkv_grad = contract(first, dqkv, 0, 0).astype(BF16)
    grad_first_norm = collect(contract(dqkv, qkv_weight, 1, 1).astype(BF16))
    grad_first, grad_gain_one, grad_shift_one = norm_back(
        grad_first_norm, first_normed, first_inverse, gain_one
    )
    tokens_grad = lax.ppermute(
        (grad_middle + grad_first).astype(BF16), axes, back
    ).reshape(1, local, width)

    def scatter_half(values):
        values = values.reshape(2, -1, values.shape[-1])
        other = swap_half(pick(values, 1 - half, 0))
        return (pick(values, half, 0).astype(F32) + other.astype(F32)).astype(BF16)

    def both_cores(values):
        return join(values, lax.ppermute(values, "core", SWAP), core)

    def finish_columns(values):
        if quarter > 1:
            values = values.reshape(quarter, own_rows, 1, -1)
            values = lax.all_to_all(values, "gq", split_axis=0, concat_axis=2, tiled=True)
        values = values.reshape(own_rows, quarter, -1)
        return both_cores(values).transpose(1, 0, 2, 3)

    def natural_columns(values):
        values = values.reshape(own_rows, 2, quarter, 2, -1)
        return values.transpose(0, 3, 2, 1, 4).reshape(own_rows, -1).astype(F32)

    up_half = scatter_half(up_grad)
    down_half = scatter_half(down_grad)
    up_half, down_half = lax.psum((up_half, down_half), "rz")
    up_weight_grad = natural_columns(finish_columns(up_half))
    down_weight_grad = both_cores(down_half).reshape(-1, width).astype(F32)

    out_half = scatter_half(out_grad)
    qkv_half = scatter_half(qkv_grad)
    out_half, qkv_half, up_half = lax.optimization_barrier((out_half, qkv_half, up_half))
    out_half, qkv_half = lax.psum((out_half, qkv_half), "rz")
    out_weight_grad = both_cores(out_half).reshape(-1, width).astype(F32)
    columns = finish_columns(qkv_half).reshape(own_rows, 2, quarter, pairs, 3, PAIR)
    query_weight_grad, key_weight_grad, value_weight_grad = [
        natural_columns(columns[:, :, :, :, i]) for i in range(3)
    ]

    dqkv_sums = jnp.sum(dqkv.astype(F32), axis=0).reshape(pairs, 3, PAIR)

    def place_entries(values, size):
        parts = values.reshape(2, 1, 1, -1)
        empty = jnp.zeros((2, quarter, 2, size // (2 * grp)), F32)
        zero = jnp.zeros((), core.dtype)
        return lax.dynamic_update_slice(
            empty, parts, (zero, lax.axis_index("gq"), core, zero)
        ).reshape(-1)

    sums = [
        place_entries(dqkv_sums[:, 0], width),
        place_entries(dqkv_sums[:, 2], width),
        jnp.sum(grad_middle_low.astype(F32), axis=0),
        grad_gain_one, grad_shift_one, grad_gain_two, grad_shift_two,
        jnp.sum(grad_wide, axis=0),
    ]
    sums = jnp.concatenate(
        [s.reshape(grp, -1) for s in sums] + [place_entries(up_bias_grad, hidden).reshape(grp, -1)],
        axis=1,
    )
    sums = lax.psum(sums, ("rz", "core", "half", "gq"))
    sums = pick(sums, half * quarter + lax.axis_index("gq"), 0)
    small = [sums[i * own_rows : (i + 1) * own_rows] for i in range(8)]
    return (
        layer_out, tokens_grad, query_weight_grad, key_weight_grad, value_weight_grad,
        small[0], small[1], out_weight_grad, small[2], small[3], small[4], small[5], small[6],
        up_weight_grad, sums[8 * own_rows :], down_weight_grad, small[7],
    )


def solution(mesh):
    rep, grp = mesh.shape["rep"], mesh.shape["grp"]
    split = Mesh(
        mesh.devices.reshape(rep // 2, 2, 2, grp // 2), ("rz", "core", "half", "gq")
    )
    clip = P(("rz", "core"), ("half", "gq"), None)
    matrix = P(("half", "gq"), None)
    vector = P(("half", "gq"))
    return jax.shard_map(
        functools.partial(body, grp),
        mesh=split,
        in_specs=(
            clip, matrix, matrix, matrix, vector, vector, matrix, vector, vector, vector, vector,
            vector, matrix, vector, matrix, vector, clip,
        ),
        out_specs=(
            clip, clip, matrix, matrix, matrix, vector, vector, matrix, vector, vector, vector,
            vector, vector, matrix, vector, matrix, vector,
        ),
        check_vma=False,
    )
```

```python
import functools

import jax
import jax.numpy as jnp
from jax import lax
from jax.experimental import pallas as pl
from jax.experimental.pallas import tpu as pltpu
from jax.sharding import Mesh
from jax.sharding import PartitionSpec as P

HEAD_DIM = 64
PAIR = 2 * HEAD_DIM
EPS = 1e-06
LOG2E = 1.4426950408889634
F32 = jnp.float32
BF16 = jnp.bfloat16
SWAP = [(0, 1), (1, 0)]
VMEM_LIMIT = 62 << 20


def contract(left, right, left_dim, right_dim):
    return lax.dot_general(
        left, right, (((left_dim,), (right_dim,)), ((), ())), preferred_element_type=F32
    )


def attend_kernel(tile, rows, padded, qkv_ref, out_ref, lse_ref, q_t, v_t, out_t):
    scale = HEAD_DIM**-0.5 * LOG2E
    ones = jnp.ones((16, rows), BF16)
    q_t[:, :rows] = qkv_ref[:, :PAIR].T
    if padded > rows:
        q_t[:, rows:] = jnp.zeros((PAIR, padded - rows), BF16)
    values_t = qkv_ref[:, 2 * PAIR :].T
    step = HEAD_DIM + 16
    for head in range(2):
        v_t[head * step : head * step + HEAD_DIM, :] = values_t[
            head * HEAD_DIM : (head + 1) * HEAD_DIM, :
        ]
        v_t[head * step + HEAD_DIM : (head + 1) * step, :] = ones

    def block(index, carry):
        columns = pl.ds(pl.multiple_of(index * tile, tile), tile)
        empty = jnp.zeros((HEAD_DIM, tile), BF16)
        for head in range(2):
            lanes = slice(head * HEAD_DIM, (head + 1) * HEAD_DIM)
            query = q_t[lanes, columns]
            query = jnp.concatenate([query, empty] if head == 0 else [empty, query], axis=0)
            scores = contract(qkv_ref[:, PAIR : 2 * PAIR], query, 1, 0)
            highest = jnp.max(scores, axis=0, keepdims=True) * scale
            expon = jnp.exp2(scores * scale - highest).astype(BF16)
            mixed = contract(v_t[head * step : (head + 1) * step, :], expon, 1, 0)
            total = mixed[HEAD_DIM : HEAD_DIM + 1, :]
            out_t[lanes, columns] = mixed[:HEAD_DIM, :] / total
            lse_ref[head : head + 1, columns] = highest + jnp.log2(total)
        return carry

    lax.fori_loop(0, padded // tile, block, 0)
    out_ref[...] = out_t[...].T[:rows, :].astype(BF16)


def attend(qkv, first_pair, last_pair, kept=None, tile=512):
    rows, width = qkv.shape
    pairs = width // (3 * PAIR)
    padded = -(-rows // tile) * tile
    count = last_pair - first_pair
    kernel = functools.partial(attend_kernel, tile, rows, padded)
    anywhere = pl.BlockSpec(memory_space=pl.ANY)
    return pl.pallas_call(
        kernel if kept is None else lambda ref, a, b, *rest: kernel(ref, *rest),
        grid=(count,),
        in_specs=[pl.BlockSpec((rows, 3 * PAIR), lambda i: (0, i + first_pair))]
        + ([] if kept is None else [anywhere] * 2),
        out_specs=[
            pl.BlockSpec((rows, PAIR), lambda i: (0, i + first_pair)),
            pl.BlockSpec((None, 2, padded), lambda i: (i + first_pair, 0, 0)),
        ],
        out_shape=[
            jax.ShapeDtypeStruct((rows, pairs * PAIR), BF16),
            jax.ShapeDtypeStruct((pairs, 2, padded), F32),
        ],
        scratch_shapes=[
            pltpu.VMEM((PAIR, padded), BF16),
            pltpu.VMEM((PAIR + 32, rows), BF16),
            pltpu.VMEM((PAIR, padded), F32),
        ],
        input_output_aliases={} if kept is None else {1: 0, 2: 1},
        compiler_params=pltpu.CompilerParams(vmem_limit_bytes=VMEM_LIMIT),
        cost_estimate=pl.CostEstimate(
            flops=64 * rows * rows * PAIR * count,
            bytes_accessed=8 * rows * PAIR * count,
            transcendentals=2 * rows * rows * count,
        ),
        name="attend",
    )(qkv, *(() if kept is None else kept))


def attend_back_kernel(
    tile, rows, padded, qkv_ref, grad_ref, out_ref, lse_ref, dqkv_ref, q_t, g_t, k_t, delta,
    dq_t, dk_t, dv_t,
):
    scale = HEAD_DIM**-0.5
    q_t[:, :rows] = qkv_ref[:, :PAIR].T
    g_t[:, :rows] = grad_ref[...].T
    if padded > rows:
        q_t[:, rows:] = jnp.zeros((PAIR, padded - rows), BF16)
        g_t[:, rows:] = jnp.zeros((PAIR, padded - rows), BF16)
        delta[:, rows:] = jnp.zeros((2, padded - rows), F32)
    k_t[...] = qkv_ref[:, PAIR : 2 * PAIR].T
    product = (grad_ref[...].astype(F32) * out_ref[...].astype(F32)).T
    delta[0:1, :rows] = jnp.sum(product[:HEAD_DIM, :], axis=0, keepdims=True)
    delta[1:2, :rows] = jnp.sum(product[HEAD_DIM:, :], axis=0, keepdims=True)
    dk_t[...] = jnp.zeros_like(dk_t)
    dv_t[...] = jnp.zeros_like(dv_t)

    def block(index, carry):
        columns = pl.ds(pl.multiple_of(index * tile, tile), tile)
        empty = jnp.zeros((HEAD_DIM, tile), BF16)
        for head in range(2):
            lanes = slice(head * HEAD_DIM, (head + 1) * HEAD_DIM)
            query = q_t[lanes, columns]
            grad = g_t[lanes, columns]
            query_pad = jnp.concatenate([query, empty] if head == 0 else [empty, query], axis=0)
            grad_pad = jnp.concatenate([grad, empty] if head == 0 else [empty, grad], axis=0)
            scores = contract(qkv_ref[:, PAIR : 2 * PAIR], query_pad, 1, 0)
            grad_probs = contract(qkv_ref[:, 2 * PAIR :], grad_pad, 1, 0)
            weights = jnp.exp2(scores * (scale * LOG2E) - lse_ref[head : head + 1, columns])
            grad_scores = (weights * (grad_probs - delta[head : head + 1, columns])).astype(BF16)
            dv_t[lanes, :] += contract(grad, weights.astype(BF16), 1, 1)
            dq_t[lanes, columns] = contract(k_t[lanes, :], grad_scores, 1, 0)
            dk_t[lanes, :] += contract(query, grad_scores, 1, 1)
        return carry

    lax.fori_loop(0, padded // tile, block, 0)
    dqkv_ref[:, :PAIR] = (dq_t[...].T[:rows, :] * scale).astype(BF16)
    dqkv_ref[:, PAIR : 2 * PAIR] = (dk_t[...].T * scale).astype(BF16)
    dqkv_ref[:, 2 * PAIR :] = dv_t[...].T.astype(BF16)


def attend_back(qkv, grad, out, lse, first_pair, last_pair, tile=256):
    rows, width = qkv.shape
    padded = -(-rows // tile) * tile
    count = last_pair - first_pair
    return pl.pallas_call(
        functools.partial(attend_back_kernel, tile, rows, padded),
        grid=(count,),
        in_specs=[
            pl.BlockSpec((rows, 3 * PAIR), lambda i: (0, i + first_pair)),
            pl.BlockSpec((rows, PAIR), lambda i: (0, i + first_pair)),
            pl.BlockSpec((rows, PAIR), lambda i: (0, i + first_pair)),
            pl.BlockSpec((None, 2, lse.shape[2]), lambda i: (i + first_pair, 0, 0)),
        ],
        out_specs=pl.BlockSpec((rows, 3 * PAIR), lambda i: (0, i)),
        out_shape=jax.ShapeDtypeStruct((rows, 3 * PAIR * count), BF16),
        scratch_shapes=[
            pltpu.VMEM((PAIR, padded), BF16),
            pltpu.VMEM((PAIR, padded), BF16),
            pltpu.VMEM((PAIR, rows), BF16),
            pltpu.VMEM((2, padded), F32),
            pltpu.VMEM((PAIR, padded), F32),
            pltpu.VMEM((PAIR, rows), F32),
            pltpu.VMEM((PAIR, rows), F32),
        ],
        compiler_params=pltpu.CompilerParams(vmem_limit_bytes=VMEM_LIMIT),
        cost_estimate=pl.CostEstimate(
            flops=160 * rows * rows * PAIR * count,
            bytes_accessed=16 * rows * PAIR * count,
            transcendentals=2 * rows * rows * count,
        ),
        name="attend_back",
    )(qkv, grad, out, lse)


def feed_kernel(
    half_ref, *refs, parts, make, chunk,
):
    xs, refs = refs[:parts], refs[parts:]
    dys, refs = refs[:parts], refs[parts:]
    if not make:
        x_t, refs = refs[0], refs[1:]
    up_ref, bias_ref, down_ref, *refs = refs
    hidden_ref, d_pre_ref, up_send, up_keep, down_send, down_keep, bias_grad_ref, *refs = refs
    if make:
        x_t, refs = refs[0], refs[1:]
    x, dy, sems = refs
    index = pl.program_id(0)
    half = half_ref[0]
    rows, width = x.shape
    block = rows // parts
    own = width // 2
    tile = up_ref.shape[1]

    @pl.when(index == 0)
    def _():
        copies = []
        for i in range(parts):
            part = pl.ds(i * block, block)
            copies.append(pltpu.make_async_copy(xs[i], x.at[part], sems.at[i]))
            copies.append(pltpu.make_async_copy(dys[i], dy.at[part], sems.at[parts + i]))
        for copy in copies:
            copy.start()
        for copy in copies:
            copy.wait()
        if make:
            x_t[...] = x[...].T

    bias_grad = jnp.zeros(bias_grad_ref.shape, F32)
    for start in range(0, rows, chunk):
        part = slice(start, start + chunk)
        pre = contract(x[part, :], up_ref[...], 1, 0) + bias_ref[...]
        d_hidden = contract(dy[part, :], down_ref[...], 1, 1)
        share = 0.5 * (1.0 + lax.erf(pre * 0.7071067811865476))
        hidden_ref[part, :] = (pre * share).astype(BF16)
        slope = share + pre * (jnp.exp(-0.5 * pre * pre) * 0.3989422804014327)
        d_low = (d_hidden * slope).astype(BF16)
        d_pre_ref[part, :] = d_low
        bias_grad = bias_grad + jnp.sum(d_low.astype(F32), axis=0, keepdims=True)
    bias_grad_ref[...] = bias_grad
    columns = pl.ds(pl.multiple_of(index * tile, tile), tile)
    mine = pl.ds(pl.multiple_of(half * own, own), own)
    theirs = pl.ds(pl.multiple_of((1 - half) * own, own), own)
    up_keep[:, columns] = contract(x_t[mine, :], d_pre_ref[...], 1, 0).astype(BF16)
    up_send[:, columns] = contract(x_t[theirs, :], d_pre_ref[...], 1, 0).astype(BF16)
    down_grad = contract(hidden_ref[...], dy[...], 0, 0).astype(BF16)

    @pl.when(index == half)
    def _():
        down_keep[...] = down_grad

    @pl.when(index != half)
    def _():
        down_send[...] = down_grad


def feed(half, xs, dys, x_t, up, bias, down):
    parts = len(xs)
    width = xs[0].shape[1]
    rows = sum(part.shape[0] for part in xs)
    hidden = up.shape[1]
    tile = hidden // 2
    make = x_t is None
    chunk = rows // 2 if rows % 32 == 0 else rows
    anywhere = pl.BlockSpec(memory_space=pl.ANY)
    fixed = lambda shape: pl.BlockSpec(shape, lambda j, s: (0, 0), pipeline_mode=pl.Buffered(1))
    across = lambda size: pl.BlockSpec((size, tile), lambda j, s: (0, j))
    out_specs = [across(rows)] * 2 + [fixed((width // 2, hidden))] * 2
    out_specs += [fixed((tile, width))] * 2 + [across(1)]
    out_shape = [
        jax.ShapeDtypeStruct((rows, hidden), BF16),
        jax.ShapeDtypeStruct((rows, hidden), BF16),
        jax.ShapeDtypeStruct((width // 2, hidden), BF16),
        jax.ShapeDtypeStruct((width // 2, hidden), BF16),
        jax.ShapeDtypeStruct((tile, width), BF16),
        jax.ShapeDtypeStruct((tile, width), BF16),
        jax.ShapeDtypeStruct((1, hidden), F32),
    ]
    if make:
        out_specs.append(fixed((width, rows)))
        out_shape.append(jax.ShapeDtypeStruct((width, rows), BF16))
    return pl.pallas_call(
        functools.partial(feed_kernel, parts=parts, make=make, chunk=chunk),
        grid_spec=pltpu.PrefetchScalarGridSpec(
            num_scalar_prefetch=1,
            grid=(2,),
            in_specs=[anywhere] * (2 * parts)
            + ([] if make else [fixed((width, rows))])
            + [across(width), across(1), pl.BlockSpec((tile, width), lambda j, s: (j, 0))],
            out_specs=out_specs,
            scratch_shapes=[
                pltpu.VMEM((rows, width), BF16),
                pltpu.VMEM((rows, width), BF16),
                pltpu.SemaphoreType.DMA((2 * parts,)),
            ],
        ),
        out_shape=out_shape,
        compiler_params=pltpu.CompilerParams(vmem_limit_bytes=VMEM_LIMIT),
        cost_estimate=pl.CostEstimate(
            flops=8 * rows * width * hidden,
            bytes_accessed=8 * rows * width + 8 * width * hidden,
            transcendentals=2 * rows * hidden,
        ),
        name="feed",
    )(half.reshape(1), *xs, *dys, *(() if make else (x_t,)), up, bias, down)


def finish_feed_kernel(core_ref, *refs, ranges, tile):
    owns, refs = refs[: 2 * ranges], refs[2 * ranges :]
    others, (up_out, down_out) = refs[: 2 * ranges], refs[2 * ranges :]
    first = core_ref[0] == 0
    for j in range(ranges):
        for kind in range(2):
            own, other = owns[2 * j + kind][...], others[2 * j + kind][...]
            values = (jnp.where(first, own, other), jnp.where(first, other, own))
            for c in range(2):
                wide = values[c].astype(F32)
                if kind == 1:
                    down_out[c, j] = wide
                    continue
                for h in range(2):
                    start = ((h * 2 + c) * ranges + j) * tile
                    up_out[:, start : start + tile] = wide[:, h * tile : (h + 1) * tile]


def finish_feed(core, owns, others):
    ranges = len(owns) // 2
    rows, columns = owns[0].shape
    tile, width = owns[1].shape
    steps = 4
    up_spec = pl.BlockSpec((rows // steps, columns), lambda i, s: (i, 0))
    down_spec = pl.BlockSpec((tile // steps, width), lambda i, s: (i, 0))
    up, down = pl.pallas_call(
        functools.partial(finish_feed_kernel, ranges=ranges, tile=tile),
        grid_spec=pltpu.PrefetchScalarGridSpec(
            num_scalar_prefetch=1,
            grid=(steps,),
            in_specs=[up_spec, down_spec] * (2 * ranges),
            out_specs=[
                pl.BlockSpec((rows // steps, 2 * ranges * columns), lambda i, s: (i, 0)),
                pl.BlockSpec((2, ranges, tile // steps, width), lambda i, s: (0, 0, i, 0)),
            ],
        ),
        out_shape=[
            jax.ShapeDtypeStruct((rows, 2 * ranges * columns), F32),
            jax.ShapeDtypeStruct((2, ranges, tile, width), F32),
        ],
        compiler_params=pltpu.CompilerParams(vmem_limit_bytes=VMEM_LIMIT),
        name="finish_feed",
    )(core.reshape(1), *owns, *others)
    return up, down.reshape(2 * ranges * tile, width)


def finish_qkv_kernel(core_ref, *refs, pairs):
    owns, others, outs = refs[:2], refs[2:4], refs[4:]
    first = core_ref[0] == 0
    for h in range(2):
        own, other = owns[h][...], others[h][...]
        values = (jnp.where(first, own, other), jnp.where(first, other, own))
        for c in range(2):
            for p in range(pairs):
                for i in range(3):
                    start = (p * 3 + i) * PAIR
                    goal = ((h * 2 + c) * pairs + p) * PAIR
                    outs[i][:, goal : goal + PAIR] = values[c][:, start : start + PAIR].astype(F32)


def finish_qkv(core, owns, others):
    rows, columns = owns[0].shape
    pairs = columns // (3 * PAIR)
    steps = 4
    spec = pl.BlockSpec((rows // steps, columns), lambda i, s: (i, 0))
    return pl.pallas_call(
        functools.partial(finish_qkv_kernel, pairs=pairs),
        grid_spec=pltpu.PrefetchScalarGridSpec(
            num_scalar_prefetch=1,
            grid=(steps,),
            in_specs=[spec] * 4,
            out_specs=[pl.BlockSpec((rows // steps, 4 * pairs * PAIR), lambda i, s: (i, 0))] * 3,
        ),
        out_shape=[jax.ShapeDtypeStruct((rows, 4 * pairs * PAIR), F32)] * 3,
        compiler_params=pltpu.CompilerParams(vmem_limit_bytes=VMEM_LIMIT),
        name="finish_qkv",
    )(core.reshape(1), *owns, *others)


def norm_parts(values, gain, shift):
    average = jnp.mean(values, axis=-1, keepdims=True)
    centred = values - average
    spread = jnp.mean(centred * centred, axis=-1, keepdims=True)
    inverse = lax.rsqrt(spread + EPS)
    normed = centred * inverse
    return (normed * gain + shift, normed, inverse)


def norm_back(grad, normed, inverse, gain):
    scaled = grad * gain
    first_term = jnp.mean(scaled, axis=-1, keepdims=True)
    second_term = jnp.mean(scaled * normed, axis=-1, keepdims=True)
    result = inverse * (scaled - first_term - normed * second_term)
    return (result, jnp.sum(grad * normed, axis=0), jnp.sum(grad, axis=0))


def pick(values, index, axis):
    return lax.dynamic_index_in_dim(values, index, axis, keepdims=False)


def join(own, other, index):
    return jnp.where(index == 0, jnp.stack([own, other]), jnp.stack([other, own]))


def after(values, *earlier):
    return lax.optimization_barrier((values,) + earlier)[0]


def body(
    rep, grp, tokens, query_weight, key_weight, value_weight, query_bias, value_bias, out_weight,
    out_bias, first_gain, first_shift, second_gain, second_shift, up_weight, up_bias,
    down_weight, down_bias, cotangent,
):
    clips, local, width = tokens.shape
    assert clips == 1
    quarter = grp // 2
    ring = rep // 2
    deep = ring // 2
    core = lax.axis_index("core")
    half = lax.axis_index("half")
    gq = lax.axis_index("gq")
    place = lax.axis_index("rz")
    low = place % 2
    high = place // 2
    own_rows = width // grp
    pairs = own_rows // PAIR
    hidden = up_weight.shape[1]
    set_hidden = hidden // grp
    ranges = max(1, set_hidden // width)
    tile = set_hidden // (2 * ranges)

    there = []
    for b in range(2):
        for h in range(2):
            for q in range(quarter):
                g = h * quarter + q
                source = (b * 2 + h) * quarter + q
                target = ((g % 2) * 2 + b) * quarter + g // 2
                if source != target:
                    there.append((source, target))
    back = [(target, source) for source, target in there]
    block = half * quarter + gq
    stays = (block % 2 == core) & (block // 2 == gq) & (half == core)
    axes = ("core", "half", "gq")
    beside = [(i, i ^ 1) for i in range(ring)]

    def move(values, route):
        return jnp.where(stays, values, lax.ppermute(values, axes, route))

    def swap_half(values):
        return lax.ppermute(values, "half", SWAP)

    def swap_core(values):
        return lax.ppermute(values, "core", SWAP)

    def spread(values):
        if grp == 2:
            return [values, swap_core(values)]
        return [lax.all_gather(values, ("gq", "core"), axis=0, tiled=True)]

    def collect(values):
        if grp == 2:
            other = swap_core(values(slice(local, None)).astype(BF16))
            return values(slice(None, local)) + other.astype(F32)
        return lax.psum_scatter(
            values(slice(None)).astype(BF16), ("gq", "core"), scatter_dimension=0, tiled=True
        ).astype(F32)

    def other_half(pieces):
        mine = pick(jnp.stack(pieces), low, 0)
        first = swap_half(mine)
        second = lax.ppermute(first, "rz", beside)
        return first, jnp.where(low == 0, first, second), jnp.where(low == 0, second, first)

    def by_half(own, other):
        return join(own, other, half).reshape(-1, own.shape[-1])

    def set_columns(values, inner=1):
        parts = values.reshape(values.shape[0], 2, quarter, 2, inner, -1)
        return pick(parts, core, 3).transpose(0, 2, 3, 1, 4)

    def gather_rows(values):
        if quarter > 1:
            values = lax.all_to_all(values, "gq", split_axis=1, concat_axis=0, tiled=True)
        return values.reshape(-1, values.shape[-1])

    def set_entries(values, inner=1):
        parts = values.reshape(2, quarter, 2, inner, -1)
        return pick(pick(parts, core, 2), gq, 1).transpose(1, 0, 2).reshape(inner, 1, -1)

    clip_tokens = move(tokens.reshape(local, width), there)
    vectors = jnp.concatenate(
        [query_bias, value_bias, out_bias, first_gain, first_shift, second_gain, second_shift,
         down_bias, up_bias]
    )
    if quarter > 1:
        vectors = lax.all_gather(vectors, "gq", axis=0)
    vectors = join(vectors, swap_half(vectors), half).reshape(grp, -1)
    (full_qbias, full_vbias, full_obias, gain_one, shift_one, gain_two, shift_two, full_dbias) = [
        vectors[:, i * own_rows : (i + 1) * own_rows].reshape(-1) for i in range(8)
    ]
    bias_sets = set_entries(vectors[:, 8 * own_rows :].reshape(-1), ranges)

    parts = [
        set_columns(w).reshape(own_rows, quarter, pairs, PAIR)
        for w in (query_weight, key_weight, value_weight)
    ]
    own_qkv = gather_rows(jnp.stack(parts, axis=3).reshape(own_rows, quarter, 3 * own_rows))
    own_qkv = own_qkv.reshape(2, -1, 3 * own_rows)
    qkv_x, low_rows, high_rows = other_half([own_qkv[0], own_qkv[1]])
    qkv_weight = by_half(
        own_qkv.reshape(-1, 3 * own_rows), jnp.concatenate([low_rows, high_rows], axis=0)
    )
    own_out = pick(out_weight.reshape(2, -1, width), core, 0)
    out_x, low_rows, high_rows = other_half(
        [after(own_out, qkv_x)[: own_rows // 4], own_out[own_rows // 4 :]]
    )
    out_set = by_half(own_out, jnp.concatenate([low_rows, high_rows], axis=0))

    own_up = set_columns(up_weight, ranges)
    own_down = pick(down_weight.reshape(2, ranges, tile, width), core, 0)
    up_sets, down_sets, stages = [], [], [out_x]
    for j in range(ranges):
        up_part = gather_rows(own_up[:, :, j].reshape(own_rows, quarter, 2 * tile))
        down_part = own_down[j]
        if up_part.shape == down_part.shape:
            stage, other_up, other_down = other_half([after(up_part, stages[-1]), down_part])
        else:
            stage, other_up = swap_half(after(up_part, stages[-1])), None
            other_up, other_down = stage, swap_half(down_part)
        stages.append(stage)
        up_sets.append(by_half(up_part, other_up))
        down_sets.append(by_half(down_part, other_down))
    grad_out = move(after(cotangent.reshape(local, width), stages[1]), there)

    zeros = jnp.zeros((1, own_rows), F32)
    qkv_bias = jnp.stack(
        [
            b.reshape(pairs, PAIR)
            for b in (set_entries(full_qbias), zeros, set_entries(full_vbias))
        ],
        axis=1,
    ).reshape(1, 3 * own_rows)

    inputs = clip_tokens.astype(F32)
    first_norm, first_normed, first_inverse = norm_parts(inputs, gain_one, shift_one)
    first = jnp.concatenate(spread(first_norm.astype(BF16)), axis=0)
    qkv = (contract(first, qkv_weight, 1, 0) + qkv_bias).astype(BF16)
    if pairs > 1:
        kept = attend(qkv, 0, pairs // 2)
        mixed, lse = attend(qkv, pairs // 2, pairs, kept)
    else:
        mixed, lse = attend(qkv, 0, pairs)
    middle = collect(lambda rows: contract(mixed[rows], out_set, 1, 0)) + inputs + full_obias
    second_norm, second_normed, second_inverse = norm_parts(middle, gain_two, shift_two)
    seconds = spread(second_norm.astype(BF16))
    grads_out = spread(grad_out)
    x_t = None
    feeds = []
    for j in range(ranges):
        outs = feed(
            half, seconds, grads_out, x_t, up_sets[j],
            bias_sets[j] if j == 0 else after(bias_sets[j], feeds[-1][6]), down_sets[j],
        )
        x_t = outs[7] if j == 0 else x_t
        feeds.append(outs)

    def reduce_ring(pair):
        send, keep = pair
        total = keep.astype(F32) + lax.ppermute(send, "rz", beside).astype(F32)
        total = total.astype(BF16).reshape(deep, -1, keep.shape[-1])
        shifts = range(1, deep)

        def route(shift):
            return [(i, (i + 2 * shift) % ring) for i in range(ring)]

        pieces = [
            lax.ppermute(pick(total, (high + s) % deep, 0), "rz", route(s)) for s in shifts
        ]
        piece = pick(total, high, 0).astype(F32)
        for other in pieces:
            piece = piece + other.astype(F32)
        piece = piece.astype(BF16)
        gathered = [piece] + [lax.ppermute(piece, "rz", route(s)) for s in shifts]
        whole = jnp.stack(
            [
                functools.reduce(
                    lambda rest, s: jnp.where((high - s) % deep == i, gathered[s], rest),
                    shifts,
                    piece,
                )
                for i in range(deep)
            ]
        ).reshape(keep.shape)
        return whole, lax.ppermute(whole, "rz", beside)

    def reduce_parts(parts):
        stacked = jnp.stack(parts)
        own, other = reduce_ring((pick(stacked, 1 - low, 0), pick(stacked, low, 0)))
        return jnp.where(low == 0, own, other), jnp.where(low == 0, other, own)

    def add_half(keep, send):
        return (keep.astype(F32) + swap_half(send).astype(F32)).astype(BF16)

    def reduce_rows(values):
        size = values.shape[0]
        if size % (16 * ring):
            return lax.psum(values, "rz")
        return jnp.concatenate(reduce_parts([values[: size // 2], values[size // 2 :]]), axis=0)

    def scatter_half(values):
        values = values.reshape(2, -1, values.shape[-1])
        return add_half(pick(values, half, 0), pick(values, 1 - half, 0))

    sums_feed = []
    for outs in feeds:
        up_part, down_part = add_half(outs[3], outs[2]), add_half(outs[5], outs[4])
        if up_part.shape == down_part.shape:
            sums_feed.extend(reduce_parts([up_part, down_part]))
        else:
            sums_feed.extend([reduce_rows(up_part), reduce_rows(down_part)])

    grad_wide = grad_out.astype(F32)
    grad_second = collect(
        lambda rows: functools.reduce(
            jnp.add, [contract(feeds[j][1][rows], up_sets[j], 1, 1) for j in range(ranges)]
        )
    )
    grad_second, grad_gain_two, grad_shift_two = norm_back(
        grad_second, second_normed, second_inverse, gain_two
    )
    grad_middle = grad_wide + grad_second
    grad_middle_low = grad_middle.astype(BF16)
    grad_middle_all = jnp.concatenate(spread(grad_middle_low), axis=0)
    grad_mixed = contract(grad_middle_all, out_set, 1, 1).astype(BF16)
    out_half = reduce_rows(scatter_half(contract(mixed, grad_middle_all, 0, 0).astype(BF16)))
    spans = [(0, pairs // 2), (pairs // 2, pairs)] if pairs > 1 else [(0, pairs)]
    dqkvs, qkv_halves = [], []
    for begin, end in spans:
        gate = lse if not dqkvs else after(lse, qkv_halves[-1])
        dqkvs.append(attend_back(qkv, grad_mixed, mixed, gate, begin, end))
        qkv_halves.append(contract(first, dqkvs[-1], 0, 0).astype(BF16))
    qkv_halves = [reduce_rows(scatter_half(values)) for values in qkv_halves]

    result = collect(
        lambda rows: functools.reduce(
            jnp.add, [contract(feeds[j][0][rows], down_sets[j], 1, 0) for j in range(ranges)]
        )
    )
    result = (middle + result + full_dbias).astype(BF16)
    layer_out = move(result, back).reshape(1, local, width)

    def weight_of(span):
        return qkv_weight[:, span[0] * 3 * PAIR : span[1] * 3 * PAIR]

    grad_first_norm = collect(
        lambda rows: functools.reduce(
            jnp.add,
            [contract(d[rows], weight_of(span), 1, 1) for d, span in zip(dqkvs, spans)],
        )
    )
    grad_first, grad_gain_one, grad_shift_one = norm_back(
        grad_first_norm, first_normed, first_inverse, gain_one
    )
    tokens_grad = move((grad_middle + grad_first).astype(BF16), back).reshape(1, local, width)

    out_weight_grad = join(out_half, swap_core(out_half), core).reshape(-1, width).astype(F32)
    if grp == 2:
        up_weight_grad, down_weight_grad = finish_feed(
            core, sums_feed, [swap_core(values) for values in sums_feed]
        )
        query_weight_grad, key_weight_grad, value_weight_grad = finish_qkv(
            core, qkv_halves, [swap_core(values) for values in qkv_halves]
        )
    else:

        def finish_columns(values):
            values = values.reshape(quarter, own_rows, 1, -1)
            values = lax.all_to_all(values, "gq", split_axis=0, concat_axis=2, tiled=True)
            values = values.reshape(own_rows, quarter, -1)
            return join(values, swap_core(values), core).transpose(1, 0, 2, 3)

        def natural_columns(values, inner=1):
            values = values.reshape(own_rows, 2, quarter, inner, 2, -1)
            return values.transpose(0, 4, 2, 1, 3, 5).reshape(own_rows, -1).astype(F32)

        ups = jnp.stack([finish_columns(values) for values in sums_feed[::2]], axis=3)
        up_weight_grad = natural_columns(ups, ranges)
        downs = jnp.stack(sums_feed[1::2])
        down_weight_grad = join(downs, swap_core(downs), core).reshape(-1, width).astype(F32)
        columns = jnp.concatenate([finish_columns(values) for values in qkv_halves], axis=3)
        columns = columns.reshape(own_rows, 2, quarter, pairs, 3, PAIR)
        query_weight_grad, key_weight_grad, value_weight_grad = [
            natural_columns(columns[:, :, :, :, i]) for i in range(3)
        ]

    def place_entries(values, inner=1):
        values = values.reshape(inner, 2, 1, 1, -1).transpose(1, 2, 3, 0, 4)
        shape = (2, quarter, 2) + values.shape[3:]
        zero = jnp.zeros((), core.dtype)
        return lax.dynamic_update_slice(
            jnp.zeros(shape, F32), values, (zero, gq, core, zero, zero)
        ).reshape(grp, -1)

    dqkv_sums = jnp.concatenate([jnp.sum(d.astype(F32), axis=0) for d in dqkvs])
    dqkv_sums = dqkv_sums.reshape(pairs, 3, PAIR)
    sums = [
        place_entries(dqkv_sums[:, 0]),
        place_entries(dqkv_sums[:, 2]),
        jnp.sum(grad_middle_low.astype(F32), axis=0),
        grad_gain_one, grad_shift_one, grad_gain_two, grad_shift_two,
        jnp.sum(grad_wide, axis=0),
        place_entries(jnp.stack([outs[6] for outs in feeds]), ranges),
    ]
    sums = jnp.concatenate([s.reshape(grp, -1) for s in sums], axis=1)
    if grp == 2 and ring & (ring - 1) == 0:
        sums = sums + swap_core(sums)
        sums = pick(sums, half, 0) + swap_half(pick(sums, 1 - half, 0))
        step = 1
        while step < ring:
            sums = sums + lax.ppermute(sums, "rz", [(i, i ^ step) for i in range(ring)])
            step *= 2
    else:
        sums = lax.psum(sums, ("rz", "core", "half", "gq"))
        sums = pick(sums, half * quarter + gq, 0)
    small = [sums[i * own_rows : (i + 1) * own_rows] for i in range(8)]
    return (
        layer_out, tokens_grad, query_weight_grad, key_weight_grad, value_weight_grad,
        small[0], small[1], out_weight_grad, small[2], small[3], small[4], small[5], small[6],
        up_weight_grad, sums[8 * own_rows :], down_weight_grad, small[7],
    )


def solution(mesh):
    rep, grp = mesh.shape["rep"], mesh.shape["grp"]
    split = Mesh(
        mesh.devices.reshape(rep // 2, 2, 2, grp // 2), ("rz", "core", "half", "gq")
    )
    clip = P(("rz", "core"), ("half", "gq"), None)
    matrix = P(("half", "gq"), None)
    vector = P(("half", "gq"))
    return jax.shard_map(
        functools.partial(body, rep, grp),
        mesh=split,
        in_specs=(
            clip, matrix, matrix, matrix, vector, vector, matrix, vector, vector, vector, vector,
            vector, matrix, vector, matrix, vector, clip,
        ),
        out_specs=(
            clip, clip, matrix, matrix, matrix, vector, vector, matrix, vector, vector, vector,
            vector, vector, matrix, vector, matrix, vector,
        ),
        check_vma=False,
    )
```

```python
import functools

import jax
import jax.numpy as jnp
from jax import lax
from jax.experimental import pallas as pl
from jax.experimental.pallas import tpu as pltpu
from jax.sharding import Mesh
from jax.sharding import PartitionSpec as P

HEAD_DIM = 64
PAIR = 2 * HEAD_DIM
EPS = 1e-06
LOG2E = 1.4426950408889634
F32 = jnp.float32
BF16 = jnp.bfloat16
SWAP = [(0, 1), (1, 0)]
VMEM_LIMIT = 62 << 20


def contract(left, right, left_dim, right_dim):
    return lax.dot_general(
        left, right, (((left_dim,), (right_dim,)), ((), ())), preferred_element_type=F32
    )


def attend_kernel(tile, rows, padded, qkv_ref, out_ref, lse_ref, q_t, v_t, out_t):
    scale = HEAD_DIM**-0.5 * LOG2E
    ones = jnp.ones((16, rows), BF16)
    q_t[:, :rows] = qkv_ref[:, :PAIR].T
    if padded > rows:
        q_t[:, rows:] = jnp.zeros((PAIR, padded - rows), BF16)
    values_t = qkv_ref[:, 2 * PAIR :].T
    step = HEAD_DIM + 16
    for head in range(2):
        v_t[head * step : head * step + HEAD_DIM, :] = values_t[
            head * HEAD_DIM : (head + 1) * HEAD_DIM, :
        ]
        v_t[head * step + HEAD_DIM : (head + 1) * step, :] = ones

    def block(index, carry):
        columns = pl.ds(pl.multiple_of(index * tile, tile), tile)
        empty = jnp.zeros((HEAD_DIM, tile), BF16)
        for head in range(2):
            lanes = slice(head * HEAD_DIM, (head + 1) * HEAD_DIM)
            query = q_t[lanes, columns]
            query = jnp.concatenate([query, empty] if head == 0 else [empty, query], axis=0)
            scores = contract(qkv_ref[:, PAIR : 2 * PAIR], query, 1, 0)
            highest = jnp.max(scores, axis=0, keepdims=True) * scale
            expon = jnp.exp2(scores * scale - highest).astype(BF16)
            mixed = contract(v_t[head * step : (head + 1) * step, :], expon, 1, 0)
            total = mixed[HEAD_DIM : HEAD_DIM + 1, :]
            out_t[lanes, columns] = mixed[:HEAD_DIM, :] / total
            lse_ref[head : head + 1, columns] = highest + jnp.log2(total)
        return carry

    lax.fori_loop(0, padded // tile, block, 0)
    out_ref[...] = out_t[...].T[:rows, :].astype(BF16)


def attend(qkv, first_pair, last_pair, kept=None, tile=512):
    rows, width = qkv.shape
    pairs = width // (3 * PAIR)
    padded = -(-rows // tile) * tile
    count = last_pair - first_pair
    kernel = functools.partial(attend_kernel, tile, rows, padded)
    anywhere = pl.BlockSpec(memory_space=pl.ANY)
    return pl.pallas_call(
        kernel if kept is None else lambda ref, a, b, *rest: kernel(ref, *rest),
        grid=(count,),
        in_specs=[pl.BlockSpec((rows, 3 * PAIR), lambda i: (0, i + first_pair))]
        + ([] if kept is None else [anywhere] * 2),
        out_specs=[
            pl.BlockSpec((rows, PAIR), lambda i: (0, i + first_pair)),
            pl.BlockSpec((None, 2, padded), lambda i: (i + first_pair, 0, 0)),
        ],
        out_shape=[
            jax.ShapeDtypeStruct((rows, pairs * PAIR), BF16),
            jax.ShapeDtypeStruct((pairs, 2, padded), F32),
        ],
        scratch_shapes=[
            pltpu.VMEM((PAIR, padded), BF16),
            pltpu.VMEM((PAIR + 32, rows), BF16),
            pltpu.VMEM((PAIR, padded), F32),
        ],
        input_output_aliases={} if kept is None else {1: 0, 2: 1},
        compiler_params=pltpu.CompilerParams(vmem_limit_bytes=VMEM_LIMIT),
        cost_estimate=pl.CostEstimate(
            flops=64 * rows * rows * PAIR * count,
            bytes_accessed=8 * rows * PAIR * count,
            transcendentals=2 * rows * rows * count,
        ),
        name="attend",
    )(qkv, *(() if kept is None else kept))


def attend_back_kernel(
    tile, rows, padded, s_ref, qkv_ref, grad_ref, out_ref, lse_ref, first_ref, dqkv_ref, send_ref,
    keep_ref, sums_ref, q_t, g_t, k_t, delta, dq_t, dk_t, dv_t, all_t,
):
    scale = HEAD_DIM**-0.5
    q_t[:, :rows] = qkv_ref[:, :PAIR].T
    g_t[:, :rows] = grad_ref[...].T
    if padded > rows:
        q_t[:, rows:] = jnp.zeros((PAIR, padded - rows), BF16)
        g_t[:, rows:] = jnp.zeros((PAIR, padded - rows), BF16)
        delta[:, rows:] = jnp.zeros((2, padded - rows), F32)
    k_t[...] = qkv_ref[:, PAIR : 2 * PAIR].T
    product = (grad_ref[...].astype(F32) * out_ref[...].astype(F32)).T
    delta[0:1, :rows] = jnp.sum(product[:HEAD_DIM, :], axis=0, keepdims=True)
    delta[1:2, :rows] = jnp.sum(product[HEAD_DIM:, :], axis=0, keepdims=True)
    dk_t[...] = jnp.zeros_like(dk_t)
    dv_t[...] = jnp.zeros_like(dv_t)

    def block(index, carry):
        columns = pl.ds(pl.multiple_of(index * tile, tile), tile)
        empty = jnp.zeros((HEAD_DIM, tile), BF16)
        for head in range(2):
            lanes = slice(head * HEAD_DIM, (head + 1) * HEAD_DIM)
            query = q_t[lanes, columns]
            grad = g_t[lanes, columns]
            query_pad = jnp.concatenate([query, empty] if head == 0 else [empty, query], axis=0)
            grad_pad = jnp.concatenate([grad, empty] if head == 0 else [empty, grad], axis=0)
            scores = contract(qkv_ref[:, PAIR : 2 * PAIR], query_pad, 1, 0)
            grad_probs = contract(qkv_ref[:, 2 * PAIR :], grad_pad, 1, 0)
            weights = jnp.exp2(scores * (scale * LOG2E) - lse_ref[head : head + 1, columns])
            grad_scores = (weights * (grad_probs - delta[head : head + 1, columns])).astype(BF16)
            dv_t[lanes, :] += contract(grad, weights.astype(BF16), 1, 1)
            dq_t[lanes, columns] = contract(k_t[lanes, :], grad_scores, 1, 0)
            dk_t[lanes, :] += contract(query, grad_scores, 1, 1)
        return carry

    lax.fori_loop(0, padded // tile, block, 0)
    all_t[:PAIR, :] = (dq_t[:, :rows] * scale).astype(BF16)
    all_t[PAIR : 2 * PAIR, :] = (dk_t[...] * scale).astype(BF16)
    all_t[2 * PAIR :, :] = dv_t[...].astype(BF16)
    for part in range(3):
        lanes = slice(part * PAIR, (part + 1) * PAIR)
        dqkv_ref[:, lanes] = all_t[lanes, :].T
    sums_ref[...] = contract(jnp.ones((8, rows), BF16), all_t[...], 1, 1)
    own = first_ref.shape[1] // 2
    for h in range(2):
        grad = contract(all_t[...], first_ref[:, h * own : (h + 1) * own], 1, 0).astype(BF16)

        @pl.when(s_ref[0] == h)
        def _():
            keep_ref[...] = grad

        @pl.when(s_ref[0] != h)
        def _():
            send_ref[...] = grad


def attend_back(scal, qkv, grad, out, lse, first, first_pair, last_pair, tile=256):
    rows, full = qkv.shape
    width = first.shape[1]
    padded = -(-rows // tile) * tile
    count = last_pair - first_pair
    return pl.pallas_call(
        functools.partial(attend_back_kernel, tile, rows, padded),
        grid_spec=pltpu.PrefetchScalarGridSpec(
            num_scalar_prefetch=1,
            grid=(count,),
            in_specs=[
                pl.BlockSpec((rows, 3 * PAIR), lambda i, s: (0, i + first_pair)),
                pl.BlockSpec((rows, PAIR), lambda i, s: (0, i + first_pair)),
                pl.BlockSpec((rows, PAIR), lambda i, s: (0, i + first_pair)),
                pl.BlockSpec((None, 2, lse.shape[2]), lambda i, s: (i + first_pair, 0, 0)),
                pl.BlockSpec((rows, width), lambda i, s: (0, 0), pipeline_mode=pl.Buffered(1)),
            ],
            out_specs=[
                pl.BlockSpec((rows, 3 * PAIR), lambda i, s: (0, i)),
                pl.BlockSpec((3 * PAIR, width // 2), lambda i, s: (i, 0)),
                pl.BlockSpec((3 * PAIR, width // 2), lambda i, s: (i, 0)),
                pl.BlockSpec((8, 3 * PAIR), lambda i, s: (0, i)),
            ],
            scratch_shapes=[
                pltpu.VMEM((PAIR, padded), BF16),
                pltpu.VMEM((PAIR, padded), BF16),
                pltpu.VMEM((PAIR, rows), BF16),
                pltpu.VMEM((2, padded), F32),
                pltpu.VMEM((PAIR, padded), F32),
                pltpu.VMEM((PAIR, rows), F32),
                pltpu.VMEM((PAIR, rows), F32),
                pltpu.VMEM((3 * PAIR, rows), BF16),
            ],
        ),
        out_shape=[
            jax.ShapeDtypeStruct((rows, 3 * PAIR * count), BF16),
            jax.ShapeDtypeStruct((3 * PAIR * count, width // 2), BF16),
            jax.ShapeDtypeStruct((3 * PAIR * count, width // 2), BF16),
            jax.ShapeDtypeStruct((8, 3 * PAIR * count), F32),
        ],
        compiler_params=pltpu.CompilerParams(vmem_limit_bytes=VMEM_LIMIT),
        cost_estimate=pl.CostEstimate(
            flops=160 * rows * rows * PAIR * count,
            bytes_accessed=16 * rows * PAIR * count,
            transcendentals=2 * rows * rows * count,
        ),
        name="attend_back",
    )(scal, qkv, grad, out, lse, first)


def feed_kernel(
    s_ref, x_own, x_other, dy_own, dy_other, *refs, make,
):
    if not make:
        x_t, refs = refs[0], refs[1:]
    up_ref, down_ref, piece, beside, bias_ref, *refs = refs
    hidden_ref, d_pre_ref, up_send, up_keep, down_send, down_keep, bias_grad_ref, *refs = refs
    up_full, down_full, *refs = refs
    if make:
        x_t, refs = refs[0], refs[1:]
    x, dy, sems = refs
    index = pl.program_id(0)
    half = s_ref[0]
    even = s_ref[1] == 0
    rows, width = x.shape
    block = rows // 2
    own = width // 2
    tile = up_ref.shape[1]
    columns = pl.ds(pl.multiple_of(index * tile, tile), tile)
    mine = pl.ds(pl.multiple_of(half * own, own), own)
    theirs = pl.ds(pl.multiple_of((1 - half) * own, own), own)

    @pl.when(index == 0)
    def _():
        copies = []
        for i, ref in enumerate((x_own, x_other)):
            copies.append(pltpu.make_async_copy(ref, x.at[pl.ds(i * block, block)], sems.at[i]))
        for i, ref in enumerate((dy_own, dy_other)):
            copies.append(
                pltpu.make_async_copy(ref, dy.at[pl.ds(i * block, block)], sems.at[2 + i])
            )
        for copy in copies:
            copy.start()
        for copy in copies:
            copy.wait()
        if make:
            x_t[...] = x[...].T

    up_full[mine, :] = up_ref[...]
    down_full[...] = down_ref[...]

    @pl.when(even)
    def _():
        up_full[theirs, :] = piece[:, columns]

    @pl.when(jnp.logical_not(even))
    def _():
        up_full[theirs, :] = beside[:, columns]

    @pl.when((index != half) & even)
    def _():
        down_full[...] = beside[...]

    @pl.when((index != half) & jnp.logical_not(even))
    def _():
        down_full[...] = piece[...]

    bias_grad = jnp.zeros(bias_grad_ref.shape, F32)
    for start in range(0, rows, block):
        part = slice(start, start + block)
        pre = contract(x[part, :], up_full[...], 1, 0) + bias_ref[...]
        d_hidden = contract(dy[part, :], down_full[...], 1, 1)
        share = 0.5 * (1.0 + lax.erf(pre * 0.7071067811865476))
        hidden_ref[part, :] = (pre * share).astype(BF16)
        slope = share + pre * (jnp.exp(-0.5 * pre * pre) * 0.3989422804014327)
        d_low = (d_hidden * slope).astype(BF16)
        d_pre_ref[part, :] = d_low
        bias_grad = bias_grad + jnp.sum(d_low.astype(F32), axis=0, keepdims=True)
    bias_grad_ref[...] = bias_grad
    up_keep[:, columns] = contract(x_t[mine, :], d_pre_ref[...], 1, 0).astype(BF16)
    up_send[:, columns] = contract(x_t[theirs, :], d_pre_ref[...], 1, 0).astype(BF16)
    down_grad = contract(hidden_ref[...], dy[...], 0, 0).astype(BF16)

    @pl.when(index == half)
    def _():
        down_keep[...] = down_grad

    @pl.when(index != half)
    def _():
        down_send[...] = down_grad


def feed(scal, seconds, grads, x_t, up, down, piece, beside, bias, j, ranges):
    local, width = seconds[0].shape
    rows = 2 * local
    tile = down.shape[0] // (2 * ranges)
    hidden = 2 * tile
    make = x_t is None
    anywhere = pl.BlockSpec(memory_space=pl.ANY)

    def fixed(*shape):
        return pl.BlockSpec(shape, lambda t, s: (0, 0), pipeline_mode=pl.Buffered(1))

    def across(size):
        return pl.BlockSpec((size, tile), lambda t, s: (0, t))

    shape = jax.ShapeDtypeStruct
    out_specs = [across(rows)] * 2 + [fixed(width // 2, hidden)] * 2 + [fixed(tile, width)] * 2
    out_specs += [across(1), across(width), pl.BlockSpec((tile, width), lambda t, s: (t, 0))]
    out_shape = [shape((rows, hidden), BF16)] * 2 + [shape((width // 2, hidden), BF16)] * 2
    out_shape += [shape((tile, width), BF16)] * 2
    out_shape += [shape((1, hidden), F32), shape((width, hidden), BF16), shape((hidden, width), BF16)]
    if make:
        out_specs.append(fixed(width, rows))
        out_shape.append(shape((width, rows), BF16))
    return pl.pallas_call(
        functools.partial(feed_kernel, make=make),
        grid_spec=pltpu.PrefetchScalarGridSpec(
            num_scalar_prefetch=1,
            grid=(2,),
            in_specs=[anywhere] * 4
            + ([] if make else [fixed(width, rows)])
            + [
                pl.BlockSpec((width // 2, tile), lambda t, s: (0, (t * 2 + s[2]) * ranges + j)),
                pl.BlockSpec((tile, width), lambda t, s: (s[2] * ranges + j, 0)),
                fixed(width // 2, hidden),
                fixed(tile, width),
                across(1),
            ],
            out_specs=out_specs,
            scratch_shapes=[
                pltpu.VMEM((rows, width), BF16),
                pltpu.VMEM((rows, width), BF16),
                pltpu.SemaphoreType.DMA((4,)),
            ],
        ),
        out_shape=out_shape,
        compiler_params=pltpu.CompilerParams(vmem_limit_bytes=VMEM_LIMIT),
        cost_estimate=pl.CostEstimate(
            flops=16 * rows * width * hidden,
            bytes_accessed=8 * rows * width + 8 * width * hidden,
            transcendentals=2 * rows * hidden,
        ),
        name="feed",
    )(scal, *seconds, *grads, *(() if make else (x_t,)), up, down, piece, beside, bias)


def run(kernel, name, scal, grid, in_specs, out_specs, out_shape, args, flops=0, scratch=()):
    moved = sum(a.size * a.dtype.itemsize for a in args)
    return pl.pallas_call(
        kernel,
        grid_spec=pltpu.PrefetchScalarGridSpec(
            num_scalar_prefetch=1,
            grid=grid,
            in_specs=in_specs,
            out_specs=out_specs,
            scratch_shapes=scratch,
        ),
        out_shape=out_shape,
        compiler_params=pltpu.CompilerParams(vmem_limit_bytes=VMEM_LIMIT),
        cost_estimate=pl.CostEstimate(flops=flops, bytes_accessed=2 * moved, transcendentals=0),
        name=name,
    )(scal, *args)


def spec(shape, index):
    return pl.BlockSpec(shape, index)


def held(*shape):
    return pl.BlockSpec(shape, lambda i, s: (0,) * len(shape), pipeline_mode=pl.Buffered(1))


def struct(*shape, dtype=BF16):
    return jax.ShapeDtypeStruct(shape, dtype)


def pack_qkv(scal, weights):
    rows, width = weights[0].shape
    pairs = width // (2 * PAIR)
    per = pairs // 2

    def kernel(s_ref, q_ref, k_ref, v_ref, own_ref, mine_ref):
        for i, ref in enumerate((q_ref, k_ref, v_ref)):
            own_ref[:, i * PAIR : (i + 1) * PAIR] = ref[...]
        start = pl.multiple_of(s_ref[1] * (rows // 2), rows // 2)
        mine_ref[...] = own_ref[pl.ds(start, rows // 2), :]

    block = spec((rows, PAIR), lambda p, s: (0, ((p // per) * 2 + s[2]) * per + p % per))
    return run(
        kernel, "pack_qkv", scal, (pairs,), [block] * 3,
        [
            spec((rows, 3 * PAIR), lambda p, s: (0, p)),
            spec((rows // 2, 3 * PAIR), lambda p, s: (0, p)),
        ],
        [struct(rows, 3 * PAIR * pairs), struct(rows // 2, 3 * PAIR * pairs)],
        weights,
    )


def pack_feed(scal, up, down, j, ranges):
    rows, hidden = up.shape
    tile = hidden // (4 * ranges)
    columns = down.shape[1] // 2

    def kernel(s_ref, up_ref, down_ref, out_ref):
        out_ref[...] = jnp.where(s_ref[1] == 0, up_ref[...], down_ref[...])

    return run(
        kernel, "pack_feed", scal, (2,),
        [
            spec((rows, tile), lambda t, s: (0, (t * 2 + s[2]) * ranges + j)),
            spec((tile, columns), lambda t, s: (s[2] * ranges + j, t)),
        ],
        spec((rows, tile), lambda t, s: (0, t)), struct(rows, 2 * tile), (up, down),
    )


def normalize(values):
    centred = values - jnp.mean(values, axis=-1, keepdims=True)
    spread = jnp.mean(centred * centred, axis=-1, keepdims=True)
    inverse = lax.rsqrt(spread + EPS)
    return centred * inverse, inverse


def first_norm(scal, tokens, received, gain, shift):
    rows, width = tokens.shape
    step = rows // 2

    def kernel(s_ref, t_ref, r_ref, gain_ref, shift_ref, x_ref, first_ref):
        x = jnp.where(s_ref[3] == 1, t_ref[...], r_ref[...])
        x_ref[...] = x
        normed, _ = normalize(x.astype(F32))
        first_ref[...] = (normed * gain_ref[...] + shift_ref[...]).astype(BF16)

    block = spec((step, width), lambda i, s: (i, 0))
    return run(
        kernel, "first_norm", scal, (2,), [block, block, held(1, width), held(1, width)],
        [block, block], [struct(rows, width)] * 2, (tokens, received, gain, shift),
    )


def project(scal, firsts, own, piece, beside, bias):
    local, width = firsts[0].shape
    rows, total = 2 * local, own.shape[1]
    block = 3 * PAIR
    half_rows, quarter_rows = width // 2, width // 4

    def kernel(
        s_ref, mine_ref, theirs_ref, own_ref, piece_ref, beside_ref, bias_ref, qkv_ref, w_ref,
        all_ref, sems,
    ):
        @pl.when(pl.program_id(0) == 0)
        def _():
            copies = [
                pltpu.make_async_copy(ref, all_ref.at[pl.ds(i * local, local)], sems.at[i])
                for i, ref in enumerate((mine_ref, theirs_ref))
            ]
            for copy in copies:
                copy.start()
            for copy in copies:
                copy.wait()

        half, low = s_ref[0], s_ref[1]
        other = (1 - half) * half_rows
        w_ref[pl.ds(pl.multiple_of(half * half_rows, half_rows), half_rows), :] = own_ref[...]
        start = pl.multiple_of(other + low * quarter_rows, quarter_rows)
        w_ref[pl.ds(start, quarter_rows), :] = piece_ref[...]
        start = pl.multiple_of(other + (1 - low) * quarter_rows, quarter_rows)
        w_ref[pl.ds(start, quarter_rows), :] = beside_ref[...]
        qkv_ref[...] = (contract(all_ref[...], w_ref[...], 1, 0) + bias_ref[...]).astype(BF16)

    def columns(size):
        return spec((size, block), lambda p, s: (0, p))

    anywhere = pl.BlockSpec(memory_space=pl.ANY)
    return run(
        kernel, "project", scal, (total // block,),
        [anywhere] * 2
        + [columns(half_rows), columns(quarter_rows), columns(quarter_rows), columns(1)],
        [columns(rows), columns(width), held(rows, width)],
        [struct(rows, total), struct(width, total), struct(rows, width)],
        (*firsts, own, piece, beside, bias), flops=2 * rows * width * total,
        scratch=[pltpu.SemaphoreType.DMA((2,))],
    )


def out_other(scal, mixed, weight, piece, beside):
    rows, set_width = mixed.shape
    local, width = rows // 2, weight.shape[1]
    block, small = set_width // 2, set_width // 4

    def kernel(s_ref, mixed_ref, own_ref, piece_ref, beside_ref, out_ref, set_ref):
        half, low = s_ref[0], s_ref[1]
        other = (1 - half) * block
        set_ref[pl.ds(pl.multiple_of(half * block, block), block), :] = own_ref[...]
        set_ref[pl.ds(pl.multiple_of(other + low * small, small), small), :] = piece_ref[...]
        start = pl.multiple_of(other + (1 - low) * small, small)
        set_ref[pl.ds(start, small), :] = beside_ref[...]
        out_ref[...] = contract(mixed_ref[...], set_ref[...], 1, 0).astype(BF16)

    return run(
        kernel, "out_other", scal, (1,),
        [
            spec((local, set_width), lambda i, s: (1, 0)),
            spec((block, width), lambda i, s: (s[2], 0)),
            held(small, width), held(small, width),
        ],
        [held(local, width), held(set_width, width)],
        [struct(local, width), struct(set_width, width)],
        (mixed, weight, piece, beside), flops=2 * local * set_width * width,
    )


def second_norm(scal, mixed, out_set, x, received, bias, gain, shift):
    rows, set_width = mixed.shape
    local, width = x.shape
    step = local // 2

    def kernel(
        s_ref, mixed_ref, w_ref, x_ref, r_ref, bias_ref, gain_ref, shift_ref, mid_ref, second_ref
    ):
        middle = contract(mixed_ref[...], w_ref[...], 1, 0) + r_ref[...].astype(F32)
        middle = middle + x_ref[...].astype(F32) + bias_ref[...]
        mid_ref[...] = middle
        normed, _ = normalize(middle)
        second_ref[...] = (normed * gain_ref[...] + shift_ref[...]).astype(BF16)

    block = spec((step, width), lambda i, s: (i, 0))
    return run(
        kernel, "second_norm", scal, (2,),
        [spec((step, set_width), lambda i, s: (i, 0)), held(set_width, width), block, block]
        + [held(1, width)] * 3,
        [block, block], [struct(local, width, dtype=F32), struct(local, width)],
        (mixed, out_set, x, received, bias, gain, shift), flops=2 * local * set_width * width,
    )


def other_rows(scal, lefts, rights, name):
    rows = lefts[0].shape[0]
    width = rights[0].shape[0]
    local = rows // 2
    count = len(lefts)
    step = width // 4

    def kernel(s_ref, *refs):
        total = contract(refs[0][...], refs[count][...], 1, 1)
        for j in range(1, count):
            total = total + contract(refs[j][...], refs[count + j][...], 1, 1)
        refs[-1][...] = total.astype(BF16)

    def fixed(size):
        return pl.BlockSpec((local, size), lambda i, s: (1, 0), pipeline_mode=pl.Buffered(1))

    return run(
        kernel, name, scal, (4,),
        [fixed(a.shape[1]) for a in lefts]
        + [spec((step, a.shape[1]), lambda i, s: (i, 0)) for a in rights],
        spec((local, step), lambda i, s: (0, i)), struct(local, width), (*lefts, *rights),
        flops=sum(2 * local * a.shape[1] * width for a in lefts),
    )


def norm_back_rows(grad, normed, inverse, gain):
    scaled = grad * gain
    first_term = jnp.mean(scaled, axis=-1, keepdims=True)
    second_term = jnp.mean(scaled * normed, axis=-1, keepdims=True)
    return inverse * (scaled - first_term - normed * second_term)


def column_sums(refs, values):
    @pl.when(pl.program_id(0) == 0)
    def _():
        refs[...] = jnp.zeros_like(refs)

    for i, value in enumerate(values):
        refs[i : i + 1, :] += jnp.sum(value, axis=0, keepdims=True)


def second_back(scal, d_pres, ups, received, middle, dy, gain):
    local, width = middle.shape
    step = local // 2
    count = len(d_pres)

    def kernel(s_ref, *refs):
        r_ref, mid_ref, dy_ref, gain_ref, wide_ref, low_ref, sums_ref = refs[2 * count :]
        grad = r_ref[...].astype(F32)
        for j in range(count):
            grad = grad + contract(refs[j][...], refs[count + j][...], 1, 1)
        normed, inverse = normalize(mid_ref[...])
        dy_wide = dy_ref[...].astype(F32)
        wide = dy_wide + norm_back_rows(grad, normed, inverse, gain_ref[...])
        low = wide.astype(BF16)
        wide_ref[...] = wide
        low_ref[...] = low
        column_sums(sums_ref, (grad * normed, grad, dy_wide, low.astype(F32)))

    block = spec((step, width), lambda i, s: (i, 0))
    return run(
        kernel, "second_back", scal, (2,),
        [spec((step, a.shape[1]), lambda i, s: (i, 0)) for a in d_pres]
        + [held(*a.shape) for a in ups] + [block] * 3 + [held(1, width)],
        [block, block, held(8, width)],
        [struct(local, width, dtype=F32), struct(local, width), struct(8, width, dtype=F32)],
        (*d_pres, *ups, received, middle, dy, gain),
        flops=sum(2 * local * a.shape[1] * width for a in d_pres),
    )


def mixed_back(scal, lows, out_set, mixed):
    local, width = lows[0].shape
    rows, set_width = mixed.shape
    block = set_width // 2

    def kernel(
        s_ref, mine_ref, theirs_ref, w_ref, mixed_ref, d_ref, send_ref, keep_ref, low, sems
    ):
        @pl.when(pl.program_id(0) == 0)
        def _():
            copies = [
                pltpu.make_async_copy(ref, low.at[pl.ds(i * local, local)], sems.at[i])
                for i, ref in enumerate((mine_ref, theirs_ref))
            ]
            for copy in copies:
                copy.start()
            for copy in copies:
                copy.wait()

        d_ref[...] = contract(low[...], w_ref[...], 1, 1).astype(BF16)
        grad = contract(mixed_ref[...], low[...], 0, 0).astype(BF16)

        @pl.when(pl.program_id(0) == s_ref[0])
        def _():
            keep_ref[...] = grad

        @pl.when(pl.program_id(0) != s_ref[0])
        def _():
            send_ref[...] = grad

    anywhere = pl.BlockSpec(memory_space=pl.ANY)
    across = spec((rows, block), lambda t, s: (0, t))
    return run(
        kernel, "mixed_back", scal, (2,),
        [anywhere] * 2 + [spec((block, width), lambda t, s: (t, 0)), across],
        [across, held(block, width), held(block, width)],
        [struct(rows, set_width), struct(block, width), struct(block, width)],
        (*lows, out_set, mixed), flops=4 * rows * set_width * width,
        scratch=[pltpu.VMEM((rows, width), BF16), pltpu.SemaphoreType.DMA((2,))],
    )


def first_back(scal, dqkvs, weights, received, x, wide, gain):
    local, width = x.shape
    step = local // 2
    count = len(dqkvs)

    def kernel(s_ref, *refs):
        r_ref, x_ref, wide_ref, gain_ref, out_ref, sums_ref = refs[2 * count :]
        grad = r_ref[...].astype(F32)
        for j in range(count):
            grad = grad + contract(refs[j][...], refs[count + j][...], 1, 1)
        normed, inverse = normalize(x_ref[...].astype(F32))
        total = wide_ref[...] + norm_back_rows(grad, normed, inverse, gain_ref[...])
        out_ref[...] = total.astype(BF16)
        column_sums(sums_ref, (grad * normed, grad))

    block = spec((step, width), lambda i, s: (i, 0))
    return run(
        kernel, "first_back", scal, (2,),
        [spec((step, a.shape[1]), lambda i, s: (i, 0)) for a in dqkvs]
        + [
            pl.BlockSpec((width, a.shape[1]), functools.partial(lambda j, i, s: (0, j), j),
                         pipeline_mode=pl.Buffered(1))
            for j, a in enumerate(dqkvs)
        ]
        + [block] * 3 + [held(1, width)],
        [block, held(8, width)],
        [struct(local, width), struct(8, width, dtype=F32)],
        (*dqkvs, *([weights] * count), received, x, wide, gain),
        flops=sum(2 * local * a.shape[1] * width for a in dqkvs),
    )


def first_other(scal, dqkvs, weights):
    rows = dqkvs[0].shape[0]
    width = weights.shape[0]
    local = rows // 2
    count = len(dqkvs)
    step = width // 4

    def kernel(s_ref, *refs):
        total = contract(refs[0][...], refs[count][...], 1, 1)
        for j in range(1, count):
            total = total + contract(refs[j][...], refs[count + j][...], 1, 1)
        refs[-1][...] = total.astype(BF16)

    return run(
        kernel, "first_other", scal, (4,),
        [
            pl.BlockSpec((local, a.shape[1]), lambda i, s: (1, 0), pipeline_mode=pl.Buffered(1))
            for a in dqkvs
        ]
        + [
            pl.BlockSpec((step, a.shape[1]), functools.partial(lambda j, i, s: (i, j), j))
            for j, a in enumerate(dqkvs)
        ],
        spec((local, step), lambda i, s: (0, i)), struct(local, width),
        (*dqkvs, *([weights] * count)),
        flops=sum(2 * local * a.shape[1] * width for a in dqkvs),
    )


def layer_other(scal, hiddens, downs):
    rows = hiddens[0].shape[0]
    width = downs[0].shape[1]
    local = rows // 2
    count = len(hiddens)
    step = width // 4

    def kernel(s_ref, *refs):
        total = contract(refs[0][...], refs[count][...], 1, 0)
        for j in range(1, count):
            total = total + contract(refs[j][...], refs[count + j][...], 1, 0)
        refs[-1][...] = total.astype(BF16)

    return run(
        kernel, "layer_other", scal, (4,),
        [
            pl.BlockSpec((local, a.shape[1]), lambda i, s: (1, 0), pipeline_mode=pl.Buffered(1))
            for a in hiddens
        ]
        + [spec((a.shape[0], step), lambda i, s: (0, i)) for a in downs],
        spec((local, step), lambda i, s: (0, i)), struct(local, width), (*hiddens, *downs),
        flops=sum(2 * local * a.shape[1] * width for a in hiddens),
    )


def layer_own(scal, hiddens, downs, received, middle, bias):
    local, width = middle.shape
    count = len(hiddens)
    step = width // 4

    def kernel(s_ref, *refs):
        r_ref, mid_ref, bias_ref, out_ref = refs[2 * count :]
        total = mid_ref[...] + r_ref[...].astype(F32) + bias_ref[...]
        for j in range(count):
            total = total + contract(refs[j][...], refs[count + j][...], 1, 0)
        out_ref[...] = total.astype(BF16)

    across = spec((local, step), lambda i, s: (0, i))
    return run(
        kernel, "layer_own", scal, (4,),
        [
            pl.BlockSpec((local, a.shape[1]), lambda i, s: (0, 0), pipeline_mode=pl.Buffered(1))
            for a in hiddens
        ]
        + [spec((a.shape[0], step), lambda i, s: (0, i)) for a in downs]
        + [across, across, spec((1, step), lambda i, s: (0, i))],
        across, struct(local, width), (*hiddens, *downs, received, middle, bias),
        flops=sum(2 * local * a.shape[1] * width for a in hiddens),
    )


def finish_feed_kernel(core_ref, *refs, ranges, tile):
    owns, refs = refs[: 2 * ranges], refs[2 * ranges :]
    others, (up_out, down_out) = refs[: 2 * ranges], refs[2 * ranges :]
    first = core_ref[0] == 0
    for j in range(ranges):
        for kind in range(2):
            own, other = owns[2 * j + kind][...], others[2 * j + kind][...]
            values = (jnp.where(first, own, other), jnp.where(first, other, own))
            for c in range(2):
                wide = values[c].astype(F32)
                if kind == 1:
                    down_out[c, j] = wide
                    continue
                for h in range(2):
                    start = ((h * 2 + c) * ranges + j) * tile
                    up_out[:, start : start + tile] = wide[:, h * tile : (h + 1) * tile]


def finish_feed(core, owns, others):
    ranges = len(owns) // 2
    rows, columns = owns[0].shape
    tile, width = owns[1].shape
    steps = 4
    up_spec = pl.BlockSpec((rows // steps, columns), lambda i, s: (i, 0))
    down_spec = pl.BlockSpec((tile // steps, width), lambda i, s: (i, 0))
    up, down = pl.pallas_call(
        functools.partial(finish_feed_kernel, ranges=ranges, tile=tile),
        grid_spec=pltpu.PrefetchScalarGridSpec(
            num_scalar_prefetch=1,
            grid=(steps,),
            in_specs=[up_spec, down_spec] * (2 * ranges),
            out_specs=[
                pl.BlockSpec((rows // steps, 2 * ranges * columns), lambda i, s: (i, 0)),
                pl.BlockSpec((2, ranges, tile // steps, width), lambda i, s: (0, 0, i, 0)),
            ],
        ),
        out_shape=[
            jax.ShapeDtypeStruct((rows, 2 * ranges * columns), F32),
            jax.ShapeDtypeStruct((2, ranges, tile, width), F32),
        ],
        compiler_params=pltpu.CompilerParams(vmem_limit_bytes=VMEM_LIMIT),
        name="finish_feed",
    )(core.reshape(1), *owns, *others)
    return up, down.reshape(2 * ranges * tile, width)


def finish_qkv_kernel(core_ref, *refs, pairs):
    outs = refs[-3:]
    count = (len(refs) - 3) // 2
    owns, others = refs[:count], refs[count : 2 * count]
    first = core_ref[0] == 0
    per = pairs // count
    half_pairs = pairs // 2
    for g in range(count):
        own, other = owns[g][...], others[g][...]
        values = (jnp.where(first, own, other), jnp.where(first, other, own))
        for c in range(2):
            wide = values[c].astype(F32).T
            for q in range(per):
                pair = g * per + q
                h, p = pair // half_pairs, pair % half_pairs
                goal = ((h * 2 + c) * half_pairs + p) * PAIR
                for i in range(3):
                    start = (q * 3 + i) * PAIR
                    outs[i][:, goal : goal + PAIR] = wide[:, start : start + PAIR]


def finish_qkv(core, owns, others):
    columns, rows = owns[0].shape
    pairs = len(owns) * columns // (3 * PAIR)
    steps = 4
    block = pl.BlockSpec((columns, rows // steps), lambda i, s: (0, i))
    return pl.pallas_call(
        functools.partial(finish_qkv_kernel, pairs=pairs),
        grid_spec=pltpu.PrefetchScalarGridSpec(
            num_scalar_prefetch=1,
            grid=(steps,),
            in_specs=[block] * (2 * len(owns)),
            out_specs=[pl.BlockSpec((rows // steps, 2 * pairs * PAIR), lambda i, s: (i, 0))] * 3,
        ),
        out_shape=[jax.ShapeDtypeStruct((rows, 2 * pairs * PAIR), F32)] * 3,
        compiler_params=pltpu.CompilerParams(vmem_limit_bytes=VMEM_LIMIT),
        name="finish_qkv",
    )(core.reshape(1), *owns, *others)


def wide_back_kernel(
    tile, rows, padded, qkv_ref, grad_ref, out_ref, lse_ref, dqkv_ref, q_t, g_t, k_t, delta,
    dq_t, dk_t, dv_t,
):
    scale = HEAD_DIM**-0.5
    q_t[:, :rows] = qkv_ref[:, :PAIR].T
    g_t[:, :rows] = grad_ref[...].T
    if padded > rows:
        q_t[:, rows:] = jnp.zeros((PAIR, padded - rows), BF16)
        g_t[:, rows:] = jnp.zeros((PAIR, padded - rows), BF16)
        delta[:, rows:] = jnp.zeros((2, padded - rows), F32)
    k_t[...] = qkv_ref[:, PAIR : 2 * PAIR].T
    product = (grad_ref[...].astype(F32) * out_ref[...].astype(F32)).T
    delta[0:1, :rows] = jnp.sum(product[:HEAD_DIM, :], axis=0, keepdims=True)
    delta[1:2, :rows] = jnp.sum(product[HEAD_DIM:, :], axis=0, keepdims=True)
    dk_t[...] = jnp.zeros_like(dk_t)
    dv_t[...] = jnp.zeros_like(dv_t)

    def block(index, carry):
        columns = pl.ds(pl.multiple_of(index * tile, tile), tile)
        empty = jnp.zeros((HEAD_DIM, tile), BF16)
        for head in range(2):
            lanes = slice(head * HEAD_DIM, (head + 1) * HEAD_DIM)
            query = q_t[lanes, columns]
            grad = g_t[lanes, columns]
            query_pad = jnp.concatenate([query, empty] if head == 0 else [empty, query], axis=0)
            grad_pad = jnp.concatenate([grad, empty] if head == 0 else [empty, grad], axis=0)
            scores = contract(qkv_ref[:, PAIR : 2 * PAIR], query_pad, 1, 0)
            grad_probs = contract(qkv_ref[:, 2 * PAIR :], grad_pad, 1, 0)
            weights = jnp.exp2(scores * (scale * LOG2E) - lse_ref[head : head + 1, columns])
            grad_scores = (weights * (grad_probs - delta[head : head + 1, columns])).astype(BF16)
            dv_t[lanes, :] += contract(grad, weights.astype(BF16), 1, 1)
            dq_t[lanes, columns] = contract(k_t[lanes, :], grad_scores, 1, 0)
            dk_t[lanes, :] += contract(query, grad_scores, 1, 1)
        return carry

    lax.fori_loop(0, padded // tile, block, 0)
    dqkv_ref[:, :PAIR] = (dq_t[...].T[:rows, :] * scale).astype(BF16)
    dqkv_ref[:, PAIR : 2 * PAIR] = (dk_t[...].T * scale).astype(BF16)
    dqkv_ref[:, 2 * PAIR :] = dv_t[...].T.astype(BF16)


def wide_back(qkv, grad, out, lse, first_pair, last_pair, tile=256):
    rows, width = qkv.shape
    padded = -(-rows // tile) * tile
    count = last_pair - first_pair
    return pl.pallas_call(
        functools.partial(wide_back_kernel, tile, rows, padded),
        grid=(count,),
        in_specs=[
            pl.BlockSpec((rows, 3 * PAIR), lambda i: (0, i + first_pair)),
            pl.BlockSpec((rows, PAIR), lambda i: (0, i + first_pair)),
            pl.BlockSpec((rows, PAIR), lambda i: (0, i + first_pair)),
            pl.BlockSpec((None, 2, lse.shape[2]), lambda i: (i + first_pair, 0, 0)),
        ],
        out_specs=pl.BlockSpec((rows, 3 * PAIR), lambda i: (0, i)),
        out_shape=jax.ShapeDtypeStruct((rows, 3 * PAIR * count), BF16),
        scratch_shapes=[
            pltpu.VMEM((PAIR, padded), BF16),
            pltpu.VMEM((PAIR, padded), BF16),
            pltpu.VMEM((PAIR, rows), BF16),
            pltpu.VMEM((2, padded), F32),
            pltpu.VMEM((PAIR, padded), F32),
            pltpu.VMEM((PAIR, rows), F32),
            pltpu.VMEM((PAIR, rows), F32),
        ],
        compiler_params=pltpu.CompilerParams(vmem_limit_bytes=VMEM_LIMIT),
        cost_estimate=pl.CostEstimate(
            flops=160 * rows * rows * PAIR * count,
            bytes_accessed=16 * rows * PAIR * count,
            transcendentals=2 * rows * rows * count,
        ),
        name="wide_back",
    )(qkv, grad, out, lse)


def wide_feed_kernel(
    half_ref, *refs, parts, make, chunk,
):
    xs, refs = refs[:parts], refs[parts:]
    dys, refs = refs[:parts], refs[parts:]
    if not make:
        x_t, refs = refs[0], refs[1:]
    up_ref, bias_ref, down_ref, *refs = refs
    hidden_ref, d_pre_ref, up_send, up_keep, down_send, down_keep, bias_grad_ref, *refs = refs
    if make:
        x_t, refs = refs[0], refs[1:]
    x, dy, sems = refs
    index = pl.program_id(0)
    half = half_ref[0]
    rows, width = x.shape
    block = rows // parts
    own = width // 2
    tile = up_ref.shape[1]

    @pl.when(index == 0)
    def _():
        copies = []
        for i in range(parts):
            part = pl.ds(i * block, block)
            copies.append(pltpu.make_async_copy(xs[i], x.at[part], sems.at[i]))
            copies.append(pltpu.make_async_copy(dys[i], dy.at[part], sems.at[parts + i]))
        for copy in copies:
            copy.start()
        for copy in copies:
            copy.wait()
        if make:
            x_t[...] = x[...].T

    bias_grad = jnp.zeros(bias_grad_ref.shape, F32)
    for start in range(0, rows, chunk):
        part = slice(start, start + chunk)
        pre = contract(x[part, :], up_ref[...], 1, 0) + bias_ref[...]
        d_hidden = contract(dy[part, :], down_ref[...], 1, 1)
        share = 0.5 * (1.0 + lax.erf(pre * 0.7071067811865476))
        hidden_ref[part, :] = (pre * share).astype(BF16)
        slope = share + pre * (jnp.exp(-0.5 * pre * pre) * 0.3989422804014327)
        d_low = (d_hidden * slope).astype(BF16)
        d_pre_ref[part, :] = d_low
        bias_grad = bias_grad + jnp.sum(d_low.astype(F32), axis=0, keepdims=True)
    bias_grad_ref[...] = bias_grad
    columns = pl.ds(pl.multiple_of(index * tile, tile), tile)
    mine = pl.ds(pl.multiple_of(half * own, own), own)
    theirs = pl.ds(pl.multiple_of((1 - half) * own, own), own)
    up_keep[:, columns] = contract(x_t[mine, :], d_pre_ref[...], 1, 0).astype(BF16)
    up_send[:, columns] = contract(x_t[theirs, :], d_pre_ref[...], 1, 0).astype(BF16)
    down_grad = contract(hidden_ref[...], dy[...], 0, 0).astype(BF16)

    @pl.when(index == half)
    def _():
        down_keep[...] = down_grad

    @pl.when(index != half)
    def _():
        down_send[...] = down_grad


def wide_feed(half, xs, dys, x_t, up, bias, down):
    parts = len(xs)
    width = xs[0].shape[1]
    rows = sum(part.shape[0] for part in xs)
    hidden = up.shape[1]
    tile = hidden // 2
    make = x_t is None
    chunk = rows // 2 if rows % 32 == 0 else rows
    anywhere = pl.BlockSpec(memory_space=pl.ANY)
    fixed = lambda shape: pl.BlockSpec(shape, lambda j, s: (0, 0), pipeline_mode=pl.Buffered(1))
    across = lambda size: pl.BlockSpec((size, tile), lambda j, s: (0, j))
    out_specs = [across(rows)] * 2 + [fixed((width // 2, hidden))] * 2
    out_specs += [fixed((tile, width))] * 2 + [across(1)]
    out_shape = [
        jax.ShapeDtypeStruct((rows, hidden), BF16),
        jax.ShapeDtypeStruct((rows, hidden), BF16),
        jax.ShapeDtypeStruct((width // 2, hidden), BF16),
        jax.ShapeDtypeStruct((width // 2, hidden), BF16),
        jax.ShapeDtypeStruct((tile, width), BF16),
        jax.ShapeDtypeStruct((tile, width), BF16),
        jax.ShapeDtypeStruct((1, hidden), F32),
    ]
    if make:
        out_specs.append(fixed((width, rows)))
        out_shape.append(jax.ShapeDtypeStruct((width, rows), BF16))
    return pl.pallas_call(
        functools.partial(wide_feed_kernel, parts=parts, make=make, chunk=chunk),
        grid_spec=pltpu.PrefetchScalarGridSpec(
            num_scalar_prefetch=1,
            grid=(2,),
            in_specs=[anywhere] * (2 * parts)
            + ([] if make else [fixed((width, rows))])
            + [across(width), across(1), pl.BlockSpec((tile, width), lambda j, s: (j, 0))],
            out_specs=out_specs,
            scratch_shapes=[
                pltpu.VMEM((rows, width), BF16),
                pltpu.VMEM((rows, width), BF16),
                pltpu.SemaphoreType.DMA((2 * parts,)),
            ],
        ),
        out_shape=out_shape,
        compiler_params=pltpu.CompilerParams(vmem_limit_bytes=VMEM_LIMIT),
        cost_estimate=pl.CostEstimate(
            flops=8 * rows * width * hidden,
            bytes_accessed=8 * rows * width + 8 * width * hidden,
            transcendentals=2 * rows * hidden,
        ),
        name="wide_feed",
    )(half.reshape(1), *xs, *dys, *(() if make else (x_t,)), up, bias, down)


def norm_parts(values, gain, shift):
    average = jnp.mean(values, axis=-1, keepdims=True)
    centred = values - average
    spread = jnp.mean(centred * centred, axis=-1, keepdims=True)
    inverse = lax.rsqrt(spread + EPS)
    normed = centred * inverse
    return (normed * gain + shift, normed, inverse)


def norm_back(grad, normed, inverse, gain):
    scaled = grad * gain
    first_term = jnp.mean(scaled, axis=-1, keepdims=True)
    second_term = jnp.mean(scaled * normed, axis=-1, keepdims=True)
    result = inverse * (scaled - first_term - normed * second_term)
    return (result, jnp.sum(grad * normed, axis=0), jnp.sum(grad, axis=0))


def pick(values, index, axis):
    return lax.dynamic_index_in_dim(values, index, axis, keepdims=False)


def join(own, other, index):
    return jnp.where(index == 0, jnp.stack([own, other]), jnp.stack([other, own]))


def after(values, *earlier):
    return lax.optimization_barrier((values,) + earlier)[0]


def wide_body(
    rep, grp, tokens, query_weight, key_weight, value_weight, query_bias, value_bias, out_weight,
    out_bias, first_gain, first_shift, second_gain, second_shift, up_weight, up_bias,
    down_weight, down_bias, cotangent,
):
    clips, local, width = tokens.shape
    assert clips == 1
    quarter = grp // 2
    ring = rep // 2
    deep = ring // 2
    core = lax.axis_index("core")
    half = lax.axis_index("half")
    gq = lax.axis_index("gq")
    place = lax.axis_index("rz")
    low = place % 2
    high = place // 2
    own_rows = width // grp
    pairs = own_rows // PAIR
    hidden = up_weight.shape[1]
    set_hidden = hidden // grp
    ranges = max(1, set_hidden // width)
    tile = set_hidden // (2 * ranges)

    there = []
    for b in range(2):
        for h in range(2):
            for q in range(quarter):
                g = h * quarter + q
                source = (b * 2 + h) * quarter + q
                target = ((g % 2) * 2 + b) * quarter + g // 2
                if source != target:
                    there.append((source, target))
    back = [(target, source) for source, target in there]
    block = half * quarter + gq
    stays = (block % 2 == core) & (block // 2 == gq) & (half == core)
    axes = ("core", "half", "gq")
    beside = [(i, i ^ 1) for i in range(ring)]

    def move(values, route):
        return jnp.where(stays, values, lax.ppermute(values, axes, route))

    def swap_half(values):
        return lax.ppermute(values, "half", SWAP)

    def swap_core(values):
        return lax.ppermute(values, "core", SWAP)

    def spread(values):
        if grp == 2:
            return [values, swap_core(values)]
        return [lax.all_gather(values, ("gq", "core"), axis=0, tiled=True)]

    def collect(values):
        if grp == 2:
            other = swap_core(values(slice(local, None)).astype(BF16))
            return values(slice(None, local)) + other.astype(F32)
        return lax.psum_scatter(
            values(slice(None)).astype(BF16), ("gq", "core"), scatter_dimension=0, tiled=True
        ).astype(F32)

    def other_half(pieces):
        mine = pick(jnp.stack(pieces), low, 0)
        first = swap_half(mine)
        second = lax.ppermute(first, "rz", beside)
        return first, jnp.where(low == 0, first, second), jnp.where(low == 0, second, first)

    def by_half(own, other):
        return join(own, other, half).reshape(-1, own.shape[-1])

    def set_columns(values, inner=1):
        parts = values.reshape(values.shape[0], 2, quarter, 2, inner, -1)
        return pick(parts, core, 3).transpose(0, 2, 3, 1, 4)

    def gather_rows(values):
        if quarter > 1:
            values = lax.all_to_all(values, "gq", split_axis=1, concat_axis=0, tiled=True)
        return values.reshape(-1, values.shape[-1])

    def set_entries(values, inner=1):
        parts = values.reshape(2, quarter, 2, inner, -1)
        return pick(pick(parts, core, 2), gq, 1).transpose(1, 0, 2).reshape(inner, 1, -1)

    clip_tokens = move(tokens.reshape(local, width), there)
    vectors = jnp.concatenate(
        [query_bias, value_bias, out_bias, first_gain, first_shift, second_gain, second_shift,
         down_bias, up_bias]
    )
    if quarter > 1:
        vectors = lax.all_gather(vectors, "gq", axis=0)
    vectors = join(vectors, swap_half(vectors), half).reshape(grp, -1)
    (full_qbias, full_vbias, full_obias, gain_one, shift_one, gain_two, shift_two, full_dbias) = [
        vectors[:, i * own_rows : (i + 1) * own_rows].reshape(-1) for i in range(8)
    ]
    bias_sets = set_entries(vectors[:, 8 * own_rows :].reshape(-1), ranges)

    parts = [
        set_columns(w).reshape(own_rows, quarter, pairs, PAIR)
        for w in (query_weight, key_weight, value_weight)
    ]
    own_qkv = gather_rows(jnp.stack(parts, axis=3).reshape(own_rows, quarter, 3 * own_rows))
    own_qkv = own_qkv.reshape(2, -1, 3 * own_rows)
    qkv_x, low_rows, high_rows = other_half([own_qkv[0], own_qkv[1]])
    qkv_weight = by_half(
        own_qkv.reshape(-1, 3 * own_rows), jnp.concatenate([low_rows, high_rows], axis=0)
    )
    own_out = pick(out_weight.reshape(2, -1, width), core, 0)
    out_x, low_rows, high_rows = other_half(
        [after(own_out, qkv_x)[: own_rows // 4], own_out[own_rows // 4 :]]
    )
    out_set = by_half(own_out, jnp.concatenate([low_rows, high_rows], axis=0))

    own_up = set_columns(up_weight, ranges)
    own_down = pick(down_weight.reshape(2, ranges, tile, width), core, 0)
    up_sets, down_sets, stages = [], [], [out_x]
    for j in range(ranges):
        up_part = gather_rows(own_up[:, :, j].reshape(own_rows, quarter, 2 * tile))
        down_part = own_down[j]
        if up_part.shape == down_part.shape:
            stage, other_up, other_down = other_half([after(up_part, stages[-1]), down_part])
        else:
            stage, other_up = swap_half(after(up_part, stages[-1])), None
            other_up, other_down = stage, swap_half(down_part)
        stages.append(stage)
        up_sets.append(by_half(up_part, other_up))
        down_sets.append(by_half(down_part, other_down))
    grad_out = move(after(cotangent.reshape(local, width), stages[1]), there)

    zeros = jnp.zeros((1, own_rows), F32)
    qkv_bias = jnp.stack(
        [
            b.reshape(pairs, PAIR)
            for b in (set_entries(full_qbias), zeros, set_entries(full_vbias))
        ],
        axis=1,
    ).reshape(1, 3 * own_rows)

    inputs = clip_tokens.astype(F32)
    first_norm, first_normed, first_inverse = norm_parts(inputs, gain_one, shift_one)
    first = jnp.concatenate(spread(first_norm.astype(BF16)), axis=0)
    qkv = (contract(first, qkv_weight, 1, 0) + qkv_bias).astype(BF16)
    if pairs > 1:
        kept = attend(qkv, 0, pairs // 2)
        mixed, lse = attend(qkv, pairs // 2, pairs, kept)
    else:
        mixed, lse = attend(qkv, 0, pairs)
    middle = collect(lambda rows: contract(mixed[rows], out_set, 1, 0)) + inputs + full_obias
    second_norm, second_normed, second_inverse = norm_parts(middle, gain_two, shift_two)
    seconds = spread(second_norm.astype(BF16))
    grads_out = spread(grad_out)
    x_t = None
    feeds = []
    for j in range(ranges):
        outs = wide_feed(
            half, seconds, grads_out, x_t, up_sets[j],
            bias_sets[j] if j == 0 else after(bias_sets[j], feeds[-1][6]), down_sets[j],
        )
        x_t = outs[7] if j == 0 else x_t
        feeds.append(outs)

    def reduce_ring(pair):
        send, keep = pair
        total = keep.astype(F32) + lax.ppermute(send, "rz", beside).astype(F32)
        total = total.astype(BF16).reshape(deep, -1, keep.shape[-1])
        shifts = range(1, deep)

        def route(shift):
            return [(i, (i + 2 * shift) % ring) for i in range(ring)]

        pieces = [
            lax.ppermute(pick(total, (high + s) % deep, 0), "rz", route(s)) for s in shifts
        ]
        piece = pick(total, high, 0).astype(F32)
        for other in pieces:
            piece = piece + other.astype(F32)
        piece = piece.astype(BF16)
        gathered = [piece] + [lax.ppermute(piece, "rz", route(s)) for s in shifts]
        whole = jnp.stack(
            [
                functools.reduce(
                    lambda rest, s: jnp.where((high - s) % deep == i, gathered[s], rest),
                    shifts,
                    piece,
                )
                for i in range(deep)
            ]
        ).reshape(keep.shape)
        return whole, lax.ppermute(whole, "rz", beside)

    def reduce_parts(parts):
        stacked = jnp.stack(parts)
        own, other = reduce_ring((pick(stacked, 1 - low, 0), pick(stacked, low, 0)))
        return jnp.where(low == 0, own, other), jnp.where(low == 0, other, own)

    def add_half(keep, send):
        return (keep.astype(F32) + swap_half(send).astype(F32)).astype(BF16)

    def reduce_rows(values):
        size = values.shape[0]
        if size % (16 * ring):
            return lax.psum(values, "rz")
        return jnp.concatenate(reduce_parts([values[: size // 2], values[size // 2 :]]), axis=0)

    def scatter_half(values):
        values = values.reshape(2, -1, values.shape[-1])
        return add_half(pick(values, half, 0), pick(values, 1 - half, 0))

    sums_feed = []
    for outs in feeds:
        up_part, down_part = add_half(outs[3], outs[2]), add_half(outs[5], outs[4])
        if up_part.shape == down_part.shape:
            sums_feed.extend(reduce_parts([up_part, down_part]))
        else:
            sums_feed.extend([reduce_rows(up_part), reduce_rows(down_part)])

    grad_wide = grad_out.astype(F32)
    grad_second = collect(
        lambda rows: functools.reduce(
            jnp.add, [contract(feeds[j][1][rows], up_sets[j], 1, 1) for j in range(ranges)]
        )
    )
    grad_second, grad_gain_two, grad_shift_two = norm_back(
        grad_second, second_normed, second_inverse, gain_two
    )
    grad_middle = grad_wide + grad_second
    grad_middle_low = grad_middle.astype(BF16)
    grad_middle_all = jnp.concatenate(spread(grad_middle_low), axis=0)
    grad_mixed = contract(grad_middle_all, out_set, 1, 1).astype(BF16)
    out_half = reduce_rows(scatter_half(contract(mixed, grad_middle_all, 0, 0).astype(BF16)))
    spans = [(0, pairs // 2), (pairs // 2, pairs)] if pairs > 1 else [(0, pairs)]
    dqkvs, qkv_halves = [], []
    for begin, end in spans:
        gate = lse if not dqkvs else after(lse, qkv_halves[-1])
        dqkvs.append(wide_back(qkv, grad_mixed, mixed, gate, begin, end))
        qkv_halves.append(contract(first, dqkvs[-1], 0, 0).astype(BF16))
    qkv_halves = [reduce_rows(scatter_half(values)) for values in qkv_halves]

    result = collect(
        lambda rows: functools.reduce(
            jnp.add, [contract(feeds[j][0][rows], down_sets[j], 1, 0) for j in range(ranges)]
        )
    )
    result = (middle + result + full_dbias).astype(BF16)
    layer_out = move(result, back).reshape(1, local, width)

    def weight_of(span):
        return qkv_weight[:, span[0] * 3 * PAIR : span[1] * 3 * PAIR]

    grad_first_norm = collect(
        lambda rows: functools.reduce(
            jnp.add,
            [contract(d[rows], weight_of(span), 1, 1) for d, span in zip(dqkvs, spans)],
        )
    )
    grad_first, grad_gain_one, grad_shift_one = norm_back(
        grad_first_norm, first_normed, first_inverse, gain_one
    )
    tokens_grad = move((grad_middle + grad_first).astype(BF16), back).reshape(1, local, width)

    out_weight_grad = join(out_half, swap_core(out_half), core).reshape(-1, width).astype(F32)
    if True:

        def finish_columns(values):
            values = values.reshape(quarter, own_rows, 1, -1)
            values = lax.all_to_all(values, "gq", split_axis=0, concat_axis=2, tiled=True)
            values = values.reshape(own_rows, quarter, -1)
            return join(values, swap_core(values), core).transpose(1, 0, 2, 3)

        def natural_columns(values, inner=1):
            values = values.reshape(own_rows, 2, quarter, inner, 2, -1)
            return values.transpose(0, 4, 2, 1, 3, 5).reshape(own_rows, -1).astype(F32)

        ups = jnp.stack([finish_columns(values) for values in sums_feed[::2]], axis=3)
        up_weight_grad = natural_columns(ups, ranges)
        downs = jnp.stack(sums_feed[1::2])
        down_weight_grad = join(downs, swap_core(downs), core).reshape(-1, width).astype(F32)
        columns = jnp.concatenate([finish_columns(values) for values in qkv_halves], axis=3)
        columns = columns.reshape(own_rows, 2, quarter, pairs, 3, PAIR)
        query_weight_grad, key_weight_grad, value_weight_grad = [
            natural_columns(columns[:, :, :, :, i]) for i in range(3)
        ]

    def place_entries(values, inner=1):
        values = values.reshape(inner, 2, 1, 1, -1).transpose(1, 2, 3, 0, 4)
        shape = (2, quarter, 2) + values.shape[3:]
        zero = jnp.zeros((), core.dtype)
        return lax.dynamic_update_slice(
            jnp.zeros(shape, F32), values, (zero, gq, core, zero, zero)
        ).reshape(grp, -1)

    dqkv_sums = jnp.concatenate([jnp.sum(d.astype(F32), axis=0) for d in dqkvs])
    dqkv_sums = dqkv_sums.reshape(pairs, 3, PAIR)
    sums = [
        place_entries(dqkv_sums[:, 0]),
        place_entries(dqkv_sums[:, 2]),
        jnp.sum(grad_middle_low.astype(F32), axis=0),
        grad_gain_one, grad_shift_one, grad_gain_two, grad_shift_two,
        jnp.sum(grad_wide, axis=0),
        place_entries(jnp.stack([outs[6] for outs in feeds]), ranges),
    ]
    sums = jnp.concatenate([s.reshape(grp, -1) for s in sums], axis=1)
    if grp == 2 and ring & (ring - 1) == 0:
        sums = sums + swap_core(sums)
        sums = pick(sums, half, 0) + swap_half(pick(sums, 1 - half, 0))
        step = 1
        while step < ring:
            sums = sums + lax.ppermute(sums, "rz", [(i, i ^ step) for i in range(ring)])
            step *= 2
    else:
        sums = lax.psum(sums, ("rz", "core", "half", "gq"))
        sums = pick(sums, half * quarter + gq, 0)
    small = [sums[i * own_rows : (i + 1) * own_rows] for i in range(8)]
    return (
        layer_out, tokens_grad, query_weight_grad, key_weight_grad, value_weight_grad,
        small[0], small[1], out_weight_grad, small[2], small[3], small[4], small[5], small[6],
        up_weight_grad, sums[8 * own_rows :], down_weight_grad, small[7],
    )


class RingSum:
    def __init__(self, place, ring, sends, keeps):
        self.low, self.high = place % 2, place // 2
        self.ring, self.deep = ring, ring // 2
        self.beside = [(i, i ^ 1) for i in range(ring)]
        self.keeps = keeps
        self.sends = sends
        self.received = [lax.ppermute(send, "half", SWAP) for send in sends]

    def route(self, shift):
        return [(i, (i + 2 * shift) % self.ring) for i in range(self.ring)]

    def to_neighbour(self, *gates):
        received = list(after_all(self.received, *gates))
        totals = [
            (keep.astype(F32) + other.astype(F32)).astype(BF16)
            for keep, other in zip(self.keeps, received)
        ]
        if len(totals) == 1:
            size = totals[0].shape[0] // 2
            totals = [totals[0][:size], totals[0][size:]]
        even = self.low == 0
        self.keep = jnp.where(even, totals[0], totals[1])
        self.sent = jnp.where(even, totals[1], totals[0])
        self.received = [lax.ppermute(self.sent, "rz", self.beside)]
        return self.sent

    def along(self, *gates):
        (received,) = after_all(self.received, *gates)
        total = (self.keep.astype(F32) + received.astype(F32)).astype(BF16)
        self.shape = total.shape
        total = total.reshape(self.deep, -1, total.shape[-1])
        self.keep = pick(total, self.high, 0)
        shifts = range(1, self.deep)
        sent = [pick(total, (self.high + s) % self.deep, 0) for s in shifts]
        self.received = [lax.ppermute(p, "rz", self.route(s)) for p, s in zip(sent, shifts)]
        return sent[0]

    def spread(self, *gates):
        piece = self.keep.astype(F32)
        for other in after_all(self.received, *gates):
            piece = piece + other.astype(F32)
        self.piece = piece.astype(BF16)
        self.received = [
            lax.ppermute(self.piece, "rz", self.route(s)) for s in range(1, self.deep)
        ]
        return self.piece

    def back_to_neighbour(self, *gates):
        gathered = [self.piece] + list(after_all(self.received, *gates))
        deep = self.deep
        self.whole = jnp.stack(
            [
                functools.reduce(
                    lambda rest, s: jnp.where((self.high - s) % deep == i, gathered[s], rest),
                    range(1, deep),
                    gathered[0],
                )
                for i in range(deep)
            ]
        ).reshape(self.shape)
        self.received = [
            lax.ppermute(self.whole, "rz", self.beside),
            lax.ppermute(self.whole, "core", SWAP),
        ]
        return self.whole

    def to_core(self, *gates):
        neighbour, whole = after_all(self.received, *gates)
        crossed = lax.ppermute(neighbour, "core", SWAP)
        even = self.low == 0
        self.own = (jnp.where(even, self.whole, neighbour), jnp.where(even, neighbour, self.whole))
        self.other = (jnp.where(even, whole, crossed), jnp.where(even, crossed, whole))
        return neighbour


def after_all(values, *gates):
    if not gates:
        return tuple(values)
    return lax.optimization_barrier(tuple(values) + gates)[: len(values)]


def pair_body(
    rep, grp, tokens, query_weight, key_weight, value_weight, query_bias, value_bias, out_weight,
    out_bias, first_gain, first_shift, second_gain, second_shift, up_weight, up_bias,
    down_weight, down_bias, cotangent,
):
    clips, local, width = tokens.shape
    assert clips == 1
    ring = rep // 2
    core, half, place = lax.axis_index("core"), lax.axis_index("half"), lax.axis_index("rz")
    low = place % 2
    own_rows = width // 2
    pairs = own_rows // PAIR
    hidden = up_weight.shape[1]
    ranges = hidden // (2 * width)
    tile = hidden // (4 * ranges)
    stays = core == half
    scal = jnp.stack([half, low, core, stays.astype(jnp.int32)]).astype(jnp.int32)
    cross = [(1, 2), (2, 1)]
    beside = [(i, i ^ 1) for i in range(ring)]

    def swap_half(values):
        return lax.ppermute(values, "half", SWAP)

    def swap_core(values):
        return lax.ppermute(values, "core", SWAP)

    def swap_low(values):
        return lax.ppermute(values, "rz", beside)

    def cross_over(values):
        return lax.ppermute(values, ("core", "half"), cross)

    tokens, cotangent = tokens.reshape(local, width), cotangent.reshape(local, width)

    tokens_in = cross_over(tokens)
    own_qkv, mine = pack_qkv(scal, (query_weight, key_weight, value_weight))
    qkv_x = swap_half(mine)
    vectors = jnp.concatenate(
        [query_bias, value_bias, out_bias, first_gain, first_shift, second_gain, second_shift,
         down_bias, up_bias]
    )
    vectors = join(vectors, swap_half(vectors), half)
    (full_qbias, full_vbias, full_obias, gain_one, shift_one, gain_two, shift_two, full_dbias) = [
        vectors[:, i * own_rows : (i + 1) * own_rows].reshape(1, width) for i in range(8)
    ]

    def set_entries(values, inner=1):
        return pick(values.reshape(2, 2, inner, -1), core, 1).transpose(1, 0, 2).reshape(inner, -1)

    bias_sets = set_entries(vectors[:, 8 * own_rows :], ranges)
    packed_feed = [pack_feed(scal, up_weight, down_weight, j, ranges) for j in range(ranges)]
    quarter = own_rows // 4
    out_mine = lax.dynamic_slice(
        out_weight, (core * (own_rows // 2) + low * quarter, 0 * core), (quarter, width)
    )

    x, first = first_norm(scal, tokens, tokens_in, gain_one, shift_one)
    first_in = swap_core(first)
    qkv_x, out_mine, *packed_feed = lax.optimization_barrier((qkv_x, out_mine, *packed_feed))
    qkv_y = swap_low(qkv_x)
    out_x = swap_half(out_mine)
    feed_x = [swap_half(packed_feed[0])]
    cotangent_in = cross_over(after(cotangent, qkv_x))
    zeros = jnp.zeros((pairs, PAIR), F32)
    qkv_bias = jnp.stack(
        [set_entries(full_qbias).reshape(pairs, PAIR), zeros,
         set_entries(full_vbias).reshape(pairs, PAIR)],
        axis=1,
    ).reshape(1, 3 * own_rows)
    qkv, qkv_weight, first_all = project(
        scal, (first, first_in), own_qkv, qkv_x, qkv_y, qkv_bias
    )

    kept = attend(qkv, 0, pairs // 2)
    out_x, feed_x[0], lse = lax.optimization_barrier((out_x, feed_x[0], kept[1]))
    out_y = swap_low(out_x)
    feed_y = [swap_low(feed_x[0])]
    for j in range(1, ranges):
        feed_x.append(swap_half(after(packed_feed[j], lse)))
    mixed, lse = attend(qkv, pairs // 2, pairs, (kept[0], lse))
    for j in range(1, ranges):
        feed_x[j], lse = lax.optimization_barrier((feed_x[j], lse))
        feed_y.append(swap_low(feed_x[j]))
    out_part, out_set = out_other(scal, mixed, out_weight, out_x, out_y)
    out_in = swap_core(out_part)
    grad_out = jnp.where(stays, cotangent, cotangent_in)
    grad_out_in = swap_core(grad_out)
    middle, second = second_norm(
        scal, mixed, out_set, x, out_in, full_obias, gain_two, shift_two
    )
    second_in = swap_core(second)

    feeds, sums = [], []
    x_t = None
    for j in range(ranges):
        bias = bias_sets[j : j + 1]
        if feeds:
            bias = after(bias, feeds[-1][6], feeds[-1][2])
        outs = feed(
            scal, (second, second_in), (grad_out, grad_out_in), x_t, up_weight, down_weight,
            feed_x[j], feed_y[j], bias, j, ranges,
        )
        x_t = outs[9] if j == 0 else x_t
        feeds.append(outs)
        sums.append(RingSum(place, ring, [outs[2], outs[4]], [outs[3], outs[5]]))
    hiddens, d_pres = [f[0] for f in feeds], [f[1] for f in feeds]
    ups, downs = [f[7] for f in feeds], [f[8] for f in feeds]
    grad_part = other_rows(scal, d_pres, ups, "feed_other")
    grad_in = swap_core(grad_part)
    layer_part = layer_other(scal, hiddens, downs)
    grad_wide, grad_low, sums_two = second_back(
        scal, d_pres, ups, grad_in, middle, grad_out, gain_two
    )
    grad_low_in = swap_core(grad_low)
    grad_mixed, out_send, out_keep = mixed_back(scal, (grad_low, grad_low_in), out_set, mixed)

    first_sum, last_sum = sums[0], sums[-1]
    issued = [first_sum.to_neighbour(grad_mixed)]
    out_sum = None
    backs, qkv_sums = [], []
    groups = 2
    per = pairs // groups
    for pair in range(pairs):
        gate = after(lse, *issued)
        outs = attend_back(scal, qkv, grad_mixed, mixed, gate, first_all, pair, pair + 1)
        backs.append(outs)
        done = outs[3]
        issued = [done]
        if pair == 0:
            issued.append(first_sum.along(done))
        elif pair == 1:
            issued.append(first_sum.spread(done))
            issued.append(last_sum.to_neighbour(done))
            out_sum = RingSum(place, ring, [after(out_send, done)], [out_keep])
        elif pair == 2:
            issued.append(first_sum.back_to_neighbour(done))
            issued.append(last_sum.along(done))
            issued.append(out_sum.to_neighbour(done))
    qkv_sums = [RingSum(place, ring, [b[1]], [b[2]]) for b in backs]
    done = backs[-1][3]
    grad_part = first_other(scal, [b[0] for b in backs], qkv_weight)
    grad_in = swap_core(grad_part)
    first_sum.to_core(done)
    last_sum.spread(done)
    out_sum.along(done)
    layer_in = swap_core(layer_part)
    layer_out = layer_own(scal, hiddens, downs, layer_in, middle, full_dbias)
    layer_out = jnp.where(stays, layer_out, cross_over(layer_out))
    tokens_grad, sums_one = first_back(
        scal, [b[0] for b in backs], qkv_weight, grad_in, x, grad_wide, gain_one
    )
    tokens_grad = jnp.where(stays, tokens_grad, cross_over(tokens_grad))
    for item in qkv_sums:
        item.to_neighbour()
    last_sum.back_to_neighbour()
    out_sum.spread()
    for item in qkv_sums:
        item.along()
    out_sum.back_to_neighbour()
    last_sum.to_core()
    for item in qkv_sums:
        item.spread()
    out_sum.to_core()
    for item in qkv_sums:
        item.back_to_neighbour()
    for item in qkv_sums:
        item.to_core()

    up_weight_grad, down_weight_grad = finish_feed(
        core,
        [v for item in sums for v in item.own],
        [v for item in sums for v in item.other],
    )
    query_weight_grad, key_weight_grad, value_weight_grad = finish_qkv(
        core,
        [jnp.concatenate(item.own, axis=0) for item in qkv_sums],
        [jnp.concatenate(item.other, axis=0) for item in qkv_sums],
    )
    out_own = jnp.concatenate(out_sum.own, axis=0)
    out_other_core = jnp.concatenate(out_sum.other, axis=0)
    out_weight_grad = join(out_own, out_other_core, core).reshape(own_rows, width).astype(F32)

    def place_entries(values, inner=1):
        values = values.reshape(inner, 2, 1, -1).transpose(1, 2, 0, 3)
        empty = jnp.zeros_like(values)
        return join(values[:, 0], empty[:, 0], core).transpose(1, 0, 2, 3).reshape(2, -1)

    parts = jnp.concatenate([b[3][0] for b in backs]).reshape(pairs, 3, PAIR)
    entries = [
        place_entries(parts[:, 0]), place_entries(parts[:, 2]), sums_two[3], sums_one[0],
        sums_one[1], sums_two[0], sums_two[1], sums_two[2],
        place_entries(jnp.stack([f[6] for f in feeds]), ranges),
    ]
    entries = jnp.concatenate([e.reshape(2, -1) for e in entries], axis=1)
    entries = entries + swap_core(entries)
    entries = pick(entries, half, 0) + swap_half(pick(entries, 1 - half, 0))
    step = 1
    while step < ring:
        if ring & (ring - 1):
            entries = lax.psum(entries, "rz")
            break
        entries = entries + lax.ppermute(entries, "rz", [(i, i ^ step) for i in range(ring)])
        step *= 2
    small = [entries[i * own_rows : (i + 1) * own_rows] for i in range(8)]
    return (
        layer_out.reshape(1, local, width), tokens_grad.reshape(1, local, width),
        query_weight_grad, key_weight_grad, value_weight_grad, small[0], small[1],
        out_weight_grad, small[2], small[3], small[4], small[5], small[6], up_weight_grad,
        entries[8 * own_rows :], down_weight_grad, small[7],
    )


def solution(mesh):
    rep, grp = mesh.shape["rep"], mesh.shape["grp"]
    split = Mesh(
        mesh.devices.reshape(rep // 2, 2, 2, grp // 2), ("rz", "core", "half", "gq")
    )
    clip = P(("rz", "core"), ("half", "gq"), None)
    matrix = P(("half", "gq"), None)
    vector = P(("half", "gq"))
    return jax.shard_map(
        functools.partial(pair_body if grp == 2 and rep % 4 == 0 else wide_body, rep, grp),
        mesh=split,
        in_specs=(
            clip, matrix, matrix, matrix, vector, vector, matrix, vector, vector, vector, vector,
            vector, matrix, vector, matrix, vector, clip,
        ),
        out_specs=(
            clip, clip, matrix, matrix, matrix, vector, vector, matrix, vector, vector, vector,
            vector, vector, matrix, vector, matrix, vector,
        ),
        check_vma=False,
    )
```

```python
import functools

import jax
import jax.numpy as jnp
from jax import lax
from jax.experimental import pallas as pl
from jax.experimental.pallas import tpu as pltpu
from jax.sharding import Mesh
from jax.sharding import PartitionSpec as P

HEAD_DIM = 64
PAIR = 2 * HEAD_DIM
EPS = 1e-06
LOG2E = 1.4426950408889634
F32 = jnp.float32
BF16 = jnp.bfloat16
SWAP = [(0, 1), (1, 0)]
VMEM_LIMIT = 62 << 20


def contract(left, right, left_dim, right_dim):
    return lax.dot_general(
        left, right, (((left_dim,), (right_dim,)), ((), ())), preferred_element_type=F32
    )


def attend_kernel(tile, rows, padded, qkv_ref, out_ref, lse_ref, q_t, v_t, out_t):
    scale = HEAD_DIM**-0.5 * LOG2E
    ones = jnp.ones((16, rows), BF16)
    q_t[:, :rows] = qkv_ref[:, :PAIR].T
    if padded > rows:
        q_t[:, rows:] = jnp.zeros((PAIR, padded - rows), BF16)
    values_t = qkv_ref[:, 2 * PAIR :].T
    step = HEAD_DIM + 16
    for head in range(2):
        v_t[head * step : head * step + HEAD_DIM, :] = values_t[
            head * HEAD_DIM : (head + 1) * HEAD_DIM, :
        ]
        v_t[head * step + HEAD_DIM : (head + 1) * step, :] = ones

    def block(index, carry):
        columns = pl.ds(pl.multiple_of(index * tile, tile), tile)
        empty = jnp.zeros((HEAD_DIM, tile), BF16)
        for head in range(2):
            lanes = slice(head * HEAD_DIM, (head + 1) * HEAD_DIM)
            query = q_t[lanes, columns]
            query = jnp.concatenate([query, empty] if head == 0 else [empty, query], axis=0)
            scores = contract(qkv_ref[:, PAIR : 2 * PAIR], query, 1, 0)
            highest = jnp.max(scores, axis=0, keepdims=True) * scale
            expon = jnp.exp2(scores * scale - highest).astype(BF16)
            mixed = contract(v_t[head * step : (head + 1) * step, :], expon, 1, 0)
            total = mixed[HEAD_DIM : HEAD_DIM + 1, :]
            out_t[lanes, columns] = mixed[:HEAD_DIM, :] / total
            lse_ref[head : head + 1, columns] = highest + jnp.log2(total)
        return carry

    lax.fori_loop(0, padded // tile, block, 0)
    out_ref[...] = out_t[...].T[:rows, :].astype(BF16)


def attend(qkv, first_pair, last_pair, kept=None, tile=512):
    rows, width = qkv.shape
    pairs = width // (3 * PAIR)
    padded = -(-rows // tile) * tile
    count = last_pair - first_pair
    kernel = functools.partial(attend_kernel, tile, rows, padded)
    anywhere = pl.BlockSpec(memory_space=pl.ANY)
    return pl.pallas_call(
        kernel if kept is None else lambda ref, a, b, *rest: kernel(ref, *rest),
        grid=(count,),
        in_specs=[pl.BlockSpec((rows, 3 * PAIR), lambda i: (0, i + first_pair))]
        + ([] if kept is None else [anywhere] * 2),
        out_specs=[
            pl.BlockSpec((rows, PAIR), lambda i: (0, i + first_pair)),
            pl.BlockSpec((None, 2, padded), lambda i: (i + first_pair, 0, 0)),
        ],
        out_shape=[
            jax.ShapeDtypeStruct((rows, pairs * PAIR), BF16),
            jax.ShapeDtypeStruct((pairs, 2, padded), F32),
        ],
        scratch_shapes=[
            pltpu.VMEM((PAIR, padded), BF16),
            pltpu.VMEM((PAIR + 32, rows), BF16),
            pltpu.VMEM((PAIR, padded), F32),
        ],
        input_output_aliases={} if kept is None else {1: 0, 2: 1},
        compiler_params=pltpu.CompilerParams(vmem_limit_bytes=VMEM_LIMIT),
        cost_estimate=pl.CostEstimate(
            flops=64 * rows * rows * PAIR * count,
            bytes_accessed=8 * rows * PAIR * count,
            transcendentals=2 * rows * rows * count,
        ),
        name="attend",
    )(qkv, *(() if kept is None else kept))


def attend_back_kernel(
    tile, rows, padded, s_ref, qkv_ref, grad_ref, out_ref, lse_ref, first_ref, dqkv_ref, send_ref,
    keep_ref, sums_ref, q_t, g_t, k_t, delta, dq_t, dk_t, dv_t, all_t,
):
    scale = HEAD_DIM**-0.5
    q_t[:, :rows] = qkv_ref[:, :PAIR].T
    g_t[:, :rows] = grad_ref[...].T
    if padded > rows:
        q_t[:, rows:] = jnp.zeros((PAIR, padded - rows), BF16)
        g_t[:, rows:] = jnp.zeros((PAIR, padded - rows), BF16)
        delta[:, rows:] = jnp.zeros((2, padded - rows), F32)
    k_t[...] = qkv_ref[:, PAIR : 2 * PAIR].T
    product = (grad_ref[...].astype(F32) * out_ref[...].astype(F32)).T
    delta[0:1, :rows] = jnp.sum(product[:HEAD_DIM, :], axis=0, keepdims=True)
    delta[1:2, :rows] = jnp.sum(product[HEAD_DIM:, :], axis=0, keepdims=True)
    dk_t[...] = jnp.zeros_like(dk_t)
    dv_t[...] = jnp.zeros_like(dv_t)

    def block(index, carry):
        columns = pl.ds(pl.multiple_of(index * tile, tile), tile)
        empty = jnp.zeros((HEAD_DIM, tile), BF16)
        for head in range(2):
            lanes = slice(head * HEAD_DIM, (head + 1) * HEAD_DIM)
            query = q_t[lanes, columns]
            grad = g_t[lanes, columns]
            query_pad = jnp.concatenate([query, empty] if head == 0 else [empty, query], axis=0)
            grad_pad = jnp.concatenate([grad, empty] if head == 0 else [empty, grad], axis=0)
            scores = contract(qkv_ref[:, PAIR : 2 * PAIR], query_pad, 1, 0)
            grad_probs = contract(qkv_ref[:, 2 * PAIR :], grad_pad, 1, 0)
            weights = jnp.exp2(scores * (scale * LOG2E) - lse_ref[head : head + 1, columns])
            grad_scores = (weights * (grad_probs - delta[head : head + 1, columns])).astype(BF16)
            dv_t[lanes, :] += contract(grad, weights.astype(BF16), 1, 1)
            dq_t[lanes, columns] = contract(k_t[lanes, :], grad_scores, 1, 0)
            dk_t[lanes, :] += contract(query, grad_scores, 1, 1)
        return carry

    lax.fori_loop(0, padded // tile, block, 0)
    all_t[:PAIR, :] = (dq_t[:, :rows] * scale).astype(BF16)
    all_t[PAIR : 2 * PAIR, :] = (dk_t[...] * scale).astype(BF16)
    all_t[2 * PAIR :, :] = dv_t[...].astype(BF16)
    for part in range(3):
        lanes = slice(part * PAIR, (part + 1) * PAIR)
        dqkv_ref[:, lanes] = all_t[lanes, :].T
    sums_ref[...] = contract(jnp.ones((8, rows), BF16), all_t[...], 1, 1)
    own = first_ref.shape[1] // 2
    for h in range(2):
        grad = contract(all_t[...], first_ref[:, h * own : (h + 1) * own], 1, 0).astype(BF16)

        @pl.when(s_ref[0] == h)
        def _():
            keep_ref[...] = grad

        @pl.when(s_ref[0] != h)
        def _():
            send_ref[...] = grad


def attend_back(scal, qkv, grad, out, lse, first, first_pair, last_pair, tile=256):
    rows, full = qkv.shape
    width = first.shape[1]
    padded = -(-rows // tile) * tile
    count = last_pair - first_pair
    return pl.pallas_call(
        functools.partial(attend_back_kernel, tile, rows, padded),
        grid_spec=pltpu.PrefetchScalarGridSpec(
            num_scalar_prefetch=1,
            grid=(count,),
            in_specs=[
                pl.BlockSpec((rows, 3 * PAIR), lambda i, s: (0, i + first_pair)),
                pl.BlockSpec((rows, PAIR), lambda i, s: (0, i + first_pair)),
                pl.BlockSpec((rows, PAIR), lambda i, s: (0, i + first_pair)),
                pl.BlockSpec((None, 2, lse.shape[2]), lambda i, s: (i + first_pair, 0, 0)),
                pl.BlockSpec((rows, width), lambda i, s: (0, 0), pipeline_mode=pl.Buffered(1)),
            ],
            out_specs=[
                pl.BlockSpec((rows, 3 * PAIR), lambda i, s: (0, i)),
                pl.BlockSpec((3 * PAIR, width // 2), lambda i, s: (i, 0)),
                pl.BlockSpec((3 * PAIR, width // 2), lambda i, s: (i, 0)),
                pl.BlockSpec((8, 3 * PAIR), lambda i, s: (0, i)),
            ],
            scratch_shapes=[
                pltpu.VMEM((PAIR, padded), BF16),
                pltpu.VMEM((PAIR, padded), BF16),
                pltpu.VMEM((PAIR, rows), BF16),
                pltpu.VMEM((2, padded), F32),
                pltpu.VMEM((PAIR, padded), F32),
                pltpu.VMEM((PAIR, rows), F32),
                pltpu.VMEM((PAIR, rows), F32),
                pltpu.VMEM((3 * PAIR, rows), BF16),
            ],
        ),
        out_shape=[
            jax.ShapeDtypeStruct((rows, 3 * PAIR * count), BF16),
            jax.ShapeDtypeStruct((3 * PAIR * count, width // 2), BF16),
            jax.ShapeDtypeStruct((3 * PAIR * count, width // 2), BF16),
            jax.ShapeDtypeStruct((8, 3 * PAIR * count), F32),
        ],
        compiler_params=pltpu.CompilerParams(vmem_limit_bytes=VMEM_LIMIT),
        cost_estimate=pl.CostEstimate(
            flops=160 * rows * rows * PAIR * count,
            bytes_accessed=16 * rows * PAIR * count,
            transcendentals=2 * rows * rows * count,
        ),
        name="attend_back",
    )(scal, qkv, grad, out, lse, first)


def feed_kernel(
    s_ref, x_own, x_other, dy_own, dy_other, up_ref, down_ref, x_piece, x_beside, z_piece, z_beside,
    bias_ref, out_own, out_other, dx_own, dx_other, up_send, up_keep, down_send, down_keep,
    low_send, low_keep, bias_grad_ref, x, dy, x_t, out_sum, dx_sum, up_full, down_full, hidden,
    d_pre, sems,
):
    index = pl.program_id(0)
    half = s_ref[0]
    rows, width = x.shape
    block = rows // 2
    own = width // 2
    tile = up_ref.shape[1]
    first_range = index < 2
    side = index % 2
    columns = pl.ds(pl.multiple_of(side * tile, tile), tile)
    mine = pl.ds(pl.multiple_of(half * own, own), own)
    theirs = pl.ds(pl.multiple_of((1 - half) * own, own), own)

    @pl.when(index == 0)
    def _():
        copies = []
        for i, ref in enumerate((x_own, x_other)):
            copies.append(pltpu.make_async_copy(ref, x.at[pl.ds(i * block, block)], sems.at[i]))
        for i, ref in enumerate((dy_own, dy_other)):
            copies.append(
                pltpu.make_async_copy(ref, dy.at[pl.ds(i * block, block)], sems.at[2 + i])
            )
        for copy in copies:
            copy.start()
        for copy in copies:
            copy.wait()
        x_t[...] = x[...].T
        out_sum[...] = jnp.zeros_like(out_sum)
        dx_sum[...] = jnp.zeros_like(dx_sum)

    up_full[mine, :] = up_ref[...]

    @pl.when(side == half)
    def _():
        down_full[...] = down_ref[...]

    for chosen, place, piece, beside in (
        (first_range, 1, x_piece, x_beside), (jnp.logical_not(first_range), 4, z_piece, z_beside)
    ):
        even = s_ref[place] == 0

        @pl.when(chosen & even)
        def _():
            up_full[theirs, :] = piece[:, columns]

        @pl.when(chosen & jnp.logical_not(even))
        def _():
            up_full[theirs, :] = beside[:, columns]

        @pl.when(chosen & (side != half) & even)
        def _():
            down_full[...] = beside[...]

        @pl.when(chosen & (side != half) & jnp.logical_not(even))
        def _():
            down_full[...] = piece[...]

    bias_grad = jnp.zeros(bias_grad_ref.shape, F32)
    for start in range(0, rows, block):
        part = slice(start, start + block)
        pre = contract(x[part, :], up_full[...], 1, 0) + bias_ref[...]
        d_hidden = contract(dy[part, :], down_full[...], 1, 1)
        share = 0.5 * (1.0 + lax.erf(pre * 0.7071067811865476))
        hidden[part, :] = (pre * share).astype(BF16)
        slope = share + pre * (jnp.exp(-0.5 * pre * pre) * 0.3989422804014327)
        d_low = (d_hidden * slope).astype(BF16)
        d_pre[part, :] = d_low
        bias_grad = bias_grad + jnp.sum(d_low.astype(F32), axis=0, keepdims=True)
        out_sum[part, :] += contract(hidden[part, :], down_full[...], 1, 0)
        dx_sum[part, :] += contract(d_pre[part, :], up_full[...], 1, 1)
    bias_grad_ref[...] = bias_grad
    down_grad = contract(hidden[...], dy[...], 0, 0).astype(BF16)
    side_rows = pl.ds(pl.multiple_of(side * tile, tile), tile)

    @pl.when(first_range)
    def _():
        up_keep[:, columns] = contract(x_t[mine, :], d_pre[...], 1, 0).astype(BF16)
        up_send[:, columns] = contract(x_t[theirs, :], d_pre[...], 1, 0).astype(BF16)

    @pl.when(first_range & (side == half))
    def _():
        down_keep[...] = down_grad

    @pl.when(first_range & (side != half))
    def _():
        down_send[...] = down_grad

    for even in (True, False):
        up_goal, down_goal = (low_keep, low_send) if even else (low_send, low_keep)

        @pl.when(jnp.logical_not(first_range) & ((s_ref[1] == 0) == even))
        def _():
            up_goal[:, columns] = contract(x_t[...], d_pre[...], 1, 0).astype(BF16)
            down_goal[side_rows, :] = down_grad

    @pl.when(index == pl.num_programs(0) - 1)
    def _():
        out_own[...] = out_sum[:block, :].astype(BF16)
        out_other[...] = out_sum[block:, :].astype(BF16)
        dx_own[...] = dx_sum[:block, :].astype(BF16)
        dx_other[...] = dx_sum[block:, :].astype(BF16)


def feed(scal, seconds, grads, up, down, pieces, bias):
    local, width = seconds[0].shape
    rows = 2 * local
    tile = down.shape[0] // 4
    anywhere = pl.BlockSpec(memory_space=pl.ANY)

    def fixed(*shape):
        return pl.BlockSpec(shape, lambda t, s: (0, 0), pipeline_mode=pl.Buffered(1))

    shapes = [(local, width)] * 4 + [(width // 2, 2 * tile)] * 2 + [(tile, width)] * 2
    shapes += [(width, 2 * tile)] * 2
    across = pl.BlockSpec((1, tile), lambda t, s: (0, t))
    return pl.pallas_call(
        feed_kernel,
        grid_spec=pltpu.PrefetchScalarGridSpec(
            num_scalar_prefetch=1,
            grid=(4,),
            in_specs=[anywhere] * 4
            + [
                pl.BlockSpec(
                    (width // 2, tile), lambda t, s: (0, ((t % 2) * 2 + s[2]) * 2 + t // 2)
                ),
                pl.BlockSpec((tile, width), lambda t, s: (s[2] * 2 + t // 2, 0)),
            ]
            + [fixed(width // 2, 2 * tile)] * 4
            + [across],
            out_specs=[fixed(*shape) for shape in shapes] + [across],
            scratch_shapes=[
                pltpu.VMEM((rows, width), BF16),
                pltpu.VMEM((rows, width), BF16),
                pltpu.VMEM((width, rows), BF16),
                pltpu.VMEM((rows, width), F32),
                pltpu.VMEM((rows, width), F32),
                pltpu.VMEM((width, tile), BF16),
                pltpu.VMEM((tile, width), BF16),
                pltpu.VMEM((rows, tile), BF16),
                pltpu.VMEM((rows, tile), BF16),
                pltpu.SemaphoreType.DMA((4,)),
            ],
        ),
        out_shape=[jax.ShapeDtypeStruct(shape, BF16) for shape in shapes]
        + [jax.ShapeDtypeStruct((1, 4 * tile), F32)],
        compiler_params=pltpu.CompilerParams(vmem_limit_bytes=VMEM_LIMIT),
        cost_estimate=pl.CostEstimate(
            flops=48 * rows * width * tile,
            bytes_accessed=16 * rows * width,
            transcendentals=8 * rows * tile,
        ),
        name="feed",
    )(scal, *seconds, *grads, up, down, *pieces, bias)


def run(kernel, name, scal, grid, in_specs, out_specs, out_shape, args, flops=0, scratch=()):
    moved = sum(a.size * a.dtype.itemsize for a in args)
    return pl.pallas_call(
        kernel,
        grid_spec=pltpu.PrefetchScalarGridSpec(
            num_scalar_prefetch=1,
            grid=grid,
            in_specs=in_specs,
            out_specs=out_specs,
            scratch_shapes=scratch,
        ),
        out_shape=out_shape,
        compiler_params=pltpu.CompilerParams(vmem_limit_bytes=VMEM_LIMIT),
        cost_estimate=pl.CostEstimate(flops=flops, bytes_accessed=2 * moved, transcendentals=0),
        name=name,
    )(scal, *args)


def spec(shape, index):
    return pl.BlockSpec(shape, index)


def held(*shape):
    return pl.BlockSpec(shape, lambda i, s: (0,) * len(shape), pipeline_mode=pl.Buffered(1))


def struct(*shape, dtype=BF16):
    return jax.ShapeDtypeStruct(shape, dtype)


def pack_qkv(scal, weights):
    rows, width = weights[0].shape
    pairs = width // (2 * PAIR)
    per = pairs // 2

    def kernel(s_ref, q_ref, k_ref, v_ref, own_ref, mine_ref):
        for i, ref in enumerate((q_ref, k_ref, v_ref)):
            own_ref[:, i * PAIR : (i + 1) * PAIR] = ref[...]
        start = pl.multiple_of(s_ref[1] * (rows // 2), rows // 2)
        mine_ref[...] = own_ref[pl.ds(start, rows // 2), :]

    block = spec((rows, PAIR), lambda p, s: (0, ((p // per) * 2 + s[2]) * per + p % per))
    return run(
        kernel, "pack_qkv", scal, (pairs,), [block] * 3,
        [
            spec((rows, 3 * PAIR), lambda p, s: (0, p)),
            spec((rows // 2, 3 * PAIR), lambda p, s: (0, p)),
        ],
        [struct(rows, 3 * PAIR * pairs), struct(rows // 2, 3 * PAIR * pairs)],
        weights,
    )


def pack_feed(scal, up, down, j, ranges, bit):
    rows, hidden = up.shape
    tile = hidden // (4 * ranges)
    columns = down.shape[1] // 2

    def kernel(s_ref, up_ref, down_ref, out_ref):
        out_ref[...] = jnp.where(s_ref[bit] == 0, up_ref[...], down_ref[...])

    return run(
        kernel, "pack_feed", scal, (2,),
        [
            spec((rows, tile), lambda t, s: (0, (t * 2 + s[2]) * ranges + j)),
            spec((tile, columns), lambda t, s: (s[2] * ranges + j, t)),
        ],
        spec((rows, tile), lambda t, s: (0, t)), struct(rows, 2 * tile), (up, down),
    )


def normalize(values):
    centred = values - jnp.mean(values, axis=-1, keepdims=True)
    spread = jnp.mean(centred * centred, axis=-1, keepdims=True)
    inverse = lax.rsqrt(spread + EPS)
    return centred * inverse, inverse


def first_norm(scal, tokens, received, gain, shift):
    rows, width = tokens.shape
    step = rows // 2

    def kernel(s_ref, t_ref, r_ref, gain_ref, shift_ref, x_ref, first_ref):
        x = jnp.where(s_ref[3] == 1, t_ref[...], r_ref[...])
        x_ref[...] = x
        normed, _ = normalize(x.astype(F32))
        first_ref[...] = (normed * gain_ref[...] + shift_ref[...]).astype(BF16)

    block = spec((step, width), lambda i, s: (i, 0))
    return run(
        kernel, "first_norm", scal, (2,), [block, block, held(1, width), held(1, width)],
        [block, block], [struct(rows, width)] * 2, (tokens, received, gain, shift),
    )


def project(scal, firsts, own, piece, beside, bias):
    local, width = firsts[0].shape
    rows, total = 2 * local, own.shape[1]
    block = 3 * PAIR
    half_rows, quarter_rows = width // 2, width // 4

    def kernel(
        s_ref, mine_ref, theirs_ref, own_ref, piece_ref, beside_ref, bias_ref, qkv_ref, w_ref,
        all_ref, sems,
    ):
        @pl.when(pl.program_id(0) == 0)
        def _():
            copies = [
                pltpu.make_async_copy(ref, all_ref.at[pl.ds(i * local, local)], sems.at[i])
                for i, ref in enumerate((mine_ref, theirs_ref))
            ]
            for copy in copies:
                copy.start()
            for copy in copies:
                copy.wait()

        half, low = s_ref[0], s_ref[1]
        other = (1 - half) * half_rows
        w_ref[pl.ds(pl.multiple_of(half * half_rows, half_rows), half_rows), :] = own_ref[...]
        start = pl.multiple_of(other + low * quarter_rows, quarter_rows)
        w_ref[pl.ds(start, quarter_rows), :] = piece_ref[...]
        start = pl.multiple_of(other + (1 - low) * quarter_rows, quarter_rows)
        w_ref[pl.ds(start, quarter_rows), :] = beside_ref[...]
        qkv_ref[...] = (contract(all_ref[...], w_ref[...], 1, 0) + bias_ref[...]).astype(BF16)

    def columns(size):
        return spec((size, block), lambda p, s: (0, p))

    anywhere = pl.BlockSpec(memory_space=pl.ANY)
    return run(
        kernel, "project", scal, (total // block,),
        [anywhere] * 2
        + [columns(half_rows), columns(quarter_rows), columns(quarter_rows), columns(1)],
        [columns(rows), columns(width), held(rows, width)],
        [struct(rows, total), struct(width, total), struct(rows, width)],
        (*firsts, own, piece, beside, bias), flops=2 * rows * width * total,
        scratch=[pltpu.SemaphoreType.DMA((2,))],
    )


def out_other(scal, mixed, weight, piece, beside):
    rows, set_width = mixed.shape
    local, width = rows // 2, weight.shape[1]
    block, small = set_width // 2, set_width // 4

    def kernel(s_ref, mixed_ref, own_ref, piece_ref, beside_ref, out_ref, set_ref):
        half, low = s_ref[0], s_ref[1]
        other = (1 - half) * block
        set_ref[pl.ds(pl.multiple_of(half * block, block), block), :] = own_ref[...]
        set_ref[pl.ds(pl.multiple_of(other + low * small, small), small), :] = piece_ref[...]
        start = pl.multiple_of(other + (1 - low) * small, small)
        set_ref[pl.ds(start, small), :] = beside_ref[...]
        out_ref[...] = contract(mixed_ref[...], set_ref[...], 1, 0).astype(BF16)

    return run(
        kernel, "out_other", scal, (1,),
        [
            spec((local, set_width), lambda i, s: (1, 0)),
            spec((block, width), lambda i, s: (s[2], 0)),
            held(small, width), held(small, width),
        ],
        [held(local, width), held(set_width, width)],
        [struct(local, width), struct(set_width, width)],
        (mixed, weight, piece, beside), flops=2 * local * set_width * width,
    )


def second_norm(scal, mixed, out_set, x, received, bias, gain, shift):
    rows, set_width = mixed.shape
    local, width = x.shape
    step = local // 2

    def kernel(
        s_ref, mixed_ref, w_ref, x_ref, r_ref, bias_ref, gain_ref, shift_ref, mid_ref, second_ref
    ):
        middle = contract(mixed_ref[...], w_ref[...], 1, 0) + r_ref[...].astype(F32)
        middle = middle + x_ref[...].astype(F32) + bias_ref[...]
        mid_ref[...] = middle
        normed, _ = normalize(middle)
        second_ref[...] = (normed * gain_ref[...] + shift_ref[...]).astype(BF16)

    block = spec((step, width), lambda i, s: (i, 0))
    return run(
        kernel, "second_norm", scal, (2,),
        [spec((step, set_width), lambda i, s: (i, 0)), held(set_width, width), block, block]
        + [held(1, width)] * 3,
        [block, block], [struct(local, width, dtype=F32), struct(local, width)],
        (mixed, out_set, x, received, bias, gain, shift), flops=2 * local * set_width * width,
    )


def norm_back_rows(grad, normed, inverse, gain):
    scaled = grad * gain
    first_term = jnp.mean(scaled, axis=-1, keepdims=True)
    second_term = jnp.mean(scaled * normed, axis=-1, keepdims=True)
    return inverse * (scaled - first_term - normed * second_term)


def column_sums(refs, values):
    @pl.when(pl.program_id(0) == 0)
    def _():
        refs[...] = jnp.zeros_like(refs)

    for i, value in enumerate(values):
        refs[i : i + 1, :] += jnp.sum(value, axis=0, keepdims=True)


def row_step(rows):
    return rows // 7 if rows % 112 == 0 else rows


def second_back(scal, grad, received, middle, dy, gain):
    local, width = middle.shape
    step = row_step(local)

    def kernel(s_ref, g_ref, r_ref, mid_ref, dy_ref, gain_ref, low_ref, sums_ref):
        grad = g_ref[...].astype(F32) + r_ref[...].astype(F32)
        normed, inverse = normalize(mid_ref[...])
        dy_wide = dy_ref[...].astype(F32)
        low = (dy_wide + norm_back_rows(grad, normed, inverse, gain_ref[...])).astype(BF16)
        low_ref[...] = low
        column_sums(sums_ref, (grad * normed, grad, dy_wide, low.astype(F32)))

    block = spec((step, width), lambda i, s: (i, 0))
    return run(
        kernel, "second_back", scal, (local // step,), [block] * 4 + [held(1, width)],
        [block, held(8, width)], [struct(local, width), struct(8, width, dtype=F32)],
        (grad, received, middle, dy, gain),
    )


def mixed_back(scal, lows, out_set, mixed):
    local, width = lows[0].shape
    rows, set_width = mixed.shape
    block = set_width // 2

    def kernel(
        s_ref, mine_ref, theirs_ref, w_ref, mixed_ref, d_ref, send_ref, keep_ref, low, sems
    ):
        @pl.when(pl.program_id(0) == 0)
        def _():
            copies = [
                pltpu.make_async_copy(ref, low.at[pl.ds(i * local, local)], sems.at[i])
                for i, ref in enumerate((mine_ref, theirs_ref))
            ]
            for copy in copies:
                copy.start()
            for copy in copies:
                copy.wait()

        d_ref[...] = contract(low[...], w_ref[...], 1, 1).astype(BF16)
        for c in range(2):
            columns = slice(c * (width // 2), (c + 1) * (width // 2))
            part = slice(c * block, (c + 1) * block)
            grad = contract(mixed_ref[...], low[:, columns], 0, 0).astype(BF16)

            @pl.when(pl.program_id(0) == s_ref[0])
            def _():
                keep_ref[part, :] = grad

            @pl.when(pl.program_id(0) != s_ref[0])
            def _():
                send_ref[part, :] = grad

    anywhere = pl.BlockSpec(memory_space=pl.ANY)
    across = spec((rows, block), lambda t, s: (0, t))
    return run(
        kernel, "mixed_back", scal, (2,),
        [anywhere] * 2 + [spec((block, width), lambda t, s: (t, 0)), across],
        [across, held(2 * block, width // 2), held(2 * block, width // 2)],
        [struct(rows, set_width)] + [struct(2 * block, width // 2)] * 2,
        (*lows, out_set, mixed), flops=4 * rows * set_width * width,
        scratch=[pltpu.VMEM((rows, width), BF16), pltpu.SemaphoreType.DMA((2,))],
    )


def first_grad(scal, dqkvs, weights):
    rows = dqkvs[0].shape[0]
    width = weights.shape[0]
    local = rows // 2
    count = len(dqkvs)
    step = width // 4

    def kernel(s_ref, *refs):
        total = contract(refs[0][...], refs[count][...], 1, 1)
        for j in range(1, count):
            total = total + contract(refs[j][...], refs[count + j][...], 1, 1)
        refs[-2][...] = total[:local].astype(BF16)
        refs[-1][...] = total[local:].astype(BF16)

    across = spec((local, step), lambda i, s: (0, i))
    return run(
        kernel, "first_grad", scal, (4,),
        [held(*a.shape) for a in dqkvs]
        + [
            pl.BlockSpec((step, a.shape[1]), functools.partial(lambda j, i, s: (i, j), j))
            for j, a in enumerate(dqkvs)
        ],
        [across, across], [struct(local, width)] * 2, (*dqkvs, *([weights] * count)),
        flops=sum(2 * rows * a.shape[1] * width for a in dqkvs),
    )


def first_back(scal, grad, received, x, wide, gain):
    local, width = x.shape
    step = row_step(local)

    def kernel(s_ref, g_ref, r_ref, x_ref, wide_ref, gain_ref, out_ref, sums_ref):
        grad = g_ref[...].astype(F32) + r_ref[...].astype(F32)
        normed, inverse = normalize(x_ref[...].astype(F32))
        total = wide_ref[...].astype(F32) + norm_back_rows(grad, normed, inverse, gain_ref[...])
        out_ref[...] = total.astype(BF16)
        column_sums(sums_ref, (grad * normed, grad))

    block = spec((step, width), lambda i, s: (i, 0))
    return run(
        kernel, "first_back", scal, (local // step,), [block] * 4 + [held(1, width)],
        [block, held(8, width)], [struct(local, width), struct(8, width, dtype=F32)],
        (grad, received, x, wide, gain),
    )


def layer_rows(scal, own, received, middle, bias):
    local, width = middle.shape
    step = row_step(local)

    def kernel(s_ref, o_ref, r_ref, mid_ref, bias_ref, out_ref):
        total = mid_ref[...] + o_ref[...].astype(F32) + r_ref[...].astype(F32) + bias_ref[...]
        out_ref[...] = total.astype(BF16)

    block = spec((step, width), lambda i, s: (i, 0))
    return run(
        kernel, "layer_rows", scal, (local // step,), [block] * 3 + [held(1, width)],
        block, struct(local, width), (own, received, middle, bias),
    )


def finish_feed_kernel(s_ref, *refs, tile):
    sums, (up_out, down_out) = refs[:8], refs[8:]
    first = s_ref[2] == 0
    even = s_ref[1] == 0
    for j in range(2):
        mine, beside, mine_across, beside_across = [ref[...] for ref in sums[4 * j : 4 * j + 4]]
        if j == 1:
            mine, beside = jnp.where(even, mine, beside), jnp.where(even, beside, mine)
            mine_across, beside_across = (
                jnp.where(even, mine_across, beside_across),
                jnp.where(even, beside_across, mine_across),
            )
        for kind, own, other in ((0, mine, mine_across), (1, beside, beside_across)):
            for c in range(2):
                wide = jnp.where(first == (c == 0), own, other).astype(F32)
                if kind == 1:
                    down_out[c, j] = wide
                    continue
                for h in range(2):
                    start = ((h * 2 + c) * 2 + j) * tile
                    up_out[:, start : start + tile] = wide[:, h * tile : (h + 1) * tile]


def finish_feed(scal, sums):
    rows, width = sums[0].shape
    tile = rows
    steps = 4
    block = spec((rows // steps, width), lambda i, s: (i, 0))
    up, down = run(
        functools.partial(finish_feed_kernel, tile=tile), "finish_feed", scal, (steps,),
        [block] * 8,
        [
            spec((rows // steps, 4 * width), lambda i, s: (i, 0)),
            spec((2, 2, rows // steps, width), lambda i, s: (0, 0, i, 0)),
        ],
        [struct(rows, 4 * width, dtype=F32), struct(2, 2, rows, width, dtype=F32)],
        sums,
    )
    return up, down.reshape(4 * rows, width)


def finish_qkv_kernel(s_ref, *refs, pairs, spans):
    outs = refs[-3:]
    count = len(spans)
    owns, others = refs[:count], refs[count : 2 * count]
    first = s_ref[2] == 0
    half_pairs = pairs // 2
    for g, (begin, end) in enumerate(spans):
        own, other = owns[g][...], others[g][...]
        for c in range(2):
            wide = jnp.where(first == (c == 0), own, other).astype(F32).T
            for q in range(end - begin):
                pair = begin + q
                h, p = pair // half_pairs, pair % half_pairs
                goal = ((h * 2 + c) * half_pairs + p) * PAIR
                for i in range(3):
                    start = (q * 3 + i) * PAIR
                    outs[i][:, goal : goal + PAIR] = wide[:, start : start + PAIR]


def finish_qkv(scal, owns, others, spans):
    rows = owns[0].shape[1]
    pairs = spans[-1][1]
    steps = 4
    blocks = [
        spec((3 * PAIR * (end - begin), rows // steps), lambda i, s: (0, i)) for begin, end in spans
    ]
    return run(
        functools.partial(finish_qkv_kernel, pairs=pairs, spans=spans), "finish_qkv", scal,
        (steps,), blocks * 2,
        [spec((rows // steps, 2 * pairs * PAIR), lambda i, s: (i, 0))] * 3,
        [struct(rows, 2 * pairs * PAIR, dtype=F32)] * 3, (*owns, *others),
    )


def wide_back_kernel(
    tile, rows, padded, qkv_ref, grad_ref, out_ref, lse_ref, dqkv_ref, q_t, g_t, k_t, delta,
    dq_t, dk_t, dv_t,
):
    scale = HEAD_DIM**-0.5
    q_t[:, :rows] = qkv_ref[:, :PAIR].T
    g_t[:, :rows] = grad_ref[...].T
    if padded > rows:
        q_t[:, rows:] = jnp.zeros((PAIR, padded - rows), BF16)
        g_t[:, rows:] = jnp.zeros((PAIR, padded - rows), BF16)
        delta[:, rows:] = jnp.zeros((2, padded - rows), F32)
    k_t[...] = qkv_ref[:, PAIR : 2 * PAIR].T
    product = (grad_ref[...].astype(F32) * out_ref[...].astype(F32)).T
    delta[0:1, :rows] = jnp.sum(product[:HEAD_DIM, :], axis=0, keepdims=True)
    delta[1:2, :rows] = jnp.sum(product[HEAD_DIM:, :], axis=0, keepdims=True)
    dk_t[...] = jnp.zeros_like(dk_t)
    dv_t[...] = jnp.zeros_like(dv_t)

    def block(index, carry):
        columns = pl.ds(pl.multiple_of(index * tile, tile), tile)
        empty = jnp.zeros((HEAD_DIM, tile), BF16)
        for head in range(2):
            lanes = slice(head * HEAD_DIM, (head + 1) * HEAD_DIM)
            query = q_t[lanes, columns]
            grad = g_t[lanes, columns]
            query_pad = jnp.concatenate([query, empty] if head == 0 else [empty, query], axis=0)
            grad_pad = jnp.concatenate([grad, empty] if head == 0 else [empty, grad], axis=0)
            scores = contract(qkv_ref[:, PAIR : 2 * PAIR], query_pad, 1, 0)
            grad_probs = contract(qkv_ref[:, 2 * PAIR :], grad_pad, 1, 0)
            weights = jnp.exp2(scores * (scale * LOG2E) - lse_ref[head : head + 1, columns])
            grad_scores = (weights * (grad_probs - delta[head : head + 1, columns])).astype(BF16)
            dv_t[lanes, :] += contract(grad, weights.astype(BF16), 1, 1)
            dq_t[lanes, columns] = contract(k_t[lanes, :], grad_scores, 1, 0)
            dk_t[lanes, :] += contract(query, grad_scores, 1, 1)
        return carry

    lax.fori_loop(0, padded // tile, block, 0)
    dqkv_ref[:, :PAIR] = (dq_t[...].T[:rows, :] * scale).astype(BF16)
    dqkv_ref[:, PAIR : 2 * PAIR] = (dk_t[...].T * scale).astype(BF16)
    dqkv_ref[:, 2 * PAIR :] = dv_t[...].T.astype(BF16)


def wide_back(qkv, grad, out, lse, first_pair, last_pair, tile=256):
    rows, width = qkv.shape
    padded = -(-rows // tile) * tile
    count = last_pair - first_pair
    return pl.pallas_call(
        functools.partial(wide_back_kernel, tile, rows, padded),
        grid=(count,),
        in_specs=[
            pl.BlockSpec((rows, 3 * PAIR), lambda i: (0, i + first_pair)),
            pl.BlockSpec((rows, PAIR), lambda i: (0, i + first_pair)),
            pl.BlockSpec((rows, PAIR), lambda i: (0, i + first_pair)),
            pl.BlockSpec((None, 2, lse.shape[2]), lambda i: (i + first_pair, 0, 0)),
        ],
        out_specs=pl.BlockSpec((rows, 3 * PAIR), lambda i: (0, i)),
        out_shape=jax.ShapeDtypeStruct((rows, 3 * PAIR * count), BF16),
        scratch_shapes=[
            pltpu.VMEM((PAIR, padded), BF16),
            pltpu.VMEM((PAIR, padded), BF16),
            pltpu.VMEM((PAIR, rows), BF16),
            pltpu.VMEM((2, padded), F32),
            pltpu.VMEM((PAIR, padded), F32),
            pltpu.VMEM((PAIR, rows), F32),
            pltpu.VMEM((PAIR, rows), F32),
        ],
        compiler_params=pltpu.CompilerParams(vmem_limit_bytes=VMEM_LIMIT),
        cost_estimate=pl.CostEstimate(
            flops=160 * rows * rows * PAIR * count,
            bytes_accessed=16 * rows * PAIR * count,
            transcendentals=2 * rows * rows * count,
        ),
        name="wide_back",
    )(qkv, grad, out, lse)


def wide_feed_kernel(
    half_ref, *refs, parts, make, chunk,
):
    xs, refs = refs[:parts], refs[parts:]
    dys, refs = refs[:parts], refs[parts:]
    if not make:
        x_t, refs = refs[0], refs[1:]
    up_ref, bias_ref, down_ref, *refs = refs
    hidden_ref, d_pre_ref, up_send, up_keep, down_send, down_keep, bias_grad_ref, *refs = refs
    if make:
        x_t, refs = refs[0], refs[1:]
    x, dy, sems = refs
    index = pl.program_id(0)
    half = half_ref[0]
    rows, width = x.shape
    block = rows // parts
    own = width // 2
    tile = up_ref.shape[1]

    @pl.when(index == 0)
    def _():
        copies = []
        for i in range(parts):
            part = pl.ds(i * block, block)
            copies.append(pltpu.make_async_copy(xs[i], x.at[part], sems.at[i]))
            copies.append(pltpu.make_async_copy(dys[i], dy.at[part], sems.at[parts + i]))
        for copy in copies:
            copy.start()
        for copy in copies:
            copy.wait()
        if make:
            x_t[...] = x[...].T

    bias_grad = jnp.zeros(bias_grad_ref.shape, F32)
    for start in range(0, rows, chunk):
        part = slice(start, start + chunk)
        pre = contract(x[part, :], up_ref[...], 1, 0) + bias_ref[...]
        d_hidden = contract(dy[part, :], down_ref[...], 1, 1)
        share = 0.5 * (1.0 + lax.erf(pre * 0.7071067811865476))
        hidden_ref[part, :] = (pre * share).astype(BF16)
        slope = share + pre * (jnp.exp(-0.5 * pre * pre) * 0.3989422804014327)
        d_low = (d_hidden * slope).astype(BF16)
        d_pre_ref[part, :] = d_low
        bias_grad = bias_grad + jnp.sum(d_low.astype(F32), axis=0, keepdims=True)
    bias_grad_ref[...] = bias_grad
    columns = pl.ds(pl.multiple_of(index * tile, tile), tile)
    mine = pl.ds(pl.multiple_of(half * own, own), own)
    theirs = pl.ds(pl.multiple_of((1 - half) * own, own), own)
    up_keep[:, columns] = contract(x_t[mine, :], d_pre_ref[...], 1, 0).astype(BF16)
    up_send[:, columns] = contract(x_t[theirs, :], d_pre_ref[...], 1, 0).astype(BF16)
    down_grad = contract(hidden_ref[...], dy[...], 0, 0).astype(BF16)

    @pl.when(index == half)
    def _():
        down_keep[...] = down_grad

    @pl.when(index != half)
    def _():
        down_send[...] = down_grad


def wide_feed(half, xs, dys, x_t, up, bias, down):
    parts = len(xs)
    width = xs[0].shape[1]
    rows = sum(part.shape[0] for part in xs)
    hidden = up.shape[1]
    tile = hidden // 2
    make = x_t is None
    chunk = rows // 2 if rows % 32 == 0 else rows
    anywhere = pl.BlockSpec(memory_space=pl.ANY)
    fixed = lambda shape: pl.BlockSpec(shape, lambda j, s: (0, 0), pipeline_mode=pl.Buffered(1))
    across = lambda size: pl.BlockSpec((size, tile), lambda j, s: (0, j))
    out_specs = [across(rows)] * 2 + [fixed((width // 2, hidden))] * 2
    out_specs += [fixed((tile, width))] * 2 + [across(1)]
    out_shape = [
        jax.ShapeDtypeStruct((rows, hidden), BF16),
        jax.ShapeDtypeStruct((rows, hidden), BF16),
        jax.ShapeDtypeStruct((width // 2, hidden), BF16),
        jax.ShapeDtypeStruct((width // 2, hidden), BF16),
        jax.ShapeDtypeStruct((tile, width), BF16),
        jax.ShapeDtypeStruct((tile, width), BF16),
        jax.ShapeDtypeStruct((1, hidden), F32),
    ]
    if make:
        out_specs.append(fixed((width, rows)))
        out_shape.append(jax.ShapeDtypeStruct((width, rows), BF16))
    return pl.pallas_call(
        functools.partial(wide_feed_kernel, parts=parts, make=make, chunk=chunk),
        grid_spec=pltpu.PrefetchScalarGridSpec(
            num_scalar_prefetch=1,
            grid=(2,),
            in_specs=[anywhere] * (2 * parts)
            + ([] if make else [fixed((width, rows))])
            + [across(width), across(1), pl.BlockSpec((tile, width), lambda j, s: (j, 0))],
            out_specs=out_specs,
            scratch_shapes=[
                pltpu.VMEM((rows, width), BF16),
                pltpu.VMEM((rows, width), BF16),
                pltpu.SemaphoreType.DMA((2 * parts,)),
            ],
        ),
        out_shape=out_shape,
        compiler_params=pltpu.CompilerParams(vmem_limit_bytes=VMEM_LIMIT),
        cost_estimate=pl.CostEstimate(
            flops=8 * rows * width * hidden,
            bytes_accessed=8 * rows * width + 8 * width * hidden,
            transcendentals=2 * rows * hidden,
        ),
        name="wide_feed",
    )(half.reshape(1), *xs, *dys, *(() if make else (x_t,)), up, bias, down)


def norm_parts(values, gain, shift):
    average = jnp.mean(values, axis=-1, keepdims=True)
    centred = values - average
    spread = jnp.mean(centred * centred, axis=-1, keepdims=True)
    inverse = lax.rsqrt(spread + EPS)
    normed = centred * inverse
    return (normed * gain + shift, normed, inverse)


def norm_back(grad, normed, inverse, gain):
    scaled = grad * gain
    first_term = jnp.mean(scaled, axis=-1, keepdims=True)
    second_term = jnp.mean(scaled * normed, axis=-1, keepdims=True)
    result = inverse * (scaled - first_term - normed * second_term)
    return (result, jnp.sum(grad * normed, axis=0), jnp.sum(grad, axis=0))


def pick(values, index, axis):
    return lax.dynamic_index_in_dim(values, index, axis, keepdims=False)


def join(own, other, index):
    return jnp.where(index == 0, jnp.stack([own, other]), jnp.stack([other, own]))


def after(values, *earlier):
    return lax.optimization_barrier((values,) + earlier)[0]


def wide_body(
    rep, grp, tokens, query_weight, key_weight, value_weight, query_bias, value_bias, out_weight,
    out_bias, first_gain, first_shift, second_gain, second_shift, up_weight, up_bias,
    down_weight, down_bias, cotangent,
):
    clips, local, width = tokens.shape
    assert clips == 1
    quarter = grp // 2
    ring = rep // 2
    deep = ring // 2
    core = lax.axis_index("core")
    half = lax.axis_index("half")
    gq = lax.axis_index("gq")
    place = lax.axis_index("rz")
    low = place % 2
    high = place // 2
    own_rows = width // grp
    pairs = own_rows // PAIR
    hidden = up_weight.shape[1]
    set_hidden = hidden // grp
    ranges = max(1, set_hidden // width)
    tile = set_hidden // (2 * ranges)

    there = []
    for b in range(2):
        for h in range(2):
            for q in range(quarter):
                g = h * quarter + q
                source = (b * 2 + h) * quarter + q
                target = ((g % 2) * 2 + b) * quarter + g // 2
                if source != target:
                    there.append((source, target))
    back = [(target, source) for source, target in there]
    block = half * quarter + gq
    stays = (block % 2 == core) & (block // 2 == gq) & (half == core)
    axes = ("core", "half", "gq")
    beside = [(i, i ^ 1) for i in range(ring)]

    def move(values, route):
        return jnp.where(stays, values, lax.ppermute(values, axes, route))

    def swap_half(values):
        return lax.ppermute(values, "half", SWAP)

    def swap_core(values):
        return lax.ppermute(values, "core", SWAP)

    def spread(values):
        if grp == 2:
            return [values, swap_core(values)]
        return [lax.all_gather(values, ("gq", "core"), axis=0, tiled=True)]

    def collect(values):
        if grp == 2:
            other = swap_core(values(slice(local, None)).astype(BF16))
            return values(slice(None, local)) + other.astype(F32)
        return lax.psum_scatter(
            values(slice(None)).astype(BF16), ("gq", "core"), scatter_dimension=0, tiled=True
        ).astype(F32)

    def other_half(pieces):
        mine = pick(jnp.stack(pieces), low, 0)
        first = swap_half(mine)
        second = lax.ppermute(first, "rz", beside)
        return first, jnp.where(low == 0, first, second), jnp.where(low == 0, second, first)

    def by_half(own, other):
        return join(own, other, half).reshape(-1, own.shape[-1])

    def set_columns(values, inner=1):
        parts = values.reshape(values.shape[0], 2, quarter, 2, inner, -1)
        return pick(parts, core, 3).transpose(0, 2, 3, 1, 4)

    def gather_rows(values):
        if quarter > 1:
            values = lax.all_to_all(values, "gq", split_axis=1, concat_axis=0, tiled=True)
        return values.reshape(-1, values.shape[-1])

    def set_entries(values, inner=1):
        parts = values.reshape(2, quarter, 2, inner, -1)
        return pick(pick(parts, core, 2), gq, 1).transpose(1, 0, 2).reshape(inner, 1, -1)

    clip_tokens = move(tokens.reshape(local, width), there)
    vectors = jnp.concatenate(
        [query_bias, value_bias, out_bias, first_gain, first_shift, second_gain, second_shift,
         down_bias, up_bias]
    )
    if quarter > 1:
        vectors = lax.all_gather(vectors, "gq", axis=0)
    vectors = join(vectors, swap_half(vectors), half).reshape(grp, -1)
    (full_qbias, full_vbias, full_obias, gain_one, shift_one, gain_two, shift_two, full_dbias) = [
        vectors[:, i * own_rows : (i + 1) * own_rows].reshape(-1) for i in range(8)
    ]
    bias_sets = set_entries(vectors[:, 8 * own_rows :].reshape(-1), ranges)

    parts = [
        set_columns(w).reshape(own_rows, quarter, pairs, PAIR)
        for w in (query_weight, key_weight, value_weight)
    ]
    own_qkv = gather_rows(jnp.stack(parts, axis=3).reshape(own_rows, quarter, 3 * own_rows))
    own_qkv = own_qkv.reshape(2, -1, 3 * own_rows)
    qkv_x, low_rows, high_rows = other_half([own_qkv[0], own_qkv[1]])
    qkv_weight = by_half(
        own_qkv.reshape(-1, 3 * own_rows), jnp.concatenate([low_rows, high_rows], axis=0)
    )
    own_out = pick(out_weight.reshape(2, -1, width), core, 0)
    out_x, low_rows, high_rows = other_half(
        [after(own_out, qkv_x)[: own_rows // 4], own_out[own_rows // 4 :]]
    )
    out_set = by_half(own_out, jnp.concatenate([low_rows, high_rows], axis=0))

    own_up = set_columns(up_weight, ranges)
    own_down = pick(down_weight.reshape(2, ranges, tile, width), core, 0)
    up_sets, down_sets, stages = [], [], [out_x]
    for j in range(ranges):
        up_part = gather_rows(own_up[:, :, j].reshape(own_rows, quarter, 2 * tile))
        down_part = own_down[j]
        if up_part.shape == down_part.shape:
            stage, other_up, other_down = other_half([after(up_part, stages[-1]), down_part])
        else:
            stage, other_up = swap_half(after(up_part, stages[-1])), None
            other_up, other_down = stage, swap_half(down_part)
        stages.append(stage)
        up_sets.append(by_half(up_part, other_up))
        down_sets.append(by_half(down_part, other_down))
    grad_out = move(after(cotangent.reshape(local, width), stages[1]), there)

    zeros = jnp.zeros((1, own_rows), F32)
    qkv_bias = jnp.stack(
        [
            b.reshape(pairs, PAIR)
            for b in (set_entries(full_qbias), zeros, set_entries(full_vbias))
        ],
        axis=1,
    ).reshape(1, 3 * own_rows)

    inputs = clip_tokens.astype(F32)
    first_norm, first_normed, first_inverse = norm_parts(inputs, gain_one, shift_one)
    first = jnp.concatenate(spread(first_norm.astype(BF16)), axis=0)
    qkv = (contract(first, qkv_weight, 1, 0) + qkv_bias).astype(BF16)
    if pairs > 1:
        kept = attend(qkv, 0, pairs // 2)
        mixed, lse = attend(qkv, pairs // 2, pairs, kept)
    else:
        mixed, lse = attend(qkv, 0, pairs)
    middle = collect(lambda rows: contract(mixed[rows], out_set, 1, 0)) + inputs + full_obias
    second_norm, second_normed, second_inverse = norm_parts(middle, gain_two, shift_two)
    seconds = spread(second_norm.astype(BF16))
    grads_out = spread(grad_out)
    x_t = None
    feeds = []
    for j in range(ranges):
        outs = wide_feed(
            half, seconds, grads_out, x_t, up_sets[j],
            bias_sets[j] if j == 0 else after(bias_sets[j], feeds[-1][6]), down_sets[j],
        )
        x_t = outs[7] if j == 0 else x_t
        feeds.append(outs)

    def reduce_ring(pair):
        send, keep = pair
        total = keep.astype(F32) + lax.ppermute(send, "rz", beside).astype(F32)
        total = total.astype(BF16).reshape(deep, -1, keep.shape[-1])
        shifts = range(1, deep)

        def route(shift):
            return [(i, (i + 2 * shift) % ring) for i in range(ring)]

        pieces = [
            lax.ppermute(pick(total, (high + s) % deep, 0), "rz", route(s)) for s in shifts
        ]
        piece = pick(total, high, 0).astype(F32)
        for other in pieces:
            piece = piece + other.astype(F32)
        piece = piece.astype(BF16)
        gathered = [piece] + [lax.ppermute(piece, "rz", route(s)) for s in shifts]
        whole = jnp.stack(
            [
                functools.reduce(
                    lambda rest, s: jnp.where((high - s) % deep == i, gathered[s], rest),
                    shifts,
                    piece,
                )
                for i in range(deep)
            ]
        ).reshape(keep.shape)
        return whole, lax.ppermute(whole, "rz", beside)

    def reduce_parts(parts):
        stacked = jnp.stack(parts)
        own, other = reduce_ring((pick(stacked, 1 - low, 0), pick(stacked, low, 0)))
        return jnp.where(low == 0, own, other), jnp.where(low == 0, other, own)

    def add_half(keep, send):
        return (keep.astype(F32) + swap_half(send).astype(F32)).astype(BF16)

    def reduce_rows(values):
        size = values.shape[0]
        if size % (16 * ring):
            return lax.psum(values, "rz")
        return jnp.concatenate(reduce_parts([values[: size // 2], values[size // 2 :]]), axis=0)

    def scatter_half(values):
        values = values.reshape(2, -1, values.shape[-1])
        return add_half(pick(values, half, 0), pick(values, 1 - half, 0))

    sums_feed = []
    for outs in feeds:
        up_part, down_part = add_half(outs[3], outs[2]), add_half(outs[5], outs[4])
        if up_part.shape == down_part.shape:
            sums_feed.extend(reduce_parts([up_part, down_part]))
        else:
            sums_feed.extend([reduce_rows(up_part), reduce_rows(down_part)])

    grad_wide = grad_out.astype(F32)
    grad_second = collect(
        lambda rows: functools.reduce(
            jnp.add, [contract(feeds[j][1][rows], up_sets[j], 1, 1) for j in range(ranges)]
        )
    )
    grad_second, grad_gain_two, grad_shift_two = norm_back(
        grad_second, second_normed, second_inverse, gain_two
    )
    grad_middle = grad_wide + grad_second
    grad_middle_low = grad_middle.astype(BF16)
    grad_middle_all = jnp.concatenate(spread(grad_middle_low), axis=0)
    grad_mixed = contract(grad_middle_all, out_set, 1, 1).astype(BF16)
    out_half = reduce_rows(scatter_half(contract(mixed, grad_middle_all, 0, 0).astype(BF16)))
    spans = [(0, pairs // 2), (pairs // 2, pairs)] if pairs > 1 else [(0, pairs)]
    dqkvs, qkv_halves = [], []
    for begin, end in spans:
        gate = lse if not dqkvs else after(lse, qkv_halves[-1])
        dqkvs.append(wide_back(qkv, grad_mixed, mixed, gate, begin, end))
        qkv_halves.append(contract(first, dqkvs[-1], 0, 0).astype(BF16))
    qkv_halves = [reduce_rows(scatter_half(values)) for values in qkv_halves]

    result = collect(
        lambda rows: functools.reduce(
            jnp.add, [contract(feeds[j][0][rows], down_sets[j], 1, 0) for j in range(ranges)]
        )
    )
    result = (middle + result + full_dbias).astype(BF16)
    layer_out = move(result, back).reshape(1, local, width)

    def weight_of(span):
        return qkv_weight[:, span[0] * 3 * PAIR : span[1] * 3 * PAIR]

    grad_first_norm = collect(
        lambda rows: functools.reduce(
            jnp.add,
            [contract(d[rows], weight_of(span), 1, 1) for d, span in zip(dqkvs, spans)],
        )
    )
    grad_first, grad_gain_one, grad_shift_one = norm_back(
        grad_first_norm, first_normed, first_inverse, gain_one
    )
    tokens_grad = move((grad_middle + grad_first).astype(BF16), back).reshape(1, local, width)

    out_weight_grad = join(out_half, swap_core(out_half), core).reshape(-1, width).astype(F32)
    if True:

        def finish_columns(values):
            values = values.reshape(quarter, own_rows, 1, -1)
            values = lax.all_to_all(values, "gq", split_axis=0, concat_axis=2, tiled=True)
            values = values.reshape(own_rows, quarter, -1)
            return join(values, swap_core(values), core).transpose(1, 0, 2, 3)

        def natural_columns(values, inner=1):
            values = values.reshape(own_rows, 2, quarter, inner, 2, -1)
            return values.transpose(0, 4, 2, 1, 3, 5).reshape(own_rows, -1).astype(F32)

        ups = jnp.stack([finish_columns(values) for values in sums_feed[::2]], axis=3)
        up_weight_grad = natural_columns(ups, ranges)
        downs = jnp.stack(sums_feed[1::2])
        down_weight_grad = join(downs, swap_core(downs), core).reshape(-1, width).astype(F32)
        columns = jnp.concatenate([finish_columns(values) for values in qkv_halves], axis=3)
        columns = columns.reshape(own_rows, 2, quarter, pairs, 3, PAIR)
        query_weight_grad, key_weight_grad, value_weight_grad = [
            natural_columns(columns[:, :, :, :, i]) for i in range(3)
        ]

    def place_entries(values, inner=1):
        values = values.reshape(inner, 2, 1, 1, -1).transpose(1, 2, 3, 0, 4)
        shape = (2, quarter, 2) + values.shape[3:]
        zero = jnp.zeros((), core.dtype)
        return lax.dynamic_update_slice(
            jnp.zeros(shape, F32), values, (zero, gq, core, zero, zero)
        ).reshape(grp, -1)

    dqkv_sums = jnp.concatenate([jnp.sum(d.astype(F32), axis=0) for d in dqkvs])
    dqkv_sums = dqkv_sums.reshape(pairs, 3, PAIR)
    sums = [
        place_entries(dqkv_sums[:, 0]),
        place_entries(dqkv_sums[:, 2]),
        jnp.sum(grad_middle_low.astype(F32), axis=0),
        grad_gain_one, grad_shift_one, grad_gain_two, grad_shift_two,
        jnp.sum(grad_wide, axis=0),
        place_entries(jnp.stack([outs[6] for outs in feeds]), ranges),
    ]
    sums = jnp.concatenate([s.reshape(grp, -1) for s in sums], axis=1)
    if grp == 2 and ring & (ring - 1) == 0:
        sums = sums + swap_core(sums)
        sums = pick(sums, half, 0) + swap_half(pick(sums, 1 - half, 0))
        step = 1
        while step < ring:
            sums = sums + lax.ppermute(sums, "rz", [(i, i ^ step) for i in range(ring)])
            step *= 2
    else:
        sums = lax.psum(sums, ("rz", "core", "half", "gq"))
        sums = pick(sums, half * quarter + gq, 0)
    small = [sums[i * own_rows : (i + 1) * own_rows] for i in range(8)]
    return (
        layer_out, tokens_grad, query_weight_grad, key_weight_grad, value_weight_grad,
        small[0], small[1], out_weight_grad, small[2], small[3], small[4], small[5], small[6],
        up_weight_grad, sums[8 * own_rows :], down_weight_grad, small[7],
    )


class LineSum:
    def __init__(self, place, ring, values):
        self.high, self.ring, self.deep = place // 2, ring, ring // 2
        self.shape = values.shape
        pieces = values.reshape(self.deep, -1, values.shape[-1])
        self.piece = pick(pieces, self.high, 0)
        self.sent = [pick(pieces, (self.high + s) % self.deep, 0) for s in range(1, self.deep)]
        self.received = [
            lax.ppermute(piece, "rz", self.route(s))
            for s, piece in enumerate(self.sent, start=1)
        ]

    def route(self, shift):
        return [(i, (i + 2 * shift) % self.ring) for i in range(self.ring)]

    def spread(self, *gates):
        piece = self.piece.astype(F32)
        for other in after_all(self.received, *gates):
            piece = piece + other.astype(F32)
        self.piece = piece.astype(BF16)
        self.received = [
            lax.ppermute(self.piece, "rz", self.route(s)) for s in range(1, self.deep)
        ]
        return self.piece

    def whole(self, *gates):
        gathered = [self.piece] + list(after_all(self.received, *gates))
        return jnp.concatenate(
            [
                functools.reduce(
                    lambda rest, s: jnp.where((self.high - s) % self.deep == i, gathered[s], rest),
                    range(1, self.deep),
                    gathered[0],
                )
                for i in range(self.deep)
            ],
            axis=0,
        ).reshape(self.shape)


def add_low(left, right):
    return (left.astype(F32) + right.astype(F32)).astype(BF16)


def after_all(values, *gates):
    if not gates:
        return tuple(values)
    return lax.optimization_barrier(tuple(values) + gates)[: len(values)]


def pair_body(
    rep, grp, tokens, query_weight, key_weight, value_weight, query_bias, value_bias, out_weight,
    out_bias, first_gain, first_shift, second_gain, second_shift, up_weight, up_bias,
    down_weight, down_bias, cotangent,
):
    clips, local, width = tokens.shape
    assert clips == 1
    ring = rep // 2
    deep = ring // 2
    core, half, place = lax.axis_index("core"), lax.axis_index("half"), lax.axis_index("rz")
    low, high = place % 2, (place // 2) % 2
    own_rows = width // 2
    pairs = own_rows // PAIR
    hidden = up_weight.shape[1]
    stays = core == half
    scal = jnp.stack([half, low, core, stays.astype(jnp.int32), high]).astype(jnp.int32)
    cross = [(1, 2), (2, 1)]

    def swap_half(values):
        return lax.ppermute(values, "half", SWAP)

    def swap_core(values):
        return lax.ppermute(values, "core", SWAP)

    def swap_low(values):
        return lax.ppermute(values, "rz", [(i, i ^ 1) for i in range(ring)])

    def swap_high(values):
        return lax.ppermute(values, "rz", [(i, i ^ 2) for i in range(ring)])

    def cross_over(values):
        return lax.ppermute(values, ("core", "half"), cross)

    tokens, cotangent = tokens.reshape(local, width), cotangent.reshape(local, width)

    own_qkv, mine = pack_qkv(scal, (query_weight, key_weight, value_weight))
    qkv_x = swap_half(mine)
    vectors = jnp.concatenate(
        [query_bias, value_bias, out_bias, first_gain, first_shift, second_gain, second_shift,
         down_bias, up_bias]
    )
    vectors = join(vectors, swap_half(vectors), half)
    (full_qbias, full_vbias, full_obias, gain_one, shift_one, gain_two, shift_two, full_dbias) = [
        vectors[:, i * own_rows : (i + 1) * own_rows].reshape(1, width) for i in range(8)
    ]

    def set_entries(values, inner=1):
        return pick(values.reshape(2, 2, inner, -1), core, 1).transpose(1, 0, 2).reshape(inner, -1)

    bias_set = set_entries(vectors[:, 8 * own_rows :], 2).reshape(1, -1)
    packed = [pack_feed(scal, up_weight, down_weight, j, 2, (1, 4)[j]) for j in range(2)]
    quarter = own_rows // 4
    out_mine = lax.dynamic_slice(
        out_weight, (core * (own_rows // 2) + low * quarter, 0 * core), (quarter, width)
    )
    tokens, qkv_x, *packed = lax.optimization_barrier((tokens, qkv_x, *packed))
    qkv_y = swap_low(qkv_x)
    tokens_in = cross_over(tokens)
    x, first = first_norm(scal, tokens, tokens_in, gain_one, shift_one)
    first_in = swap_core(first)
    out_mine, packed[0], packed[1], x = lax.optimization_barrier(
        (out_mine, packed[0], packed[1], x)
    )
    out_x = swap_half(out_mine)
    feed_x = [swap_half(values) for values in packed]
    zeros = jnp.zeros((pairs, PAIR), F32)
    qkv_bias = jnp.stack(
        [set_entries(full_qbias).reshape(pairs, PAIR), zeros,
         set_entries(full_vbias).reshape(pairs, PAIR)],
        axis=1,
    ).reshape(1, 3 * own_rows)
    qkv, qkv_weight, first_all = project(
        scal, (first, first_in), own_qkv, qkv_x, qkv_y, qkv_bias
    )

    mixed, lse = attend(qkv, 0, pairs // 2)
    out_x, feed_x[0], feed_x[1], cotangent, lse = lax.optimization_barrier(
        (out_x, feed_x[0], feed_x[1], cotangent, lse)
    )
    out_y = swap_low(out_x)
    feed_y = [swap_low(feed_x[0]), swap_high(feed_x[1])]
    cotangent_in = cross_over(cotangent)
    mixed, lse = attend(qkv, pairs // 2, pairs, (mixed, lse))
    out_part, out_set = out_other(scal, mixed, out_weight, out_x, out_y)
    out_in = swap_core(out_part)
    grad_out = jnp.where(stays, cotangent, after(cotangent_in, lse))
    grad_out_in = swap_core(grad_out)
    middle, second = second_norm(
        scal, mixed, out_set, x, out_in, full_obias, gain_two, shift_two
    )
    second_in = swap_core(second)

    (
        out_own, out_part, dx_own, dx_part, up_send, up_keep, down_send, down_keep, low_send,
        low_keep, up_bias_grad,
    ) = feed(
        scal, (second, second_in), (grad_out, grad_out_in), up_weight, down_weight,
        (feed_x[0], feed_y[0], feed_x[1], feed_y[1]), bias_set,
    )
    first_in_half = [swap_half(up_send), swap_half(down_send)]
    second_in_low = swap_low(low_send)
    dx_in = swap_core(dx_part)
    grad_low, sums_two = second_back(scal, dx_own, dx_in, middle, grad_out, gain_two)
    grad_low_in = swap_core(grad_low)
    grad_mixed, out_send, out_keep = mixed_back(scal, (grad_low, grad_low_in), out_set, mixed)

    backs = []

    def back(pair, *issued):
        gate = after(lse, *issued) if issued else lse
        backs.append(attend_back(scal, qkv, grad_mixed, mixed, gate, first_all, pair, pair + 1))
        return backs[-1][3]

    done = back(0)
    up_in, down_in, low_in = after_all((*first_in_half, second_in_low), done)
    up_sum, down_sum = add_low(up_keep, up_in), add_low(down_keep, down_in)
    range_sum = add_low(low_keep, low_in).reshape(2, own_rows, width)
    half_send, half_keep = pick(range_sum, 1 - half, 0), pick(range_sum, half, 0)
    half_in = swap_half(half_send)
    up_sum, down_sum = lax.psum((up_sum, down_sum), "rz")

    done = back(1, half_send)
    (half_in,) = after_all((half_in,), done)
    line = LineSum(place, ring, add_low(half_keep, half_in))

    done = back(2, *line.sent)
    issued = line.spread(done)
    split = 3 * PAIR * (pairs - 1)

    def start_half(sends, keeps, *gates):
        send, keep = jnp.concatenate(sends, axis=0), jnp.concatenate(keeps, axis=0)
        send = after(send, *gates) if gates else send
        return send, keep, swap_half(send)

    most_send, most_keep, most_in = start_half(
        [b[1] for b in backs] + [out_send], [b[2] for b in backs] + [out_keep]
    )

    done = back(3, issued, most_send)
    last_send, last_keep, last_in = start_half([backs[3][1]], [backs[3][2]])

    def halves(values):
        parts = values.reshape(deep, 2, -1, values.shape[-1])
        return (
            pick(parts, low, 1).reshape(-1, values.shape[-1]),
            pick(parts, 1 - low, 1).reshape(-1, values.shape[-1]),
        )

    def meet(own, other):
        width_in = own.shape[-1]
        return join(
            own.reshape(deep, -1, width_in), other.reshape(deep, -1, width_in), low
        ).transpose(1, 0, 2, 3).reshape(-1, width_in)

    first_own, first_part = first_grad(scal, [b[0] for b in backs], qkv_weight)
    first_part_in = swap_core(first_part)
    range_whole = line.whole(done)
    range_beside = swap_low(range_whole)
    range_across = swap_core(range_whole)

    most_in, last_in = after_all((most_in, last_in), first_own)
    most_keep, most_send = halves(add_low(most_keep, most_in))
    last_keep, last_send = halves(add_low(last_keep, last_in))
    most_low, last_low = swap_low(most_send), swap_low(last_send)
    tokens_out, sums_one = first_back(
        scal, first_own, after(first_part_in, most_send, last_send), x, grad_low, gain_one
    )
    out_in = swap_core(out_part)
    layer = layer_rows(scal, out_own, out_in, middle, full_dbias)
    layer_out = jnp.where(stays, layer, cross_over(layer))
    tokens_grad = jnp.where(stays, tokens_out, cross_over(tokens_out))

    most_line = LineSum(place, ring, add_low(most_keep, most_low))
    last_line = LineSum(place, ring, add_low(last_keep, last_low))
    most_line.spread()
    last_line.spread()
    most_whole, last_whole = most_line.whole(), last_line.whole()
    most_sum = meet(most_whole, swap_low(most_whole))
    last_sum = meet(last_whole, swap_low(last_whole))

    up_weight_grad, down_weight_grad = finish_feed(
        scal,
        (
            up_sum, down_sum, swap_core(up_sum), swap_core(down_sum),
            range_whole, range_beside, range_across, swap_core(range_beside),
        ),
    )
    most_across, last_across = swap_core(most_sum), swap_core(last_sum)
    query_weight_grad, key_weight_grad, value_weight_grad = finish_qkv(
        scal, (most_sum, last_sum), (most_across, last_across),
        ((0, pairs - 1), (pairs - 1, pairs)),
    )
    out_weight_grad = join(most_sum[split:], most_across[split:], core)
    out_weight_grad = out_weight_grad.reshape(2, 2, own_rows // 2, own_rows)
    out_weight_grad = jnp.concatenate([out_weight_grad[:, 0], out_weight_grad[:, 1]], axis=2)
    out_weight_grad = out_weight_grad.reshape(own_rows, width).astype(F32)

    def place_entries(values, inner=1):
        values = values.reshape(inner, 2, 1, -1).transpose(1, 2, 0, 3)
        empty = jnp.zeros_like(values)
        return join(values[:, 0], empty[:, 0], core).transpose(1, 0, 2, 3).reshape(2, -1)

    parts = jnp.concatenate([b[3][0] for b in backs]).reshape(pairs, 3, PAIR)
    entries = [
        place_entries(parts[:, 0]), place_entries(parts[:, 2]), sums_two[3], sums_one[0],
        sums_one[1], sums_two[0], sums_two[1], sums_two[2], place_entries(up_bias_grad, 2),
    ]
    entries = jnp.concatenate([e.reshape(2, -1) for e in entries], axis=1)
    entries = entries + swap_core(entries)
    entries = pick(entries, half, 0) + swap_half(pick(entries, 1 - half, 0))
    step = 1
    while step < ring:
        if ring & (ring - 1):
            entries = lax.psum(entries, "rz")
            break
        entries = entries + lax.ppermute(entries, "rz", [(i, i ^ step) for i in range(ring)])
        step *= 2
    small = [entries[i * own_rows : (i + 1) * own_rows] for i in range(8)]
    return (
        layer_out.reshape(1, local, width), tokens_grad.reshape(1, local, width),
        query_weight_grad, key_weight_grad, value_weight_grad, small[0], small[1],
        out_weight_grad, small[2], small[3], small[4], small[5], small[6], up_weight_grad,
        entries[8 * own_rows :], down_weight_grad, small[7],
    )


def solution(mesh):
    rep, grp = mesh.shape["rep"], mesh.shape["grp"]
    split = Mesh(
        mesh.devices.reshape(rep // 2, 2, 2, grp // 2), ("rz", "core", "half", "gq")
    )
    clip = P(("rz", "core"), ("half", "gq"), None)
    matrix = P(("half", "gq"), None)
    vector = P(("half", "gq"))
    return jax.shard_map(
        functools.partial(pair_body if grp == 2 and rep % 8 == 0 else wide_body, rep, grp),
        mesh=split,
        in_specs=(
            clip, matrix, matrix, matrix, vector, vector, matrix, vector, vector, vector, vector,
            vector, matrix, vector, matrix, vector, clip,
        ),
        out_specs=(
            clip, clip, matrix, matrix, matrix, vector, vector, matrix, vector, vector, vector,
            vector, vector, matrix, vector, matrix, vector,
        ),
        check_vma=False,
    )
```

```python
import functools

import jax
import jax.numpy as jnp
from jax import lax
from jax.experimental import pallas as pl
from jax.experimental.pallas import tpu as pltpu
from jax.sharding import Mesh
from jax.sharding import PartitionSpec as P

HEAD_DIM = 64
PAIR = 2 * HEAD_DIM
EPS = 1e-06
LOG2E = 1.4426950408889634
F32 = jnp.float32
BF16 = jnp.bfloat16
SWAP = [(0, 1), (1, 0)]
VMEM_LIMIT = 62 << 20


def contract(left, right, left_dim, right_dim):
    return lax.dot_general(
        left, right, (((left_dim,), (right_dim,)), ((), ())), preferred_element_type=F32
    )


def attend_kernel(tile, rows, padded, qkv_ref, out_ref, lse_ref, q_t, v_t, out_t):
    scale = HEAD_DIM**-0.5 * LOG2E
    ones = jnp.ones((16, rows), BF16)
    q_t[:, :rows] = qkv_ref[:, :PAIR].T
    if padded > rows:
        q_t[:, rows:] = jnp.zeros((PAIR, padded - rows), BF16)
    values_t = qkv_ref[:, 2 * PAIR :].T
    step = HEAD_DIM + 16
    for head in range(2):
        v_t[head * step : head * step + HEAD_DIM, :] = values_t[
            head * HEAD_DIM : (head + 1) * HEAD_DIM, :
        ]
        v_t[head * step + HEAD_DIM : (head + 1) * step, :] = ones

    def block(index, carry):
        columns = pl.ds(pl.multiple_of(index * tile, tile), tile)
        empty = jnp.zeros((HEAD_DIM, tile), BF16)
        for head in range(2):
            lanes = slice(head * HEAD_DIM, (head + 1) * HEAD_DIM)
            query = q_t[lanes, columns]
            query = jnp.concatenate([query, empty] if head == 0 else [empty, query], axis=0)
            scores = contract(qkv_ref[:, PAIR : 2 * PAIR], query, 1, 0)
            highest = jnp.max(scores, axis=0, keepdims=True) * scale
            expon = jnp.exp2(scores * scale - highest).astype(BF16)
            mixed = contract(v_t[head * step : (head + 1) * step, :], expon, 1, 0)
            total = mixed[HEAD_DIM : HEAD_DIM + 1, :]
            out_t[lanes, columns] = mixed[:HEAD_DIM, :] / total
            lse_ref[head : head + 1, columns] = highest + jnp.log2(total)
        return carry

    lax.fori_loop(0, padded // tile, block, 0)
    out_ref[...] = out_t[...].T[:rows, :].astype(BF16)


def attend(qkv, first_pair, last_pair, kept=None, tile=512):
    rows, width = qkv.shape
    pairs = width // (3 * PAIR)
    padded = -(-rows // tile) * tile
    count = last_pair - first_pair
    kernel = functools.partial(attend_kernel, tile, rows, padded)
    anywhere = pl.BlockSpec(memory_space=pl.ANY)
    return pl.pallas_call(
        kernel if kept is None else lambda ref, a, b, *rest: kernel(ref, *rest),
        grid=(count,),
        in_specs=[pl.BlockSpec((rows, 3 * PAIR), lambda i: (0, i + first_pair))]
        + ([] if kept is None else [anywhere] * 2),
        out_specs=[
            pl.BlockSpec((rows, PAIR), lambda i: (0, i + first_pair)),
            pl.BlockSpec((None, 2, padded), lambda i: (i + first_pair, 0, 0)),
        ],
        out_shape=[
            jax.ShapeDtypeStruct((rows, pairs * PAIR), BF16),
            jax.ShapeDtypeStruct((pairs, 2, padded), F32),
        ],
        scratch_shapes=[
            pltpu.VMEM((PAIR, padded), BF16),
            pltpu.VMEM((PAIR + 32, rows), BF16),
            pltpu.VMEM((PAIR, padded), F32),
        ],
        input_output_aliases={} if kept is None else {1: 0, 2: 1},
        compiler_params=pltpu.CompilerParams(vmem_limit_bytes=VMEM_LIMIT),
        cost_estimate=pl.CostEstimate(
            flops=64 * rows * rows * PAIR * count,
            bytes_accessed=8 * rows * PAIR * count,
            transcendentals=2 * rows * rows * count,
        ),
        name="attend",
    )(qkv, *(() if kept is None else kept))


def attend_back_kernel(
    tile, rows, padded, s_ref, qkv_ref, grad_ref, out_ref, lse_ref, first_ref, dqkv_ref, send_ref,
    keep_ref, sums_ref, q_t, g_t, k_t, delta, dq_t, dk_t, dv_t, all_t,
):
    scale = HEAD_DIM**-0.5
    q_t[:, :rows] = qkv_ref[:, :PAIR].T
    g_t[:, :rows] = grad_ref[...].T
    if padded > rows:
        q_t[:, rows:] = jnp.zeros((PAIR, padded - rows), BF16)
        g_t[:, rows:] = jnp.zeros((PAIR, padded - rows), BF16)
        delta[:, rows:] = jnp.zeros((2, padded - rows), F32)
    k_t[...] = qkv_ref[:, PAIR : 2 * PAIR].T
    product = (grad_ref[...].astype(F32) * out_ref[...].astype(F32)).T
    delta[0:1, :rows] = jnp.sum(product[:HEAD_DIM, :], axis=0, keepdims=True)
    delta[1:2, :rows] = jnp.sum(product[HEAD_DIM:, :], axis=0, keepdims=True)
    dk_t[...] = jnp.zeros_like(dk_t)
    dv_t[...] = jnp.zeros_like(dv_t)

    def block(index, carry):
        columns = pl.ds(pl.multiple_of(index * tile, tile), tile)
        empty = jnp.zeros((HEAD_DIM, tile), BF16)
        for head in range(2):
            lanes = slice(head * HEAD_DIM, (head + 1) * HEAD_DIM)
            query = q_t[lanes, columns]
            grad = g_t[lanes, columns]
            query_pad = jnp.concatenate([query, empty] if head == 0 else [empty, query], axis=0)
            grad_pad = jnp.concatenate([grad, empty] if head == 0 else [empty, grad], axis=0)
            scores = contract(qkv_ref[:, PAIR : 2 * PAIR], query_pad, 1, 0)
            grad_probs = contract(qkv_ref[:, 2 * PAIR :], grad_pad, 1, 0)
            weights = jnp.exp2(scores * (scale * LOG2E) - lse_ref[head : head + 1, columns])
            grad_scores = (weights * (grad_probs - delta[head : head + 1, columns])).astype(BF16)
            dv_t[lanes, :] += contract(grad, weights.astype(BF16), 1, 1)
            dq_t[lanes, columns] = contract(k_t[lanes, :], grad_scores, 1, 0)
            dk_t[lanes, :] += contract(query, grad_scores, 1, 1)
        return carry

    lax.fori_loop(0, padded // tile, block, 0)
    all_t[:PAIR, :] = (dq_t[:, :rows] * scale).astype(BF16)
    all_t[PAIR : 2 * PAIR, :] = (dk_t[...] * scale).astype(BF16)
    all_t[2 * PAIR :, :] = dv_t[...].astype(BF16)
    for part in range(3):
        lanes = slice(part * PAIR, (part + 1) * PAIR)
        dqkv_ref[:, lanes] = all_t[lanes, :].T
    sums_ref[...] = contract(jnp.ones((8, rows), BF16), all_t[...], 1, 1)
    own = first_ref.shape[1] // 2
    for h in range(2):
        grad = contract(all_t[...], first_ref[:, h * own : (h + 1) * own], 1, 0).astype(BF16)

        @pl.when(s_ref[0] == h)
        def _():
            keep_ref[...] = grad

        @pl.when(s_ref[0] != h)
        def _():
            send_ref[...] = grad


def attend_back(scal, qkv, grad, out, lse, first, first_pair, last_pair, tile=256):
    rows, full = qkv.shape
    width = first.shape[1]
    padded = -(-rows // tile) * tile
    count = last_pair - first_pair
    return pl.pallas_call(
        functools.partial(attend_back_kernel, tile, rows, padded),
        grid_spec=pltpu.PrefetchScalarGridSpec(
            num_scalar_prefetch=1,
            grid=(count,),
            in_specs=[
                pl.BlockSpec((rows, 3 * PAIR), lambda i, s: (0, i + first_pair)),
                pl.BlockSpec((rows, PAIR), lambda i, s: (0, i + first_pair)),
                pl.BlockSpec((rows, PAIR), lambda i, s: (0, i + first_pair)),
                pl.BlockSpec((None, 2, lse.shape[2]), lambda i, s: (i + first_pair, 0, 0)),
                pl.BlockSpec((rows, width), lambda i, s: (0, 0), pipeline_mode=pl.Buffered(1)),
            ],
            out_specs=[
                pl.BlockSpec((rows, 3 * PAIR), lambda i, s: (0, i)),
                pl.BlockSpec((3 * PAIR, width // 2), lambda i, s: (i, 0)),
                pl.BlockSpec((3 * PAIR, width // 2), lambda i, s: (i, 0)),
                pl.BlockSpec((8, 3 * PAIR), lambda i, s: (0, i)),
            ],
            scratch_shapes=[
                pltpu.VMEM((PAIR, padded), BF16),
                pltpu.VMEM((PAIR, padded), BF16),
                pltpu.VMEM((PAIR, rows), BF16),
                pltpu.VMEM((2, padded), F32),
                pltpu.VMEM((PAIR, padded), F32),
                pltpu.VMEM((PAIR, rows), F32),
                pltpu.VMEM((PAIR, rows), F32),
                pltpu.VMEM((3 * PAIR, rows), BF16),
            ],
        ),
        out_shape=[
            jax.ShapeDtypeStruct((rows, 3 * PAIR * count), BF16),
            jax.ShapeDtypeStruct((3 * PAIR * count, width // 2), BF16),
            jax.ShapeDtypeStruct((3 * PAIR * count, width // 2), BF16),
            jax.ShapeDtypeStruct((8, 3 * PAIR * count), F32),
        ],
        compiler_params=pltpu.CompilerParams(vmem_limit_bytes=VMEM_LIMIT),
        cost_estimate=pl.CostEstimate(
            flops=160 * rows * rows * PAIR * count,
            bytes_accessed=16 * rows * PAIR * count,
            transcendentals=2 * rows * rows * count,
        ),
        name="attend_back",
    )(scal, qkv, grad, out, lse, first)


def feed_kernel(
    s_ref, x_own, x_other, dy_own, dy_other, up_ref, down_ref, x_piece, x_beside, z_piece, z_beside,
    bias_ref, out_own, out_other, dx_own, dx_other, up_send, up_keep, down_send, down_keep,
    low_send, low_keep, bias_grad_ref, x, dy, x_t, out_sum, dx_sum, up_full, down_full, hidden,
    d_pre, sems,
):
    index = pl.program_id(0)
    half = s_ref[0]
    rows, width = x.shape
    block = rows // 2
    own = width // 2
    tile = up_ref.shape[1]
    first_range = index < 2
    side = index % 2
    columns = pl.ds(pl.multiple_of(side * tile, tile), tile)
    mine = pl.ds(pl.multiple_of(half * own, own), own)
    theirs = pl.ds(pl.multiple_of((1 - half) * own, own), own)

    @pl.when(index == 0)
    def _():
        copies = []
        for i, ref in enumerate((x_own, x_other)):
            copies.append(pltpu.make_async_copy(ref, x.at[pl.ds(i * block, block)], sems.at[i]))
        for i, ref in enumerate((dy_own, dy_other)):
            copies.append(
                pltpu.make_async_copy(ref, dy.at[pl.ds(i * block, block)], sems.at[2 + i])
            )
        for copy in copies:
            copy.start()
        for copy in copies:
            copy.wait()
        x_t[...] = x[...].T
        out_sum[...] = jnp.zeros_like(out_sum)
        dx_sum[...] = jnp.zeros_like(dx_sum)

    up_full[mine, :] = up_ref[...]

    @pl.when(side == half)
    def _():
        down_full[...] = down_ref[...]

    for chosen, place, piece, beside in (
        (first_range, 1, x_piece, x_beside), (jnp.logical_not(first_range), 4, z_piece, z_beside)
    ):
        even = s_ref[place] == 0

        @pl.when(chosen & even)
        def _():
            up_full[theirs, :] = piece[:, columns]

        @pl.when(chosen & jnp.logical_not(even))
        def _():
            up_full[theirs, :] = beside[:, columns]

        @pl.when(chosen & (side != half) & even)
        def _():
            down_full[...] = beside[...]

        @pl.when(chosen & (side != half) & jnp.logical_not(even))
        def _():
            down_full[...] = piece[...]

    bias_grad = jnp.zeros(bias_grad_ref.shape, F32)
    for start in range(0, rows, block):
        part = slice(start, start + block)
        pre = contract(x[part, :], up_full[...], 1, 0) + bias_ref[...]
        d_hidden = contract(dy[part, :], down_full[...], 1, 1)
        share = 0.5 * (1.0 + lax.erf(pre * 0.7071067811865476))
        hidden[part, :] = (pre * share).astype(BF16)
        slope = share + pre * (jnp.exp(-0.5 * pre * pre) * 0.3989422804014327)
        d_low = (d_hidden * slope).astype(BF16)
        d_pre[part, :] = d_low
        bias_grad = bias_grad + jnp.sum(d_low.astype(F32), axis=0, keepdims=True)
        out_sum[part, :] += contract(hidden[part, :], down_full[...], 1, 0)
        dx_sum[part, :] += contract(d_pre[part, :], up_full[...], 1, 1)
    bias_grad_ref[...] = bias_grad
    down_grad = contract(hidden[...], dy[...], 0, 0).astype(BF16)
    side_rows = pl.ds(pl.multiple_of(side * tile, tile), tile)

    @pl.when(first_range)
    def _():
        up_keep[:, columns] = contract(x_t[mine, :], d_pre[...], 1, 0).astype(BF16)
        up_send[:, columns] = contract(x_t[theirs, :], d_pre[...], 1, 0).astype(BF16)

    @pl.when(first_range & (side == half))
    def _():
        down_keep[...] = down_grad

    @pl.when(first_range & (side != half))
    def _():
        down_send[...] = down_grad

    for even in (True, False):
        up_goal, down_goal = (low_keep, low_send) if even else (low_send, low_keep)

        @pl.when(jnp.logical_not(first_range) & ((s_ref[1] == 0) == even))
        def _():
            up_goal[:, columns] = contract(x_t[...], d_pre[...], 1, 0).astype(BF16)
            down_goal[side_rows, :] = down_grad

    @pl.when(index == pl.num_programs(0) - 1)
    def _():
        out_own[...] = out_sum[:block, :].astype(BF16)
        out_other[...] = out_sum[block:, :].astype(BF16)
        dx_own[...] = dx_sum[:block, :].astype(BF16)
        dx_other[...] = dx_sum[block:, :].astype(BF16)


def feed(scal, seconds, grads, up, down, pieces, bias):
    local, width = seconds[0].shape
    rows = 2 * local
    tile = down.shape[0] // 4
    anywhere = pl.BlockSpec(memory_space=pl.ANY)

    def fixed(*shape):
        return pl.BlockSpec(shape, lambda t, s: (0, 0), pipeline_mode=pl.Buffered(1))

    shapes = [(local, width)] * 4 + [(width // 2, 2 * tile)] * 2 + [(tile, width)] * 2
    shapes += [(width, 2 * tile)] * 2
    across = pl.BlockSpec((1, tile), lambda t, s: (0, t))
    return pl.pallas_call(
        feed_kernel,
        grid_spec=pltpu.PrefetchScalarGridSpec(
            num_scalar_prefetch=1,
            grid=(4,),
            in_specs=[anywhere] * 4
            + [
                pl.BlockSpec(
                    (width // 2, tile), lambda t, s: (0, ((t % 2) * 2 + s[2]) * 2 + t // 2)
                ),
                pl.BlockSpec((tile, width), lambda t, s: (s[2] * 2 + t // 2, 0)),
            ]
            + [fixed(width // 2, 2 * tile)] * 4
            + [across],
            out_specs=[fixed(*shape) for shape in shapes] + [across],
            scratch_shapes=[
                pltpu.VMEM((rows, width), BF16),
                pltpu.VMEM((rows, width), BF16),
                pltpu.VMEM((width, rows), BF16),
                pltpu.VMEM((rows, width), F32),
                pltpu.VMEM((rows, width), F32),
                pltpu.VMEM((width, tile), BF16),
                pltpu.VMEM((tile, width), BF16),
                pltpu.VMEM((rows, tile), BF16),
                pltpu.VMEM((rows, tile), BF16),
                pltpu.SemaphoreType.DMA((4,)),
            ],
        ),
        out_shape=[jax.ShapeDtypeStruct(shape, BF16) for shape in shapes]
        + [jax.ShapeDtypeStruct((1, 4 * tile), F32)],
        compiler_params=pltpu.CompilerParams(vmem_limit_bytes=VMEM_LIMIT),
        cost_estimate=pl.CostEstimate(
            flops=48 * rows * width * tile,
            bytes_accessed=16 * rows * width,
            transcendentals=8 * rows * tile,
        ),
        name="feed",
    )(scal, *seconds, *grads, up, down, *pieces, bias)


def run(kernel, name, scal, grid, in_specs, out_specs, out_shape, args, flops=0, scratch=()):
    moved = sum(a.size * a.dtype.itemsize for a in args)
    return pl.pallas_call(
        kernel,
        grid_spec=pltpu.PrefetchScalarGridSpec(
            num_scalar_prefetch=1,
            grid=grid,
            in_specs=in_specs,
            out_specs=out_specs,
            scratch_shapes=scratch,
        ),
        out_shape=out_shape,
        compiler_params=pltpu.CompilerParams(vmem_limit_bytes=VMEM_LIMIT),
        cost_estimate=pl.CostEstimate(flops=flops, bytes_accessed=2 * moved, transcendentals=0),
        name=name,
    )(scal, *args)


def spec(shape, index):
    return pl.BlockSpec(shape, index)


def held(*shape):
    return pl.BlockSpec(shape, lambda i, s: (0,) * len(shape), pipeline_mode=pl.Buffered(1))


def struct(*shape, dtype=BF16):
    return jax.ShapeDtypeStruct(shape, dtype)


def pack_qkv(scal, weights):
    rows, width = weights[0].shape
    pairs = width // (2 * PAIR)
    per = pairs // 2

    def kernel(s_ref, q_ref, k_ref, v_ref, own_ref, mine_ref):
        for i, ref in enumerate((q_ref, k_ref, v_ref)):
            own_ref[:, i * PAIR : (i + 1) * PAIR] = ref[...]
        start = pl.multiple_of(s_ref[1] * (rows // 2), rows // 2)
        mine_ref[...] = own_ref[pl.ds(start, rows // 2), :]

    block = spec((rows, PAIR), lambda p, s: (0, ((p // per) * 2 + s[2]) * per + p % per))
    return run(
        kernel, "pack_qkv", scal, (pairs,), [block] * 3,
        [
            spec((rows, 3 * PAIR), lambda p, s: (0, p)),
            spec((rows // 2, 3 * PAIR), lambda p, s: (0, p)),
        ],
        [struct(rows, 3 * PAIR * pairs), struct(rows // 2, 3 * PAIR * pairs)],
        weights,
    )


def pack_feed(scal, up, down, j, ranges, bit):
    rows, hidden = up.shape
    tile = hidden // (4 * ranges)
    columns = down.shape[1] // 2

    def kernel(s_ref, up_ref, down_ref, out_ref):
        out_ref[...] = jnp.where(s_ref[bit] == 0, up_ref[...], down_ref[...])

    return run(
        kernel, "pack_feed", scal, (2,),
        [
            spec((rows, tile), lambda t, s: (0, (t * 2 + s[2]) * ranges + j)),
            spec((tile, columns), lambda t, s: (s[2] * ranges + j, t)),
        ],
        spec((rows, tile), lambda t, s: (0, t)), struct(rows, 2 * tile), (up, down),
    )


def normalize(values):
    centred = values - jnp.mean(values, axis=-1, keepdims=True)
    spread = jnp.mean(centred * centred, axis=-1, keepdims=True)
    inverse = lax.rsqrt(spread + EPS)
    return centred * inverse, inverse


def first_norm(scal, tokens, received, gain, shift):
    rows, width = tokens.shape
    step = rows // 2

    def kernel(s_ref, t_ref, r_ref, gain_ref, shift_ref, x_ref, first_ref):
        x = jnp.where(s_ref[3] == 1, t_ref[...], r_ref[...])
        x_ref[...] = x
        normed, _ = normalize(x.astype(F32))
        first_ref[...] = (normed * gain_ref[...] + shift_ref[...]).astype(BF16)

    block = spec((step, width), lambda i, s: (i, 0))
    return run(
        kernel, "first_norm", scal, (2,), [block, block, held(1, width), held(1, width)],
        [block, block], [struct(rows, width)] * 2, (tokens, received, gain, shift),
    )


def project(scal, firsts, own, piece, beside, bias):
    local, width = firsts[0].shape
    rows, total = 2 * local, own.shape[1]
    block = 6 * PAIR
    half_rows, quarter_rows = width // 2, width // 4

    def kernel(
        s_ref, mine_ref, theirs_ref, own_ref, piece_ref, beside_ref, bias_ref, qkv_ref, w_ref,
        all_ref, sems,
    ):
        @pl.when(pl.program_id(0) == 0)
        def _():
            copies = [
                pltpu.make_async_copy(ref, all_ref.at[pl.ds(i * local, local)], sems.at[i])
                for i, ref in enumerate((mine_ref, theirs_ref))
            ]
            for copy in copies:
                copy.start()
            for copy in copies:
                copy.wait()

        half, low = s_ref[0], s_ref[1]
        other = (1 - half) * half_rows
        w_ref[pl.ds(pl.multiple_of(half * half_rows, half_rows), half_rows), :] = own_ref[...]
        start = pl.multiple_of(other + low * quarter_rows, quarter_rows)
        w_ref[pl.ds(start, quarter_rows), :] = piece_ref[...]
        start = pl.multiple_of(other + (1 - low) * quarter_rows, quarter_rows)
        w_ref[pl.ds(start, quarter_rows), :] = beside_ref[...]
        qkv_ref[...] = (contract(all_ref[...], w_ref[...], 1, 0) + bias_ref[...]).astype(BF16)

    def columns(size):
        return spec((size, block), lambda p, s: (0, p))

    anywhere = pl.BlockSpec(memory_space=pl.ANY)
    return run(
        kernel, "project", scal, (total // block,),
        [anywhere] * 2
        + [columns(half_rows), columns(quarter_rows), columns(quarter_rows), columns(1)],
        [columns(rows), columns(width), held(rows, width)],
        [struct(rows, total), struct(width, total), struct(rows, width)],
        (*firsts, own, piece, beside, bias), flops=2 * rows * width * total,
        scratch=[pltpu.SemaphoreType.DMA((2,))],
    )


def out_other(scal, mixed, weight, piece, beside):
    rows, set_width = mixed.shape
    local, width = rows // 2, weight.shape[1]
    block, small = set_width // 2, set_width // 4

    def kernel(s_ref, mixed_ref, own_ref, piece_ref, beside_ref, out_ref, set_ref):
        half, low = s_ref[0], s_ref[1]
        other = (1 - half) * block
        set_ref[pl.ds(pl.multiple_of(half * block, block), block), :] = own_ref[...]
        set_ref[pl.ds(pl.multiple_of(other + low * small, small), small), :] = piece_ref[...]
        start = pl.multiple_of(other + (1 - low) * small, small)
        set_ref[pl.ds(start, small), :] = beside_ref[...]
        out_ref[...] = contract(mixed_ref[...], set_ref[...], 1, 0).astype(BF16)

    return run(
        kernel, "out_other", scal, (1,),
        [
            spec((local, set_width), lambda i, s: (1, 0)),
            spec((block, width), lambda i, s: (s[2], 0)),
            held(small, width), held(small, width),
        ],
        [held(local, width), held(set_width, width)],
        [struct(local, width), struct(set_width, width)],
        (mixed, weight, piece, beside), flops=2 * local * set_width * width,
    )


def second_norm(scal, mixed, out_set, x, received, bias, gain, shift):
    rows, set_width = mixed.shape
    local, width = x.shape
    step = local // 2

    def kernel(
        s_ref, mixed_ref, w_ref, x_ref, r_ref, bias_ref, gain_ref, shift_ref, mid_ref, second_ref
    ):
        middle = contract(mixed_ref[...], w_ref[...], 1, 0) + r_ref[...].astype(F32)
        middle = middle + x_ref[...].astype(F32) + bias_ref[...]
        mid_ref[...] = middle
        normed, _ = normalize(middle)
        second_ref[...] = (normed * gain_ref[...] + shift_ref[...]).astype(BF16)

    block = spec((step, width), lambda i, s: (i, 0))
    return run(
        kernel, "second_norm", scal, (2,),
        [spec((step, set_width), lambda i, s: (i, 0)), held(set_width, width), block, block]
        + [held(1, width)] * 3,
        [block, block], [struct(local, width, dtype=F32), struct(local, width)],
        (mixed, out_set, x, received, bias, gain, shift), flops=2 * local * set_width * width,
    )


def norm_back_rows(grad, normed, inverse, gain):
    scaled = grad * gain
    first_term = jnp.mean(scaled, axis=-1, keepdims=True)
    second_term = jnp.mean(scaled * normed, axis=-1, keepdims=True)
    return inverse * (scaled - first_term - normed * second_term)


def column_sums(refs, values):
    @pl.when(pl.program_id(0) == 0)
    def _():
        refs[...] = jnp.zeros_like(refs)

    for i, value in enumerate(values):
        refs[i : i + 1, :] += jnp.sum(value, axis=0, keepdims=True)


def row_step(rows):
    return rows // 7 if rows % 112 == 0 else rows


def second_back(scal, grad, received, middle, dy, gain):
    local, width = middle.shape
    step = row_step(local)

    def kernel(s_ref, g_ref, r_ref, mid_ref, dy_ref, gain_ref, low_ref, sums_ref):
        grad = g_ref[...].astype(F32) + r_ref[...].astype(F32)
        normed, inverse = normalize(mid_ref[...])
        dy_wide = dy_ref[...].astype(F32)
        low = (dy_wide + norm_back_rows(grad, normed, inverse, gain_ref[...])).astype(BF16)
        low_ref[...] = low
        column_sums(sums_ref, (grad * normed, grad, dy_wide, low.astype(F32)))

    block = spec((step, width), lambda i, s: (i, 0))
    return run(
        kernel, "second_back", scal, (local // step,), [block] * 4 + [held(1, width)],
        [block, held(8, width)], [struct(local, width), struct(8, width, dtype=F32)],
        (grad, received, middle, dy, gain),
    )


def mixed_back(scal, lows, out_set, mixed):
    local, width = lows[0].shape
    rows, set_width = mixed.shape
    block = set_width // 2

    def kernel(
        s_ref, mine_ref, theirs_ref, w_ref, mixed_ref, d_ref, send_ref, keep_ref, low, sems
    ):
        @pl.when(pl.program_id(0) == 0)
        def _():
            copies = [
                pltpu.make_async_copy(ref, low.at[pl.ds(i * local, local)], sems.at[i])
                for i, ref in enumerate((mine_ref, theirs_ref))
            ]
            for copy in copies:
                copy.start()
            for copy in copies:
                copy.wait()

        d_ref[...] = contract(low[...], w_ref[...], 1, 1).astype(BF16)
        grad = contract(mixed_ref[...], low[...], 0, 0).astype(BF16)

        def store(goal):
            for c in range(2):
                for i in range(width // (2 * PAIR)):
                    start = (2 * i + c) * PAIR
                    goal[c * block : (c + 1) * block, i * PAIR : (i + 1) * PAIR] = (
                        grad[:, start : start + PAIR]
                    )

        @pl.when(pl.program_id(0) == s_ref[0])
        def _():
            store(keep_ref)

        @pl.when(pl.program_id(0) != s_ref[0])
        def _():
            store(send_ref)

    anywhere = pl.BlockSpec(memory_space=pl.ANY)
    across = spec((rows, block), lambda t, s: (0, t))
    return run(
        kernel, "mixed_back", scal, (2,),
        [anywhere] * 2 + [spec((block, width), lambda t, s: (t, 0)), across],
        [across, held(2 * block, width // 2), held(2 * block, width // 2)],
        [struct(rows, set_width)] + [struct(2 * block, width // 2)] * 2,
        (*lows, out_set, mixed), flops=4 * rows * set_width * width,
        scratch=[pltpu.VMEM((rows, width), BF16), pltpu.SemaphoreType.DMA((2,))],
    )


def first_grad(scal, dqkvs, weights):
    rows = dqkvs[0].shape[0]
    width = weights.shape[0]
    local = rows // 2
    count = len(dqkvs)
    step = width // 4

    def kernel(s_ref, *refs):
        left = jnp.concatenate([refs[j][...] for j in range(count)], axis=1)
        total = contract(left, refs[count][...], 1, 1)
        refs[-2][...] = total[:local].astype(BF16)
        refs[-1][...] = total[local:].astype(BF16)

    across = spec((local, step), lambda i, s: (0, i))
    return run(
        kernel, "first_grad", scal, (4,),
        [held(*a.shape) for a in dqkvs] + [spec((step, weights.shape[1]), lambda i, s: (i, 0))],
        [across, across], [struct(local, width)] * 2, (*dqkvs, weights),
        flops=sum(2 * rows * a.shape[1] * width for a in dqkvs),
    )


def first_back(scal, grad, received, x, wide, gain):
    local, width = x.shape
    step = row_step(local)

    def kernel(s_ref, g_ref, r_ref, x_ref, wide_ref, gain_ref, out_ref, sums_ref):
        grad = g_ref[...].astype(F32) + r_ref[...].astype(F32)
        normed, inverse = normalize(x_ref[...].astype(F32))
        total = wide_ref[...].astype(F32) + norm_back_rows(grad, normed, inverse, gain_ref[...])
        out_ref[...] = total.astype(BF16)
        column_sums(sums_ref, (grad * normed, grad))

    block = spec((step, width), lambda i, s: (i, 0))
    return run(
        kernel, "first_back", scal, (local // step,), [block] * 4 + [held(1, width)],
        [block, held(8, width)], [struct(local, width), struct(8, width, dtype=F32)],
        (grad, received, x, wide, gain),
    )


def layer_rows(scal, own, received, middle, bias):
    local, width = middle.shape
    step = row_step(local)

    def kernel(s_ref, o_ref, r_ref, mid_ref, bias_ref, out_ref):
        total = mid_ref[...] + o_ref[...].astype(F32) + r_ref[...].astype(F32) + bias_ref[...]
        out_ref[...] = total.astype(BF16)

    block = spec((step, width), lambda i, s: (i, 0))
    return run(
        kernel, "layer_rows", scal, (local // step,), [block] * 3 + [held(1, width)],
        block, struct(local, width), (own, received, middle, bias),
    )


def finish_feed_kernel(s_ref, *refs, tile):
    sums, (up_out, down_out) = refs[:8], refs[8:]
    first = s_ref[2] == 0
    even = s_ref[1] == 0
    for j in range(2):
        mine, beside, mine_across, beside_across = [ref[...] for ref in sums[4 * j : 4 * j + 4]]
        mine, beside = jnp.where(even, mine, beside), jnp.where(even, beside, mine)
        mine_across, beside_across = (
            jnp.where(even, mine_across, beside_across),
            jnp.where(even, beside_across, mine_across),
        )
        for kind, own, other in ((0, mine, mine_across), (1, beside, beside_across)):
            for c in range(2):
                wide = jnp.where(first == (c == 0), own, other).astype(F32)
                if kind == 1:
                    down_out[c, j] = wide
                    continue
                for h in range(2):
                    start = ((h * 2 + c) * 2 + j) * tile
                    up_out[:, start : start + tile] = wide[:, h * tile : (h + 1) * tile]


def finish_feed(scal, sums):
    rows, width = sums[0].shape
    tile = rows
    steps = 4
    block = spec((rows // steps, width), lambda i, s: (i, 0))
    up, down = run(
        functools.partial(finish_feed_kernel, tile=tile), "finish_feed", scal, (steps,),
        [block] * 8,
        [
            spec((rows // steps, 4 * width), lambda i, s: (i, 0)),
            spec((2, 2, rows // steps, width), lambda i, s: (0, 0, i, 0)),
        ],
        [struct(rows, 4 * width, dtype=F32), struct(2, 2, rows, width, dtype=F32)],
        sums,
    )
    return up, down.reshape(4 * rows, width)


def finish_attention_kernel(s_ref, *refs, pairs, spans):
    q_out, k_out, v_out, out_out = refs[-4:]
    first, even = s_ref[2] == 0, s_ref[1] == 0
    half_pairs = pairs // 2
    for g, (begin, end) in enumerate(spans):
        if g == 0:
            mine, beside, mine_across, beside_across = [ref[...] for ref in refs[:4]]
            own = jnp.concatenate(
                [jnp.where(even, mine, beside), jnp.where(even, beside, mine)], axis=0
            )
            other = jnp.concatenate(
                [
                    jnp.where(even, mine_across, beside_across),
                    jnp.where(even, beside_across, mine_across),
                ],
                axis=0,
            )
        else:
            own, other = refs[2 * g + 2][...], refs[2 * g + 3][...]
        for c in range(2):
            total = jnp.where(first == (c == 0), own, other).astype(F32)
            wide = total[: (end - begin) * 3 * PAIR].T
            for q in range(end - begin):
                pair = begin + q
                h, p = pair // half_pairs, pair % half_pairs
                goal = ((h * 2 + c) * half_pairs + p) * PAIR
                for i, out in enumerate((q_out, k_out, v_out)):
                    start = (q * 3 + i) * PAIR
                    out[:, goal : goal + PAIR] = wide[:, start : start + PAIR]
            if g == 0:
                rest = total[(end - begin) * 3 * PAIR :]
                rows = rest.shape[0] // 2
                out_out[c * rows : (c + 1) * rows, :PAIR] = rest[:rows]
                out_out[c * rows : (c + 1) * rows, PAIR:] = rest[rows:]


def finish_attention(scal, sums, spans):
    rows = sums[0].shape[1]
    pairs = spans[-1][1]
    steps = rows // PAIR
    return run(
        functools.partial(finish_attention_kernel, pairs=pairs, spans=spans), "finish_attention",
        scal, (steps,),
        [spec((values.shape[0], PAIR), lambda i, s: (0, i)) for values in sums],
        [spec((PAIR, 2 * pairs * PAIR), lambda i, s: (i, 0))] * 3
        + [spec((rows, 2 * PAIR), lambda i, s: (0, i))],
        [struct(rows, 2 * pairs * PAIR, dtype=F32)] * 3 + [struct(rows, 2 * rows, dtype=F32)],
        sums,
    )


def wide_back_kernel(
    tile, rows, padded, qkv_ref, grad_ref, out_ref, lse_ref, dqkv_ref, q_t, g_t, k_t, delta,
    dq_t, dk_t, dv_t,
):
    scale = HEAD_DIM**-0.5
    q_t[:, :rows] = qkv_ref[:, :PAIR].T
    g_t[:, :rows] = grad_ref[...].T
    if padded > rows:
        q_t[:, rows:] = jnp.zeros((PAIR, padded - rows), BF16)
        g_t[:, rows:] = jnp.zeros((PAIR, padded - rows), BF16)
        delta[:, rows:] = jnp.zeros((2, padded - rows), F32)
    k_t[...] = qkv_ref[:, PAIR : 2 * PAIR].T
    product = (grad_ref[...].astype(F32) * out_ref[...].astype(F32)).T
    delta[0:1, :rows] = jnp.sum(product[:HEAD_DIM, :], axis=0, keepdims=True)
    delta[1:2, :rows] = jnp.sum(product[HEAD_DIM:, :], axis=0, keepdims=True)
    dk_t[...] = jnp.zeros_like(dk_t)
    dv_t[...] = jnp.zeros_like(dv_t)

    def block(index, carry):
        columns = pl.ds(pl.multiple_of(index * tile, tile), tile)
        empty = jnp.zeros((HEAD_DIM, tile), BF16)
        for head in range(2):
            lanes = slice(head * HEAD_DIM, (head + 1) * HEAD_DIM)
            query = q_t[lanes, columns]
            grad = g_t[lanes, columns]
            query_pad = jnp.concatenate([query, empty] if head == 0 else [empty, query], axis=0)
            grad_pad = jnp.concatenate([grad, empty] if head == 0 else [empty, grad], axis=0)
            scores = contract(qkv_ref[:, PAIR : 2 * PAIR], query_pad, 1, 0)
            grad_probs = contract(qkv_ref[:, 2 * PAIR :], grad_pad, 1, 0)
            weights = jnp.exp2(scores * (scale * LOG2E) - lse_ref[head : head + 1, columns])
            grad_scores = (weights * (grad_probs - delta[head : head + 1, columns])).astype(BF16)
            dv_t[lanes, :] += contract(grad, weights.astype(BF16), 1, 1)
            dq_t[lanes, columns] = contract(k_t[lanes, :], grad_scores, 1, 0)
            dk_t[lanes, :] += contract(query, grad_scores, 1, 1)
        return carry

    lax.fori_loop(0, padded // tile, block, 0)
    dqkv_ref[:, :PAIR] = (dq_t[...].T[:rows, :] * scale).astype(BF16)
    dqkv_ref[:, PAIR : 2 * PAIR] = (dk_t[...].T * scale).astype(BF16)
    dqkv_ref[:, 2 * PAIR :] = dv_t[...].T.astype(BF16)


def wide_back(qkv, grad, out, lse, first_pair, last_pair, tile=256):
    rows, width = qkv.shape
    padded = -(-rows // tile) * tile
    count = last_pair - first_pair
    return pl.pallas_call(
        functools.partial(wide_back_kernel, tile, rows, padded),
        grid=(count,),
        in_specs=[
            pl.BlockSpec((rows, 3 * PAIR), lambda i: (0, i + first_pair)),
            pl.BlockSpec((rows, PAIR), lambda i: (0, i + first_pair)),
            pl.BlockSpec((rows, PAIR), lambda i: (0, i + first_pair)),
            pl.BlockSpec((None, 2, lse.shape[2]), lambda i: (i + first_pair, 0, 0)),
        ],
        out_specs=pl.BlockSpec((rows, 3 * PAIR), lambda i: (0, i)),
        out_shape=jax.ShapeDtypeStruct((rows, 3 * PAIR * count), BF16),
        scratch_shapes=[
            pltpu.VMEM((PAIR, padded), BF16),
            pltpu.VMEM((PAIR, padded), BF16),
            pltpu.VMEM((PAIR, rows), BF16),
            pltpu.VMEM((2, padded), F32),
            pltpu.VMEM((PAIR, padded), F32),
            pltpu.VMEM((PAIR, rows), F32),
            pltpu.VMEM((PAIR, rows), F32),
        ],
        compiler_params=pltpu.CompilerParams(vmem_limit_bytes=VMEM_LIMIT),
        cost_estimate=pl.CostEstimate(
            flops=160 * rows * rows * PAIR * count,
            bytes_accessed=16 * rows * PAIR * count,
            transcendentals=2 * rows * rows * count,
        ),
        name="wide_back",
    )(qkv, grad, out, lse)


def wide_feed_kernel(
    half_ref, *refs, parts, make, chunk,
):
    xs, refs = refs[:parts], refs[parts:]
    dys, refs = refs[:parts], refs[parts:]
    if not make:
        x_t, refs = refs[0], refs[1:]
    up_ref, bias_ref, down_ref, *refs = refs
    hidden_ref, d_pre_ref, up_send, up_keep, down_send, down_keep, bias_grad_ref, *refs = refs
    if make:
        x_t, refs = refs[0], refs[1:]
    x, dy, sems = refs
    index = pl.program_id(0)
    half = half_ref[0]
    rows, width = x.shape
    block = rows // parts
    own = width // 2
    tile = up_ref.shape[1]

    @pl.when(index == 0)
    def _():
        copies = []
        for i in range(parts):
            part = pl.ds(i * block, block)
            copies.append(pltpu.make_async_copy(xs[i], x.at[part], sems.at[i]))
            copies.append(pltpu.make_async_copy(dys[i], dy.at[part], sems.at[parts + i]))
        for copy in copies:
            copy.start()
        for copy in copies:
            copy.wait()
        if make:
            x_t[...] = x[...].T

    bias_grad = jnp.zeros(bias_grad_ref.shape, F32)
    for start in range(0, rows, chunk):
        part = slice(start, start + chunk)
        pre = contract(x[part, :], up_ref[...], 1, 0) + bias_ref[...]
        d_hidden = contract(dy[part, :], down_ref[...], 1, 1)
        share = 0.5 * (1.0 + lax.erf(pre * 0.7071067811865476))
        hidden_ref[part, :] = (pre * share).astype(BF16)
        slope = share + pre * (jnp.exp(-0.5 * pre * pre) * 0.3989422804014327)
        d_low = (d_hidden * slope).astype(BF16)
        d_pre_ref[part, :] = d_low
        bias_grad = bias_grad + jnp.sum(d_low.astype(F32), axis=0, keepdims=True)
    bias_grad_ref[...] = bias_grad
    columns = pl.ds(pl.multiple_of(index * tile, tile), tile)
    mine = pl.ds(pl.multiple_of(half * own, own), own)
    theirs = pl.ds(pl.multiple_of((1 - half) * own, own), own)
    up_keep[:, columns] = contract(x_t[mine, :], d_pre_ref[...], 1, 0).astype(BF16)
    up_send[:, columns] = contract(x_t[theirs, :], d_pre_ref[...], 1, 0).astype(BF16)
    down_grad = contract(hidden_ref[...], dy[...], 0, 0).astype(BF16)

    @pl.when(index == half)
    def _():
        down_keep[...] = down_grad

    @pl.when(index != half)
    def _():
        down_send[...] = down_grad


def wide_feed(half, xs, dys, x_t, up, bias, down):
    parts = len(xs)
    width = xs[0].shape[1]
    rows = sum(part.shape[0] for part in xs)
    hidden = up.shape[1]
    tile = hidden // 2
    make = x_t is None
    chunk = rows // 2 if rows % 32 == 0 else rows
    anywhere = pl.BlockSpec(memory_space=pl.ANY)
    fixed = lambda shape: pl.BlockSpec(shape, lambda j, s: (0, 0), pipeline_mode=pl.Buffered(1))
    across = lambda size: pl.BlockSpec((size, tile), lambda j, s: (0, j))
    out_specs = [across(rows)] * 2 + [fixed((width // 2, hidden))] * 2
    out_specs += [fixed((tile, width))] * 2 + [across(1)]
    out_shape = [
        jax.ShapeDtypeStruct((rows, hidden), BF16),
        jax.ShapeDtypeStruct((rows, hidden), BF16),
        jax.ShapeDtypeStruct((width // 2, hidden), BF16),
        jax.ShapeDtypeStruct((width // 2, hidden), BF16),
        jax.ShapeDtypeStruct((tile, width), BF16),
        jax.ShapeDtypeStruct((tile, width), BF16),
        jax.ShapeDtypeStruct((1, hidden), F32),
    ]
    if make:
        out_specs.append(fixed((width, rows)))
        out_shape.append(jax.ShapeDtypeStruct((width, rows), BF16))
    return pl.pallas_call(
        functools.partial(wide_feed_kernel, parts=parts, make=make, chunk=chunk),
        grid_spec=pltpu.PrefetchScalarGridSpec(
            num_scalar_prefetch=1,
            grid=(2,),
            in_specs=[anywhere] * (2 * parts)
            + ([] if make else [fixed((width, rows))])
            + [across(width), across(1), pl.BlockSpec((tile, width), lambda j, s: (j, 0))],
            out_specs=out_specs,
            scratch_shapes=[
                pltpu.VMEM((rows, width), BF16),
                pltpu.VMEM((rows, width), BF16),
                pltpu.SemaphoreType.DMA((2 * parts,)),
            ],
        ),
        out_shape=out_shape,
        compiler_params=pltpu.CompilerParams(vmem_limit_bytes=VMEM_LIMIT),
        cost_estimate=pl.CostEstimate(
            flops=8 * rows * width * hidden,
            bytes_accessed=8 * rows * width + 8 * width * hidden,
            transcendentals=2 * rows * hidden,
        ),
        name="wide_feed",
    )(half.reshape(1), *xs, *dys, *(() if make else (x_t,)), up, bias, down)


def norm_parts(values, gain, shift):
    average = jnp.mean(values, axis=-1, keepdims=True)
    centred = values - average
    spread = jnp.mean(centred * centred, axis=-1, keepdims=True)
    inverse = lax.rsqrt(spread + EPS)
    normed = centred * inverse
    return (normed * gain + shift, normed, inverse)


def norm_back(grad, normed, inverse, gain):
    scaled = grad * gain
    first_term = jnp.mean(scaled, axis=-1, keepdims=True)
    second_term = jnp.mean(scaled * normed, axis=-1, keepdims=True)
    result = inverse * (scaled - first_term - normed * second_term)
    return (result, jnp.sum(grad * normed, axis=0), jnp.sum(grad, axis=0))


def pick(values, index, axis):
    return lax.dynamic_index_in_dim(values, index, axis, keepdims=False)


def join(own, other, index):
    return jnp.where(index == 0, jnp.stack([own, other]), jnp.stack([other, own]))


def after(values, *earlier):
    return lax.optimization_barrier((values,) + earlier)[0]


def wide_body(
    rep, grp, tokens, query_weight, key_weight, value_weight, query_bias, value_bias, out_weight,
    out_bias, first_gain, first_shift, second_gain, second_shift, up_weight, up_bias,
    down_weight, down_bias, cotangent,
):
    clips, local, width = tokens.shape
    assert clips == 1
    quarter = grp // 2
    ring = rep // 2
    deep = ring // 2
    core = lax.axis_index("core")
    half = lax.axis_index("half")
    gq = lax.axis_index("gq")
    place = lax.axis_index("rz")
    low = place % 2
    high = place // 2
    own_rows = width // grp
    pairs = own_rows // PAIR
    hidden = up_weight.shape[1]
    set_hidden = hidden // grp
    ranges = max(1, set_hidden // width)
    tile = set_hidden // (2 * ranges)

    there = []
    for b in range(2):
        for h in range(2):
            for q in range(quarter):
                g = h * quarter + q
                source = (b * 2 + h) * quarter + q
                target = ((g % 2) * 2 + b) * quarter + g // 2
                if source != target:
                    there.append((source, target))
    back = [(target, source) for source, target in there]
    block = half * quarter + gq
    stays = (block % 2 == core) & (block // 2 == gq) & (half == core)
    axes = ("core", "half", "gq")
    beside = [(i, i ^ 1) for i in range(ring)]

    def move(values, route):
        return jnp.where(stays, values, lax.ppermute(values, axes, route))

    def swap_half(values):
        return lax.ppermute(values, "half", SWAP)

    def swap_core(values):
        return lax.ppermute(values, "core", SWAP)

    def spread(values):
        if grp == 2:
            return [values, swap_core(values)]
        return [lax.all_gather(values, ("gq", "core"), axis=0, tiled=True)]

    def collect(values):
        if grp == 2:
            other = swap_core(values(slice(local, None)).astype(BF16))
            return values(slice(None, local)) + other.astype(F32)
        return lax.psum_scatter(
            values(slice(None)).astype(BF16), ("gq", "core"), scatter_dimension=0, tiled=True
        ).astype(F32)

    def other_half(pieces):
        mine = pick(jnp.stack(pieces), low, 0)
        first = swap_half(mine)
        second = lax.ppermute(first, "rz", beside)
        return first, jnp.where(low == 0, first, second), jnp.where(low == 0, second, first)

    def by_half(own, other):
        return join(own, other, half).reshape(-1, own.shape[-1])

    def set_columns(values, inner=1):
        parts = values.reshape(values.shape[0], 2, quarter, 2, inner, -1)
        return pick(parts, core, 3).transpose(0, 2, 3, 1, 4)

    def gather_rows(values):
        if quarter > 1:
            values = lax.all_to_all(values, "gq", split_axis=1, concat_axis=0, tiled=True)
        return values.reshape(-1, values.shape[-1])

    def set_entries(values, inner=1):
        parts = values.reshape(2, quarter, 2, inner, -1)
        return pick(pick(parts, core, 2), gq, 1).transpose(1, 0, 2).reshape(inner, 1, -1)

    clip_tokens = move(tokens.reshape(local, width), there)
    vectors = jnp.concatenate(
        [query_bias, value_bias, out_bias, first_gain, first_shift, second_gain, second_shift,
         down_bias, up_bias]
    )
    if quarter > 1:
        vectors = lax.all_gather(vectors, "gq", axis=0)
    vectors = join(vectors, swap_half(vectors), half).reshape(grp, -1)
    (full_qbias, full_vbias, full_obias, gain_one, shift_one, gain_two, shift_two, full_dbias) = [
        vectors[:, i * own_rows : (i + 1) * own_rows].reshape(-1) for i in range(8)
    ]
    bias_sets = set_entries(vectors[:, 8 * own_rows :].reshape(-1), ranges)

    parts = [
        set_columns(w).reshape(own_rows, quarter, pairs, PAIR)
        for w in (query_weight, key_weight, value_weight)
    ]
    own_qkv = gather_rows(jnp.stack(parts, axis=3).reshape(own_rows, quarter, 3 * own_rows))
    own_qkv = own_qkv.reshape(2, -1, 3 * own_rows)
    qkv_x, low_rows, high_rows = other_half([own_qkv[0], own_qkv[1]])
    qkv_weight = by_half(
        own_qkv.reshape(-1, 3 * own_rows), jnp.concatenate([low_rows, high_rows], axis=0)
    )
    own_out = pick(out_weight.reshape(2, -1, width), core, 0)
    out_x, low_rows, high_rows = other_half(
        [after(own_out, qkv_x)[: own_rows // 4], own_out[own_rows // 4 :]]
    )
    out_set = by_half(own_out, jnp.concatenate([low_rows, high_rows], axis=0))

    own_up = set_columns(up_weight, ranges)
    own_down = pick(down_weight.reshape(2, ranges, tile, width), core, 0)
    up_sets, down_sets, stages = [], [], [out_x]
    for j in range(ranges):
        up_part = gather_rows(own_up[:, :, j].reshape(own_rows, quarter, 2 * tile))
        down_part = own_down[j]
        if up_part.shape == down_part.shape:
            stage, other_up, other_down = other_half([after(up_part, stages[-1]), down_part])
        else:
            stage, other_up = swap_half(after(up_part, stages[-1])), None
            other_up, other_down = stage, swap_half(down_part)
        stages.append(stage)
        up_sets.append(by_half(up_part, other_up))
        down_sets.append(by_half(down_part, other_down))
    grad_out = move(after(cotangent.reshape(local, width), stages[1]), there)

    zeros = jnp.zeros((1, own_rows), F32)
    qkv_bias = jnp.stack(
        [
            b.reshape(pairs, PAIR)
            for b in (set_entries(full_qbias), zeros, set_entries(full_vbias))
        ],
        axis=1,
    ).reshape(1, 3 * own_rows)

    inputs = clip_tokens.astype(F32)
    first_norm, first_normed, first_inverse = norm_parts(inputs, gain_one, shift_one)
    first = jnp.concatenate(spread(first_norm.astype(BF16)), axis=0)
    qkv = (contract(first, qkv_weight, 1, 0) + qkv_bias).astype(BF16)
    if pairs > 1:
        kept = attend(qkv, 0, pairs // 2)
        mixed, lse = attend(qkv, pairs // 2, pairs, kept)
    else:
        mixed, lse = attend(qkv, 0, pairs)
    middle = collect(lambda rows: contract(mixed[rows], out_set, 1, 0)) + inputs + full_obias
    second_norm, second_normed, second_inverse = norm_parts(middle, gain_two, shift_two)
    seconds = spread(second_norm.astype(BF16))
    grads_out = spread(grad_out)
    x_t = None
    feeds = []
    for j in range(ranges):
        outs = wide_feed(
            half, seconds, grads_out, x_t, up_sets[j],
            bias_sets[j] if j == 0 else after(bias_sets[j], feeds[-1][6]), down_sets[j],
        )
        x_t = outs[7] if j == 0 else x_t
        feeds.append(outs)

    def reduce_ring(pair):
        send, keep = pair
        total = keep.astype(F32) + lax.ppermute(send, "rz", beside).astype(F32)
        total = total.astype(BF16).reshape(deep, -1, keep.shape[-1])
        shifts = range(1, deep)

        def route(shift):
            return [(i, (i + 2 * shift) % ring) for i in range(ring)]

        pieces = [
            lax.ppermute(pick(total, (high + s) % deep, 0), "rz", route(s)) for s in shifts
        ]
        piece = pick(total, high, 0).astype(F32)
        for other in pieces:
            piece = piece + other.astype(F32)
        piece = piece.astype(BF16)
        gathered = [piece] + [lax.ppermute(piece, "rz", route(s)) for s in shifts]
        whole = jnp.stack(
            [
                functools.reduce(
                    lambda rest, s: jnp.where((high - s) % deep == i, gathered[s], rest),
                    shifts,
                    piece,
                )
                for i in range(deep)
            ]
        ).reshape(keep.shape)
        return whole, lax.ppermute(whole, "rz", beside)

    def reduce_parts(parts):
        stacked = jnp.stack(parts)
        own, other = reduce_ring((pick(stacked, 1 - low, 0), pick(stacked, low, 0)))
        return jnp.where(low == 0, own, other), jnp.where(low == 0, other, own)

    def add_half(keep, send):
        return (keep.astype(F32) + swap_half(send).astype(F32)).astype(BF16)

    def reduce_rows(values):
        size = values.shape[0]
        if size % (16 * ring):
            return lax.psum(values, "rz")
        return jnp.concatenate(reduce_parts([values[: size // 2], values[size // 2 :]]), axis=0)

    def scatter_half(values):
        values = values.reshape(2, -1, values.shape[-1])
        return add_half(pick(values, half, 0), pick(values, 1 - half, 0))

    sums_feed = []
    for outs in feeds:
        up_part, down_part = add_half(outs[3], outs[2]), add_half(outs[5], outs[4])
        if up_part.shape == down_part.shape:
            sums_feed.extend(reduce_parts([up_part, down_part]))
        else:
            sums_feed.extend([reduce_rows(up_part), reduce_rows(down_part)])

    grad_wide = grad_out.astype(F32)
    grad_second = collect(
        lambda rows: functools.reduce(
            jnp.add, [contract(feeds[j][1][rows], up_sets[j], 1, 1) for j in range(ranges)]
        )
    )
    grad_second, grad_gain_two, grad_shift_two = norm_back(
        grad_second, second_normed, second_inverse, gain_two
    )
    grad_middle = grad_wide + grad_second
    grad_middle_low = grad_middle.astype(BF16)
    grad_middle_all = jnp.concatenate(spread(grad_middle_low), axis=0)
    grad_mixed = contract(grad_middle_all, out_set, 1, 1).astype(BF16)
    out_half = reduce_rows(scatter_half(contract(mixed, grad_middle_all, 0, 0).astype(BF16)))
    spans = [(0, pairs // 2), (pairs // 2, pairs)] if pairs > 1 else [(0, pairs)]
    dqkvs, qkv_halves = [], []
    for begin, end in spans:
        gate = lse if not dqkvs else after(lse, qkv_halves[-1])
        dqkvs.append(wide_back(qkv, grad_mixed, mixed, gate, begin, end))
        qkv_halves.append(contract(first, dqkvs[-1], 0, 0).astype(BF16))
    qkv_halves = [reduce_rows(scatter_half(values)) for values in qkv_halves]

    result = collect(
        lambda rows: functools.reduce(
            jnp.add, [contract(feeds[j][0][rows], down_sets[j], 1, 0) for j in range(ranges)]
        )
    )
    result = (middle + result + full_dbias).astype(BF16)
    layer_out = move(result, back).reshape(1, local, width)

    def weight_of(span):
        return qkv_weight[:, span[0] * 3 * PAIR : span[1] * 3 * PAIR]

    grad_first_norm = collect(
        lambda rows: functools.reduce(
            jnp.add,
            [contract(d[rows], weight_of(span), 1, 1) for d, span in zip(dqkvs, spans)],
        )
    )
    grad_first, grad_gain_one, grad_shift_one = norm_back(
        grad_first_norm, first_normed, first_inverse, gain_one
    )
    tokens_grad = move((grad_middle + grad_first).astype(BF16), back).reshape(1, local, width)

    out_weight_grad = join(out_half, swap_core(out_half), core).reshape(-1, width).astype(F32)
    if True:

        def finish_columns(values):
            values = values.reshape(quarter, own_rows, 1, -1)
            values = lax.all_to_all(values, "gq", split_axis=0, concat_axis=2, tiled=True)
            values = values.reshape(own_rows, quarter, -1)
            return join(values, swap_core(values), core).transpose(1, 0, 2, 3)

        def natural_columns(values, inner=1):
            values = values.reshape(own_rows, 2, quarter, inner, 2, -1)
            return values.transpose(0, 4, 2, 1, 3, 5).reshape(own_rows, -1).astype(F32)

        ups = jnp.stack([finish_columns(values) for values in sums_feed[::2]], axis=3)
        up_weight_grad = natural_columns(ups, ranges)
        downs = jnp.stack(sums_feed[1::2])
        down_weight_grad = join(downs, swap_core(downs), core).reshape(-1, width).astype(F32)
        columns = jnp.concatenate([finish_columns(values) for values in qkv_halves], axis=3)
        columns = columns.reshape(own_rows, 2, quarter, pairs, 3, PAIR)
        query_weight_grad, key_weight_grad, value_weight_grad = [
            natural_columns(columns[:, :, :, :, i]) for i in range(3)
        ]

    def place_entries(values, inner=1):
        values = values.reshape(inner, 2, 1, 1, -1).transpose(1, 2, 3, 0, 4)
        shape = (2, quarter, 2) + values.shape[3:]
        zero = jnp.zeros((), core.dtype)
        return lax.dynamic_update_slice(
            jnp.zeros(shape, F32), values, (zero, gq, core, zero, zero)
        ).reshape(grp, -1)

    dqkv_sums = jnp.concatenate([jnp.sum(d.astype(F32), axis=0) for d in dqkvs])
    dqkv_sums = dqkv_sums.reshape(pairs, 3, PAIR)
    sums = [
        place_entries(dqkv_sums[:, 0]),
        place_entries(dqkv_sums[:, 2]),
        jnp.sum(grad_middle_low.astype(F32), axis=0),
        grad_gain_one, grad_shift_one, grad_gain_two, grad_shift_two,
        jnp.sum(grad_wide, axis=0),
        place_entries(jnp.stack([outs[6] for outs in feeds]), ranges),
    ]
    sums = jnp.concatenate([s.reshape(grp, -1) for s in sums], axis=1)
    if grp == 2 and ring & (ring - 1) == 0:
        sums = sums + swap_core(sums)
        sums = pick(sums, half, 0) + swap_half(pick(sums, 1 - half, 0))
        step = 1
        while step < ring:
            sums = sums + lax.ppermute(sums, "rz", [(i, i ^ step) for i in range(ring)])
            step *= 2
    else:
        sums = lax.psum(sums, ("rz", "core", "half", "gq"))
        sums = pick(sums, half * quarter + gq, 0)
    small = [sums[i * own_rows : (i + 1) * own_rows] for i in range(8)]
    return (
        layer_out, tokens_grad, query_weight_grad, key_weight_grad, value_weight_grad,
        small[0], small[1], out_weight_grad, small[2], small[3], small[4], small[5], small[6],
        up_weight_grad, sums[8 * own_rows :], down_weight_grad, small[7],
    )


class Order:
    def __init__(self):
        self.before = ()

    def pin(self, *values):
        pinned = lax.optimization_barrier(values + self.before)[: len(values)]
        self.before = tuple(pinned) + self.before
        return pinned[0] if len(values) == 1 else list(pinned)

    def fence(self, *values):
        self.before = values


class LineSum:
    def __init__(self, order, axes, size, values):
        self.order, self.axes, self.size = order, axes, size
        self.shape = values.shape
        if axes == "line":
            self.place = lax.axis_index("line")
            pieces = values.reshape(size, -1, values.shape[-1])
            sent = [pick(pieces, (self.place + s) % size, 0) for s in range(1, size)]
            self.piece, *sent = order.pin(pick(pieces, self.place, 0), *sent)
            self.received = [self.shift(values, s) for s, values in enumerate(sent, start=1)]
            return
        values = order.pin(values)
        self.received = self.exchange(values.reshape(size, -1, values.shape[-1]))

    def shift(self, values, s):
        return lax.ppermute(values, "line", [(i, (i + s) % self.size) for i in range(self.size)])

    def exchange(self, values):
        return lax.all_to_all(values, self.axes, split_axis=0, concat_axis=0, tiled=True)

    def spread(self):
        if self.axes == "line":
            piece = self.piece.astype(F32)
            for other in self.order.pin(*self.received):
                piece = piece + other.astype(F32)
            self.piece = self.order.pin(piece.astype(BF16))
            self.received = [self.shift(self.piece, s) for s in range(1, self.size)]
            return
        received = self.order.pin(self.received)
        piece = received[0].astype(F32)
        for i in range(1, self.size):
            piece = piece + received[i].astype(F32)
        piece = piece.astype(BF16)
        copies = self.order.pin(jnp.broadcast_to(piece[None], (self.size,) + piece.shape))
        self.received = self.exchange(copies)

    def gather(self):
        if self.axes != "line":
            return self.order.pin(self.received).reshape(self.shape)
        gathered = [self.piece] + list(self.order.pin(*self.received))
        whole = [
            functools.reduce(
                lambda rest, s: jnp.where((self.place - s) % self.size == i, gathered[s], rest),
                range(1, self.size),
                gathered[0],
            )
            for i in range(self.size)
        ]
        return self.order.pin(jnp.concatenate(whole, axis=0))

    def meet(self):
        self.whole = self.gather()
        if self.axes == "line":
            self.beside = lax.ppermute(self.whole, "low", SWAP)
        self.across = lax.ppermute(self.whole, "core", SWAP)

    def cross(self):
        if self.axes != "line":
            return self.whole, self.order.pin(self.across)
        self.beside = self.order.pin(self.beside)
        self.beside_across = lax.ppermute(self.beside, "core", SWAP)
        return self.whole, self.beside, self.across, self.beside_across


class PlaneSum:
    def __init__(self, order, low, deep, send, keep, both=False):
        self.order, self.low, self.deep, self.both = order, low, deep, both
        send, self.keep = order.pin(send, keep)
        self.received = lax.ppermute(send, "half", SWAP)

    def to_neighbour(self):
        total = add_low(self.keep, self.order.pin(self.received))
        if self.both:
            self.line = LineSum(self.order, ("line", "low"), 2 * self.deep, total)
            return
        parts = total.reshape(2, -1, total.shape[-1])
        send, self.keep = self.order.pin(pick(parts, 1 - self.low, 0), pick(parts, self.low, 0))
        self.received = lax.ppermute(send, "low", SWAP)

    def along(self):
        received = self.order.pin(self.received)
        self.line = LineSum(self.order, "line", self.deep, add_low(self.keep, received))

    def spread(self):
        self.line.spread()

    def meet(self):
        self.line.meet()

    def cross(self):
        return self.line.cross()


def add_low(left, right):
    return (left.astype(F32) + right.astype(F32)).astype(BF16)


def after_all(values, *gates):
    if not gates:
        return tuple(values)
    return lax.optimization_barrier(tuple(values) + gates)[: len(values)]


def pair_body(
    rep, grp, tokens, query_weight, key_weight, value_weight, query_bias, value_bias, out_weight,
    out_bias, first_gain, first_shift, second_gain, second_shift, up_weight, up_bias,
    down_weight, down_bias, cotangent,
):
    clips, local, width = tokens.shape
    assert clips == 1
    ring = rep // 2
    deep = ring // 2
    core, half = lax.axis_index("core"), lax.axis_index("half")
    low, high = lax.axis_index("low"), lax.axis_index("line") % 2
    own_rows = width // 2
    pairs = own_rows // PAIR
    hidden = up_weight.shape[1]
    stays = core == half
    scal = jnp.stack([half, low, core, stays.astype(jnp.int32), high]).astype(jnp.int32)
    cross = [(1, 2), (2, 1)]

    def swap_half(values):
        return lax.ppermute(values, "half", SWAP)

    def swap_core(values):
        return lax.ppermute(values, "core", SWAP)

    def swap_low(values):
        return lax.ppermute(values, "low", SWAP)

    def swap_high(values):
        return lax.ppermute(values, "line", [(i, i ^ 1) for i in range(deep)])

    def cross_over(values):
        return lax.ppermute(values, ("core", "half"), cross)

    tokens, cotangent = tokens.reshape(local, width), cotangent.reshape(local, width)

    own_qkv, mine = pack_qkv(scal, (query_weight, key_weight, value_weight))
    qkv_x = swap_half(mine)
    vectors = jnp.concatenate(
        [query_bias, value_bias, out_bias, first_gain, first_shift, second_gain, second_shift,
         down_bias, up_bias]
    )
    vectors = join(vectors, swap_half(vectors), half)
    (full_qbias, full_vbias, full_obias, gain_one, shift_one, gain_two, shift_two, full_dbias) = [
        vectors[:, i * own_rows : (i + 1) * own_rows].reshape(1, width) for i in range(8)
    ]

    def set_entries(values, inner=1):
        return pick(values.reshape(2, 2, inner, -1), core, 1).transpose(1, 0, 2).reshape(inner, -1)

    bias_set = set_entries(vectors[:, 8 * own_rows :], 2).reshape(1, -1)
    packed = [pack_feed(scal, up_weight, down_weight, j, 2, (1, 4)[j]) for j in range(2)]
    quarter = own_rows // 4
    out_mine = lax.dynamic_slice(
        out_weight, (core * (own_rows // 2) + low * quarter, 0 * core), (quarter, width)
    )
    order = Order()
    order.pin(*packed)
    tokens, qkv_x = order.pin(tokens, qkv_x)
    tokens_in = cross_over(tokens)
    qkv_y = swap_low(qkv_x)
    out_mine = order.pin(out_mine)
    tokens_in, qkv_y = order.pin(tokens_in, qkv_y)
    out_x = swap_half(after(out_mine, tokens_in))
    packed = after_all(packed, tokens_in)
    x, first = first_norm(scal, tokens, tokens_in, gain_one, shift_one)
    x, first = order.pin(x, first)
    order.fence(x)
    first_in = swap_core(first)
    feed_x = [swap_half(values) for values in packed]
    zeros = jnp.zeros((pairs, PAIR), F32)
    qkv_bias = jnp.stack(
        [set_entries(full_qbias).reshape(pairs, PAIR), zeros,
         set_entries(full_vbias).reshape(pairs, PAIR)],
        axis=1,
    ).reshape(1, 3 * own_rows)
    first_in = order.pin(first_in)
    qkv, qkv_weight, first_all = project(
        scal, (first, first_in), own_qkv, qkv_x, qkv_y, qkv_bias
    )

    qkv, out_x = order.pin(qkv, out_x)
    order.fence(qkv)
    out_y = swap_low(out_x)
    mixed, lse = attend(qkv, 0, pairs - 1)
    lse, out_y, *feed_x = order.pin(lse, out_y, *feed_x)
    feed_y = [swap_low(feed_x[0]), swap_high(feed_x[1])]
    cotangent_in = cross_over(after(cotangent, lse))
    mixed, lse = attend(qkv, pairs - 1, pairs, (mixed, lse))
    mixed = order.pin(mixed)
    out_part, out_set = out_other(scal, mixed, out_weight, out_x, out_y)
    out_part, cotangent_in, *feed_y = order.pin(out_part, cotangent_in, *feed_y)
    out_in = swap_core(out_part)
    grad_out = order.pin(jnp.where(stays, cotangent, cotangent_in))
    grad_out_in = swap_core(grad_out)
    middle, second = second_norm(
        scal, mixed, out_set, x, order.pin(out_in), full_obias, gain_two, shift_two
    )
    middle, second = order.pin(middle, second)
    order.fence(second)
    second_in = swap_core(second)

    second_in = order.pin(second_in)
    (
        out_own, out_part, dx_own, dx_part, up_send, up_keep, down_send, down_keep, low_send,
        low_keep, up_bias_grad,
    ) = feed(
        scal, (second, second_in), (grad_out, grad_out_in), up_weight, down_weight,
        (feed_x[0], feed_y[0], feed_x[1], feed_y[1]), bias_set,
    )
    dx_part, up_send, down_send, low_send, out_part = order.pin(
        dx_part, up_send, down_send, low_send, out_part
    )
    order.fence(dx_part)
    dx_in = swap_core(dx_part)
    up_in, down_in, low_in = swap_half(up_send), swap_half(down_send), swap_low(low_send)
    out_in = swap_core(out_part)
    grad_low, sums_two = second_back(
        scal, dx_own, order.pin(dx_in), middle, grad_out, gain_two
    )
    grad_low = order.pin(grad_low)
    grad_low_in = swap_core(grad_low)
    layer = layer_rows(scal, out_own, order.pin(out_in), middle, full_dbias)
    grad_low_in, layer = order.pin(grad_low_in, layer)
    grad_mixed, out_send, out_keep = mixed_back(scal, (grad_low, grad_low_in), out_set, mixed)
    grad_mixed = order.pin(grad_mixed)

    backs = []

    def back(pair):
        gate = order.pin(lse)
        backs.append(attend_back(scal, qkv, grad_mixed, mixed, gate, first_all, pair, pair + 1))
        backs[-1] = order.pin(*backs[-1])
        order.fence(backs[-1][3])

    back(0)
    up_in, down_in, low_in = order.pin(up_in, down_in, low_in)
    up_sum, down_sum = add_low(up_keep, up_in), add_low(down_keep, down_in)
    even = low == 0
    low_mine, low_other = order.pin(
        jnp.where(even, up_sum, down_sum), jnp.where(even, down_sum, up_sum)
    )
    one_in = lax.ppermute(low_other, "low", SWAP)
    range_sum = add_low(low_keep, low_in).reshape(2, own_rows, width)
    half_send, half_keep = order.pin(pick(range_sum, 1 - half, 0), pick(range_sum, half, 0))
    half_in = swap_half(half_send)

    back(1)
    one = LineSum(order, "line", deep, add_low(low_mine, order.pin(one_in)))
    early = PlaneSum(
        order, low, deep,
        jnp.concatenate([backs[0][1], backs[1][1], out_send], axis=0),
        jnp.concatenate([backs[0][2], backs[1][2], out_keep], axis=0),
    )

    back(2)
    one.spread()
    two = LineSum(order, "line", deep, add_low(half_keep, order.pin(half_in)))
    early.to_neighbour()

    back(3)
    one.meet()
    late = PlaneSum(
        order, low, deep,
        jnp.concatenate([backs[2][1], backs[3][1]], axis=0),
        jnp.concatenate([backs[2][2], backs[3][2]], axis=0), both=True,
    )
    early.along()
    layer_in = cross_over(order.pin(layer))
    first_own, first_part = first_grad(
        scal, [order.pin(backs[0][0])] + [b[0] for b in backs[1:]], qkv_weight
    )
    first_own, first_part = order.pin(first_own, first_part)
    order.fence(first_part)
    first_part_in = swap_core(first_part)
    late.to_neighbour()
    early.spread()
    two.spread()
    tokens_out, sums_one = first_back(
        scal, first_own, order.pin(first_part_in), x, grad_low, gain_one
    )
    tokens_out, sums_one = order.pin(tokens_out, sums_one)
    order.fence(sums_one)

    def place_entries(values, inner=1):
        values = values.reshape(inner, 2, 1, -1).transpose(1, 2, 0, 3)
        empty = jnp.zeros_like(values)
        return join(values[:, 0], empty[:, 0], core).transpose(1, 0, 2, 3).reshape(2, -1)

    parts = jnp.concatenate([b[3][0] for b in backs]).reshape(pairs, 3, PAIR)
    entries = [
        place_entries(parts[:, 0]), place_entries(parts[:, 2]), sums_two[3], sums_one[0],
        sums_one[1], sums_two[0], sums_two[1], sums_two[2], place_entries(up_bias_grad, 2),
    ]
    entries = order.pin(jnp.concatenate([e.reshape(2, -1) for e in entries], axis=1))
    entries_in = swap_core(entries)
    late.spread()
    entries = entries + order.pin(entries_in)
    keep, send = order.pin(pick(entries, half, 0), pick(entries, 1 - half, 0))
    entries_in = swap_half(send)
    tokens_in = cross_over(after(tokens_out, send))
    early.meet()
    one_parts = one.cross()
    steps = [("line", 1 << bit, deep) for bit in range((deep - 1).bit_length())] + [("low", 1, 2)]

    def exchange(axis, step, size):
        return lax.ppermute(entries, axis, [(i, i ^ step) for i in range(size)])

    entries = order.pin(keep + order.pin(entries_in))
    entries_in = exchange(*steps[0])
    two.meet()
    for step in steps[1:]:
        entries = order.pin(entries + order.pin(entries_in))
        entries_in = exchange(*step)
    late.meet()
    early_parts = early.cross()
    two_parts = two.cross()
    up_weight_grad, down_weight_grad = finish_feed(
        scal, order.pin(*one_parts, *two_parts)
    )
    entries = entries + entries_in
    late_parts = late.cross()
    query_weight_grad, key_weight_grad, value_weight_grad, out_weight_grad = finish_attention(
        scal, (*early_parts, *late_parts), ((0, 2), (2, 4))
    )
    layer_out = jnp.where(stays, layer, layer_in)
    tokens_grad = jnp.where(stays, tokens_out, tokens_in)
    small = [entries[i * own_rows : (i + 1) * own_rows] for i in range(8)]
    return (
        layer_out.reshape(1, local, width), tokens_grad.reshape(1, local, width),
        query_weight_grad, key_weight_grad, value_weight_grad, small[0], small[1],
        out_weight_grad, small[2], small[3], small[4], small[5], small[6], up_weight_grad,
        entries[8 * own_rows :], down_weight_grad, small[7],
    )


def solution(mesh):
    rep, grp = mesh.shape["rep"], mesh.shape["grp"]
    paired = grp == 2 and rep >= 8 and rep & (rep - 1) == 0
    if paired:
        sizes, names = (rep // 4, 2, 2, 2), ("line", "low", "core", "half")
        reps, groups, body = ("line", "low", "core"), "half", pair_body
    else:
        sizes, names = (rep // 2, 2, 2, grp // 2), ("rz", "core", "half", "gq")
        reps, groups, body = ("rz", "core"), ("half", "gq"), wide_body
    clip, matrix, vector = P(reps, groups, None), P(groups, None), P(groups)
    return jax.shard_map(
        functools.partial(body, rep, grp),
        mesh=Mesh(mesh.devices.reshape(sizes), names),
        in_specs=(
            clip, matrix, matrix, matrix, vector, vector, matrix, vector, vector, vector, vector,
            vector, matrix, vector, matrix, vector, clip,
        ),
        out_specs=(
            clip, clip, matrix, matrix, matrix, vector, vector, matrix, vector, vector, vector,
            vector, vector, matrix, vector, matrix, vector,
        ),
        check_vma=False,
    )
```

```python
import functools

import jax
import jax.numpy as jnp
from jax import lax
from jax.experimental import pallas as pl
from jax.experimental.pallas import tpu as pltpu
from jax.sharding import Mesh
from jax.sharding import PartitionSpec as P

HEAD_DIM = 64
PAIR = 2 * HEAD_DIM
EPS = 1e-06
LOG2E = 1.4426950408889634
F32 = jnp.float32
BF16 = jnp.bfloat16
SWAP = [(0, 1), (1, 0)]
VMEM_LIMIT = 62 << 20


def contract(left, right, left_dim, right_dim):
    return lax.dot_general(
        left, right, (((left_dim,), (right_dim,)), ((), ())), preferred_element_type=F32
    )


def padded_rows(rows, tile):
    full = rows // tile
    return full * tile + -(-(rows - full * tile) // PAIR) * PAIR


def walk(rows, tile, start, finish):
    full = rows // tile
    rest = padded_rows(rows, tile) - full * tile
    start(0, pl.ds(0, tile), tile)

    def step(columns, size, following, following_size):
        start(1, columns, size)
        finish(0, columns, size)
        if following is not None:
            start(0, following, following_size)
        finish(1, columns, size)

    def block(index, carry):
        first = pl.multiple_of(index * tile, tile)
        following = pl.multiple_of(index * tile + tile, tile)
        step(pl.ds(first, tile), tile, pl.ds(following, tile), tile)
        return carry

    lax.fori_loop(0, full - 1, block, 0)
    last = pl.ds(full * tile, rest) if rest else None
    step(pl.ds((full - 1) * tile, tile), tile, last, rest)
    if rest:
        step(last, rest, None, 0)


def one_head(values_t, head, columns, size):
    empty = jnp.zeros((HEAD_DIM, size), BF16)
    values = values_t[head * HEAD_DIM : (head + 1) * HEAD_DIM, columns]
    return jnp.concatenate([values, empty] if head == 0 else [empty, values], axis=0)


def attend_kernel(tile, rows, padded, qkv_ref, out_ref, lse_ref, q_t, v_t, out_t, scores):
    scale = HEAD_DIM**-0.5 * LOG2E
    ones = jnp.ones((16, rows), BF16)
    q_t[:, :rows] = qkv_ref[:, :PAIR].T
    if padded > rows:
        q_t[:, rows:] = jnp.zeros((PAIR, padded - rows), BF16)
    values_t = qkv_ref[:, 2 * PAIR :].T
    step = HEAD_DIM + 16
    for head in range(2):
        v_t[head * step : head * step + HEAD_DIM, :] = values_t[
            head * HEAD_DIM : (head + 1) * HEAD_DIM, :
        ]
        v_t[head * step + HEAD_DIM : (head + 1) * step, :] = ones

    def start(head, columns, size):
        query = one_head(q_t, head, columns, size)
        scores[head, :, :size] = contract(qkv_ref[:, PAIR : 2 * PAIR], query, 1, 0)

    def finish(head, columns, size):
        values = scores[head, :, :size]
        highest = jnp.max(values, axis=0, keepdims=True) * scale
        expon = jnp.exp2(values * scale - highest).astype(BF16)
        mixed = contract(v_t[head * step : (head + 1) * step, :], expon, 1, 0)
        total = mixed[HEAD_DIM : HEAD_DIM + 1, :]
        out_t[head * HEAD_DIM : (head + 1) * HEAD_DIM, columns] = mixed[:HEAD_DIM, :] / total
        lse_ref[head : head + 1, columns] = highest + jnp.log2(total)

    walk(rows, tile, start, finish)
    out_ref[...] = out_t[...].T[:rows, :].astype(BF16)


def attend(qkv, first_pair, last_pair, kept=None, tile=512):
    rows, width = qkv.shape
    pairs = width // (3 * PAIR)
    padded = padded_rows(rows, tile)
    count = last_pair - first_pair
    kernel = functools.partial(attend_kernel, tile, rows, padded)
    anywhere = pl.BlockSpec(memory_space=pl.ANY)
    return pl.pallas_call(
        kernel if kept is None else lambda ref, a, b, *rest: kernel(ref, *rest),
        grid=(count,),
        in_specs=[pl.BlockSpec((rows, 3 * PAIR), lambda i: (0, i + first_pair))]
        + ([] if kept is None else [anywhere] * 2),
        out_specs=[
            pl.BlockSpec((rows, PAIR), lambda i: (0, i + first_pair)),
            pl.BlockSpec((None, 2, padded), lambda i: (i + first_pair, 0, 0)),
        ],
        out_shape=[
            jax.ShapeDtypeStruct((rows, pairs * PAIR), BF16),
            jax.ShapeDtypeStruct((pairs, 2, padded), F32),
        ],
        scratch_shapes=[
            pltpu.VMEM((PAIR, padded), BF16),
            pltpu.VMEM((PAIR + 32, rows), BF16),
            pltpu.VMEM((PAIR, padded), F32),
            pltpu.VMEM((2, rows, tile), F32),
        ],
        input_output_aliases={} if kept is None else {1: 0, 2: 1},
        compiler_params=pltpu.CompilerParams(vmem_limit_bytes=VMEM_LIMIT),
        cost_estimate=pl.CostEstimate(
            flops=64 * rows * rows * PAIR * count,
            bytes_accessed=8 * rows * PAIR * count,
            transcendentals=2 * rows * rows * count,
        ),
        name="attend",
    )(qkv, *(() if kept is None else kept))


def attend_back_kernel(
    tile, rows, padded, s_ref, qkv_ref, grad_ref, out_ref, lse_ref, first_ref, dqkv_ref, send_ref,
    keep_ref, sums_ref, q_t, g_t, k_t, delta, dq_t, dk_t, dv_t, all_t, scores, d_probs,
):
    scale = HEAD_DIM**-0.5
    q_t[:, :rows] = qkv_ref[:, :PAIR].T
    g_t[:, :rows] = grad_ref[...].T
    if padded > rows:
        q_t[:, rows:] = jnp.zeros((PAIR, padded - rows), BF16)
        g_t[:, rows:] = jnp.zeros((PAIR, padded - rows), BF16)
        delta[:, rows:] = jnp.zeros((2, padded - rows), F32)
    k_t[...] = qkv_ref[:, PAIR : 2 * PAIR].T
    product = (grad_ref[...].astype(F32) * out_ref[...].astype(F32)).T
    delta[0:1, :rows] = jnp.sum(product[:HEAD_DIM, :], axis=0, keepdims=True)
    delta[1:2, :rows] = jnp.sum(product[HEAD_DIM:, :], axis=0, keepdims=True)
    dk_t[...] = jnp.zeros_like(dk_t)
    dv_t[...] = jnp.zeros_like(dv_t)

    def start(head, columns, size):
        query, grad = one_head(q_t, head, columns, size), one_head(g_t, head, columns, size)
        scores[head, :, :size] = contract(qkv_ref[:, PAIR : 2 * PAIR], query, 1, 0)
        d_probs[head, :, :size] = contract(qkv_ref[:, 2 * PAIR :], grad, 1, 0)

    def finish(head, columns, size):
        lanes = slice(head * HEAD_DIM, (head + 1) * HEAD_DIM)
        log_total = lse_ref[head : head + 1, columns]
        weights = jnp.exp2(scores[head, :, :size] * (scale * LOG2E) - log_total)
        inner = delta[head : head + 1, columns]
        d_scores = (weights * (d_probs[head, :, :size] - inner)).astype(BF16)
        dv_t[lanes, :] += contract(g_t[lanes, columns], weights.astype(BF16), 1, 1)
        dq_t[lanes, columns] = contract(k_t[lanes, :], d_scores, 1, 0)
        dk_t[lanes, :] += contract(q_t[lanes, columns], d_scores, 1, 1)

    walk(rows, tile, start, finish)
    all_t[:PAIR, :] = (dq_t[:, :rows] * scale).astype(BF16)
    all_t[PAIR : 2 * PAIR, :] = (dk_t[...] * scale).astype(BF16)
    all_t[2 * PAIR :, :] = dv_t[...].astype(BF16)
    for part in range(3):
        lanes = slice(part * PAIR, (part + 1) * PAIR)
        dqkv_ref[:, lanes] = all_t[lanes, :].T
    sums_ref[...] = contract(jnp.ones((8, rows), BF16), all_t[...], 1, 1)
    own = first_ref.shape[1] // 2
    for h in range(2):
        grad = contract(all_t[...], first_ref[:, h * own : (h + 1) * own], 1, 0).astype(BF16)

        @pl.when(s_ref[0] == h)
        def _():
            keep_ref[...] = grad

        @pl.when(s_ref[0] != h)
        def _():
            send_ref[...] = grad


def attend_back(scal, qkv, grad, out, lse, first, first_pair, last_pair, tile=256):
    rows, full = qkv.shape
    width = first.shape[1]
    padded = padded_rows(rows, tile)
    count = last_pair - first_pair
    return pl.pallas_call(
        functools.partial(attend_back_kernel, tile, rows, padded),
        grid_spec=pltpu.PrefetchScalarGridSpec(
            num_scalar_prefetch=1,
            grid=(count,),
            in_specs=[
                pl.BlockSpec((rows, 3 * PAIR), lambda i, s: (0, i + first_pair)),
                pl.BlockSpec((rows, PAIR), lambda i, s: (0, i + first_pair)),
                pl.BlockSpec((rows, PAIR), lambda i, s: (0, i + first_pair)),
                pl.BlockSpec((None, 2, lse.shape[2]), lambda i, s: (i + first_pair, 0, 0)),
                pl.BlockSpec((rows, width), lambda i, s: (0, 0), pipeline_mode=pl.Buffered(1)),
            ],
            out_specs=[
                pl.BlockSpec((rows, 3 * PAIR), lambda i, s: (0, i)),
                pl.BlockSpec((3 * PAIR, width // 2), lambda i, s: (i, 0)),
                pl.BlockSpec((3 * PAIR, width // 2), lambda i, s: (i, 0)),
                pl.BlockSpec((8, 3 * PAIR), lambda i, s: (0, i)),
            ],
            scratch_shapes=[
                pltpu.VMEM((PAIR, padded), BF16),
                pltpu.VMEM((PAIR, padded), BF16),
                pltpu.VMEM((PAIR, rows), BF16),
                pltpu.VMEM((2, padded), F32),
                pltpu.VMEM((PAIR, padded), F32),
                pltpu.VMEM((PAIR, rows), F32),
                pltpu.VMEM((PAIR, rows), F32),
                pltpu.VMEM((3 * PAIR, rows), BF16),
                pltpu.VMEM((2, rows, tile), F32),
                pltpu.VMEM((2, rows, tile), F32),
            ],
        ),
        out_shape=[
            jax.ShapeDtypeStruct((rows, 3 * PAIR * count), BF16),
            jax.ShapeDtypeStruct((3 * PAIR * count, width // 2), BF16),
            jax.ShapeDtypeStruct((3 * PAIR * count, width // 2), BF16),
            jax.ShapeDtypeStruct((8, 3 * PAIR * count), F32),
        ],
        compiler_params=pltpu.CompilerParams(vmem_limit_bytes=VMEM_LIMIT),
        cost_estimate=pl.CostEstimate(
            flops=160 * rows * rows * PAIR * count,
            bytes_accessed=16 * rows * PAIR * count,
            transcendentals=2 * rows * rows * count,
        ),
        name="attend_back",
    )(scal, qkv, grad, out, lse, first)


def feed_kernel(
    s_ref, x_own, x_other, dy_own, dy_other, up_ref, down_ref, x_piece, x_beside, z_piece, z_beside,
    bias_ref, out_own, out_other, dx_own, dx_other, up_send, up_keep, down_send, down_keep,
    low_send, low_keep, bias_grad_ref, x, dy, x_t, out_sum, dx_sum, up_full, down_full, hidden,
    d_pre, sems,
):
    index = pl.program_id(0)
    half = s_ref[0]
    rows, width = x.shape
    block = rows // 2
    own = width // 2
    tile = up_ref.shape[1]
    first_range = index < 2
    side = index % 2
    columns = pl.ds(pl.multiple_of(side * tile, tile), tile)
    mine = pl.ds(pl.multiple_of(half * own, own), own)
    theirs = pl.ds(pl.multiple_of((1 - half) * own, own), own)

    @pl.when(index == 0)
    def _():
        copies = []
        for i, ref in enumerate((x_own, x_other)):
            copies.append(pltpu.make_async_copy(ref, x.at[pl.ds(i * block, block)], sems.at[i]))
        for i, ref in enumerate((dy_own, dy_other)):
            copies.append(
                pltpu.make_async_copy(ref, dy.at[pl.ds(i * block, block)], sems.at[2 + i])
            )
        for copy in copies:
            copy.start()
        for copy in copies:
            copy.wait()
        x_t[...] = x[...].T
        out_sum[...] = jnp.zeros_like(out_sum)
        dx_sum[...] = jnp.zeros_like(dx_sum)

    up_full[mine, :] = up_ref[...]

    @pl.when(side == half)
    def _():
        down_full[...] = down_ref[...]

    for chosen, place, piece, beside in (
        (first_range, 1, x_piece, x_beside), (jnp.logical_not(first_range), 4, z_piece, z_beside)
    ):
        even = s_ref[place] == 0

        @pl.when(chosen & even)
        def _():
            up_full[theirs, :] = piece[:, columns]

        @pl.when(chosen & jnp.logical_not(even))
        def _():
            up_full[theirs, :] = beside[:, columns]

        @pl.when(chosen & (side != half) & even)
        def _():
            down_full[...] = beside[...]

        @pl.when(chosen & (side != half) & jnp.logical_not(even))
        def _():
            down_full[...] = piece[...]

    bias_grad = jnp.zeros(bias_grad_ref.shape, F32)
    for start in range(0, rows, block):
        part = slice(start, start + block)
        pre = contract(x[part, :], up_full[...], 1, 0) + bias_ref[...]
        d_hidden = contract(dy[part, :], down_full[...], 1, 1)
        share = 0.5 * (1.0 + lax.erf(pre * 0.7071067811865476))
        hidden[part, :] = (pre * share).astype(BF16)
        slope = share + pre * (jnp.exp(-0.5 * pre * pre) * 0.3989422804014327)
        d_low = (d_hidden * slope).astype(BF16)
        d_pre[part, :] = d_low
        bias_grad = bias_grad + jnp.sum(d_low.astype(F32), axis=0, keepdims=True)
        out_sum[part, :] += contract(hidden[part, :], down_full[...], 1, 0)
        dx_sum[part, :] += contract(d_pre[part, :], up_full[...], 1, 1)
    bias_grad_ref[...] = bias_grad
    down_grad = contract(hidden[...], dy[...], 0, 0).astype(BF16)
    side_rows = pl.ds(pl.multiple_of(side * tile, tile), tile)

    @pl.when(first_range)
    def _():
        up_keep[:, columns] = contract(x_t[mine, :], d_pre[...], 1, 0).astype(BF16)
        up_send[:, columns] = contract(x_t[theirs, :], d_pre[...], 1, 0).astype(BF16)

    @pl.when(first_range & (side == half))
    def _():
        down_keep[...] = down_grad

    @pl.when(first_range & (side != half))
    def _():
        down_send[...] = down_grad

    for even in (True, False):
        up_goal, down_goal = (low_keep, low_send) if even else (low_send, low_keep)

        @pl.when(jnp.logical_not(first_range) & ((s_ref[1] == 0) == even))
        def _():
            up_goal[:, columns] = contract(x_t[...], d_pre[...], 1, 0).astype(BF16)
            down_goal[side_rows, :] = down_grad

    @pl.when(index == pl.num_programs(0) - 1)
    def _():
        out_own[...] = out_sum[:block, :].astype(BF16)
        out_other[...] = out_sum[block:, :].astype(BF16)
        dx_own[...] = dx_sum[:block, :].astype(BF16)
        dx_other[...] = dx_sum[block:, :].astype(BF16)


def feed(scal, seconds, grads, up, down, pieces, bias):
    local, width = seconds[0].shape
    rows = 2 * local
    tile = down.shape[0] // 4
    anywhere = pl.BlockSpec(memory_space=pl.ANY)

    def fixed(*shape):
        return pl.BlockSpec(shape, lambda t, s: (0, 0), pipeline_mode=pl.Buffered(1))

    shapes = [(local, width)] * 4 + [(width // 2, 2 * tile)] * 2 + [(tile, width)] * 2
    shapes += [(width, 2 * tile)] * 2
    across = pl.BlockSpec((1, tile), lambda t, s: (0, t))
    return pl.pallas_call(
        feed_kernel,
        grid_spec=pltpu.PrefetchScalarGridSpec(
            num_scalar_prefetch=1,
            grid=(4,),
            in_specs=[anywhere] * 4
            + [
                pl.BlockSpec(
                    (width // 2, tile), lambda t, s: (0, ((t % 2) * 2 + s[2]) * 2 + t // 2)
                ),
                pl.BlockSpec((tile, width), lambda t, s: (s[2] * 2 + t // 2, 0)),
            ]
            + [fixed(width // 2, 2 * tile)] * 4
            + [across],
            out_specs=[fixed(*shape) for shape in shapes] + [across],
            scratch_shapes=[
                pltpu.VMEM((rows, width), BF16),
                pltpu.VMEM((rows, width), BF16),
                pltpu.VMEM((width, rows), BF16),
                pltpu.VMEM((rows, width), F32),
                pltpu.VMEM((rows, width), F32),
                pltpu.VMEM((width, tile), BF16),
                pltpu.VMEM((tile, width), BF16),
                pltpu.VMEM((rows, tile), BF16),
                pltpu.VMEM((rows, tile), BF16),
                pltpu.SemaphoreType.DMA((4,)),
            ],
        ),
        out_shape=[jax.ShapeDtypeStruct(shape, BF16) for shape in shapes]
        + [jax.ShapeDtypeStruct((1, 4 * tile), F32)],
        compiler_params=pltpu.CompilerParams(vmem_limit_bytes=VMEM_LIMIT),
        cost_estimate=pl.CostEstimate(
            flops=48 * rows * width * tile,
            bytes_accessed=16 * rows * width,
            transcendentals=8 * rows * tile,
        ),
        name="feed",
    )(scal, *seconds, *grads, up, down, *pieces, bias)


def run(kernel, name, scal, grid, in_specs, out_specs, out_shape, args, flops=0, scratch=()):
    moved = sum(a.size * a.dtype.itemsize for a in args)
    return pl.pallas_call(
        kernel,
        grid_spec=pltpu.PrefetchScalarGridSpec(
            num_scalar_prefetch=1,
            grid=grid,
            in_specs=in_specs,
            out_specs=out_specs,
            scratch_shapes=scratch,
        ),
        out_shape=out_shape,
        compiler_params=pltpu.CompilerParams(vmem_limit_bytes=VMEM_LIMIT),
        cost_estimate=pl.CostEstimate(flops=flops, bytes_accessed=2 * moved, transcendentals=0),
        name=name,
    )(scal, *args)


def spec(shape, index):
    return pl.BlockSpec(shape, index)


def held(*shape):
    return pl.BlockSpec(shape, lambda i, s: (0,) * len(shape), pipeline_mode=pl.Buffered(1))


def struct(*shape, dtype=BF16):
    return jax.ShapeDtypeStruct(shape, dtype)


def pack_qkv(scal, weights):
    rows, width = weights[0].shape
    pairs = width // (2 * PAIR)
    per = pairs // 2

    def kernel(s_ref, q_ref, k_ref, v_ref, own_ref, mine_ref):
        for i, ref in enumerate((q_ref, k_ref, v_ref)):
            own_ref[:, i * PAIR : (i + 1) * PAIR] = ref[...]
        start = pl.multiple_of(s_ref[1] * (rows // 2), rows // 2)
        mine_ref[...] = own_ref[pl.ds(start, rows // 2), :]

    block = spec((rows, PAIR), lambda p, s: (0, ((p // per) * 2 + s[2]) * per + p % per))
    return run(
        kernel, "pack_qkv", scal, (pairs,), [block] * 3,
        [
            spec((rows, 3 * PAIR), lambda p, s: (0, p)),
            spec((rows // 2, 3 * PAIR), lambda p, s: (0, p)),
        ],
        [struct(rows, 3 * PAIR * pairs), struct(rows // 2, 3 * PAIR * pairs)],
        weights,
    )


def pack_feed(scal, up, down, j, ranges, bit):
    rows, hidden = up.shape
    tile = hidden // (4 * ranges)
    columns = down.shape[1] // 2

    def kernel(s_ref, up_ref, down_ref, out_ref):
        out_ref[...] = jnp.where(s_ref[bit] == 0, up_ref[...], down_ref[...])

    return run(
        kernel, "pack_feed", scal, (2,),
        [
            spec((rows, tile), lambda t, s: (0, (t * 2 + s[2]) * ranges + j)),
            spec((tile, columns), lambda t, s: (s[2] * ranges + j, t)),
        ],
        spec((rows, tile), lambda t, s: (0, t)), struct(rows, 2 * tile), (up, down),
    )


def normalize(values):
    centred = values - jnp.mean(values, axis=-1, keepdims=True)
    spread = jnp.mean(centred * centred, axis=-1, keepdims=True)
    inverse = lax.rsqrt(spread + EPS)
    return centred * inverse, inverse


def first_norm(scal, tokens, received, gain, shift):
    rows, width = tokens.shape
    step = rows // 2

    def kernel(s_ref, t_ref, r_ref, gain_ref, shift_ref, x_ref, first_ref):
        x = jnp.where(s_ref[3] == 1, t_ref[...], r_ref[...])
        x_ref[...] = x
        normed, _ = normalize(x.astype(F32))
        first_ref[...] = (normed * gain_ref[...] + shift_ref[...]).astype(BF16)

    block = spec((step, width), lambda i, s: (i, 0))
    return run(
        kernel, "first_norm", scal, (2,), [block, block, held(1, width), held(1, width)],
        [block, block], [struct(rows, width)] * 2, (tokens, received, gain, shift),
    )


def project(scal, firsts, own, piece, beside, bias):
    local, width = firsts[0].shape
    rows, total = 2 * local, own.shape[1]
    block = 6 * PAIR
    half_rows, quarter_rows = width // 2, width // 4

    def kernel(
        s_ref, mine_ref, theirs_ref, own_ref, piece_ref, beside_ref, bias_ref, qkv_ref, w_ref,
        all_ref, sems,
    ):
        @pl.when(pl.program_id(0) == 0)
        def _():
            copies = [
                pltpu.make_async_copy(ref, all_ref.at[pl.ds(i * local, local)], sems.at[i])
                for i, ref in enumerate((mine_ref, theirs_ref))
            ]
            for copy in copies:
                copy.start()
            for copy in copies:
                copy.wait()

        half, low = s_ref[0], s_ref[1]
        other = (1 - half) * half_rows
        w_ref[pl.ds(pl.multiple_of(half * half_rows, half_rows), half_rows), :] = own_ref[...]
        start = pl.multiple_of(other + low * quarter_rows, quarter_rows)
        w_ref[pl.ds(start, quarter_rows), :] = piece_ref[...]
        start = pl.multiple_of(other + (1 - low) * quarter_rows, quarter_rows)
        w_ref[pl.ds(start, quarter_rows), :] = beside_ref[...]
        qkv_ref[...] = (contract(all_ref[...], w_ref[...], 1, 0) + bias_ref[...]).astype(BF16)

    def columns(size):
        return spec((size, block), lambda p, s: (0, p))

    anywhere = pl.BlockSpec(memory_space=pl.ANY)
    return run(
        kernel, "project", scal, (total // block,),
        [anywhere] * 2
        + [columns(half_rows), columns(quarter_rows), columns(quarter_rows), columns(1)],
        [columns(rows), columns(width), held(rows, width)],
        [struct(rows, total), struct(width, total), struct(rows, width)],
        (*firsts, own, piece, beside, bias), flops=2 * rows * width * total,
        scratch=[pltpu.SemaphoreType.DMA((2,))],
    )


def out_other(scal, mixed, weight, piece, beside):
    rows, set_width = mixed.shape
    local, width = rows // 2, weight.shape[1]
    block, small = set_width // 2, set_width // 4

    def kernel(s_ref, mixed_ref, own_ref, piece_ref, beside_ref, out_ref, set_ref):
        half, low = s_ref[0], s_ref[1]
        other = (1 - half) * block
        set_ref[pl.ds(pl.multiple_of(half * block, block), block), :] = own_ref[...]
        set_ref[pl.ds(pl.multiple_of(other + low * small, small), small), :] = piece_ref[...]
        start = pl.multiple_of(other + (1 - low) * small, small)
        set_ref[pl.ds(start, small), :] = beside_ref[...]
        out_ref[...] = contract(mixed_ref[...], set_ref[...], 1, 0).astype(BF16)

    return run(
        kernel, "out_other", scal, (1,),
        [
            spec((local, set_width), lambda i, s: (1, 0)),
            spec((block, width), lambda i, s: (s[2], 0)),
            held(small, width), held(small, width),
        ],
        [held(local, width), held(set_width, width)],
        [struct(local, width), struct(set_width, width)],
        (mixed, weight, piece, beside), flops=2 * local * set_width * width,
    )


def second_norm(scal, mixed, out_set, x, received, bias, gain, shift):
    rows, set_width = mixed.shape
    local, width = x.shape
    step = local // 2

    def kernel(
        s_ref, mixed_ref, w_ref, x_ref, r_ref, bias_ref, gain_ref, shift_ref, mid_ref, second_ref
    ):
        middle = contract(mixed_ref[...], w_ref[...], 1, 0) + r_ref[...].astype(F32)
        middle = middle + x_ref[...].astype(F32) + bias_ref[...]
        mid_ref[...] = middle
        normed, _ = normalize(middle)
        second_ref[...] = (normed * gain_ref[...] + shift_ref[...]).astype(BF16)

    block = spec((step, width), lambda i, s: (i, 0))
    return run(
        kernel, "second_norm", scal, (2,),
        [spec((step, set_width), lambda i, s: (i, 0)), held(set_width, width), block, block]
        + [held(1, width)] * 3,
        [block, block], [struct(local, width, dtype=F32), struct(local, width)],
        (mixed, out_set, x, received, bias, gain, shift), flops=2 * local * set_width * width,
    )


def norm_back_rows(grad, normed, inverse, gain):
    scaled = grad * gain
    first_term = jnp.mean(scaled, axis=-1, keepdims=True)
    second_term = jnp.mean(scaled * normed, axis=-1, keepdims=True)
    return inverse * (scaled - first_term - normed * second_term)


def column_sums(refs, values):
    @pl.when(pl.program_id(0) == 0)
    def _():
        refs[...] = jnp.zeros_like(refs)

    for i, value in enumerate(values):
        refs[i : i + 1, :] += jnp.sum(value, axis=0, keepdims=True)


def row_step(rows):
    return rows // 7 if rows % 112 == 0 else rows


def second_back(scal, grad, received, middle, dy, gain):
    local, width = middle.shape
    step = row_step(local)

    def kernel(s_ref, g_ref, r_ref, mid_ref, dy_ref, gain_ref, low_ref, sums_ref):
        grad = g_ref[...].astype(F32) + r_ref[...].astype(F32)
        normed, inverse = normalize(mid_ref[...])
        dy_wide = dy_ref[...].astype(F32)
        low = (dy_wide + norm_back_rows(grad, normed, inverse, gain_ref[...])).astype(BF16)
        low_ref[...] = low
        column_sums(sums_ref, (grad * normed, grad, dy_wide, low.astype(F32)))

    block = spec((step, width), lambda i, s: (i, 0))
    return run(
        kernel, "second_back", scal, (local // step,), [block] * 4 + [held(1, width)],
        [block, held(8, width)], [struct(local, width), struct(8, width, dtype=F32)],
        (grad, received, middle, dy, gain),
    )


def mixed_back(scal, lows, out_set, mixed):
    local, width = lows[0].shape
    rows, set_width = mixed.shape
    block = set_width // 2

    def kernel(
        s_ref, mine_ref, theirs_ref, w_ref, mixed_ref, d_ref, send_ref, keep_ref, low, sems
    ):
        @pl.when(pl.program_id(0) == 0)
        def _():
            copies = [
                pltpu.make_async_copy(ref, low.at[pl.ds(i * local, local)], sems.at[i])
                for i, ref in enumerate((mine_ref, theirs_ref))
            ]
            for copy in copies:
                copy.start()
            for copy in copies:
                copy.wait()

        d_ref[...] = contract(low[...], w_ref[...], 1, 1).astype(BF16)
        grad = contract(mixed_ref[...], low[...], 0, 0).astype(BF16)

        def store(goal):
            for c in range(2):
                for i in range(width // (2 * PAIR)):
                    start = (2 * i + c) * PAIR
                    goal[c * block : (c + 1) * block, i * PAIR : (i + 1) * PAIR] = (
                        grad[:, start : start + PAIR]
                    )

        @pl.when(pl.program_id(0) == s_ref[0])
        def _():
            store(keep_ref)

        @pl.when(pl.program_id(0) != s_ref[0])
        def _():
            store(send_ref)

    anywhere = pl.BlockSpec(memory_space=pl.ANY)
    across = spec((rows, block), lambda t, s: (0, t))
    return run(
        kernel, "mixed_back", scal, (2,),
        [anywhere] * 2 + [spec((block, width), lambda t, s: (t, 0)), across],
        [across, held(2 * block, width // 2), held(2 * block, width // 2)],
        [struct(rows, set_width)] + [struct(2 * block, width // 2)] * 2,
        (*lows, out_set, mixed), flops=4 * rows * set_width * width,
        scratch=[pltpu.VMEM((rows, width), BF16), pltpu.SemaphoreType.DMA((2,))],
    )


def first_grad(scal, dqkvs, weights):
    rows = dqkvs[0].shape[0]
    width = weights.shape[0]
    local = rows // 2
    count = len(dqkvs)
    step = width // 4

    def kernel(s_ref, *refs):
        left = jnp.concatenate([refs[j][...] for j in range(count)], axis=1)
        total = contract(left, refs[count][...], 1, 1)
        refs[-2][...] = total[:local].astype(BF16)
        refs[-1][...] = total[local:].astype(BF16)

    across = spec((local, step), lambda i, s: (0, i))
    return run(
        kernel, "first_grad", scal, (4,),
        [held(*a.shape) for a in dqkvs] + [spec((step, weights.shape[1]), lambda i, s: (i, 0))],
        [across, across], [struct(local, width)] * 2, (*dqkvs, weights),
        flops=sum(2 * rows * a.shape[1] * width for a in dqkvs),
    )


def first_back(scal, grad, received, x, wide, gain):
    local, width = x.shape
    step = row_step(local)

    def kernel(s_ref, g_ref, r_ref, x_ref, wide_ref, gain_ref, out_ref, sums_ref):
        grad = g_ref[...].astype(F32) + r_ref[...].astype(F32)
        normed, inverse = normalize(x_ref[...].astype(F32))
        total = wide_ref[...].astype(F32) + norm_back_rows(grad, normed, inverse, gain_ref[...])
        out_ref[...] = total.astype(BF16)
        column_sums(sums_ref, (grad * normed, grad))

    block = spec((step, width), lambda i, s: (i, 0))
    return run(
        kernel, "first_back", scal, (local // step,), [block] * 4 + [held(1, width)],
        [block, held(8, width)], [struct(local, width), struct(8, width, dtype=F32)],
        (grad, received, x, wide, gain),
    )


def layer_rows(scal, own, received, middle, bias):
    local, width = middle.shape
    step = row_step(local)

    def kernel(s_ref, o_ref, r_ref, mid_ref, bias_ref, out_ref):
        total = mid_ref[...] + o_ref[...].astype(F32) + r_ref[...].astype(F32) + bias_ref[...]
        out_ref[...] = total.astype(BF16)

    block = spec((step, width), lambda i, s: (i, 0))
    return run(
        kernel, "layer_rows", scal, (local // step,), [block] * 3 + [held(1, width)],
        block, struct(local, width), (own, received, middle, bias),
    )


def finish_feed_kernel(s_ref, *refs, tile):
    up_out, down_out = refs[8:]
    first = s_ref[2] == 0
    even = s_ref[1] == 0
    low_range = s_ref[4] == 0
    cores = []
    for refs_of in (refs[:4], refs[4:8]):
        whole, beside, along, last = [ref[...] for ref in refs_of]
        ranges = []
        for j in range(2):
            mine = jnp.where(low_range == (j == 0), whole, along)
            theirs = jnp.where(low_range == (j == 0), beside, last)
            ranges.append((jnp.where(even, mine, theirs), jnp.where(even, theirs, mine)))
        cores.append(ranges)
    for c in range(2):
        for j in range(2):
            up, down = [
                jnp.where(first == (c == 0), cores[0][j][kind], cores[1][j][kind]).astype(F32)
                for kind in range(2)
            ]
            down_out[c, j] = down
            for h in range(2):
                start = ((h * 2 + c) * 2 + j) * tile
                up_out[:, start : start + tile] = up[:, h * tile : (h + 1) * tile]


def finish_feed(scal, sums):
    rows, width = sums[0].shape
    steps = 4
    block = spec((rows // steps, width), lambda i, s: (i, 0))
    up, down = run(
        functools.partial(finish_feed_kernel, tile=rows), "finish_feed", scal, (steps,),
        [block] * 8,
        [
            spec((rows // steps, 4 * width), lambda i, s: (i, 0)),
            spec((2, 2, rows // steps, width), lambda i, s: (0, 0, i, 0)),
        ],
        [struct(rows, 4 * width, dtype=F32), struct(2, 2, rows, width, dtype=F32)],
        sums,
    )
    return up, down.reshape(4 * rows, width)


def finish_attention_kernel(s_ref, *refs, pairs, spans):
    q_out, k_out, v_out, out_out = refs[-4:]
    first, even = s_ref[2] == 0, s_ref[1] == 0
    half_pairs = pairs // 2
    for g, (begin, end) in enumerate(spans):
        mine, beside, mine_across, beside_across = [ref[...] for ref in refs[4 * g : 4 * g + 4]]
        own = jnp.concatenate(
            [jnp.where(even, mine, beside), jnp.where(even, beside, mine)], axis=0
        )
        other = jnp.concatenate(
            [
                jnp.where(even, mine_across, beside_across),
                jnp.where(even, beside_across, mine_across),
            ],
            axis=0,
        )
        for c in range(2):
            total = jnp.where(first == (c == 0), own, other).astype(F32)
            wide = total[: (end - begin) * 3 * PAIR].T
            for q in range(end - begin):
                pair = begin + q
                h, p = pair // half_pairs, pair % half_pairs
                goal = ((h * 2 + c) * half_pairs + p) * PAIR
                for i, out in enumerate((q_out, k_out, v_out)):
                    start = (q * 3 + i) * PAIR
                    out[:, goal : goal + PAIR] = wide[:, start : start + PAIR]
            if g == 0:
                rest = total[(end - begin) * 3 * PAIR :]
                rows = rest.shape[0] // 2
                out_out[c * rows : (c + 1) * rows, :PAIR] = rest[:rows]
                out_out[c * rows : (c + 1) * rows, PAIR:] = rest[rows:]


def finish_attention(scal, sums, spans):
    rows = sums[0].shape[1]
    pairs = spans[-1][1]
    steps = rows // PAIR
    return run(
        functools.partial(finish_attention_kernel, pairs=pairs, spans=spans), "finish_attention",
        scal, (steps,),
        [spec((values.shape[0], PAIR), lambda i, s: (0, i)) for values in sums],
        [spec((PAIR, 2 * pairs * PAIR), lambda i, s: (i, 0))] * 3
        + [spec((rows, 2 * PAIR), lambda i, s: (0, i))],
        [struct(rows, 2 * pairs * PAIR, dtype=F32)] * 3 + [struct(rows, 2 * rows, dtype=F32)],
        sums,
    )


def wide_back_kernel(
    tile, rows, padded, qkv_ref, grad_ref, out_ref, lse_ref, dqkv_ref, q_t, g_t, k_t, delta,
    dq_t, dk_t, dv_t,
):
    scale = HEAD_DIM**-0.5
    q_t[:, :rows] = qkv_ref[:, :PAIR].T
    g_t[:, :rows] = grad_ref[...].T
    if padded > rows:
        q_t[:, rows:] = jnp.zeros((PAIR, padded - rows), BF16)
        g_t[:, rows:] = jnp.zeros((PAIR, padded - rows), BF16)
        delta[:, rows:] = jnp.zeros((2, padded - rows), F32)
    k_t[...] = qkv_ref[:, PAIR : 2 * PAIR].T
    product = (grad_ref[...].astype(F32) * out_ref[...].astype(F32)).T
    delta[0:1, :rows] = jnp.sum(product[:HEAD_DIM, :], axis=0, keepdims=True)
    delta[1:2, :rows] = jnp.sum(product[HEAD_DIM:, :], axis=0, keepdims=True)
    dk_t[...] = jnp.zeros_like(dk_t)
    dv_t[...] = jnp.zeros_like(dv_t)

    def block(index, carry):
        columns = pl.ds(pl.multiple_of(index * tile, tile), tile)
        empty = jnp.zeros((HEAD_DIM, tile), BF16)
        for head in range(2):
            lanes = slice(head * HEAD_DIM, (head + 1) * HEAD_DIM)
            query = q_t[lanes, columns]
            grad = g_t[lanes, columns]
            query_pad = jnp.concatenate([query, empty] if head == 0 else [empty, query], axis=0)
            grad_pad = jnp.concatenate([grad, empty] if head == 0 else [empty, grad], axis=0)
            scores = contract(qkv_ref[:, PAIR : 2 * PAIR], query_pad, 1, 0)
            grad_probs = contract(qkv_ref[:, 2 * PAIR :], grad_pad, 1, 0)
            weights = jnp.exp2(scores * (scale * LOG2E) - lse_ref[head : head + 1, columns])
            grad_scores = (weights * (grad_probs - delta[head : head + 1, columns])).astype(BF16)
            dv_t[lanes, :] += contract(grad, weights.astype(BF16), 1, 1)
            dq_t[lanes, columns] = contract(k_t[lanes, :], grad_scores, 1, 0)
            dk_t[lanes, :] += contract(query, grad_scores, 1, 1)
        return carry

    lax.fori_loop(0, padded // tile, block, 0)
    dqkv_ref[:, :PAIR] = (dq_t[...].T[:rows, :] * scale).astype(BF16)
    dqkv_ref[:, PAIR : 2 * PAIR] = (dk_t[...].T * scale).astype(BF16)
    dqkv_ref[:, 2 * PAIR :] = dv_t[...].T.astype(BF16)


def wide_back(qkv, grad, out, lse, first_pair, last_pair, tile=256):
    rows, width = qkv.shape
    padded = -(-rows // tile) * tile
    lse = jnp.pad(lse, ((0, 0), (0, 0), (0, padded - lse.shape[2])))
    count = last_pair - first_pair
    return pl.pallas_call(
        functools.partial(wide_back_kernel, tile, rows, padded),
        grid=(count,),
        in_specs=[
            pl.BlockSpec((rows, 3 * PAIR), lambda i: (0, i + first_pair)),
            pl.BlockSpec((rows, PAIR), lambda i: (0, i + first_pair)),
            pl.BlockSpec((rows, PAIR), lambda i: (0, i + first_pair)),
            pl.BlockSpec((None, 2, lse.shape[2]), lambda i: (i + first_pair, 0, 0)),
        ],
        out_specs=pl.BlockSpec((rows, 3 * PAIR), lambda i: (0, i)),
        out_shape=jax.ShapeDtypeStruct((rows, 3 * PAIR * count), BF16),
        scratch_shapes=[
            pltpu.VMEM((PAIR, padded), BF16),
            pltpu.VMEM((PAIR, padded), BF16),
            pltpu.VMEM((PAIR, rows), BF16),
            pltpu.VMEM((2, padded), F32),
            pltpu.VMEM((PAIR, padded), F32),
            pltpu.VMEM((PAIR, rows), F32),
            pltpu.VMEM((PAIR, rows), F32),
        ],
        compiler_params=pltpu.CompilerParams(vmem_limit_bytes=VMEM_LIMIT),
        cost_estimate=pl.CostEstimate(
            flops=160 * rows * rows * PAIR * count,
            bytes_accessed=16 * rows * PAIR * count,
            transcendentals=2 * rows * rows * count,
        ),
        name="wide_back",
    )(qkv, grad, out, lse)


def wide_feed_kernel(
    half_ref, *refs, parts, make, chunk,
):
    xs, refs = refs[:parts], refs[parts:]
    dys, refs = refs[:parts], refs[parts:]
    if not make:
        x_t, refs = refs[0], refs[1:]
    up_ref, bias_ref, down_ref, *refs = refs
    hidden_ref, d_pre_ref, up_send, up_keep, down_send, down_keep, bias_grad_ref, *refs = refs
    if make:
        x_t, refs = refs[0], refs[1:]
    x, dy, sems = refs
    index = pl.program_id(0)
    half = half_ref[0]
    rows, width = x.shape
    block = rows // parts
    own = width // 2
    tile = up_ref.shape[1]

    @pl.when(index == 0)
    def _():
        copies = []
        for i in range(parts):
            part = pl.ds(i * block, block)
            copies.append(pltpu.make_async_copy(xs[i], x.at[part], sems.at[i]))
            copies.append(pltpu.make_async_copy(dys[i], dy.at[part], sems.at[parts + i]))
        for copy in copies:
            copy.start()
        for copy in copies:
            copy.wait()
        if make:
            x_t[...] = x[...].T

    bias_grad = jnp.zeros(bias_grad_ref.shape, F32)
    for start in range(0, rows, chunk):
        part = slice(start, start + chunk)
        pre = contract(x[part, :], up_ref[...], 1, 0) + bias_ref[...]
        d_hidden = contract(dy[part, :], down_ref[...], 1, 1)
        share = 0.5 * (1.0 + lax.erf(pre * 0.7071067811865476))
        hidden_ref[part, :] = (pre * share).astype(BF16)
        slope = share + pre * (jnp.exp(-0.5 * pre * pre) * 0.3989422804014327)
        d_low = (d_hidden * slope).astype(BF16)
        d_pre_ref[part, :] = d_low
        bias_grad = bias_grad + jnp.sum(d_low.astype(F32), axis=0, keepdims=True)
    bias_grad_ref[...] = bias_grad
    columns = pl.ds(pl.multiple_of(index * tile, tile), tile)
    mine = pl.ds(pl.multiple_of(half * own, own), own)
    theirs = pl.ds(pl.multiple_of((1 - half) * own, own), own)
    up_keep[:, columns] = contract(x_t[mine, :], d_pre_ref[...], 1, 0).astype(BF16)
    up_send[:, columns] = contract(x_t[theirs, :], d_pre_ref[...], 1, 0).astype(BF16)
    down_grad = contract(hidden_ref[...], dy[...], 0, 0).astype(BF16)

    @pl.when(index == half)
    def _():
        down_keep[...] = down_grad

    @pl.when(index != half)
    def _():
        down_send[...] = down_grad


def wide_feed(half, xs, dys, x_t, up, bias, down):
    parts = len(xs)
    width = xs[0].shape[1]
    rows = sum(part.shape[0] for part in xs)
    hidden = up.shape[1]
    tile = hidden // 2
    make = x_t is None
    chunk = rows // 2 if rows % 32 == 0 else rows
    anywhere = pl.BlockSpec(memory_space=pl.ANY)
    fixed = lambda shape: pl.BlockSpec(shape, lambda j, s: (0, 0), pipeline_mode=pl.Buffered(1))
    across = lambda size: pl.BlockSpec((size, tile), lambda j, s: (0, j))
    out_specs = [across(rows)] * 2 + [fixed((width // 2, hidden))] * 2
    out_specs += [fixed((tile, width))] * 2 + [across(1)]
    out_shape = [
        jax.ShapeDtypeStruct((rows, hidden), BF16),
        jax.ShapeDtypeStruct((rows, hidden), BF16),
        jax.ShapeDtypeStruct((width // 2, hidden), BF16),
        jax.ShapeDtypeStruct((width // 2, hidden), BF16),
        jax.ShapeDtypeStruct((tile, width), BF16),
        jax.ShapeDtypeStruct((tile, width), BF16),
        jax.ShapeDtypeStruct((1, hidden), F32),
    ]
    if make:
        out_specs.append(fixed((width, rows)))
        out_shape.append(jax.ShapeDtypeStruct((width, rows), BF16))
    return pl.pallas_call(
        functools.partial(wide_feed_kernel, parts=parts, make=make, chunk=chunk),
        grid_spec=pltpu.PrefetchScalarGridSpec(
            num_scalar_prefetch=1,
            grid=(2,),
            in_specs=[anywhere] * (2 * parts)
            + ([] if make else [fixed((width, rows))])
            + [across(width), across(1), pl.BlockSpec((tile, width), lambda j, s: (j, 0))],
            out_specs=out_specs,
            scratch_shapes=[
                pltpu.VMEM((rows, width), BF16),
                pltpu.VMEM((rows, width), BF16),
                pltpu.SemaphoreType.DMA((2 * parts,)),
            ],
        ),
        out_shape=out_shape,
        compiler_params=pltpu.CompilerParams(vmem_limit_bytes=VMEM_LIMIT),
        cost_estimate=pl.CostEstimate(
            flops=8 * rows * width * hidden,
            bytes_accessed=8 * rows * width + 8 * width * hidden,
            transcendentals=2 * rows * hidden,
        ),
        name="wide_feed",
    )(half.reshape(1), *xs, *dys, *(() if make else (x_t,)), up, bias, down)


def norm_parts(values, gain, shift):
    average = jnp.mean(values, axis=-1, keepdims=True)
    centred = values - average
    spread = jnp.mean(centred * centred, axis=-1, keepdims=True)
    inverse = lax.rsqrt(spread + EPS)
    normed = centred * inverse
    return (normed * gain + shift, normed, inverse)


def norm_back(grad, normed, inverse, gain):
    scaled = grad * gain
    first_term = jnp.mean(scaled, axis=-1, keepdims=True)
    second_term = jnp.mean(scaled * normed, axis=-1, keepdims=True)
    result = inverse * (scaled - first_term - normed * second_term)
    return (result, jnp.sum(grad * normed, axis=0), jnp.sum(grad, axis=0))


def pick(values, index, axis):
    return lax.dynamic_index_in_dim(values, index, axis, keepdims=False)


def join(own, other, index):
    return jnp.where(index == 0, jnp.stack([own, other]), jnp.stack([other, own]))


def after(values, *earlier):
    return lax.optimization_barrier((values,) + earlier)[0]


def wide_body(
    rep, grp, tokens, query_weight, key_weight, value_weight, query_bias, value_bias, out_weight,
    out_bias, first_gain, first_shift, second_gain, second_shift, up_weight, up_bias,
    down_weight, down_bias, cotangent,
):
    clips, local, width = tokens.shape
    assert clips == 1
    quarter = grp // 2
    ring = rep // 2
    deep = ring // 2
    core = lax.axis_index("core")
    half = lax.axis_index("half")
    gq = lax.axis_index("gq")
    place = lax.axis_index("rz")
    low = place % 2
    high = place // 2
    own_rows = width // grp
    pairs = own_rows // PAIR
    hidden = up_weight.shape[1]
    set_hidden = hidden // grp
    ranges = max(1, set_hidden // width)
    tile = set_hidden // (2 * ranges)

    there = []
    for b in range(2):
        for h in range(2):
            for q in range(quarter):
                g = h * quarter + q
                source = (b * 2 + h) * quarter + q
                target = ((g % 2) * 2 + b) * quarter + g // 2
                if source != target:
                    there.append((source, target))
    back = [(target, source) for source, target in there]
    block = half * quarter + gq
    stays = (block % 2 == core) & (block // 2 == gq) & (half == core)
    axes = ("core", "half", "gq")
    beside = [(i, i ^ 1) for i in range(ring)]

    def move(values, route):
        return jnp.where(stays, values, lax.ppermute(values, axes, route))

    def swap_half(values):
        return lax.ppermute(values, "half", SWAP)

    def swap_core(values):
        return lax.ppermute(values, "core", SWAP)

    def spread(values):
        if grp == 2:
            return [values, swap_core(values)]
        return [lax.all_gather(values, ("gq", "core"), axis=0, tiled=True)]

    def collect(values):
        if grp == 2:
            other = swap_core(values(slice(local, None)).astype(BF16))
            return values(slice(None, local)) + other.astype(F32)
        return lax.psum_scatter(
            values(slice(None)).astype(BF16), ("gq", "core"), scatter_dimension=0, tiled=True
        ).astype(F32)

    def other_half(pieces):
        mine = pick(jnp.stack(pieces), low, 0)
        first = swap_half(mine)
        second = lax.ppermute(first, "rz", beside)
        return first, jnp.where(low == 0, first, second), jnp.where(low == 0, second, first)

    def by_half(own, other):
        return join(own, other, half).reshape(-1, own.shape[-1])

    def set_columns(values, inner=1):
        parts = values.reshape(values.shape[0], 2, quarter, 2, inner, -1)
        return pick(parts, core, 3).transpose(0, 2, 3, 1, 4)

    def gather_rows(values):
        if quarter > 1:
            values = lax.all_to_all(values, "gq", split_axis=1, concat_axis=0, tiled=True)
        return values.reshape(-1, values.shape[-1])

    def set_entries(values, inner=1):
        parts = values.reshape(2, quarter, 2, inner, -1)
        return pick(pick(parts, core, 2), gq, 1).transpose(1, 0, 2).reshape(inner, 1, -1)

    clip_tokens = move(tokens.reshape(local, width), there)
    vectors = jnp.concatenate(
        [query_bias, value_bias, out_bias, first_gain, first_shift, second_gain, second_shift,
         down_bias, up_bias]
    )
    if quarter > 1:
        vectors = lax.all_gather(vectors, "gq", axis=0)
    vectors = join(vectors, swap_half(vectors), half).reshape(grp, -1)
    (full_qbias, full_vbias, full_obias, gain_one, shift_one, gain_two, shift_two, full_dbias) = [
        vectors[:, i * own_rows : (i + 1) * own_rows].reshape(-1) for i in range(8)
    ]
    bias_sets = set_entries(vectors[:, 8 * own_rows :].reshape(-1), ranges)

    parts = [
        set_columns(w).reshape(own_rows, quarter, pairs, PAIR)
        for w in (query_weight, key_weight, value_weight)
    ]
    own_qkv = gather_rows(jnp.stack(parts, axis=3).reshape(own_rows, quarter, 3 * own_rows))
    own_qkv = own_qkv.reshape(2, -1, 3 * own_rows)
    qkv_x, low_rows, high_rows = other_half([own_qkv[0], own_qkv[1]])
    qkv_weight = by_half(
        own_qkv.reshape(-1, 3 * own_rows), jnp.concatenate([low_rows, high_rows], axis=0)
    )
    own_out = pick(out_weight.reshape(2, -1, width), core, 0)
    out_x, low_rows, high_rows = other_half(
        [after(own_out, qkv_x)[: own_rows // 4], own_out[own_rows // 4 :]]
    )
    out_set = by_half(own_out, jnp.concatenate([low_rows, high_rows], axis=0))

    own_up = set_columns(up_weight, ranges)
    own_down = pick(down_weight.reshape(2, ranges, tile, width), core, 0)
    up_sets, down_sets, stages = [], [], [out_x]
    for j in range(ranges):
        up_part = gather_rows(own_up[:, :, j].reshape(own_rows, quarter, 2 * tile))
        down_part = own_down[j]
        if up_part.shape == down_part.shape:
            stage, other_up, other_down = other_half([after(up_part, stages[-1]), down_part])
        else:
            stage, other_up = swap_half(after(up_part, stages[-1])), None
            other_up, other_down = stage, swap_half(down_part)
        stages.append(stage)
        up_sets.append(by_half(up_part, other_up))
        down_sets.append(by_half(down_part, other_down))
    grad_out = move(after(cotangent.reshape(local, width), stages[1]), there)

    zeros = jnp.zeros((1, own_rows), F32)
    qkv_bias = jnp.stack(
        [
            b.reshape(pairs, PAIR)
            for b in (set_entries(full_qbias), zeros, set_entries(full_vbias))
        ],
        axis=1,
    ).reshape(1, 3 * own_rows)

    inputs = clip_tokens.astype(F32)
    first_norm, first_normed, first_inverse = norm_parts(inputs, gain_one, shift_one)
    first = jnp.concatenate(spread(first_norm.astype(BF16)), axis=0)
    qkv = (contract(first, qkv_weight, 1, 0) + qkv_bias).astype(BF16)
    if pairs > 1:
        kept = attend(qkv, 0, pairs // 2)
        mixed, lse = attend(qkv, pairs // 2, pairs, kept)
    else:
        mixed, lse = attend(qkv, 0, pairs)
    middle = collect(lambda rows: contract(mixed[rows], out_set, 1, 0)) + inputs + full_obias
    second_norm, second_normed, second_inverse = norm_parts(middle, gain_two, shift_two)
    seconds = spread(second_norm.astype(BF16))
    grads_out = spread(grad_out)
    x_t = None
    feeds = []
    for j in range(ranges):
        outs = wide_feed(
            half, seconds, grads_out, x_t, up_sets[j],
            bias_sets[j] if j == 0 else after(bias_sets[j], feeds[-1][6]), down_sets[j],
        )
        x_t = outs[7] if j == 0 else x_t
        feeds.append(outs)

    def reduce_ring(pair):
        send, keep = pair
        total = keep.astype(F32) + lax.ppermute(send, "rz", beside).astype(F32)
        total = total.astype(BF16).reshape(deep, -1, keep.shape[-1])
        shifts = range(1, deep)

        def route(shift):
            return [(i, (i + 2 * shift) % ring) for i in range(ring)]

        pieces = [
            lax.ppermute(pick(total, (high + s) % deep, 0), "rz", route(s)) for s in shifts
        ]
        piece = pick(total, high, 0).astype(F32)
        for other in pieces:
            piece = piece + other.astype(F32)
        piece = piece.astype(BF16)
        gathered = [piece] + [lax.ppermute(piece, "rz", route(s)) for s in shifts]
        whole = jnp.stack(
            [
                functools.reduce(
                    lambda rest, s: jnp.where((high - s) % deep == i, gathered[s], rest),
                    shifts,
                    piece,
                )
                for i in range(deep)
            ]
        ).reshape(keep.shape)
        return whole, lax.ppermute(whole, "rz", beside)

    def reduce_parts(parts):
        stacked = jnp.stack(parts)
        own, other = reduce_ring((pick(stacked, 1 - low, 0), pick(stacked, low, 0)))
        return jnp.where(low == 0, own, other), jnp.where(low == 0, other, own)

    def add_half(keep, send):
        return (keep.astype(F32) + swap_half(send).astype(F32)).astype(BF16)

    def reduce_rows(values):
        size = values.shape[0]
        if size % (16 * ring):
            return lax.psum(values, "rz")
        return jnp.concatenate(reduce_parts([values[: size // 2], values[size // 2 :]]), axis=0)

    def scatter_half(values):
        values = values.reshape(2, -1, values.shape[-1])
        return add_half(pick(values, half, 0), pick(values, 1 - half, 0))

    sums_feed = []
    for outs in feeds:
        up_part, down_part = add_half(outs[3], outs[2]), add_half(outs[5], outs[4])
        if up_part.shape == down_part.shape:
            sums_feed.extend(reduce_parts([up_part, down_part]))
        else:
            sums_feed.extend([reduce_rows(up_part), reduce_rows(down_part)])

    grad_wide = grad_out.astype(F32)
    grad_second = collect(
        lambda rows: functools.reduce(
            jnp.add, [contract(feeds[j][1][rows], up_sets[j], 1, 1) for j in range(ranges)]
        )
    )
    grad_second, grad_gain_two, grad_shift_two = norm_back(
        grad_second, second_normed, second_inverse, gain_two
    )
    grad_middle = grad_wide + grad_second
    grad_middle_low = grad_middle.astype(BF16)
    grad_middle_all = jnp.concatenate(spread(grad_middle_low), axis=0)
    grad_mixed = contract(grad_middle_all, out_set, 1, 1).astype(BF16)
    out_half = reduce_rows(scatter_half(contract(mixed, grad_middle_all, 0, 0).astype(BF16)))
    spans = [(0, pairs // 2), (pairs // 2, pairs)] if pairs > 1 else [(0, pairs)]
    dqkvs, qkv_halves = [], []
    for begin, end in spans:
        gate = lse if not dqkvs else after(lse, qkv_halves[-1])
        dqkvs.append(wide_back(qkv, grad_mixed, mixed, gate, begin, end))
        qkv_halves.append(contract(first, dqkvs[-1], 0, 0).astype(BF16))
    qkv_halves = [reduce_rows(scatter_half(values)) for values in qkv_halves]

    result = collect(
        lambda rows: functools.reduce(
            jnp.add, [contract(feeds[j][0][rows], down_sets[j], 1, 0) for j in range(ranges)]
        )
    )
    result = (middle + result + full_dbias).astype(BF16)
    layer_out = move(result, back).reshape(1, local, width)

    def weight_of(span):
        return qkv_weight[:, span[0] * 3 * PAIR : span[1] * 3 * PAIR]

    grad_first_norm = collect(
        lambda rows: functools.reduce(
            jnp.add,
            [contract(d[rows], weight_of(span), 1, 1) for d, span in zip(dqkvs, spans)],
        )
    )
    grad_first, grad_gain_one, grad_shift_one = norm_back(
        grad_first_norm, first_normed, first_inverse, gain_one
    )
    tokens_grad = move((grad_middle + grad_first).astype(BF16), back).reshape(1, local, width)

    out_weight_grad = join(out_half, swap_core(out_half), core).reshape(-1, width).astype(F32)
    if True:

        def finish_columns(values):
            values = values.reshape(quarter, own_rows, 1, -1)
            values = lax.all_to_all(values, "gq", split_axis=0, concat_axis=2, tiled=True)
            values = values.reshape(own_rows, quarter, -1)
            return join(values, swap_core(values), core).transpose(1, 0, 2, 3)

        def natural_columns(values, inner=1):
            values = values.reshape(own_rows, 2, quarter, inner, 2, -1)
            return values.transpose(0, 4, 2, 1, 3, 5).reshape(own_rows, -1).astype(F32)

        ups = jnp.stack([finish_columns(values) for values in sums_feed[::2]], axis=3)
        up_weight_grad = natural_columns(ups, ranges)
        downs = jnp.stack(sums_feed[1::2])
        down_weight_grad = join(downs, swap_core(downs), core).reshape(-1, width).astype(F32)
        columns = jnp.concatenate([finish_columns(values) for values in qkv_halves], axis=3)
        columns = columns.reshape(own_rows, 2, quarter, pairs, 3, PAIR)
        query_weight_grad, key_weight_grad, value_weight_grad = [
            natural_columns(columns[:, :, :, :, i]) for i in range(3)
        ]

    def place_entries(values, inner=1):
        values = values.reshape(inner, 2, 1, 1, -1).transpose(1, 2, 3, 0, 4)
        shape = (2, quarter, 2) + values.shape[3:]
        zero = jnp.zeros((), core.dtype)
        return lax.dynamic_update_slice(
            jnp.zeros(shape, F32), values, (zero, gq, core, zero, zero)
        ).reshape(grp, -1)

    dqkv_sums = jnp.concatenate([jnp.sum(d.astype(F32), axis=0) for d in dqkvs])
    dqkv_sums = dqkv_sums.reshape(pairs, 3, PAIR)
    sums = [
        place_entries(dqkv_sums[:, 0]),
        place_entries(dqkv_sums[:, 2]),
        jnp.sum(grad_middle_low.astype(F32), axis=0),
        grad_gain_one, grad_shift_one, grad_gain_two, grad_shift_two,
        jnp.sum(grad_wide, axis=0),
        place_entries(jnp.stack([outs[6] for outs in feeds]), ranges),
    ]
    sums = jnp.concatenate([s.reshape(grp, -1) for s in sums], axis=1)
    if grp == 2 and ring & (ring - 1) == 0:
        sums = sums + swap_core(sums)
        sums = pick(sums, half, 0) + swap_half(pick(sums, 1 - half, 0))
        step = 1
        while step < ring:
            sums = sums + lax.ppermute(sums, "rz", [(i, i ^ step) for i in range(ring)])
            step *= 2
    else:
        sums = lax.psum(sums, ("rz", "core", "half", "gq"))
        sums = pick(sums, half * quarter + gq, 0)
    small = [sums[i * own_rows : (i + 1) * own_rows] for i in range(8)]
    return (
        layer_out, tokens_grad, query_weight_grad, key_weight_grad, value_weight_grad,
        small[0], small[1], out_weight_grad, small[2], small[3], small[4], small[5], small[6],
        up_weight_grad, sums[8 * own_rows :], down_weight_grad, small[7],
    )


class Order:
    def __init__(self):
        self.before = ()

    def pin(self, *values):
        pinned = lax.optimization_barrier(values + self.before)[: len(values)]
        self.before = tuple(pinned) + self.before
        return pinned[0] if len(values) == 1 else list(pinned)

    def fence(self, *values):
        self.before = values


class Steps:
    def __init__(self, steps):
        self.steps = steps
        self.waiting = next(steps)


def advance(order, *chains):
    pinned = order.pin(*[values for chain in chains for values in chain.waiting])
    pinned = list(pinned) if isinstance(pinned, (list, tuple)) else [pinned]
    for chain in chains:
        count = len(chain.waiting)
        values, pinned = pinned[:count], pinned[count:]
        chain.waiting = chain.steps.send(values)


def line_steps(order, deep, parts, result):
    place = lax.axis_index("line")
    bits = range((deep - 1).bit_length())

    def exchange(values, bit):
        return lax.ppermute(values, "line", [(i, i ^ (1 << bit)) for i in range(deep)])

    for bit in bits:
        even = (place >> bit) % 2 == 0
        keep, send = order.pin(jnp.where(even, *parts), jnp.where(even, *parts[::-1]))
        (other,) = yield [exchange(send, bit)]
        total = add_low(keep, other)
        size = total.shape[0] // 2
        parts = (total[:size], total[size:])
    for bit in reversed(bits):
        total = order.pin(total)
        (other,) = yield [exchange(total, bit)]
        total = join(total, other, (place >> bit) % 2).reshape(-1, total.shape[-1])
    whole = order.pin(total)
    beside, across = yield [lax.ppermute(whole, "low", SWAP), lax.ppermute(whole, "core", SWAP)]
    crossed = lax.ppermute(beside, "core", SWAP)
    (crossed,) = yield [crossed]
    result.extend([whole, beside, across, crossed])
    yield []


def range_steps(order, deep, parts, result):
    place = lax.axis_index("line")
    bits = range((deep - 1).bit_length())

    def exchange(values, bit):
        return lax.ppermute(values, "line", [(i, i ^ (1 << bit)) for i in range(deep)])

    for bit in bits:
        even = (place >> bit) % 2 == 0
        keep, send = order.pin(jnp.where(even, *parts), jnp.where(even, *parts[::-1]))
        (other,) = yield [exchange(send, bit)]
        total = add_low(keep, other)
        size = total.shape[0] // 2
        parts = (total[:size], total[size:])
    for bit in reversed(bits[1:]):
        total = order.pin(total)
        (other,) = yield [exchange(total, bit)]
        total = join(total, other, (place >> bit) % 2).reshape(-1, total.shape[-1])
    whole = order.pin(total)
    beside, along = yield [lax.ppermute(whole, "low", SWAP), exchange(whole, 0)]
    last, crossed = yield [lax.ppermute(along, "low", SWAP), lax.ppermute(whole, "core", SWAP)]
    rest = yield [lax.ppermute(values, "core", SWAP) for values in (beside, along, last)]
    result.extend([whole, beside, along, last, crossed, *rest])
    yield []


def plane_steps(order, low, deep, send, keep, result):
    send, keep = order.pin(send, keep)
    (other,) = yield [lax.ppermute(send, "half", SWAP)]
    total = add_low(keep, other)
    size = total.shape[0] // 2
    parts = (total[:size], total[size:])
    even = low == 0
    keep, send = order.pin(jnp.where(even, *parts), jnp.where(even, *parts[::-1]))
    (other,) = yield [lax.ppermute(send, "low", SWAP)]
    total = add_low(keep, other)
    size = total.shape[0] // 2
    yield from line_steps(order, deep, (total[:size], total[size:]), result)


def vector_steps(order, half, deep, entries, result):
    def line(values, bit):
        return lax.ppermute(values, "line", [(i, i ^ (1 << bit)) for i in range(deep)])

    entries = order.pin(entries)
    (other,) = yield [lax.ppermute(entries, "core", SWAP)]
    entries = entries + other
    keep, send = order.pin(pick(entries, half, 0), pick(entries, 1 - half, 0))
    (other,) = yield [lax.ppermute(send, "half", SWAP)]
    total = order.pin(keep + other)
    for bit in range((deep - 1).bit_length()):
        (other,) = yield [line(total, bit)]
        total = order.pin(total + other)
    (other,) = yield [lax.ppermute(total, "low", SWAP)]
    result.append(total + other)
    yield []


def add_low(left, right):
    return (left.astype(F32) + right.astype(F32)).astype(BF16)


def after_all(values, *gates):
    if not gates:
        return tuple(values)
    return lax.optimization_barrier(tuple(values) + gates)[: len(values)]


def pair_body(
    rep, grp, tokens, query_weight, key_weight, value_weight, query_bias, value_bias, out_weight,
    out_bias, first_gain, first_shift, second_gain, second_shift, up_weight, up_bias,
    down_weight, down_bias, cotangent,
):
    clips, local, width = tokens.shape
    assert clips == 1
    ring = rep // 2
    deep = ring // 2
    core, half = lax.axis_index("core"), lax.axis_index("half")
    low, high = lax.axis_index("low"), lax.axis_index("line") % 2
    own_rows = width // 2
    pairs = own_rows // PAIR
    hidden = up_weight.shape[1]
    stays = core == half
    scal = jnp.stack([half, low, core, stays.astype(jnp.int32), high]).astype(jnp.int32)
    cross = [(1, 2), (2, 1)]

    def swap_half(values):
        return lax.ppermute(values, "half", SWAP)

    def swap_core(values):
        return lax.ppermute(values, "core", SWAP)

    def swap_low(values):
        return lax.ppermute(values, "low", SWAP)

    def swap_high(values):
        return lax.ppermute(values, "line", [(i, i ^ 1) for i in range(deep)])

    def cross_over(values):
        return lax.ppermute(values, ("core", "half"), cross)

    tokens, cotangent = tokens.reshape(local, width), cotangent.reshape(local, width)

    tokens_in = cross_over(tokens)
    own_qkv, mine = pack_qkv(scal, (query_weight, key_weight, value_weight))
    qkv_x = swap_half(mine)
    packed = [pack_feed(scal, up_weight, down_weight, j, 2, (1, 4)[j]) for j in range(2)]
    vectors = jnp.concatenate(
        [after(query_bias, mine, *packed), value_bias, out_bias, first_gain, first_shift,
         second_gain, second_shift, down_bias, up_bias]
    )
    order = Order()
    tokens_in, qkv_x, vectors, vectors_in, *packed = order.pin(
        tokens_in, qkv_x, vectors, swap_half(vectors), *packed
    )
    qkv_y = swap_low(qkv_x)
    feed_x = [swap_half(packed[0])]
    vectors = join(vectors, vectors_in, half)
    (full_qbias, full_vbias, full_obias, gain_one, shift_one, gain_two, shift_two, full_dbias) = [
        vectors[:, i * own_rows : (i + 1) * own_rows].reshape(1, width) for i in range(8)
    ]

    def set_entries(values, inner=1):
        return pick(values.reshape(2, 2, inner, -1), core, 1).transpose(1, 0, 2).reshape(inner, -1)

    bias_set = set_entries(vectors[:, 8 * own_rows :], 2).reshape(1, -1)
    quarter = own_rows // 4
    out_mine = lax.dynamic_slice(
        out_weight, (core * (own_rows // 2) + low * quarter, 0 * core), (quarter, width)
    )
    x, first = first_norm(scal, tokens, tokens_in, gain_one, shift_one)
    x, first = order.pin(x, first)
    order.fence(x)
    first, qkv_y, feed_x[0] = order.pin(first, qkv_y, feed_x[0])
    first_in = order.pin(swap_core(first))
    feed_y = [swap_low(feed_x[0])]
    out_x = swap_half(order.pin(out_mine))
    feed_x.append(swap_half(order.pin(packed[1])))
    zeros = jnp.zeros((pairs, PAIR), F32)
    qkv_bias = jnp.stack(
        [set_entries(full_qbias).reshape(pairs, PAIR), zeros,
         set_entries(full_vbias).reshape(pairs, PAIR)],
        axis=1,
    ).reshape(1, 3 * own_rows)
    qkv, qkv_weight, first_all = project(
        scal, (first, first_in), own_qkv, qkv_x, qkv_y, qkv_bias
    )

    qkv, out_x = order.pin(qkv, out_x)
    order.fence(qkv)
    out_y = swap_low(out_x)
    mixed, lse = attend(qkv, 0, pairs - 1)
    lse, out_y, feed_x[1] = order.pin(lse, out_y, feed_x[1])
    feed_y.append(swap_high(feed_x[1]))
    cotangent_in = cross_over(after(cotangent, lse))
    mixed, lse = attend(qkv, pairs - 1, pairs, (mixed, lse))
    mixed = order.pin(mixed)
    out_part, out_set = out_other(scal, mixed, out_weight, out_x, out_y)
    out_part, cotangent_in, *feed_y = order.pin(out_part, cotangent_in, *feed_y)
    out_in = swap_core(out_part)
    grad_out = order.pin(jnp.where(stays, cotangent, cotangent_in))
    grad_out_in = swap_core(grad_out)
    middle, second = second_norm(
        scal, mixed, out_set, x, order.pin(out_in), full_obias, gain_two, shift_two
    )
    middle, second = order.pin(middle, second)
    order.fence(second)
    second_in = swap_core(second)

    second_in = order.pin(second_in)
    (
        out_own, out_part, dx_own, dx_part, up_send, up_keep, down_send, down_keep, low_send,
        low_keep, up_bias_grad,
    ) = feed(
        scal, (second, second_in), (grad_out, grad_out_in), up_weight, down_weight,
        (feed_x[0], feed_y[0], feed_x[1], feed_y[1]), bias_set,
    )
    dx_part, up_send, down_send, low_send, out_part = order.pin(
        dx_part, up_send, down_send, low_send, out_part
    )
    order.fence(dx_part)
    dx_in = swap_core(dx_part)
    up_in, down_in, low_in = swap_half(up_send), swap_half(down_send), swap_low(low_send)
    out_in = swap_core(out_part)
    grad_low, sums_two = second_back(
        scal, dx_own, order.pin(dx_in), middle, grad_out, gain_two
    )
    grad_low = order.pin(grad_low)
    grad_low_in = swap_core(grad_low)
    layer = layer_rows(scal, out_own, order.pin(out_in), middle, full_dbias)
    grad_low_in, layer = order.pin(grad_low_in, layer)
    grad_mixed, out_send, out_keep = mixed_back(scal, (grad_low, grad_low_in), out_set, mixed)
    grad_mixed = order.pin(grad_mixed)

    backs = []

    def back(pair):
        gate = order.pin(lse)
        backs.append(attend_back(scal, qkv, grad_mixed, mixed, gate, first_all, pair, pair + 1))
        backs[-1] = order.pin(*backs[-1])
        order.fence(backs[-1][3])

    back(0)
    up_in, down_in, low_in = order.pin(up_in, down_in, low_in)
    up_sum, down_sum = add_low(up_keep, up_in), add_low(down_keep, down_in)
    even = low == 0
    low_mine, low_other = order.pin(
        jnp.where(even, up_sum, down_sum), jnp.where(even, down_sum, up_sum)
    )
    one_in = lax.ppermute(low_other, "low", SWAP)
    range_sum = add_low(low_keep, low_in).reshape(2, own_rows, width)
    half_send, half_keep = order.pin(pick(range_sum, 1 - half, 0), pick(range_sum, half, 0))
    half_in = swap_half(half_send)

    back(1)
    one_in, half_in = order.pin(one_in, half_in)
    feed_parts, early_parts, late_parts, vector_parts = [], [], [], []
    ranges = Steps(
        range_steps(
            order, deep, (add_low(low_mine, one_in), add_low(half_keep, half_in)), feed_parts
        )
    )
    early = Steps(
        plane_steps(
            order, low, deep,
            jnp.concatenate([backs[0][1], backs[1][1], out_send], axis=0),
            jnp.concatenate([backs[0][2], backs[1][2], out_keep], axis=0), early_parts,
        )
    )

    back(2)
    advance(order, ranges, early)
    layer_in = cross_over(order.pin(layer))

    back(3)
    layer_in = order.pin(layer_in)
    late = Steps(
        plane_steps(
            order, low, deep,
            jnp.concatenate([backs[2][1], backs[3][1]], axis=0),
            jnp.concatenate([backs[2][2], backs[3][2]], axis=0), late_parts,
        )
    )
    advance(order, ranges, early)
    first_own, first_part = first_grad(
        scal, [order.pin(backs[0][0])] + [b[0] for b in backs[1:]], qkv_weight
    )
    first_own, first_part = order.pin(first_own, first_part)
    order.fence(first_part)
    advance(order, late, early, ranges)
    first_part_in = swap_core(order.pin(first_part))
    tokens_out, sums_one = first_back(
        scal, first_own, order.pin(first_part_in), x, grad_low, gain_one
    )
    tokens_out, sums_one = order.pin(tokens_out, sums_one)
    order.fence(sums_one)
    advance(order, early, late, ranges)

    def place_entries(values, inner=1):
        values = values.reshape(inner, 2, 1, -1).transpose(1, 2, 0, 3)
        empty = jnp.zeros_like(values)
        return join(values[:, 0], empty[:, 0], core).transpose(1, 0, 2, 3).reshape(2, -1)

    parts = jnp.concatenate([b[3][0] for b in backs]).reshape(pairs, 3, PAIR)
    entries = [
        place_entries(parts[:, 0]), place_entries(parts[:, 2]), sums_two[3], sums_one[0],
        sums_one[1], sums_two[0], sums_two[1], sums_two[2], place_entries(up_bias_grad, 2),
    ]
    entries = jnp.concatenate([e.reshape(2, -1) for e in entries], axis=1)
    vectors = Steps(vector_steps(order, half, deep, entries, vector_parts))
    advance(order, vectors)
    advance(order, vectors, early, late)
    tokens_in = cross_over(order.pin(tokens_out))
    advance(order, vectors, early, late)
    advance(order, vectors, late)
    advance(order, early, ranges, late)
    advance(order, ranges, vectors, early)
    up_weight_grad, down_weight_grad = finish_feed(scal, feed_parts)
    advance(order, late)
    advance(order, late)
    (entries,) = vector_parts
    query_weight_grad, key_weight_grad, value_weight_grad, out_weight_grad = finish_attention(
        scal, (*early_parts, *late_parts), ((0, 2), (2, 4))
    )
    layer_out = jnp.where(stays, layer, layer_in)
    tokens_grad = jnp.where(stays, tokens_out, tokens_in)
    small = [entries[i * own_rows : (i + 1) * own_rows] for i in range(8)]
    return (
        layer_out.reshape(1, local, width), tokens_grad.reshape(1, local, width),
        query_weight_grad, key_weight_grad, value_weight_grad, small[0], small[1],
        out_weight_grad, small[2], small[3], small[4], small[5], small[6], up_weight_grad,
        entries[8 * own_rows :], down_weight_grad, small[7],
    )


def solution(mesh):
    rep, grp = mesh.shape["rep"], mesh.shape["grp"]
    paired = grp == 2 and rep >= 8 and rep & (rep - 1) == 0
    if paired:
        sizes, names = (rep // 4, 2, 2, 2), ("line", "low", "core", "half")
        reps, groups, body = ("line", "low", "core"), "half", pair_body
    else:
        sizes, names = (rep // 2, 2, 2, grp // 2), ("rz", "core", "half", "gq")
        reps, groups, body = ("rz", "core"), ("half", "gq"), wide_body
    clip, matrix, vector = P(reps, groups, None), P(groups, None), P(groups)
    return jax.shard_map(
        functools.partial(body, rep, grp),
        mesh=Mesh(mesh.devices.reshape(sizes), names),
        in_specs=(
            clip, matrix, matrix, matrix, vector, vector, matrix, vector, vector, vector, vector,
            vector, matrix, vector, matrix, vector, clip,
        ),
        out_specs=(
            clip, clip, matrix, matrix, matrix, vector, vector, matrix, vector, vector, vector,
            vector, vector, matrix, vector, matrix, vector,
        ),
        check_vma=False,
    )
```

```python
import functools

import jax
import jax.numpy as jnp
from jax import lax
from jax.experimental import pallas as pl
from jax.experimental.pallas import tpu as pltpu
from jax.sharding import Mesh
from jax.sharding import PartitionSpec as P

HEAD_DIM = 64
PAIR = 2 * HEAD_DIM
EPS = 1e-06
LOG2E = 1.4426950408889634
F32 = jnp.float32
BF16 = jnp.bfloat16
SWAP = [(0, 1), (1, 0)]
VMEM_LIMIT = 62 << 20


def contract(left, right, left_dim, right_dim):
    return lax.dot_general(
        left, right, (((left_dim,), (right_dim,)), ((), ())), preferred_element_type=F32
    )


def padded_rows(rows, tile):
    full = rows // tile
    return full * tile + -(-(rows - full * tile) // PAIR) * PAIR


def walk(rows, tile, start, finish):
    full = rows // tile
    rest = padded_rows(rows, tile) - full * tile
    start(0, pl.ds(0, tile), tile)

    def step(columns, size, following, following_size):
        start(1, columns, size)
        finish(0, columns, size)
        if following is not None:
            start(0, following, following_size)
        finish(1, columns, size)

    def block(index, carry):
        first = pl.multiple_of(index * tile, tile)
        following = pl.multiple_of(index * tile + tile, tile)
        step(pl.ds(first, tile), tile, pl.ds(following, tile), tile)
        return carry

    lax.fori_loop(0, full - 1, block, 0)
    last = pl.ds(full * tile, rest) if rest else None
    step(pl.ds((full - 1) * tile, tile), tile, last, rest)
    if rest:
        step(last, rest, None, 0)


def one_head(values_t, head, columns, size):
    empty = jnp.zeros((HEAD_DIM, size), BF16)
    values = values_t[head * HEAD_DIM : (head + 1) * HEAD_DIM, columns]
    return jnp.concatenate([values, empty] if head == 0 else [empty, values], axis=0)


def attend_kernel(tile, rows, padded, qkv_ref, out_ref, lse_ref, q_t, v_t, out_t, scores):
    scale = HEAD_DIM**-0.5 * LOG2E
    ones = jnp.ones((16, rows), BF16)
    q_t[:, :rows] = qkv_ref[:, :PAIR].T
    if padded > rows:
        q_t[:, rows:] = jnp.zeros((PAIR, padded - rows), BF16)
    values_t = qkv_ref[:, 2 * PAIR :].T
    step = HEAD_DIM + 16
    for head in range(2):
        v_t[head * step : head * step + HEAD_DIM, :] = values_t[
            head * HEAD_DIM : (head + 1) * HEAD_DIM, :
        ]
        v_t[head * step + HEAD_DIM : (head + 1) * step, :] = ones

    def start(head, columns, size):
        query = one_head(q_t, head, columns, size)
        scores[head, :, :size] = contract(qkv_ref[:, PAIR : 2 * PAIR], query, 1, 0)

    def finish(head, columns, size):
        values = scores[head, :, :size]
        highest = jnp.max(values, axis=0, keepdims=True) * scale
        expon = jnp.exp2(values * scale - highest).astype(BF16)
        mixed = contract(v_t[head * step : (head + 1) * step, :], expon, 1, 0)
        total = mixed[HEAD_DIM : HEAD_DIM + 1, :]
        out_t[head * HEAD_DIM : (head + 1) * HEAD_DIM, columns] = mixed[:HEAD_DIM, :] / total
        lse_ref[head : head + 1, columns] = highest + jnp.log2(total)

    walk(rows, tile, start, finish)
    out_ref[...] = out_t[...].T[:rows, :].astype(BF16)


def attend(qkv, first_pair, last_pair, kept=None, tile=512):
    rows, width = qkv.shape
    pairs = width // (3 * PAIR)
    padded = padded_rows(rows, tile)
    count = last_pair - first_pair
    kernel = functools.partial(attend_kernel, tile, rows, padded)
    anywhere = pl.BlockSpec(memory_space=pl.ANY)
    return pl.pallas_call(
        kernel if kept is None else lambda ref, a, b, *rest: kernel(ref, *rest),
        grid=(count,),
        in_specs=[pl.BlockSpec((rows, 3 * PAIR), lambda i: (0, i + first_pair))]
        + ([] if kept is None else [anywhere] * 2),
        out_specs=[
            pl.BlockSpec((rows, PAIR), lambda i: (0, i + first_pair)),
            pl.BlockSpec((None, 2, padded), lambda i: (i + first_pair, 0, 0)),
        ],
        out_shape=[
            jax.ShapeDtypeStruct((rows, pairs * PAIR), BF16),
            jax.ShapeDtypeStruct((pairs, 2, padded), F32),
        ],
        scratch_shapes=[
            pltpu.VMEM((PAIR, padded), BF16),
            pltpu.VMEM((PAIR + 32, rows), BF16),
            pltpu.VMEM((PAIR, padded), F32),
            pltpu.VMEM((2, rows, tile), F32),
        ],
        input_output_aliases={} if kept is None else {1: 0, 2: 1},
        compiler_params=pltpu.CompilerParams(vmem_limit_bytes=VMEM_LIMIT),
        cost_estimate=pl.CostEstimate(
            flops=64 * rows * rows * PAIR * count,
            bytes_accessed=8 * rows * PAIR * count,
            transcendentals=2 * rows * rows * count,
        ),
        name="attend",
    )(qkv, *(() if kept is None else kept))


def attend_back_kernel(
    tile, rows, padded, s_ref, qkv_ref, grad_ref, out_ref, lse_ref, first_ref, dqkv_ref, send_ref,
    keep_ref, sums_ref, q_t, g_t, k_t, delta, dq_t, dk_t, dv_t, all_t, scores, d_probs,
):
    scale = HEAD_DIM**-0.5
    q_t[:, :rows] = qkv_ref[:, :PAIR].T
    g_t[:, :rows] = grad_ref[...].T
    if padded > rows:
        q_t[:, rows:] = jnp.zeros((PAIR, padded - rows), BF16)
        g_t[:, rows:] = jnp.zeros((PAIR, padded - rows), BF16)
        delta[:, rows:] = jnp.zeros((2, padded - rows), F32)
    k_t[...] = qkv_ref[:, PAIR : 2 * PAIR].T
    product = (grad_ref[...].astype(F32) * out_ref[...].astype(F32)).T
    delta[0:1, :rows] = jnp.sum(product[:HEAD_DIM, :], axis=0, keepdims=True)
    delta[1:2, :rows] = jnp.sum(product[HEAD_DIM:, :], axis=0, keepdims=True)
    dk_t[...] = jnp.zeros_like(dk_t)
    dv_t[...] = jnp.zeros_like(dv_t)

    def start(head, columns, size):
        query, grad = one_head(q_t, head, columns, size), one_head(g_t, head, columns, size)
        scores[head, :, :size] = contract(qkv_ref[:, PAIR : 2 * PAIR], query, 1, 0)
        d_probs[head, :, :size] = contract(qkv_ref[:, 2 * PAIR :], grad, 1, 0)

    def finish(head, columns, size):
        lanes = slice(head * HEAD_DIM, (head + 1) * HEAD_DIM)
        log_total = lse_ref[head : head + 1, columns]
        weights = jnp.exp2(scores[head, :, :size] * (scale * LOG2E) - log_total)
        inner = delta[head : head + 1, columns]
        d_scores = (weights * (d_probs[head, :, :size] - inner)).astype(BF16)
        dv_t[lanes, :] += contract(g_t[lanes, columns], weights.astype(BF16), 1, 1)
        dq_t[lanes, columns] = contract(k_t[lanes, :], d_scores, 1, 0)
        dk_t[lanes, :] += contract(q_t[lanes, columns], d_scores, 1, 1)

    walk(rows, tile, start, finish)
    all_t[:PAIR, :] = (dq_t[:, :rows] * scale).astype(BF16)
    all_t[PAIR : 2 * PAIR, :] = (dk_t[...] * scale).astype(BF16)
    all_t[2 * PAIR :, :] = dv_t[...].astype(BF16)
    for part in range(3):
        lanes = slice(part * PAIR, (part + 1) * PAIR)
        dqkv_ref[:, lanes] = all_t[lanes, :].T
    sums_ref[...] = contract(jnp.ones((8, rows), BF16), all_t[...], 1, 1)
    own = first_ref.shape[1] // 2
    for h in range(2):
        grad = contract(all_t[...], first_ref[:, h * own : (h + 1) * own], 1, 0).astype(BF16)

        @pl.when(s_ref[0] == h)
        def _():
            keep_ref[...] = grad

        @pl.when(s_ref[0] != h)
        def _():
            send_ref[...] = grad


def attend_back(scal, qkv, grad, out, lse, first, tile=256):
    rows, full = qkv.shape
    width = first.shape[1]
    padded = padded_rows(rows, tile)
    count = 1
    return pl.pallas_call(
        functools.partial(attend_back_kernel, tile, rows, padded),
        grid_spec=pltpu.PrefetchScalarGridSpec(
            num_scalar_prefetch=1,
            grid=(count,),
            in_specs=[
                pl.BlockSpec((rows, 3 * PAIR), lambda i, s: (0, s[5])),
                pl.BlockSpec((rows, PAIR), lambda i, s: (0, s[5])),
                pl.BlockSpec((rows, PAIR), lambda i, s: (0, s[5])),
                pl.BlockSpec((None, 2, lse.shape[2]), lambda i, s: (s[5], 0, 0)),
                pl.BlockSpec((rows, width), lambda i, s: (0, 0), pipeline_mode=pl.Buffered(1)),
            ],
            out_specs=[
                pl.BlockSpec((rows, 3 * PAIR), lambda i, s: (0, i)),
                pl.BlockSpec((3 * PAIR, width // 2), lambda i, s: (i, 0)),
                pl.BlockSpec((3 * PAIR, width // 2), lambda i, s: (i, 0)),
                pl.BlockSpec((8, 3 * PAIR), lambda i, s: (0, i)),
            ],
            scratch_shapes=[
                pltpu.VMEM((PAIR, padded), BF16),
                pltpu.VMEM((PAIR, padded), BF16),
                pltpu.VMEM((PAIR, rows), BF16),
                pltpu.VMEM((2, padded), F32),
                pltpu.VMEM((PAIR, padded), F32),
                pltpu.VMEM((PAIR, rows), F32),
                pltpu.VMEM((PAIR, rows), F32),
                pltpu.VMEM((3 * PAIR, rows), BF16),
                pltpu.VMEM((2, rows, tile), F32),
                pltpu.VMEM((2, rows, tile), F32),
            ],
        ),
        out_shape=[
            jax.ShapeDtypeStruct((rows, 3 * PAIR * count), BF16),
            jax.ShapeDtypeStruct((3 * PAIR * count, width // 2), BF16),
            jax.ShapeDtypeStruct((3 * PAIR * count, width // 2), BF16),
            jax.ShapeDtypeStruct((8, 3 * PAIR * count), F32),
        ],
        compiler_params=pltpu.CompilerParams(vmem_limit_bytes=VMEM_LIMIT),
        cost_estimate=pl.CostEstimate(
            flops=160 * rows * rows * PAIR * count,
            bytes_accessed=16 * rows * PAIR * count,
            transcendentals=2 * rows * rows * count,
        ),
        name="attend_back",
    )(scal, qkv, grad, out, lse, first)


def feed_kernel(
    s_ref, x_own, x_other, dy_own, dy_other, up_ref, down_ref, x_piece, x_beside, z_piece, z_beside,
    bias_ref, out_own, out_other, dx_own, dx_other, up_send, up_keep, down_send, down_keep,
    low_send, low_keep, bias_grad_ref, x, dy, x_t, out_sum, dx_sum, up_full, down_full, hidden,
    d_pre, sems,
):
    index = pl.program_id(0)
    half = s_ref[0]
    rows, width = x.shape
    block = rows // 2
    own = width // 2
    tile = up_ref.shape[1]
    first_range = index < 2
    side = index % 2
    columns = pl.ds(pl.multiple_of(side * tile, tile), tile)
    mine = pl.ds(pl.multiple_of(half * own, own), own)
    theirs = pl.ds(pl.multiple_of((1 - half) * own, own), own)

    @pl.when(index == 0)
    def _():
        copies = []
        for i, ref in enumerate((x_own, x_other)):
            copies.append(pltpu.make_async_copy(ref, x.at[pl.ds(i * block, block)], sems.at[i]))
        for i, ref in enumerate((dy_own, dy_other)):
            copies.append(
                pltpu.make_async_copy(ref, dy.at[pl.ds(i * block, block)], sems.at[2 + i])
            )
        for copy in copies:
            copy.start()
        for copy in copies:
            copy.wait()
        x_t[...] = x[...].T
        out_sum[...] = jnp.zeros_like(out_sum)
        dx_sum[...] = jnp.zeros_like(dx_sum)

    up_full[mine, :] = up_ref[...]

    @pl.when(side == half)
    def _():
        down_full[...] = down_ref[...]

    for chosen, place, piece, beside in (
        (first_range, 1, x_piece, x_beside), (jnp.logical_not(first_range), 4, z_piece, z_beside)
    ):
        even = s_ref[place] == 0

        @pl.when(chosen & even)
        def _():
            up_full[theirs, :] = piece[:, columns]

        @pl.when(chosen & jnp.logical_not(even))
        def _():
            up_full[theirs, :] = beside[:, columns]

        @pl.when(chosen & (side != half) & even)
        def _():
            down_full[...] = beside[...]

        @pl.when(chosen & (side != half) & jnp.logical_not(even))
        def _():
            down_full[...] = piece[...]

    bias_grad = jnp.zeros(bias_grad_ref.shape, F32)
    for start in range(0, rows, block):
        part = slice(start, start + block)
        pre = contract(x[part, :], up_full[...], 1, 0) + bias_ref[...]
        d_hidden = contract(dy[part, :], down_full[...], 1, 1)
        share = 0.5 * (1.0 + lax.erf(pre * 0.7071067811865476))
        hidden[part, :] = (pre * share).astype(BF16)
        slope = share + pre * (jnp.exp(-0.5 * pre * pre) * 0.3989422804014327)
        d_low = (d_hidden * slope).astype(BF16)
        d_pre[part, :] = d_low
        bias_grad = bias_grad + jnp.sum(d_low.astype(F32), axis=0, keepdims=True)
        out_sum[part, :] += contract(hidden[part, :], down_full[...], 1, 0)
        dx_sum[part, :] += contract(d_pre[part, :], up_full[...], 1, 1)
    bias_grad_ref[...] = bias_grad
    down_grad = contract(hidden[...], dy[...], 0, 0).astype(BF16)
    side_rows = pl.ds(pl.multiple_of(side * tile, tile), tile)

    @pl.when(first_range)
    def _():
        up_keep[:, columns] = contract(x_t[mine, :], d_pre[...], 1, 0).astype(BF16)
        up_send[:, columns] = contract(x_t[theirs, :], d_pre[...], 1, 0).astype(BF16)

    @pl.when(first_range & (side == half))
    def _():
        down_keep[...] = down_grad

    @pl.when(first_range & (side != half))
    def _():
        down_send[...] = down_grad

    for even in (True, False):
        up_goal, down_goal = (low_keep, low_send) if even else (low_send, low_keep)

        @pl.when(jnp.logical_not(first_range) & ((s_ref[1] == 0) == even))
        def _():
            up_goal[:, columns] = contract(x_t[...], d_pre[...], 1, 0).astype(BF16)
            down_goal[side_rows, :] = down_grad

    @pl.when(index == pl.num_programs(0) - 1)
    def _():
        out_own[...] = out_sum[:block, :].astype(BF16)
        out_other[...] = out_sum[block:, :].astype(BF16)
        dx_own[...] = dx_sum[:block, :].astype(BF16)
        dx_other[...] = dx_sum[block:, :].astype(BF16)


def feed(scal, seconds, grads, up, down, pieces, bias):
    local, width = seconds[0].shape
    rows = 2 * local
    tile = down.shape[0] // 4
    anywhere = pl.BlockSpec(memory_space=pl.ANY)

    def fixed(*shape):
        return pl.BlockSpec(shape, lambda t, s: (0, 0), pipeline_mode=pl.Buffered(1))

    shapes = [(local, width)] * 4 + [(width // 2, 2 * tile)] * 2 + [(tile, width)] * 2
    shapes += [(width, 2 * tile)] * 2
    across = pl.BlockSpec((1, tile), lambda t, s: (0, t))
    return pl.pallas_call(
        feed_kernel,
        grid_spec=pltpu.PrefetchScalarGridSpec(
            num_scalar_prefetch=1,
            grid=(4,),
            in_specs=[anywhere] * 4
            + [
                pl.BlockSpec(
                    (width // 2, tile), lambda t, s: (0, ((t % 2) * 2 + s[2]) * 2 + t // 2)
                ),
                pl.BlockSpec((tile, width), lambda t, s: (s[2] * 2 + t // 2, 0)),
            ]
            + [fixed(width // 2, 2 * tile)] * 4
            + [across],
            out_specs=[fixed(*shape) for shape in shapes] + [across],
            scratch_shapes=[
                pltpu.VMEM((rows, width), BF16),
                pltpu.VMEM((rows, width), BF16),
                pltpu.VMEM((width, rows), BF16),
                pltpu.VMEM((rows, width), F32),
                pltpu.VMEM((rows, width), F32),
                pltpu.VMEM((width, tile), BF16),
                pltpu.VMEM((tile, width), BF16),
                pltpu.VMEM((rows, tile), BF16),
                pltpu.VMEM((rows, tile), BF16),
                pltpu.SemaphoreType.DMA((4,)),
            ],
        ),
        out_shape=[jax.ShapeDtypeStruct(shape, BF16) for shape in shapes]
        + [jax.ShapeDtypeStruct((1, 4 * tile), F32)],
        compiler_params=pltpu.CompilerParams(vmem_limit_bytes=VMEM_LIMIT),
        cost_estimate=pl.CostEstimate(
            flops=48 * rows * width * tile,
            bytes_accessed=16 * rows * width,
            transcendentals=8 * rows * tile,
        ),
        name="feed",
    )(scal, *seconds, *grads, up, down, *pieces, bias)


def run(kernel, name, scal, grid, in_specs, out_specs, out_shape, args, flops=0, scratch=()):
    moved = sum(a.size * a.dtype.itemsize for a in args)
    return pl.pallas_call(
        kernel,
        grid_spec=pltpu.PrefetchScalarGridSpec(
            num_scalar_prefetch=1,
            grid=grid,
            in_specs=in_specs,
            out_specs=out_specs,
            scratch_shapes=scratch,
        ),
        out_shape=out_shape,
        compiler_params=pltpu.CompilerParams(vmem_limit_bytes=VMEM_LIMIT),
        cost_estimate=pl.CostEstimate(flops=flops, bytes_accessed=2 * moved, transcendentals=0),
        name=name,
    )(scal, *args)


def spec(shape, index):
    return pl.BlockSpec(shape, index)


def held(*shape):
    return pl.BlockSpec(shape, lambda i, s: (0,) * len(shape), pipeline_mode=pl.Buffered(1))


def struct(*shape, dtype=BF16):
    return jax.ShapeDtypeStruct(shape, dtype)


def pack_qkv(scal, weights):
    rows, width = weights[0].shape
    pairs = width // (2 * PAIR)
    per = pairs // 2

    def kernel(s_ref, q_ref, k_ref, v_ref, own_ref, mine_ref):
        for i, ref in enumerate((q_ref, k_ref, v_ref)):
            own_ref[:, i * PAIR : (i + 1) * PAIR] = ref[...]
        start = pl.multiple_of(s_ref[1] * (rows // 2), rows // 2)
        mine_ref[...] = own_ref[pl.ds(start, rows // 2), :]

    block = spec((rows, PAIR), lambda p, s: (0, ((p // per) * 2 + s[2]) * per + p % per))
    return run(
        kernel, "pack_qkv", scal, (pairs,), [block] * 3,
        [
            spec((rows, 3 * PAIR), lambda p, s: (0, p)),
            spec((rows // 2, 3 * PAIR), lambda p, s: (0, p)),
        ],
        [struct(rows, 3 * PAIR * pairs), struct(rows // 2, 3 * PAIR * pairs)],
        weights,
    )


def pack_feed(scal, up, down, j, ranges, bit):
    rows, hidden = up.shape
    tile = hidden // (4 * ranges)
    columns = down.shape[1] // 2

    def kernel(s_ref, up_ref, down_ref, out_ref):
        out_ref[...] = jnp.where(s_ref[bit] == 0, up_ref[...], down_ref[...])

    return run(
        kernel, "pack_feed", scal, (2,),
        [
            spec((rows, tile), lambda t, s: (0, (t * 2 + s[2]) * ranges + j)),
            spec((tile, columns), lambda t, s: (s[2] * ranges + j, t)),
        ],
        spec((rows, tile), lambda t, s: (0, t)), struct(rows, 2 * tile), (up, down),
    )


def normalize(values):
    centred = values - jnp.mean(values, axis=-1, keepdims=True)
    spread = jnp.mean(centred * centred, axis=-1, keepdims=True)
    inverse = lax.rsqrt(spread + EPS)
    return centred * inverse, inverse


def first_norm(scal, tokens, received, gain, shift):
    rows, width = tokens.shape
    step = rows // 2

    def kernel(s_ref, t_ref, r_ref, gain_ref, shift_ref, x_ref, first_ref):
        x = jnp.where(s_ref[3] == 1, t_ref[...], r_ref[...])
        x_ref[...] = x
        normed, _ = normalize(x.astype(F32))
        first_ref[...] = (normed * gain_ref[...] + shift_ref[...]).astype(BF16)

    block = spec((step, width), lambda i, s: (i, 0))
    return run(
        kernel, "first_norm", scal, (2,), [block, block, held(1, width), held(1, width)],
        [block, block], [struct(rows, width)] * 2, (tokens, received, gain, shift),
    )


def project(scal, firsts, own, piece, beside, bias):
    local, width = firsts[0].shape
    rows, total = 2 * local, own.shape[1]
    block = 6 * PAIR
    half_rows, quarter_rows = width // 2, width // 4

    def kernel(
        s_ref, mine_ref, theirs_ref, own_ref, piece_ref, beside_ref, bias_ref, qkv_ref, w_ref,
        all_ref, sems,
    ):
        @pl.when(pl.program_id(0) == 0)
        def _():
            copies = [
                pltpu.make_async_copy(ref, all_ref.at[pl.ds(i * local, local)], sems.at[i])
                for i, ref in enumerate((mine_ref, theirs_ref))
            ]
            for copy in copies:
                copy.start()
            for copy in copies:
                copy.wait()

        half, low = s_ref[0], s_ref[1]
        other = (1 - half) * half_rows
        w_ref[pl.ds(pl.multiple_of(half * half_rows, half_rows), half_rows), :] = own_ref[...]
        start = pl.multiple_of(other + low * quarter_rows, quarter_rows)
        w_ref[pl.ds(start, quarter_rows), :] = piece_ref[...]
        start = pl.multiple_of(other + (1 - low) * quarter_rows, quarter_rows)
        w_ref[pl.ds(start, quarter_rows), :] = beside_ref[...]
        qkv_ref[...] = (contract(all_ref[...], w_ref[...], 1, 0) + bias_ref[...]).astype(BF16)

    def columns(size):
        return spec((size, block), lambda p, s: (0, p))

    anywhere = pl.BlockSpec(memory_space=pl.ANY)
    return run(
        kernel, "project", scal, (total // block,),
        [anywhere] * 2
        + [columns(half_rows), columns(quarter_rows), columns(quarter_rows), columns(1)],
        [columns(rows), columns(width), held(rows, width)],
        [struct(rows, total), struct(width, total), struct(rows, width)],
        (*firsts, own, piece, beside, bias), flops=2 * rows * width * total,
        scratch=[pltpu.SemaphoreType.DMA((2,))],
    )


def out_other(scal, mixed, weight, piece, beside):
    rows, set_width = mixed.shape
    local, width = rows // 2, weight.shape[1]
    block, small = set_width // 2, set_width // 4

    def kernel(s_ref, mixed_ref, own_ref, piece_ref, beside_ref, out_ref, set_ref):
        half, low = s_ref[0], s_ref[1]
        other = (1 - half) * block
        set_ref[pl.ds(pl.multiple_of(half * block, block), block), :] = own_ref[...]
        set_ref[pl.ds(pl.multiple_of(other + low * small, small), small), :] = piece_ref[...]
        start = pl.multiple_of(other + (1 - low) * small, small)
        set_ref[pl.ds(start, small), :] = beside_ref[...]
        out_ref[...] = contract(mixed_ref[...], set_ref[...], 1, 0).astype(BF16)

    return run(
        kernel, "out_other", scal, (1,),
        [
            spec((local, set_width), lambda i, s: (1, 0)),
            spec((block, width), lambda i, s: (s[2], 0)),
            held(small, width), held(small, width),
        ],
        [held(local, width), held(set_width, width)],
        [struct(local, width), struct(set_width, width)],
        (mixed, weight, piece, beside), flops=2 * local * set_width * width,
    )


def second_norm(scal, mixed, out_set, x, received, bias, gain, shift):
    rows, set_width = mixed.shape
    local, width = x.shape
    step = local // 2

    def kernel(
        s_ref, mixed_ref, w_ref, x_ref, r_ref, bias_ref, gain_ref, shift_ref, mid_ref, second_ref
    ):
        middle = contract(mixed_ref[...], w_ref[...], 1, 0) + r_ref[...].astype(F32)
        middle = middle + x_ref[...].astype(F32) + bias_ref[...]
        mid_ref[...] = middle
        normed, _ = normalize(middle)
        second_ref[...] = (normed * gain_ref[...] + shift_ref[...]).astype(BF16)

    block = spec((step, width), lambda i, s: (i, 0))
    return run(
        kernel, "second_norm", scal, (2,),
        [spec((step, set_width), lambda i, s: (i, 0)), held(set_width, width), block, block]
        + [held(1, width)] * 3,
        [block, block], [struct(local, width, dtype=F32), struct(local, width)],
        (mixed, out_set, x, received, bias, gain, shift), flops=2 * local * set_width * width,
    )


def norm_back_rows(grad, normed, inverse, gain):
    scaled = grad * gain
    first_term = jnp.mean(scaled, axis=-1, keepdims=True)
    second_term = jnp.mean(scaled * normed, axis=-1, keepdims=True)
    return inverse * (scaled - first_term - normed * second_term)


def column_sums(refs, values):
    @pl.when(pl.program_id(0) == 0)
    def _():
        refs[...] = jnp.zeros_like(refs)

    for i, value in enumerate(values):
        refs[i : i + 1, :] += jnp.sum(value, axis=0, keepdims=True)


def row_step(rows):
    return rows // 7 if rows % 112 == 0 else rows


def second_back(scal, grad, received, middle, dy, gain):
    local, width = middle.shape
    step = row_step(local)

    def kernel(s_ref, g_ref, r_ref, mid_ref, dy_ref, gain_ref, low_ref, sums_ref):
        grad = g_ref[...].astype(F32) + r_ref[...].astype(F32)
        normed, inverse = normalize(mid_ref[...])
        dy_wide = dy_ref[...].astype(F32)
        low = (dy_wide + norm_back_rows(grad, normed, inverse, gain_ref[...])).astype(BF16)
        low_ref[...] = low
        column_sums(sums_ref, (grad * normed, grad, dy_wide, low.astype(F32)))

    block = spec((step, width), lambda i, s: (i, 0))
    return run(
        kernel, "second_back", scal, (local // step,), [block] * 4 + [held(1, width)],
        [block, held(8, width)], [struct(local, width), struct(8, width, dtype=F32)],
        (grad, received, middle, dy, gain),
    )


def mixed_back(scal, lows, out_set, mixed):
    local, width = lows[0].shape
    rows, set_width = mixed.shape
    block = set_width // 2

    def kernel(
        s_ref, mine_ref, theirs_ref, w_ref, mixed_ref, d_ref, send_ref, keep_ref, low, sems
    ):
        @pl.when(pl.program_id(0) == 0)
        def _():
            copies = [
                pltpu.make_async_copy(ref, low.at[pl.ds(i * local, local)], sems.at[i])
                for i, ref in enumerate((mine_ref, theirs_ref))
            ]
            for copy in copies:
                copy.start()
            for copy in copies:
                copy.wait()

        d_ref[...] = contract(low[...], w_ref[...], 1, 1).astype(BF16)
        grad = contract(mixed_ref[...], low[...], 0, 0).astype(BF16)

        def store(goal):
            for c in range(2):
                for i in range(width // (2 * PAIR)):
                    start = (2 * i + c) * PAIR
                    goal[c * block : (c + 1) * block, i * PAIR : (i + 1) * PAIR] = (
                        grad[:, start : start + PAIR]
                    )

        @pl.when(pl.program_id(0) == s_ref[0])
        def _():
            store(keep_ref)

        @pl.when(pl.program_id(0) != s_ref[0])
        def _():
            store(send_ref)

    anywhere = pl.BlockSpec(memory_space=pl.ANY)
    across = spec((rows, block), lambda t, s: (0, t))
    return run(
        kernel, "mixed_back", scal, (2,),
        [anywhere] * 2 + [spec((block, width), lambda t, s: (t, 0)), across],
        [across, held(2 * block, width // 2), held(2 * block, width // 2)],
        [struct(rows, set_width)] + [struct(2 * block, width // 2)] * 2,
        (*lows, out_set, mixed), flops=4 * rows * set_width * width,
        scratch=[pltpu.VMEM((rows, width), BF16), pltpu.SemaphoreType.DMA((2,))],
    )


def first_grad(scal, dqkvs, weights):
    rows = dqkvs[0].shape[0]
    width = weights.shape[0]
    local = rows // 2
    count = len(dqkvs)
    step = width // 4

    def kernel(s_ref, *refs):
        left = jnp.concatenate([refs[j][...] for j in range(count)], axis=1)
        total = contract(left, refs[count][...], 1, 1)
        refs[-2][...] = total[:local].astype(BF16)
        refs[-1][...] = total[local:].astype(BF16)

    across = spec((local, step), lambda i, s: (0, i))
    return run(
        kernel, "first_grad", scal, (4,),
        [held(*a.shape) for a in dqkvs] + [spec((step, weights.shape[1]), lambda i, s: (i, 0))],
        [across, across], [struct(local, width)] * 2, (*dqkvs, weights),
        flops=sum(2 * rows * a.shape[1] * width for a in dqkvs),
    )


def first_back(scal, grad, received, x, wide, gain):
    local, width = x.shape
    step = row_step(local)

    def kernel(s_ref, g_ref, r_ref, x_ref, wide_ref, gain_ref, out_ref, sums_ref):
        grad = g_ref[...].astype(F32) + r_ref[...].astype(F32)
        normed, inverse = normalize(x_ref[...].astype(F32))
        total = wide_ref[...].astype(F32) + norm_back_rows(grad, normed, inverse, gain_ref[...])
        out_ref[...] = total.astype(BF16)
        column_sums(sums_ref, (grad * normed, grad))

    block = spec((step, width), lambda i, s: (i, 0))
    return run(
        kernel, "first_back", scal, (local // step,), [block] * 4 + [held(1, width)],
        [block, held(8, width)], [struct(local, width), struct(8, width, dtype=F32)],
        (grad, received, x, wide, gain),
    )


def layer_rows(scal, own, received, middle, bias):
    local, width = middle.shape
    step = row_step(local)

    def kernel(s_ref, o_ref, r_ref, mid_ref, bias_ref, out_ref):
        total = mid_ref[...] + o_ref[...].astype(F32) + r_ref[...].astype(F32) + bias_ref[...]
        out_ref[...] = total.astype(BF16)

    block = spec((step, width), lambda i, s: (i, 0))
    return run(
        kernel, "layer_rows", scal, (local // step,), [block] * 3 + [held(1, width)],
        block, struct(local, width), (own, received, middle, bias),
    )


def finish_feed_kernel(s_ref, *refs, tile):
    up_out, down_out = refs[8:]
    first = s_ref[2] == 0
    even = s_ref[1] == 0
    low_range = s_ref[4] == 0
    cores = []
    for refs_of in (refs[:4], refs[4:8]):
        whole, beside, along, last = [ref[...] for ref in refs_of]
        ranges = []
        for j in range(2):
            mine = jnp.where(low_range == (j == 0), whole, along)
            theirs = jnp.where(low_range == (j == 0), beside, last)
            ranges.append((jnp.where(even, mine, theirs), jnp.where(even, theirs, mine)))
        cores.append(ranges)
    for c in range(2):
        for j in range(2):
            up, down = [
                jnp.where(first == (c == 0), cores[0][j][kind], cores[1][j][kind]).astype(F32)
                for kind in range(2)
            ]
            down_out[c, j] = down
            for h in range(2):
                start = ((h * 2 + c) * 2 + j) * tile
                up_out[:, start : start + tile] = up[:, h * tile : (h + 1) * tile]


def finish_feed(scal, sums):
    rows, width = sums[0].shape
    steps = 4
    block = spec((rows // steps, width), lambda i, s: (i, 0))
    up, down = run(
        functools.partial(finish_feed_kernel, tile=rows), "finish_feed", scal, (steps,),
        [block] * 8,
        [
            spec((rows // steps, 4 * width), lambda i, s: (i, 0)),
            spec((2, 2, rows // steps, width), lambda i, s: (0, 0, i, 0)),
        ],
        [struct(rows, 4 * width, dtype=F32), struct(2, 2, rows, width, dtype=F32)],
        sums,
    )
    return up, down.reshape(4 * rows, width)


def finish_attention_kernel(s_ref, *refs, pairs, spans):
    q_out, k_out, v_out, out_out = refs[-4:]
    first, even = s_ref[2] == 0, s_ref[1] == 0
    half_pairs = pairs // 2
    for g, (begin, end) in enumerate(spans):
        mine, beside, mine_across, beside_across = [ref[...] for ref in refs[4 * g : 4 * g + 4]]
        own = jnp.concatenate(
            [jnp.where(even, mine, beside), jnp.where(even, beside, mine)], axis=0
        )
        other = jnp.concatenate(
            [
                jnp.where(even, mine_across, beside_across),
                jnp.where(even, beside_across, mine_across),
            ],
            axis=0,
        )
        for c in range(2):
            total = jnp.where(first == (c == 0), own, other).astype(F32)
            wide = total[: (end - begin) * 3 * PAIR].T
            for q in range(end - begin):
                pair = begin + q
                h, p = pair // half_pairs, pair % half_pairs
                goal = ((h * 2 + c) * half_pairs + p) * PAIR
                for i, out in enumerate((q_out, k_out, v_out)):
                    start = (q * 3 + i) * PAIR
                    out[:, goal : goal + PAIR] = wide[:, start : start + PAIR]
            if g == 0:
                rest = total[(end - begin) * 3 * PAIR :]
                rows = rest.shape[0] // 2
                out_out[c * rows : (c + 1) * rows, :PAIR] = rest[:rows]
                out_out[c * rows : (c + 1) * rows, PAIR:] = rest[rows:]


def finish_attention(scal, sums, spans):
    rows = sums[0].shape[1]
    pairs = spans[-1][1]
    steps = rows // PAIR
    return run(
        functools.partial(finish_attention_kernel, pairs=pairs, spans=spans), "finish_attention",
        scal, (steps,),
        [spec((values.shape[0], PAIR), lambda i, s: (0, i)) for values in sums],
        [spec((PAIR, 2 * pairs * PAIR), lambda i, s: (i, 0))] * 3
        + [spec((rows, 2 * PAIR), lambda i, s: (0, i))],
        [struct(rows, 2 * pairs * PAIR, dtype=F32)] * 3 + [struct(rows, 2 * rows, dtype=F32)],
        sums,
    )


def wide_back_kernel(
    tile, rows, padded, qkv_ref, grad_ref, out_ref, lse_ref, dqkv_ref, q_t, g_t, k_t, delta,
    dq_t, dk_t, dv_t,
):
    scale = HEAD_DIM**-0.5
    q_t[:, :rows] = qkv_ref[:, :PAIR].T
    g_t[:, :rows] = grad_ref[...].T
    if padded > rows:
        q_t[:, rows:] = jnp.zeros((PAIR, padded - rows), BF16)
        g_t[:, rows:] = jnp.zeros((PAIR, padded - rows), BF16)
        delta[:, rows:] = jnp.zeros((2, padded - rows), F32)
    k_t[...] = qkv_ref[:, PAIR : 2 * PAIR].T
    product = (grad_ref[...].astype(F32) * out_ref[...].astype(F32)).T
    delta[0:1, :rows] = jnp.sum(product[:HEAD_DIM, :], axis=0, keepdims=True)
    delta[1:2, :rows] = jnp.sum(product[HEAD_DIM:, :], axis=0, keepdims=True)
    dk_t[...] = jnp.zeros_like(dk_t)
    dv_t[...] = jnp.zeros_like(dv_t)

    def block(index, carry):
        columns = pl.ds(pl.multiple_of(index * tile, tile), tile)
        empty = jnp.zeros((HEAD_DIM, tile), BF16)
        for head in range(2):
            lanes = slice(head * HEAD_DIM, (head + 1) * HEAD_DIM)
            query = q_t[lanes, columns]
            grad = g_t[lanes, columns]
            query_pad = jnp.concatenate([query, empty] if head == 0 else [empty, query], axis=0)
            grad_pad = jnp.concatenate([grad, empty] if head == 0 else [empty, grad], axis=0)
            scores = contract(qkv_ref[:, PAIR : 2 * PAIR], query_pad, 1, 0)
            grad_probs = contract(qkv_ref[:, 2 * PAIR :], grad_pad, 1, 0)
            weights = jnp.exp2(scores * (scale * LOG2E) - lse_ref[head : head + 1, columns])
            grad_scores = (weights * (grad_probs - delta[head : head + 1, columns])).astype(BF16)
            dv_t[lanes, :] += contract(grad, weights.astype(BF16), 1, 1)
            dq_t[lanes, columns] = contract(k_t[lanes, :], grad_scores, 1, 0)
            dk_t[lanes, :] += contract(query, grad_scores, 1, 1)
        return carry

    lax.fori_loop(0, padded // tile, block, 0)
    dqkv_ref[:, :PAIR] = (dq_t[...].T[:rows, :] * scale).astype(BF16)
    dqkv_ref[:, PAIR : 2 * PAIR] = (dk_t[...].T * scale).astype(BF16)
    dqkv_ref[:, 2 * PAIR :] = dv_t[...].T.astype(BF16)


def wide_back(qkv, grad, out, lse, first_pair, last_pair, tile=256):
    rows, width = qkv.shape
    padded = -(-rows // tile) * tile
    lse = jnp.pad(lse, ((0, 0), (0, 0), (0, padded - lse.shape[2])))
    count = last_pair - first_pair
    return pl.pallas_call(
        functools.partial(wide_back_kernel, tile, rows, padded),
        grid=(count,),
        in_specs=[
            pl.BlockSpec((rows, 3 * PAIR), lambda i: (0, i + first_pair)),
            pl.BlockSpec((rows, PAIR), lambda i: (0, i + first_pair)),
            pl.BlockSpec((rows, PAIR), lambda i: (0, i + first_pair)),
            pl.BlockSpec((None, 2, lse.shape[2]), lambda i: (i + first_pair, 0, 0)),
        ],
        out_specs=pl.BlockSpec((rows, 3 * PAIR), lambda i: (0, i)),
        out_shape=jax.ShapeDtypeStruct((rows, 3 * PAIR * count), BF16),
        scratch_shapes=[
            pltpu.VMEM((PAIR, padded), BF16),
            pltpu.VMEM((PAIR, padded), BF16),
            pltpu.VMEM((PAIR, rows), BF16),
            pltpu.VMEM((2, padded), F32),
            pltpu.VMEM((PAIR, padded), F32),
            pltpu.VMEM((PAIR, rows), F32),
            pltpu.VMEM((PAIR, rows), F32),
        ],
        compiler_params=pltpu.CompilerParams(vmem_limit_bytes=VMEM_LIMIT),
        cost_estimate=pl.CostEstimate(
            flops=160 * rows * rows * PAIR * count,
            bytes_accessed=16 * rows * PAIR * count,
            transcendentals=2 * rows * rows * count,
        ),
        name="wide_back",
    )(qkv, grad, out, lse)


def wide_feed_kernel(
    half_ref, *refs, parts, make, chunk,
):
    xs, refs = refs[:parts], refs[parts:]
    dys, refs = refs[:parts], refs[parts:]
    if not make:
        x_t, refs = refs[0], refs[1:]
    up_ref, bias_ref, down_ref, *refs = refs
    hidden_ref, d_pre_ref, up_send, up_keep, down_send, down_keep, bias_grad_ref, *refs = refs
    if make:
        x_t, refs = refs[0], refs[1:]
    x, dy, sems = refs
    index = pl.program_id(0)
    half = half_ref[0]
    rows, width = x.shape
    block = rows // parts
    own = width // 2
    tile = up_ref.shape[1]

    @pl.when(index == 0)
    def _():
        copies = []
        for i in range(parts):
            part = pl.ds(i * block, block)
            copies.append(pltpu.make_async_copy(xs[i], x.at[part], sems.at[i]))
            copies.append(pltpu.make_async_copy(dys[i], dy.at[part], sems.at[parts + i]))
        for copy in copies:
            copy.start()
        for copy in copies:
            copy.wait()
        if make:
            x_t[...] = x[...].T

    bias_grad = jnp.zeros(bias_grad_ref.shape, F32)
    for start in range(0, rows, chunk):
        part = slice(start, start + chunk)
        pre = contract(x[part, :], up_ref[...], 1, 0) + bias_ref[...]
        d_hidden = contract(dy[part, :], down_ref[...], 1, 1)
        share = 0.5 * (1.0 + lax.erf(pre * 0.7071067811865476))
        hidden_ref[part, :] = (pre * share).astype(BF16)
        slope = share + pre * (jnp.exp(-0.5 * pre * pre) * 0.3989422804014327)
        d_low = (d_hidden * slope).astype(BF16)
        d_pre_ref[part, :] = d_low
        bias_grad = bias_grad + jnp.sum(d_low.astype(F32), axis=0, keepdims=True)
    bias_grad_ref[...] = bias_grad
    columns = pl.ds(pl.multiple_of(index * tile, tile), tile)
    mine = pl.ds(pl.multiple_of(half * own, own), own)
    theirs = pl.ds(pl.multiple_of((1 - half) * own, own), own)
    up_keep[:, columns] = contract(x_t[mine, :], d_pre_ref[...], 1, 0).astype(BF16)
    up_send[:, columns] = contract(x_t[theirs, :], d_pre_ref[...], 1, 0).astype(BF16)
    down_grad = contract(hidden_ref[...], dy[...], 0, 0).astype(BF16)

    @pl.when(index == half)
    def _():
        down_keep[...] = down_grad

    @pl.when(index != half)
    def _():
        down_send[...] = down_grad


def wide_feed(half, xs, dys, x_t, up, bias, down):
    parts = len(xs)
    width = xs[0].shape[1]
    rows = sum(part.shape[0] for part in xs)
    hidden = up.shape[1]
    tile = hidden // 2
    make = x_t is None
    chunk = rows // 2 if rows % 32 == 0 else rows
    anywhere = pl.BlockSpec(memory_space=pl.ANY)
    fixed = lambda shape: pl.BlockSpec(shape, lambda j, s: (0, 0), pipeline_mode=pl.Buffered(1))
    across = lambda size: pl.BlockSpec((size, tile), lambda j, s: (0, j))
    out_specs = [across(rows)] * 2 + [fixed((width // 2, hidden))] * 2
    out_specs += [fixed((tile, width))] * 2 + [across(1)]
    out_shape = [
        jax.ShapeDtypeStruct((rows, hidden), BF16),
        jax.ShapeDtypeStruct((rows, hidden), BF16),
        jax.ShapeDtypeStruct((width // 2, hidden), BF16),
        jax.ShapeDtypeStruct((width // 2, hidden), BF16),
        jax.ShapeDtypeStruct((tile, width), BF16),
        jax.ShapeDtypeStruct((tile, width), BF16),
        jax.ShapeDtypeStruct((1, hidden), F32),
    ]
    if make:
        out_specs.append(fixed((width, rows)))
        out_shape.append(jax.ShapeDtypeStruct((width, rows), BF16))
    return pl.pallas_call(
        functools.partial(wide_feed_kernel, parts=parts, make=make, chunk=chunk),
        grid_spec=pltpu.PrefetchScalarGridSpec(
            num_scalar_prefetch=1,
            grid=(2,),
            in_specs=[anywhere] * (2 * parts)
            + ([] if make else [fixed((width, rows))])
            + [across(width), across(1), pl.BlockSpec((tile, width), lambda j, s: (j, 0))],
            out_specs=out_specs,
            scratch_shapes=[
                pltpu.VMEM((rows, width), BF16),
                pltpu.VMEM((rows, width), BF16),
                pltpu.SemaphoreType.DMA((2 * parts,)),
            ],
        ),
        out_shape=out_shape,
        compiler_params=pltpu.CompilerParams(vmem_limit_bytes=VMEM_LIMIT),
        cost_estimate=pl.CostEstimate(
            flops=8 * rows * width * hidden,
            bytes_accessed=8 * rows * width + 8 * width * hidden,
            transcendentals=2 * rows * hidden,
        ),
        name="wide_feed",
    )(half.reshape(1), *xs, *dys, *(() if make else (x_t,)), up, bias, down)


def norm_parts(values, gain, shift):
    average = jnp.mean(values, axis=-1, keepdims=True)
    centred = values - average
    spread = jnp.mean(centred * centred, axis=-1, keepdims=True)
    inverse = lax.rsqrt(spread + EPS)
    normed = centred * inverse
    return (normed * gain + shift, normed, inverse)


def norm_back(grad, normed, inverse, gain):
    scaled = grad * gain
    first_term = jnp.mean(scaled, axis=-1, keepdims=True)
    second_term = jnp.mean(scaled * normed, axis=-1, keepdims=True)
    result = inverse * (scaled - first_term - normed * second_term)
    return (result, jnp.sum(grad * normed, axis=0), jnp.sum(grad, axis=0))


def pick(values, index, axis):
    return lax.dynamic_index_in_dim(values, index, axis, keepdims=False)


def join(own, other, index):
    return jnp.where(index == 0, jnp.stack([own, other]), jnp.stack([other, own]))


def after(values, *earlier):
    return lax.optimization_barrier((values,) + earlier)[0]


def wide_body(
    rep, grp, tokens, query_weight, key_weight, value_weight, query_bias, value_bias, out_weight,
    out_bias, first_gain, first_shift, second_gain, second_shift, up_weight, up_bias,
    down_weight, down_bias, cotangent,
):
    clips, local, width = tokens.shape
    assert clips == 1
    quarter = grp // 2
    ring = rep // 2
    deep = ring // 2
    core = lax.axis_index("core")
    half = lax.axis_index("half")
    gq = lax.axis_index("gq")
    place = lax.axis_index("rz")
    low = place % 2
    high = place // 2
    own_rows = width // grp
    pairs = own_rows // PAIR
    hidden = up_weight.shape[1]
    set_hidden = hidden // grp
    ranges = max(1, set_hidden // width)
    tile = set_hidden // (2 * ranges)

    there = []
    for b in range(2):
        for h in range(2):
            for q in range(quarter):
                g = h * quarter + q
                source = (b * 2 + h) * quarter + q
                target = ((g % 2) * 2 + b) * quarter + g // 2
                if source != target:
                    there.append((source, target))
    back = [(target, source) for source, target in there]
    block = half * quarter + gq
    stays = (block % 2 == core) & (block // 2 == gq) & (half == core)
    axes = ("core", "half", "gq")
    beside = [(i, i ^ 1) for i in range(ring)]

    def move(values, route):
        return jnp.where(stays, values, lax.ppermute(values, axes, route))

    def swap_half(values):
        return lax.ppermute(values, "half", SWAP)

    def swap_core(values):
        return lax.ppermute(values, "core", SWAP)

    def spread(values):
        if grp == 2:
            return [values, swap_core(values)]
        return [lax.all_gather(values, ("gq", "core"), axis=0, tiled=True)]

    def collect(values):
        if grp == 2:
            other = swap_core(values(slice(local, None)).astype(BF16))
            return values(slice(None, local)) + other.astype(F32)
        return lax.psum_scatter(
            values(slice(None)).astype(BF16), ("gq", "core"), scatter_dimension=0, tiled=True
        ).astype(F32)

    def other_half(pieces):
        mine = pick(jnp.stack(pieces), low, 0)
        first = swap_half(mine)
        second = lax.ppermute(first, "rz", beside)
        return first, jnp.where(low == 0, first, second), jnp.where(low == 0, second, first)

    def by_half(own, other):
        return join(own, other, half).reshape(-1, own.shape[-1])

    def set_columns(values, inner=1):
        parts = values.reshape(values.shape[0], 2, quarter, 2, inner, -1)
        return pick(parts, core, 3).transpose(0, 2, 3, 1, 4)

    def gather_rows(values):
        if quarter > 1:
            values = lax.all_to_all(values, "gq", split_axis=1, concat_axis=0, tiled=True)
        return values.reshape(-1, values.shape[-1])

    def set_entries(values, inner=1):
        parts = values.reshape(2, quarter, 2, inner, -1)
        return pick(pick(parts, core, 2), gq, 1).transpose(1, 0, 2).reshape(inner, 1, -1)

    clip_tokens = move(tokens.reshape(local, width), there)
    vectors = jnp.concatenate(
        [query_bias, value_bias, out_bias, first_gain, first_shift, second_gain, second_shift,
         down_bias, up_bias]
    )
    if quarter > 1:
        vectors = lax.all_gather(vectors, "gq", axis=0)
    vectors = join(vectors, swap_half(vectors), half).reshape(grp, -1)
    (full_qbias, full_vbias, full_obias, gain_one, shift_one, gain_two, shift_two, full_dbias) = [
        vectors[:, i * own_rows : (i + 1) * own_rows].reshape(-1) for i in range(8)
    ]
    bias_sets = set_entries(vectors[:, 8 * own_rows :].reshape(-1), ranges)

    parts = [
        set_columns(w).reshape(own_rows, quarter, pairs, PAIR)
        for w in (query_weight, key_weight, value_weight)
    ]
    own_qkv = gather_rows(jnp.stack(parts, axis=3).reshape(own_rows, quarter, 3 * own_rows))
    own_qkv = own_qkv.reshape(2, -1, 3 * own_rows)
    qkv_x, low_rows, high_rows = other_half([own_qkv[0], own_qkv[1]])
    qkv_weight = by_half(
        own_qkv.reshape(-1, 3 * own_rows), jnp.concatenate([low_rows, high_rows], axis=0)
    )
    own_out = pick(out_weight.reshape(2, -1, width), core, 0)
    out_x, low_rows, high_rows = other_half(
        [after(own_out, qkv_x)[: own_rows // 4], own_out[own_rows // 4 :]]
    )
    out_set = by_half(own_out, jnp.concatenate([low_rows, high_rows], axis=0))

    own_up = set_columns(up_weight, ranges)
    own_down = pick(down_weight.reshape(2, ranges, tile, width), core, 0)
    up_sets, down_sets, stages = [], [], [out_x]
    for j in range(ranges):
        up_part = gather_rows(own_up[:, :, j].reshape(own_rows, quarter, 2 * tile))
        down_part = own_down[j]
        if up_part.shape == down_part.shape:
            stage, other_up, other_down = other_half([after(up_part, stages[-1]), down_part])
        else:
            stage, other_up = swap_half(after(up_part, stages[-1])), None
            other_up, other_down = stage, swap_half(down_part)
        stages.append(stage)
        up_sets.append(by_half(up_part, other_up))
        down_sets.append(by_half(down_part, other_down))
    grad_out = move(after(cotangent.reshape(local, width), stages[1]), there)

    zeros = jnp.zeros((1, own_rows), F32)
    qkv_bias = jnp.stack(
        [
            b.reshape(pairs, PAIR)
            for b in (set_entries(full_qbias), zeros, set_entries(full_vbias))
        ],
        axis=1,
    ).reshape(1, 3 * own_rows)

    inputs = clip_tokens.astype(F32)
    first_norm, first_normed, first_inverse = norm_parts(inputs, gain_one, shift_one)
    first = jnp.concatenate(spread(first_norm.astype(BF16)), axis=0)
    qkv = (contract(first, qkv_weight, 1, 0) + qkv_bias).astype(BF16)
    if pairs > 1:
        kept = attend(qkv, 0, pairs // 2)
        mixed, lse = attend(qkv, pairs // 2, pairs, kept)
    else:
        mixed, lse = attend(qkv, 0, pairs)
    middle = collect(lambda rows: contract(mixed[rows], out_set, 1, 0)) + inputs + full_obias
    second_norm, second_normed, second_inverse = norm_parts(middle, gain_two, shift_two)
    seconds = spread(second_norm.astype(BF16))
    grads_out = spread(grad_out)
    x_t = None
    feeds = []
    for j in range(ranges):
        outs = wide_feed(
            half, seconds, grads_out, x_t, up_sets[j],
            bias_sets[j] if j == 0 else after(bias_sets[j], feeds[-1][6]), down_sets[j],
        )
        x_t = outs[7] if j == 0 else x_t
        feeds.append(outs)

    def reduce_ring(pair):
        send, keep = pair
        total = keep.astype(F32) + lax.ppermute(send, "rz", beside).astype(F32)
        total = total.astype(BF16).reshape(deep, -1, keep.shape[-1])
        shifts = range(1, deep)

        def route(shift):
            return [(i, (i + 2 * shift) % ring) for i in range(ring)]

        pieces = [
            lax.ppermute(pick(total, (high + s) % deep, 0), "rz", route(s)) for s in shifts
        ]
        piece = pick(total, high, 0).astype(F32)
        for other in pieces:
            piece = piece + other.astype(F32)
        piece = piece.astype(BF16)
        gathered = [piece] + [lax.ppermute(piece, "rz", route(s)) for s in shifts]
        whole = jnp.stack(
            [
                functools.reduce(
                    lambda rest, s: jnp.where((high - s) % deep == i, gathered[s], rest),
                    shifts,
                    piece,
                )
                for i in range(deep)
            ]
        ).reshape(keep.shape)
        return whole, lax.ppermute(whole, "rz", beside)

    def reduce_parts(parts):
        stacked = jnp.stack(parts)
        own, other = reduce_ring((pick(stacked, 1 - low, 0), pick(stacked, low, 0)))
        return jnp.where(low == 0, own, other), jnp.where(low == 0, other, own)

    def add_half(keep, send):
        return (keep.astype(F32) + swap_half(send).astype(F32)).astype(BF16)

    def reduce_rows(values):
        size = values.shape[0]
        if size % (16 * ring):
            return lax.psum(values, "rz")
        return jnp.concatenate(reduce_parts([values[: size // 2], values[size // 2 :]]), axis=0)

    def scatter_half(values):
        values = values.reshape(2, -1, values.shape[-1])
        return add_half(pick(values, half, 0), pick(values, 1 - half, 0))

    sums_feed = []
    for outs in feeds:
        up_part, down_part = add_half(outs[3], outs[2]), add_half(outs[5], outs[4])
        if up_part.shape == down_part.shape:
            sums_feed.extend(reduce_parts([up_part, down_part]))
        else:
            sums_feed.extend([reduce_rows(up_part), reduce_rows(down_part)])

    grad_wide = grad_out.astype(F32)
    grad_second = collect(
        lambda rows: functools.reduce(
            jnp.add, [contract(feeds[j][1][rows], up_sets[j], 1, 1) for j in range(ranges)]
        )
    )
    grad_second, grad_gain_two, grad_shift_two = norm_back(
        grad_second, second_normed, second_inverse, gain_two
    )
    grad_middle = grad_wide + grad_second
    grad_middle_low = grad_middle.astype(BF16)
    grad_middle_all = jnp.concatenate(spread(grad_middle_low), axis=0)
    grad_mixed = contract(grad_middle_all, out_set, 1, 1).astype(BF16)
    out_half = reduce_rows(scatter_half(contract(mixed, grad_middle_all, 0, 0).astype(BF16)))
    spans = [(0, pairs // 2), (pairs // 2, pairs)] if pairs > 1 else [(0, pairs)]
    dqkvs, qkv_halves = [], []
    for begin, end in spans:
        gate = lse if not dqkvs else after(lse, qkv_halves[-1])
        dqkvs.append(wide_back(qkv, grad_mixed, mixed, gate, begin, end))
        qkv_halves.append(contract(first, dqkvs[-1], 0, 0).astype(BF16))
    qkv_halves = [reduce_rows(scatter_half(values)) for values in qkv_halves]

    result = collect(
        lambda rows: functools.reduce(
            jnp.add, [contract(feeds[j][0][rows], down_sets[j], 1, 0) for j in range(ranges)]
        )
    )
    result = (middle + result + full_dbias).astype(BF16)
    layer_out = move(result, back).reshape(1, local, width)

    def weight_of(span):
        return qkv_weight[:, span[0] * 3 * PAIR : span[1] * 3 * PAIR]

    grad_first_norm = collect(
        lambda rows: functools.reduce(
            jnp.add,
            [contract(d[rows], weight_of(span), 1, 1) for d, span in zip(dqkvs, spans)],
        )
    )
    grad_first, grad_gain_one, grad_shift_one = norm_back(
        grad_first_norm, first_normed, first_inverse, gain_one
    )
    tokens_grad = move((grad_middle + grad_first).astype(BF16), back).reshape(1, local, width)

    out_weight_grad = join(out_half, swap_core(out_half), core).reshape(-1, width).astype(F32)
    if True:

        def finish_columns(values):
            values = values.reshape(quarter, own_rows, 1, -1)
            values = lax.all_to_all(values, "gq", split_axis=0, concat_axis=2, tiled=True)
            values = values.reshape(own_rows, quarter, -1)
            return join(values, swap_core(values), core).transpose(1, 0, 2, 3)

        def natural_columns(values, inner=1):
            values = values.reshape(own_rows, 2, quarter, inner, 2, -1)
            return values.transpose(0, 4, 2, 1, 3, 5).reshape(own_rows, -1).astype(F32)

        ups = jnp.stack([finish_columns(values) for values in sums_feed[::2]], axis=3)
        up_weight_grad = natural_columns(ups, ranges)
        downs = jnp.stack(sums_feed[1::2])
        down_weight_grad = join(downs, swap_core(downs), core).reshape(-1, width).astype(F32)
        columns = jnp.concatenate([finish_columns(values) for values in qkv_halves], axis=3)
        columns = columns.reshape(own_rows, 2, quarter, pairs, 3, PAIR)
        query_weight_grad, key_weight_grad, value_weight_grad = [
            natural_columns(columns[:, :, :, :, i]) for i in range(3)
        ]

    def place_entries(values, inner=1):
        values = values.reshape(inner, 2, 1, 1, -1).transpose(1, 2, 3, 0, 4)
        shape = (2, quarter, 2) + values.shape[3:]
        zero = jnp.zeros((), core.dtype)
        return lax.dynamic_update_slice(
            jnp.zeros(shape, F32), values, (zero, gq, core, zero, zero)
        ).reshape(grp, -1)

    dqkv_sums = jnp.concatenate([jnp.sum(d.astype(F32), axis=0) for d in dqkvs])
    dqkv_sums = dqkv_sums.reshape(pairs, 3, PAIR)
    sums = [
        place_entries(dqkv_sums[:, 0]),
        place_entries(dqkv_sums[:, 2]),
        jnp.sum(grad_middle_low.astype(F32), axis=0),
        grad_gain_one, grad_shift_one, grad_gain_two, grad_shift_two,
        jnp.sum(grad_wide, axis=0),
        place_entries(jnp.stack([outs[6] for outs in feeds]), ranges),
    ]
    sums = jnp.concatenate([s.reshape(grp, -1) for s in sums], axis=1)
    if grp == 2 and ring & (ring - 1) == 0:
        sums = sums + swap_core(sums)
        sums = pick(sums, half, 0) + swap_half(pick(sums, 1 - half, 0))
        step = 1
        while step < ring:
            sums = sums + lax.ppermute(sums, "rz", [(i, i ^ step) for i in range(ring)])
            step *= 2
    else:
        sums = lax.psum(sums, ("rz", "core", "half", "gq"))
        sums = pick(sums, half * quarter + gq, 0)
    small = [sums[i * own_rows : (i + 1) * own_rows] for i in range(8)]
    return (
        layer_out, tokens_grad, query_weight_grad, key_weight_grad, value_weight_grad,
        small[0], small[1], out_weight_grad, small[2], small[3], small[4], small[5], small[6],
        up_weight_grad, sums[8 * own_rows :], down_weight_grad, small[7],
    )


class Order:
    def __init__(self):
        self.before = ()

    def pin(self, *values):
        pinned = lax.optimization_barrier(values + self.before)[: len(values)]
        self.before = tuple(pinned) + self.before
        return pinned[0] if len(values) == 1 else list(pinned)

    def fence(self, *values):
        self.before = values


class Steps:
    def __init__(self, steps):
        self.steps = steps
        self.waiting = next(steps)


def advance(order, *chains):
    pinned = order.pin(*[values for chain in chains for values in chain.waiting])
    pinned = list(pinned) if isinstance(pinned, (list, tuple)) else [pinned]
    for chain in chains:
        count = len(chain.waiting)
        values, pinned = pinned[:count], pinned[count:]
        chain.waiting = chain.steps.send(values)


def line_steps(order, deep, parts, result):
    place = lax.axis_index("line")
    bits = range((deep - 1).bit_length())

    def exchange(values, bit):
        return lax.ppermute(values, "line", [(i, i ^ (1 << bit)) for i in range(deep)])

    for bit in bits:
        even = (place >> bit) % 2 == 0
        keep, send = order.pin(jnp.where(even, *parts), jnp.where(even, *parts[::-1]))
        (other,) = yield [exchange(send, bit)]
        total = add_low(keep, other)
        size = total.shape[0] // 2
        parts = (total[:size], total[size:])
    for bit in reversed(bits):
        total = order.pin(total)
        (other,) = yield [exchange(total, bit)]
        total = join(total, other, (place >> bit) % 2).reshape(-1, total.shape[-1])
    whole = order.pin(total)
    beside, across = yield [lax.ppermute(whole, "low", SWAP), lax.ppermute(whole, "core", SWAP)]
    crossed = lax.ppermute(beside, "core", SWAP)
    (crossed,) = yield [crossed]
    result.extend([whole, beside, across, crossed])
    yield []


def range_steps(order, deep, parts, result):
    place = lax.axis_index("line")
    bits = range((deep - 1).bit_length())

    def exchange(values, bit):
        return lax.ppermute(values, "line", [(i, i ^ (1 << bit)) for i in range(deep)])

    for bit in bits:
        even = (place >> bit) % 2 == 0
        keep, send = order.pin(jnp.where(even, *parts), jnp.where(even, *parts[::-1]))
        (other,) = yield [exchange(send, bit)]
        total = add_low(keep, other)
        size = total.shape[0] // 2
        parts = (total[:size], total[size:])
    for bit in reversed(bits[1:]):
        total = order.pin(total)
        (other,) = yield [exchange(total, bit)]
        total = join(total, other, (place >> bit) % 2).reshape(-1, total.shape[-1])
    whole = order.pin(total)
    beside, along = yield [lax.ppermute(whole, "low", SWAP), exchange(whole, 0)]
    last, crossed = yield [lax.ppermute(along, "low", SWAP), lax.ppermute(whole, "core", SWAP)]
    rest = yield [lax.ppermute(values, "core", SWAP) for values in (beside, along, last)]
    result.extend([whole, beside, along, last, crossed, *rest])
    yield []


def plane_steps(order, low, deep, send, keep, result):
    send, keep = order.pin(send, keep)
    (other,) = yield [lax.ppermute(send, "half", SWAP)]
    total = add_low(keep, other)
    size = total.shape[0] // 2
    parts = (total[:size], total[size:])
    even = low == 0
    keep, send = order.pin(jnp.where(even, *parts), jnp.where(even, *parts[::-1]))
    (other,) = yield [lax.ppermute(send, "low", SWAP)]
    total = add_low(keep, other)
    size = total.shape[0] // 2
    yield from line_steps(order, deep, (total[:size], total[size:]), result)


def vector_steps(order, half, deep, entries, result):
    def line(values, bit):
        return lax.ppermute(values, "line", [(i, i ^ (1 << bit)) for i in range(deep)])

    entries = order.pin(entries)
    (other,) = yield [lax.ppermute(entries, "core", SWAP)]
    entries = entries + other
    keep, send = order.pin(pick(entries, half, 0), pick(entries, 1 - half, 0))
    (other,) = yield [lax.ppermute(send, "half", SWAP)]
    total = order.pin(keep + other)
    for bit in range((deep - 1).bit_length()):
        (other,) = yield [line(total, bit)]
        total = order.pin(total + other)
    (other,) = yield [lax.ppermute(total, "low", SWAP)]
    result.append(total + other)
    yield []


def add_low(left, right):
    return (left.astype(F32) + right.astype(F32)).astype(BF16)


def after_all(values, *gates):
    if not gates:
        return tuple(values)
    return lax.optimization_barrier(tuple(values) + gates)[: len(values)]


def pair_body(
    rep, grp, tokens, query_weight, key_weight, value_weight, query_bias, value_bias, out_weight,
    out_bias, first_gain, first_shift, second_gain, second_shift, up_weight, up_bias,
    down_weight, down_bias, cotangent,
):
    clips, local, width = tokens.shape
    assert clips == 1
    ring = rep // 2
    deep = ring // 2
    core, half = lax.axis_index("core"), lax.axis_index("half")
    low, high = lax.axis_index("low"), lax.axis_index("line") % 2
    own_rows = width // 2
    pairs = own_rows // PAIR
    hidden = up_weight.shape[1]
    stays = core == half
    scal = jnp.stack([half, low, core, stays.astype(jnp.int32), high]).astype(jnp.int32)
    cross = [(1, 2), (2, 1)]

    def swap_half(values):
        return lax.ppermute(values, "half", SWAP)

    def swap_core(values):
        return lax.ppermute(values, "core", SWAP)

    def swap_low(values):
        return lax.ppermute(values, "low", SWAP)

    def swap_high(values):
        return lax.ppermute(values, "line", [(i, i ^ 1) for i in range(deep)])

    def cross_over(values):
        return lax.ppermute(values, ("core", "half"), cross)

    tokens, cotangent = tokens.reshape(local, width), cotangent.reshape(local, width)

    tokens_in = cross_over(tokens)
    own_qkv, mine = pack_qkv(scal, (query_weight, key_weight, value_weight))
    qkv_x = swap_half(mine)
    packed = [pack_feed(scal, up_weight, down_weight, j, 2, (1, 4)[j]) for j in range(2)]
    vectors = jnp.concatenate(
        [after(query_bias, mine, *packed), value_bias, out_bias, first_gain, first_shift,
         second_gain, second_shift, down_bias, up_bias]
    )
    order = Order()
    tokens_in, qkv_x, vectors, vectors_in, *packed = order.pin(
        tokens_in, qkv_x, vectors, swap_half(vectors), *packed
    )
    qkv_y = swap_low(qkv_x)
    feed_x = [swap_half(packed[0])]
    vectors = join(vectors, vectors_in, half)
    (full_qbias, full_vbias, full_obias, gain_one, shift_one, gain_two, shift_two, full_dbias) = [
        vectors[:, i * own_rows : (i + 1) * own_rows].reshape(1, width) for i in range(8)
    ]

    def set_entries(values, inner=1):
        return pick(values.reshape(2, 2, inner, -1), core, 1).transpose(1, 0, 2).reshape(inner, -1)

    bias_set = set_entries(vectors[:, 8 * own_rows :], 2).reshape(1, -1)
    quarter = own_rows // 4
    out_mine = lax.dynamic_slice(
        out_weight, (core * (own_rows // 2) + low * quarter, 0 * core), (quarter, width)
    )
    x, first = first_norm(scal, tokens, tokens_in, gain_one, shift_one)
    x, first = order.pin(x, first)
    order.fence(x)
    first, qkv_y, feed_x[0] = order.pin(first, qkv_y, feed_x[0])
    first_in = order.pin(swap_core(first))
    feed_y = [swap_low(feed_x[0])]
    out_x = swap_half(order.pin(out_mine))
    feed_x.append(swap_half(order.pin(packed[1])))
    zeros = jnp.zeros((pairs, PAIR), F32)
    qkv_bias = jnp.stack(
        [set_entries(full_qbias).reshape(pairs, PAIR), zeros,
         set_entries(full_vbias).reshape(pairs, PAIR)],
        axis=1,
    ).reshape(1, 3 * own_rows)
    qkv, qkv_weight, first_all = project(
        scal, (first, first_in), own_qkv, qkv_x, qkv_y, qkv_bias
    )

    qkv, out_x = order.pin(qkv, out_x)
    order.fence(qkv)
    out_y = swap_low(out_x)
    mixed, lse = attend(qkv, 0, pairs - 1)
    lse, out_y, feed_x[1] = order.pin(lse, out_y, feed_x[1])
    feed_y.append(swap_high(feed_x[1]))
    cotangent_in = cross_over(after(cotangent, lse))
    mixed, lse = attend(qkv, pairs - 1, pairs, (mixed, lse))
    mixed = order.pin(mixed)
    out_part, out_set = out_other(scal, mixed, out_weight, out_x, out_y)
    out_part, cotangent_in, *feed_y = order.pin(out_part, cotangent_in, *feed_y)
    out_in = swap_core(out_part)
    grad_out = order.pin(jnp.where(stays, cotangent, cotangent_in))
    grad_out_in = swap_core(grad_out)
    middle, second = second_norm(
        scal, mixed, out_set, x, order.pin(out_in), full_obias, gain_two, shift_two
    )
    middle, second = order.pin(middle, second)
    order.fence(second)
    second_in = swap_core(second)

    second_in = order.pin(second_in)
    (
        out_own, out_part, dx_own, dx_part, up_send, up_keep, down_send, down_keep, low_send,
        low_keep, up_bias_grad,
    ) = feed(
        scal, (second, second_in), (grad_out, grad_out_in), up_weight, down_weight,
        (feed_x[0], feed_y[0], feed_x[1], feed_y[1]), bias_set,
    )
    dx_part, up_send, down_send, low_send, out_part = order.pin(
        dx_part, up_send, down_send, low_send, out_part
    )
    order.fence(dx_part)
    dx_in = swap_core(dx_part)
    up_in, down_in, low_in = swap_half(up_send), swap_half(down_send), swap_low(low_send)
    out_in = swap_core(out_part)
    grad_low, sums_two = second_back(
        scal, dx_own, order.pin(dx_in), middle, grad_out, gain_two
    )
    grad_low = order.pin(grad_low)
    grad_low_in = swap_core(grad_low)
    layer = layer_rows(scal, out_own, order.pin(out_in), middle, full_dbias)
    grad_low_in, layer = order.pin(grad_low_in, layer)
    grad_mixed, out_send, out_keep = mixed_back(scal, (grad_low, grad_low_in), out_set, mixed)
    grad_mixed = order.pin(grad_mixed)

    backs = []

    def back(pair):
        gate = order.pin(lse)
        named = jnp.concatenate([scal, jnp.full((1,), pair, jnp.int32)])
        backs.append(attend_back(named, qkv, grad_mixed, mixed, gate, first_all))
        backs[-1] = order.pin(*backs[-1])
        order.fence(backs[-1][3])

    back(0)
    up_in, down_in, low_in = order.pin(up_in, down_in, low_in)
    up_sum, down_sum = add_low(up_keep, up_in), add_low(down_keep, down_in)
    even = low == 0
    low_mine, low_other = order.pin(
        jnp.where(even, up_sum, down_sum), jnp.where(even, down_sum, up_sum)
    )
    one_in = lax.ppermute(low_other, "low", SWAP)
    range_sum = add_low(low_keep, low_in).reshape(2, own_rows, width)
    half_send, half_keep = order.pin(pick(range_sum, 1 - half, 0), pick(range_sum, half, 0))
    half_in = swap_half(half_send)

    back(1)
    one_in, half_in = order.pin(one_in, half_in)
    feed_parts, early_parts, late_parts, vector_parts = [], [], [], []
    ranges = Steps(
        range_steps(
            order, deep, (add_low(low_mine, one_in), add_low(half_keep, half_in)), feed_parts
        )
    )
    early = Steps(
        plane_steps(
            order, low, deep,
            jnp.concatenate([backs[0][1], backs[1][1], out_send], axis=0),
            jnp.concatenate([backs[0][2], backs[1][2], out_keep], axis=0), early_parts,
        )
    )

    back(2)
    advance(order, ranges, early)
    layer_in = cross_over(order.pin(layer))

    back(3)
    layer_in = order.pin(layer_in)
    late = Steps(
        plane_steps(
            order, low, deep,
            jnp.concatenate([backs[2][1], backs[3][1]], axis=0),
            jnp.concatenate([backs[2][2], backs[3][2]], axis=0), late_parts,
        )
    )
    advance(order, ranges, early)
    first_own, first_part = first_grad(
        scal, [order.pin(backs[0][0])] + [b[0] for b in backs[1:]], qkv_weight
    )
    first_own, first_part = order.pin(first_own, first_part)
    order.fence(first_part)
    advance(order, late, early)
    first_part_in = swap_core(order.pin(first_part))
    advance(order, ranges)
    tokens_out, sums_one = first_back(
        scal, first_own, order.pin(first_part_in), x, grad_low, gain_one
    )
    tokens_out, sums_one = order.pin(tokens_out, sums_one)
    order.fence(sums_one)
    advance(order, early, late, ranges)

    def place_entries(values, inner=1):
        values = values.reshape(inner, 2, 1, -1).transpose(1, 2, 0, 3)
        empty = jnp.zeros_like(values)
        return join(values[:, 0], empty[:, 0], core).transpose(1, 0, 2, 3).reshape(2, -1)

    parts = jnp.concatenate([b[3][0] for b in backs]).reshape(pairs, 3, PAIR)
    entries = [
        place_entries(parts[:, 0]), place_entries(parts[:, 2]), sums_two[3], sums_one[0],
        sums_one[1], sums_two[0], sums_two[1], sums_two[2], place_entries(up_bias_grad, 2),
    ]
    entries = jnp.concatenate([e.reshape(2, -1) for e in entries], axis=1)
    vectors = Steps(vector_steps(order, half, deep, entries, vector_parts))
    advance(order, vectors)
    advance(order, vectors, early, late)
    tokens_in = cross_over(order.pin(tokens_out))
    advance(order, vectors, early, late)
    advance(order, vectors, late)
    advance(order, early, ranges, late)
    advance(order, ranges, vectors, early)
    up_weight_grad, down_weight_grad = order.pin(*finish_feed(scal, feed_parts))
    advance(order, late)
    advance(order, late)
    (entries,) = vector_parts
    query_weight_grad, key_weight_grad, value_weight_grad, out_weight_grad = finish_attention(
        scal, (*early_parts, *late_parts), ((0, 2), (2, 4))
    )
    layer_out = jnp.where(stays, layer, layer_in)
    tokens_grad = jnp.where(stays, tokens_out, tokens_in)
    small = [entries[i * own_rows : (i + 1) * own_rows] for i in range(8)]
    return (
        layer_out.reshape(1, local, width), tokens_grad.reshape(1, local, width),
        query_weight_grad, key_weight_grad, value_weight_grad, small[0], small[1],
        out_weight_grad, small[2], small[3], small[4], small[5], small[6], up_weight_grad,
        entries[8 * own_rows :], down_weight_grad, small[7],
    )


def solution(mesh):
    rep, grp = mesh.shape["rep"], mesh.shape["grp"]
    paired = grp == 2 and rep >= 8 and rep & (rep - 1) == 0
    if paired:
        sizes, names = (rep // 4, 2, 2, 2), ("line", "low", "core", "half")
        reps, groups, body = ("line", "low", "core"), "half", pair_body
    else:
        sizes, names = (rep // 2, 2, 2, grp // 2), ("rz", "core", "half", "gq")
        reps, groups, body = ("rz", "core"), ("half", "gq"), wide_body
    clip, matrix, vector = P(reps, groups, None), P(groups, None), P(groups)
    return jax.shard_map(
        functools.partial(body, rep, grp),
        mesh=Mesh(mesh.devices.reshape(sizes), names),
        in_specs=(
            clip, matrix, matrix, matrix, vector, vector, matrix, vector, vector, vector, vector,
            vector, matrix, vector, matrix, vector, clip,
        ),
        out_specs=(
            clip, clip, matrix, matrix, matrix, vector, vector, matrix, vector, vector, vector,
            vector, vector, matrix, vector, matrix, vector,
        ),
        check_vma=False,
    )
```

```python
import functools

import jax
import jax.numpy as jnp
from jax import lax
from jax.experimental import pallas as pl
from jax.experimental.pallas import tpu as pltpu
from jax.sharding import Mesh
from jax.sharding import PartitionSpec as P

HEAD_DIM = 64
PAIR = 2 * HEAD_DIM
EPS = 1e-06
LOG2E = 1.4426950408889634
F32 = jnp.float32
BF16 = jnp.bfloat16
SWAP = [(0, 1), (1, 0)]
VMEM_LIMIT = 62 << 20


def contract(left, right, left_dim, right_dim):
    return lax.dot_general(
        left, right, (((left_dim,), (right_dim,)), ((), ())), preferred_element_type=F32
    )


def padded_rows(rows, tile):
    full = rows // tile
    return full * tile + -(-(rows - full * tile) // PAIR) * PAIR


def walk(rows, tile, start, finish):
    full = rows // tile
    rest = padded_rows(rows, tile) - full * tile
    start(0, pl.ds(0, tile), tile)

    def step(columns, size, following, following_size):
        start(1, columns, size)
        finish(0, columns, size)
        if following is not None:
            start(0, following, following_size)
        finish(1, columns, size)

    def block(index, carry):
        first = pl.multiple_of(index * tile, tile)
        following = pl.multiple_of(index * tile + tile, tile)
        step(pl.ds(first, tile), tile, pl.ds(following, tile), tile)
        return carry

    lax.fori_loop(0, full - 1, block, 0)
    last = pl.ds(full * tile, rest) if rest else None
    step(pl.ds((full - 1) * tile, tile), tile, last, rest)
    if rest:
        step(last, rest, None, 0)


def one_head(values_t, head, columns, size):
    empty = jnp.zeros((HEAD_DIM, size), BF16)
    values = values_t[head * HEAD_DIM : (head + 1) * HEAD_DIM, columns]
    return jnp.concatenate([values, empty] if head == 0 else [empty, values], axis=0)


def attend_kernel(tile, rows, padded, qkv_ref, out_ref, lse_ref, q_t, v_t, out_t, scores):
    scale = HEAD_DIM**-0.5 * LOG2E
    ones = jnp.ones((16, rows), BF16)
    q_t[:, :rows] = qkv_ref[:, :PAIR].T
    if padded > rows:
        q_t[:, rows:] = jnp.zeros((PAIR, padded - rows), BF16)
    values_t = qkv_ref[:, 2 * PAIR :].T
    step = HEAD_DIM + 16
    for head in range(2):
        v_t[head * step : head * step + HEAD_DIM, :] = values_t[
            head * HEAD_DIM : (head + 1) * HEAD_DIM, :
        ]
        v_t[head * step + HEAD_DIM : (head + 1) * step, :] = ones

    def start(head, columns, size):
        query = one_head(q_t, head, columns, size)
        scores[head, :, :size] = contract(qkv_ref[:, PAIR : 2 * PAIR], query, 1, 0)

    def finish(head, columns, size):
        values = scores[head, :, :size]
        highest = jnp.max(values, axis=0, keepdims=True) * scale
        expon = jnp.exp2(values * scale - highest).astype(BF16)
        mixed = contract(v_t[head * step : (head + 1) * step, :], expon, 1, 0)
        total = mixed[HEAD_DIM : HEAD_DIM + 1, :]
        out_t[head * HEAD_DIM : (head + 1) * HEAD_DIM, columns] = mixed[:HEAD_DIM, :] / total
        lse_ref[head : head + 1, columns] = highest + jnp.log2(total)

    walk(rows, tile, start, finish)
    out_ref[...] = out_t[...].T[:rows, :].astype(BF16)


def attend(qkv, first_pair, last_pair, kept=None, tile=512):
    rows, width = qkv.shape
    pairs = width // (3 * PAIR)
    padded = padded_rows(rows, tile)
    count = last_pair - first_pair
    kernel = functools.partial(attend_kernel, tile, rows, padded)
    anywhere = pl.BlockSpec(memory_space=pl.ANY)
    return pl.pallas_call(
        kernel if kept is None else lambda ref, a, b, *rest: kernel(ref, *rest),
        grid=(count,),
        in_specs=[pl.BlockSpec((rows, 3 * PAIR), lambda i: (0, i + first_pair))]
        + ([] if kept is None else [anywhere] * 2),
        out_specs=[
            pl.BlockSpec((rows, PAIR), lambda i: (0, i + first_pair)),
            pl.BlockSpec((None, 2, padded), lambda i: (i + first_pair, 0, 0)),
        ],
        out_shape=[
            jax.ShapeDtypeStruct((rows, pairs * PAIR), BF16),
            jax.ShapeDtypeStruct((pairs, 2, padded), F32),
        ],
        scratch_shapes=[
            pltpu.VMEM((PAIR, padded), BF16),
            pltpu.VMEM((PAIR + 32, rows), BF16),
            pltpu.VMEM((PAIR, padded), F32),
            pltpu.VMEM((2, rows, tile), F32),
        ],
        input_output_aliases={} if kept is None else {1: 0, 2: 1},
        compiler_params=pltpu.CompilerParams(vmem_limit_bytes=VMEM_LIMIT),
        cost_estimate=pl.CostEstimate(
            flops=64 * rows * rows * PAIR * count,
            bytes_accessed=8 * rows * PAIR * count,
            transcendentals=2 * rows * rows * count,
        ),
        name="attend",
    )(qkv, *(() if kept is None else kept))


def attend_back_kernel(
    tile, rows, padded, s_ref, qkv_ref, grad_ref, out_ref, lse_ref, first_ref, dqkv_ref, send_ref,
    keep_ref, sums_ref, q_t, g_t, k_t, delta, dq_t, dk_t, dv_t, all_t, scores, d_probs,
):
    scale = HEAD_DIM**-0.5
    q_t[:, :rows] = qkv_ref[:, :PAIR].T
    g_t[:, :rows] = grad_ref[...].T
    if padded > rows:
        q_t[:, rows:] = jnp.zeros((PAIR, padded - rows), BF16)
        g_t[:, rows:] = jnp.zeros((PAIR, padded - rows), BF16)
        delta[:, rows:] = jnp.zeros((2, padded - rows), F32)
    k_t[...] = qkv_ref[:, PAIR : 2 * PAIR].T
    product = (grad_ref[...].astype(F32) * out_ref[...].astype(F32)).T
    delta[0:1, :rows] = jnp.sum(product[:HEAD_DIM, :], axis=0, keepdims=True)
    delta[1:2, :rows] = jnp.sum(product[HEAD_DIM:, :], axis=0, keepdims=True)
    dk_t[...] = jnp.zeros_like(dk_t)
    dv_t[...] = jnp.zeros_like(dv_t)

    def start(head, columns, size):
        query, grad = one_head(q_t, head, columns, size), one_head(g_t, head, columns, size)
        scores[head, :, :size] = contract(qkv_ref[:, PAIR : 2 * PAIR], query, 1, 0)
        d_probs[head, :, :size] = contract(qkv_ref[:, 2 * PAIR :], grad, 1, 0)

    def finish(head, columns, size):
        lanes = slice(head * HEAD_DIM, (head + 1) * HEAD_DIM)
        log_total = lse_ref[head : head + 1, columns]
        weights = jnp.exp2(scores[head, :, :size] * (scale * LOG2E) - log_total)
        inner = delta[head : head + 1, columns]
        d_scores = (weights * (d_probs[head, :, :size] - inner)).astype(BF16)
        dv_t[lanes, :] += contract(g_t[lanes, columns], weights.astype(BF16), 1, 1)
        dq_t[lanes, columns] = contract(k_t[lanes, :], d_scores, 1, 0)
        dk_t[lanes, :] += contract(q_t[lanes, columns], d_scores, 1, 1)

    walk(rows, tile, start, finish)
    all_t[:PAIR, :] = (dq_t[:, :rows] * scale).astype(BF16)
    all_t[PAIR : 2 * PAIR, :] = (dk_t[...] * scale).astype(BF16)
    all_t[2 * PAIR :, :] = dv_t[...].astype(BF16)
    for part in range(3):
        lanes = slice(part * PAIR, (part + 1) * PAIR)
        dqkv_ref[:, lanes] = all_t[lanes, :].T
    sums_ref[...] = contract(jnp.ones((8, rows), BF16), all_t[...], 1, 1)
    own = first_ref.shape[1] // 2
    for h in range(2):
        grad = contract(all_t[...], first_ref[:, h * own : (h + 1) * own], 1, 0).astype(BF16)

        @pl.when(s_ref[0] == h)
        def _():
            keep_ref[...] = grad

        @pl.when(s_ref[0] != h)
        def _():
            send_ref[...] = grad


def attend_back(scal, qkv, grad, out, lse, first, tile=256):
    rows, full = qkv.shape
    width = first.shape[1]
    padded = padded_rows(rows, tile)
    count = 1
    return pl.pallas_call(
        functools.partial(attend_back_kernel, tile, rows, padded),
        grid_spec=pltpu.PrefetchScalarGridSpec(
            num_scalar_prefetch=1,
            grid=(count,),
            in_specs=[
                pl.BlockSpec((rows, 3 * PAIR), lambda i, s: (0, s[5])),
                pl.BlockSpec((rows, PAIR), lambda i, s: (0, s[5])),
                pl.BlockSpec((rows, PAIR), lambda i, s: (0, s[5])),
                pl.BlockSpec((None, 2, lse.shape[2]), lambda i, s: (s[5], 0, 0)),
                pl.BlockSpec((rows, width), lambda i, s: (0, 0), pipeline_mode=pl.Buffered(1)),
            ],
            out_specs=[
                pl.BlockSpec((rows, 3 * PAIR), lambda i, s: (0, i)),
                pl.BlockSpec((3 * PAIR, width // 2), lambda i, s: (i, 0)),
                pl.BlockSpec((3 * PAIR, width // 2), lambda i, s: (i, 0)),
                pl.BlockSpec((8, 3 * PAIR), lambda i, s: (0, i)),
            ],
            scratch_shapes=[
                pltpu.VMEM((PAIR, padded), BF16),
                pltpu.VMEM((PAIR, padded), BF16),
                pltpu.VMEM((PAIR, rows), BF16),
                pltpu.VMEM((2, padded), F32),
                pltpu.VMEM((PAIR, padded), F32),
                pltpu.VMEM((PAIR, rows), F32),
                pltpu.VMEM((PAIR, rows), F32),
                pltpu.VMEM((3 * PAIR, rows), BF16),
                pltpu.VMEM((2, rows, tile), F32),
                pltpu.VMEM((2, rows, tile), F32),
            ],
        ),
        out_shape=[
            jax.ShapeDtypeStruct((rows, 3 * PAIR * count), BF16),
            jax.ShapeDtypeStruct((3 * PAIR * count, width // 2), BF16),
            jax.ShapeDtypeStruct((3 * PAIR * count, width // 2), BF16),
            jax.ShapeDtypeStruct((8, 3 * PAIR * count), F32),
        ],
        compiler_params=pltpu.CompilerParams(vmem_limit_bytes=VMEM_LIMIT),
        cost_estimate=pl.CostEstimate(
            flops=160 * rows * rows * PAIR * count,
            bytes_accessed=16 * rows * PAIR * count,
            transcendentals=2 * rows * rows * count,
        ),
        name="attend_back",
    )(scal, qkv, grad, out, lse, first)


def feed_kernel(
    s_ref, x_own, x_other, dy_own, dy_other, up_ref, down_ref, x_piece, x_beside, z_piece, z_beside,
    bias_ref, out_own, out_other, dx_own, dx_other, up_send, up_keep, down_send, down_keep,
    low_send, low_keep, bias_grad_ref, x, dy, x_t, out_sum, dx_sum, up_full, down_full, hidden,
    d_pre, sems,
):
    index = pl.program_id(0)
    half = s_ref[0]
    rows, width = x.shape
    block = rows // 2
    own = width // 2
    tile = up_ref.shape[1]
    first_range = index < 2
    side = index % 2
    columns = pl.ds(pl.multiple_of(side * tile, tile), tile)
    mine = pl.ds(pl.multiple_of(half * own, own), own)
    theirs = pl.ds(pl.multiple_of((1 - half) * own, own), own)

    @pl.when(index == 0)
    def _():
        copies = []
        for i, ref in enumerate((x_own, x_other)):
            copies.append(pltpu.make_async_copy(ref, x.at[pl.ds(i * block, block)], sems.at[i]))
        for i, ref in enumerate((dy_own, dy_other)):
            copies.append(
                pltpu.make_async_copy(ref, dy.at[pl.ds(i * block, block)], sems.at[2 + i])
            )
        for copy in copies:
            copy.start()
        for copy in copies:
            copy.wait()
        x_t[...] = x[...].T
        out_sum[...] = jnp.zeros_like(out_sum)
        dx_sum[...] = jnp.zeros_like(dx_sum)

    up_full[mine, :] = up_ref[...]

    @pl.when(side == half)
    def _():
        down_full[...] = down_ref[...]

    for chosen, place, piece, beside in (
        (first_range, 1, x_piece, x_beside), (jnp.logical_not(first_range), 4, z_piece, z_beside)
    ):
        even = s_ref[place] == 0

        @pl.when(chosen & even)
        def _():
            up_full[theirs, :] = piece[:, columns]

        @pl.when(chosen & jnp.logical_not(even))
        def _():
            up_full[theirs, :] = beside[:, columns]

        @pl.when(chosen & (side != half) & even)
        def _():
            down_full[...] = beside[...]

        @pl.when(chosen & (side != half) & jnp.logical_not(even))
        def _():
            down_full[...] = piece[...]

    bias_grad = jnp.zeros(bias_grad_ref.shape, F32)
    for start in range(0, rows, block):
        part = slice(start, start + block)
        pre = contract(x[part, :], up_full[...], 1, 0) + bias_ref[...]
        d_hidden = contract(dy[part, :], down_full[...], 1, 1)
        share = 0.5 * (1.0 + lax.erf(pre * 0.7071067811865476))
        hidden[part, :] = (pre * share).astype(BF16)
        slope = share + pre * (jnp.exp(-0.5 * pre * pre) * 0.3989422804014327)
        d_low = (d_hidden * slope).astype(BF16)
        d_pre[part, :] = d_low
        bias_grad = bias_grad + jnp.sum(d_low.astype(F32), axis=0, keepdims=True)
        out_sum[part, :] += contract(hidden[part, :], down_full[...], 1, 0)
        dx_sum[part, :] += contract(d_pre[part, :], up_full[...], 1, 1)
    bias_grad_ref[...] = bias_grad
    down_grad = contract(hidden[...], dy[...], 0, 0).astype(BF16)
    side_rows = pl.ds(pl.multiple_of(side * tile, tile), tile)

    @pl.when(first_range)
    def _():
        up_keep[:, columns] = contract(x_t[mine, :], d_pre[...], 1, 0).astype(BF16)
        up_send[:, columns] = contract(x_t[theirs, :], d_pre[...], 1, 0).astype(BF16)

    @pl.when(first_range & (side == half))
    def _():
        down_keep[...] = down_grad

    @pl.when(first_range & (side != half))
    def _():
        down_send[...] = down_grad

    for even in (True, False):
        up_goal, down_goal = (low_keep, low_send) if even else (low_send, low_keep)

        @pl.when(jnp.logical_not(first_range) & ((s_ref[1] == 0) == even))
        def _():
            up_goal[:, columns] = contract(x_t[...], d_pre[...], 1, 0).astype(BF16)
            down_goal[side_rows, :] = down_grad

    @pl.when(index == pl.num_programs(0) - 1)
    def _():
        out_own[...] = out_sum[:block, :].astype(BF16)
        out_other[...] = out_sum[block:, :].astype(BF16)
        dx_own[...] = dx_sum[:block, :].astype(BF16)
        dx_other[...] = dx_sum[block:, :].astype(BF16)


def feed(scal, seconds, grads, up, down, pieces, bias):
    local, width = seconds[0].shape
    rows = 2 * local
    tile = down.shape[0] // 4
    anywhere = pl.BlockSpec(memory_space=pl.ANY)

    def fixed(*shape):
        return pl.BlockSpec(shape, lambda t, s: (0, 0), pipeline_mode=pl.Buffered(1))

    shapes = [(local, width)] * 4 + [(width // 2, 2 * tile)] * 2 + [(tile, width)] * 2
    shapes += [(width, 2 * tile)] * 2
    across = pl.BlockSpec((1, tile), lambda t, s: (0, t))
    return pl.pallas_call(
        feed_kernel,
        grid_spec=pltpu.PrefetchScalarGridSpec(
            num_scalar_prefetch=1,
            grid=(4,),
            in_specs=[anywhere] * 4
            + [
                pl.BlockSpec(
                    (width // 2, tile), lambda t, s: (0, ((t % 2) * 2 + s[2]) * 2 + t // 2)
                ),
                pl.BlockSpec((tile, width), lambda t, s: (s[2] * 2 + t // 2, 0)),
            ]
            + [fixed(width // 2, 2 * tile)] * 4
            + [across],
            out_specs=[fixed(*shape) for shape in shapes] + [across],
            scratch_shapes=[
                pltpu.VMEM((rows, width), BF16),
                pltpu.VMEM((rows, width), BF16),
                pltpu.VMEM((width, rows), BF16),
                pltpu.VMEM((rows, width), F32),
                pltpu.VMEM((rows, width), F32),
                pltpu.VMEM((width, tile), BF16),
                pltpu.VMEM((tile, width), BF16),
                pltpu.VMEM((rows, tile), BF16),
                pltpu.VMEM((rows, tile), BF16),
                pltpu.SemaphoreType.DMA((4,)),
            ],
        ),
        out_shape=[jax.ShapeDtypeStruct(shape, BF16) for shape in shapes]
        + [jax.ShapeDtypeStruct((1, 4 * tile), F32)],
        compiler_params=pltpu.CompilerParams(vmem_limit_bytes=VMEM_LIMIT),
        cost_estimate=pl.CostEstimate(
            flops=48 * rows * width * tile,
            bytes_accessed=16 * rows * width,
            transcendentals=8 * rows * tile,
        ),
        name="feed",
    )(scal, *seconds, *grads, up, down, *pieces, bias)


def run(kernel, name, scal, grid, in_specs, out_specs, out_shape, args, flops=0, scratch=()):
    moved = sum(a.size * a.dtype.itemsize for a in args)
    return pl.pallas_call(
        kernel,
        grid_spec=pltpu.PrefetchScalarGridSpec(
            num_scalar_prefetch=1,
            grid=grid,
            in_specs=in_specs,
            out_specs=out_specs,
            scratch_shapes=scratch,
        ),
        out_shape=out_shape,
        compiler_params=pltpu.CompilerParams(vmem_limit_bytes=VMEM_LIMIT),
        cost_estimate=pl.CostEstimate(flops=flops, bytes_accessed=2 * moved, transcendentals=0),
        name=name,
    )(scal, *args)


def spec(shape, index):
    return pl.BlockSpec(shape, index)


def held(*shape):
    return pl.BlockSpec(shape, lambda i, s: (0,) * len(shape), pipeline_mode=pl.Buffered(1))


def struct(*shape, dtype=BF16):
    return jax.ShapeDtypeStruct(shape, dtype)


def pack_qkv(scal, weights):
    rows, width = weights[0].shape
    pairs = width // (2 * PAIR)
    per = pairs // 2

    def kernel(s_ref, q_ref, k_ref, v_ref, own_ref, mine_ref):
        for i, ref in enumerate((q_ref, k_ref, v_ref)):
            own_ref[:, i * PAIR : (i + 1) * PAIR] = ref[...]
        start = pl.multiple_of(s_ref[1] * (rows // 2), rows // 2)
        mine_ref[...] = own_ref[pl.ds(start, rows // 2), :]

    block = spec((rows, PAIR), lambda p, s: (0, ((p // per) * 2 + s[2]) * per + p % per))
    return run(
        kernel, "pack_qkv", scal, (pairs,), [block] * 3,
        [
            spec((rows, 3 * PAIR), lambda p, s: (0, p)),
            spec((rows // 2, 3 * PAIR), lambda p, s: (0, p)),
        ],
        [struct(rows, 3 * PAIR * pairs), struct(rows // 2, 3 * PAIR * pairs)],
        weights,
    )


def pack_feed(scal, up, down, j, ranges, bit):
    rows, hidden = up.shape
    tile = hidden // (4 * ranges)
    columns = down.shape[1] // 2

    def kernel(s_ref, up_ref, down_ref, out_ref):
        out_ref[...] = jnp.where(s_ref[bit] == 0, up_ref[...], down_ref[...])

    return run(
        kernel, "pack_feed", scal, (2,),
        [
            spec((rows, tile), lambda t, s: (0, (t * 2 + s[2]) * ranges + j)),
            spec((tile, columns), lambda t, s: (s[2] * ranges + j, t)),
        ],
        spec((rows, tile), lambda t, s: (0, t)), struct(rows, 2 * tile), (up, down),
    )


def normalize(values):
    centred = values - jnp.mean(values, axis=-1, keepdims=True)
    spread = jnp.mean(centred * centred, axis=-1, keepdims=True)
    inverse = lax.rsqrt(spread + EPS)
    return centred * inverse, inverse


def first_norm(scal, tokens, received, gain, shift):
    rows, width = tokens.shape
    step = rows // 2

    def kernel(s_ref, t_ref, r_ref, gain_ref, shift_ref, x_ref, first_ref):
        x = jnp.where(s_ref[3] == 1, t_ref[...], r_ref[...])
        x_ref[...] = x
        normed, _ = normalize(x.astype(F32))
        first_ref[...] = (normed * gain_ref[...] + shift_ref[...]).astype(BF16)

    block = spec((step, width), lambda i, s: (i, 0))
    return run(
        kernel, "first_norm", scal, (2,), [block, block, held(1, width), held(1, width)],
        [block, block], [struct(rows, width)] * 2, (tokens, received, gain, shift),
    )


def project(scal, firsts, own, piece, beside, bias):
    local, width = firsts[0].shape
    rows, total = 2 * local, own.shape[1]
    block = 6 * PAIR
    half_rows, quarter_rows = width // 2, width // 4

    def kernel(
        s_ref, mine_ref, theirs_ref, own_ref, piece_ref, beside_ref, bias_ref, qkv_ref, w_ref,
        all_ref, sems,
    ):
        @pl.when(pl.program_id(0) == 0)
        def _():
            copies = [
                pltpu.make_async_copy(ref, all_ref.at[pl.ds(i * local, local)], sems.at[i])
                for i, ref in enumerate((mine_ref, theirs_ref))
            ]
            for copy in copies:
                copy.start()
            for copy in copies:
                copy.wait()

        half, low = s_ref[0], s_ref[1]
        other = (1 - half) * half_rows
        w_ref[pl.ds(pl.multiple_of(half * half_rows, half_rows), half_rows), :] = own_ref[...]
        start = pl.multiple_of(other + low * quarter_rows, quarter_rows)
        w_ref[pl.ds(start, quarter_rows), :] = piece_ref[...]
        start = pl.multiple_of(other + (1 - low) * quarter_rows, quarter_rows)
        w_ref[pl.ds(start, quarter_rows), :] = beside_ref[...]
        qkv_ref[...] = (contract(all_ref[...], w_ref[...], 1, 0) + bias_ref[...]).astype(BF16)

    def columns(size):
        return spec((size, block), lambda p, s: (0, p))

    anywhere = pl.BlockSpec(memory_space=pl.ANY)
    return run(
        kernel, "project", scal, (total // block,),
        [anywhere] * 2
        + [columns(half_rows), columns(quarter_rows), columns(quarter_rows), columns(1)],
        [columns(rows), columns(width), held(rows, width)],
        [struct(rows, total), struct(width, total), struct(rows, width)],
        (*firsts, own, piece, beside, bias), flops=2 * rows * width * total,
        scratch=[pltpu.SemaphoreType.DMA((2,))],
    )


def out_other(scal, mixed, weight, piece, beside):
    rows, set_width = mixed.shape
    local, width = rows // 2, weight.shape[1]
    block, small = set_width // 2, set_width // 4

    def kernel(s_ref, mixed_ref, own_ref, piece_ref, beside_ref, out_ref, set_ref):
        half, low = s_ref[0], s_ref[1]
        other = (1 - half) * block
        set_ref[pl.ds(pl.multiple_of(half * block, block), block), :] = own_ref[...]
        set_ref[pl.ds(pl.multiple_of(other + low * small, small), small), :] = piece_ref[...]
        start = pl.multiple_of(other + (1 - low) * small, small)
        set_ref[pl.ds(start, small), :] = beside_ref[...]
        out_ref[...] = contract(mixed_ref[...], set_ref[...], 1, 0).astype(BF16)

    return run(
        kernel, "out_other", scal, (1,),
        [
            spec((local, set_width), lambda i, s: (1, 0)),
            spec((block, width), lambda i, s: (s[2], 0)),
            held(small, width), held(small, width),
        ],
        [held(local, width), held(set_width, width)],
        [struct(local, width), struct(set_width, width)],
        (mixed, weight, piece, beside), flops=2 * local * set_width * width,
    )


def second_norm(scal, mixed, out_set, x, received, bias, gain, shift):
    rows, set_width = mixed.shape
    local, width = x.shape
    step = local // 2

    def kernel(
        s_ref, mixed_ref, w_ref, x_ref, r_ref, bias_ref, gain_ref, shift_ref, mid_ref, second_ref
    ):
        middle = contract(mixed_ref[...], w_ref[...], 1, 0) + r_ref[...].astype(F32)
        middle = middle + x_ref[...].astype(F32) + bias_ref[...]
        mid_ref[...] = middle
        normed, _ = normalize(middle)
        second_ref[...] = (normed * gain_ref[...] + shift_ref[...]).astype(BF16)

    block = spec((step, width), lambda i, s: (i, 0))
    return run(
        kernel, "second_norm", scal, (2,),
        [spec((step, set_width), lambda i, s: (i, 0)), held(set_width, width), block, block]
        + [held(1, width)] * 3,
        [block, block], [struct(local, width, dtype=F32), struct(local, width)],
        (mixed, out_set, x, received, bias, gain, shift), flops=2 * local * set_width * width,
    )


def norm_back_rows(grad, normed, inverse, gain):
    scaled = grad * gain
    first_term = jnp.mean(scaled, axis=-1, keepdims=True)
    second_term = jnp.mean(scaled * normed, axis=-1, keepdims=True)
    return inverse * (scaled - first_term - normed * second_term)


def column_sums(refs, values):
    @pl.when(pl.program_id(0) == 0)
    def _():
        refs[...] = jnp.zeros_like(refs)

    for i, value in enumerate(values):
        refs[i : i + 1, :] += jnp.sum(value, axis=0, keepdims=True)


def row_step(rows):
    return rows // 7 if rows % 112 == 0 else rows


def second_back(scal, grad, received, middle, dy, gain):
    local, width = middle.shape
    step = row_step(local)

    def kernel(s_ref, g_ref, r_ref, mid_ref, dy_ref, gain_ref, low_ref, sums_ref):
        grad = g_ref[...].astype(F32) + r_ref[...].astype(F32)
        normed, inverse = normalize(mid_ref[...])
        dy_wide = dy_ref[...].astype(F32)
        low = (dy_wide + norm_back_rows(grad, normed, inverse, gain_ref[...])).astype(BF16)
        low_ref[...] = low
        column_sums(sums_ref, (grad * normed, grad, dy_wide, low.astype(F32)))

    block = spec((step, width), lambda i, s: (i, 0))
    return run(
        kernel, "second_back", scal, (local // step,), [block] * 4 + [held(1, width)],
        [block, held(8, width)], [struct(local, width), struct(8, width, dtype=F32)],
        (grad, received, middle, dy, gain),
    )


def mixed_back(scal, lows, out_set, mixed):
    local, width = lows[0].shape
    rows, set_width = mixed.shape
    block = set_width // 2

    def kernel(
        s_ref, mine_ref, theirs_ref, w_ref, mixed_ref, d_ref, send_ref, keep_ref, low, sems
    ):
        @pl.when(pl.program_id(0) == 0)
        def _():
            copies = [
                pltpu.make_async_copy(ref, low.at[pl.ds(i * local, local)], sems.at[i])
                for i, ref in enumerate((mine_ref, theirs_ref))
            ]
            for copy in copies:
                copy.start()
            for copy in copies:
                copy.wait()

        d_ref[...] = contract(low[...], w_ref[...], 1, 1).astype(BF16)
        grad = contract(mixed_ref[...], low[...], 0, 0).astype(BF16)

        def store(goal):
            for c in range(2):
                for i in range(width // (2 * PAIR)):
                    start = (2 * i + c) * PAIR
                    goal[c * block : (c + 1) * block, i * PAIR : (i + 1) * PAIR] = (
                        grad[:, start : start + PAIR]
                    )

        @pl.when(pl.program_id(0) == s_ref[0])
        def _():
            store(keep_ref)

        @pl.when(pl.program_id(0) != s_ref[0])
        def _():
            store(send_ref)

    anywhere = pl.BlockSpec(memory_space=pl.ANY)
    across = spec((rows, block), lambda t, s: (0, t))
    return run(
        kernel, "mixed_back", scal, (2,),
        [anywhere] * 2 + [spec((block, width), lambda t, s: (t, 0)), across],
        [across, held(2 * block, width // 2), held(2 * block, width // 2)],
        [struct(rows, set_width)] + [struct(2 * block, width // 2)] * 2,
        (*lows, out_set, mixed), flops=4 * rows * set_width * width,
        scratch=[pltpu.VMEM((rows, width), BF16), pltpu.SemaphoreType.DMA((2,))],
    )


def first_grad(scal, dqkvs, weights):
    rows = dqkvs[0].shape[0]
    width = weights.shape[0]
    local = rows // 2
    count = len(dqkvs)
    step = width // 4

    def kernel(s_ref, *refs):
        left = jnp.concatenate([refs[j][...] for j in range(count)], axis=1)
        total = contract(left, refs[count][...], 1, 1)
        refs[-2][...] = total[:local].astype(BF16)
        refs[-1][...] = total[local:].astype(BF16)

    across = spec((local, step), lambda i, s: (0, i))
    return run(
        kernel, "first_grad", scal, (4,),
        [held(*a.shape) for a in dqkvs] + [spec((step, weights.shape[1]), lambda i, s: (i, 0))],
        [across, across], [struct(local, width)] * 2, (*dqkvs, weights),
        flops=sum(2 * rows * a.shape[1] * width for a in dqkvs),
    )


def first_back(scal, grad, received, x, wide, gain):
    local, width = x.shape
    step = row_step(local)

    def kernel(s_ref, g_ref, r_ref, x_ref, wide_ref, gain_ref, out_ref, sums_ref):
        grad = g_ref[...].astype(F32) + r_ref[...].astype(F32)
        normed, inverse = normalize(x_ref[...].astype(F32))
        total = wide_ref[...].astype(F32) + norm_back_rows(grad, normed, inverse, gain_ref[...])
        out_ref[...] = total.astype(BF16)
        column_sums(sums_ref, (grad * normed, grad))

    block = spec((step, width), lambda i, s: (i, 0))
    return run(
        kernel, "first_back", scal, (local // step,), [block] * 4 + [held(1, width)],
        [block, held(8, width)], [struct(local, width), struct(8, width, dtype=F32)],
        (grad, received, x, wide, gain),
    )


def layer_rows(scal, own, received, middle, bias):
    local, width = middle.shape
    step = row_step(local)

    def kernel(s_ref, o_ref, r_ref, mid_ref, bias_ref, out_ref):
        total = mid_ref[...] + o_ref[...].astype(F32) + r_ref[...].astype(F32) + bias_ref[...]
        out_ref[...] = total.astype(BF16)

    block = spec((step, width), lambda i, s: (i, 0))
    return run(
        kernel, "layer_rows", scal, (local // step,), [block] * 3 + [held(1, width)],
        block, struct(local, width), (own, received, middle, bias),
    )


def finish_feed_kernel(s_ref, *refs, tile):
    up_out, down_out = refs[8:]
    first = s_ref[2] == 0
    even = s_ref[1] == 0
    low_range = s_ref[4] == 0
    cores = []
    for refs_of in (refs[:4], refs[4:8]):
        whole, beside, along, last = [ref[...] for ref in refs_of]
        ranges = []
        for j in range(2):
            mine = jnp.where(low_range == (j == 0), whole, along)
            theirs = jnp.where(low_range == (j == 0), beside, last)
            ranges.append((jnp.where(even, mine, theirs), jnp.where(even, theirs, mine)))
        cores.append(ranges)
    for c in range(2):
        for j in range(2):
            up, down = [
                jnp.where(first == (c == 0), cores[0][j][kind], cores[1][j][kind]).astype(F32)
                for kind in range(2)
            ]
            down_out[c, j] = down
            for h in range(2):
                start = ((h * 2 + c) * 2 + j) * tile
                up_out[:, start : start + tile] = up[:, h * tile : (h + 1) * tile]


def finish_feed(scal, sums):
    rows, width = sums[0].shape
    steps = 4
    block = spec((rows // steps, width), lambda i, s: (i, 0))
    up, down = run(
        functools.partial(finish_feed_kernel, tile=rows), "finish_feed", scal, (steps,),
        [block] * 8,
        [
            spec((rows // steps, 4 * width), lambda i, s: (i, 0)),
            spec((2, 2, rows // steps, width), lambda i, s: (0, 0, i, 0)),
        ],
        [struct(rows, 4 * width, dtype=F32), struct(2, 2, rows, width, dtype=F32)],
        sums,
    )
    return up, down.reshape(4 * rows, width)


def finish_attention_kernel(s_ref, *refs, pairs, spans):
    q_out, k_out, v_out, out_out = refs[-4:]
    first, even = s_ref[2] == 0, s_ref[1] == 0
    half_pairs = pairs // 2
    for g, (begin, end) in enumerate(spans):
        mine, beside, mine_across, beside_across = [ref[...] for ref in refs[4 * g : 4 * g + 4]]
        own = jnp.concatenate(
            [jnp.where(even, mine, beside), jnp.where(even, beside, mine)], axis=0
        )
        other = jnp.concatenate(
            [
                jnp.where(even, mine_across, beside_across),
                jnp.where(even, beside_across, mine_across),
            ],
            axis=0,
        )
        for c in range(2):
            total = jnp.where(first == (c == 0), own, other).astype(F32)
            wide = total[: (end - begin) * 3 * PAIR].T
            for q in range(end - begin):
                pair = begin + q
                h, p = pair // half_pairs, pair % half_pairs
                goal = ((h * 2 + c) * half_pairs + p) * PAIR
                for i, out in enumerate((q_out, k_out, v_out)):
                    start = (q * 3 + i) * PAIR
                    out[:, goal : goal + PAIR] = wide[:, start : start + PAIR]
            if g == 0:
                rest = total[(end - begin) * 3 * PAIR :]
                rows = rest.shape[0] // 2
                out_out[c * rows : (c + 1) * rows, :PAIR] = rest[:rows]
                out_out[c * rows : (c + 1) * rows, PAIR:] = rest[rows:]


def finish_attention(scal, sums, spans):
    rows = sums[0].shape[1]
    pairs = spans[-1][1]
    steps = rows // PAIR
    return run(
        functools.partial(finish_attention_kernel, pairs=pairs, spans=spans), "finish_attention",
        scal, (steps,),
        [spec((values.shape[0], PAIR), lambda i, s: (0, i)) for values in sums],
        [spec((PAIR, 2 * pairs * PAIR), lambda i, s: (i, 0))] * 3
        + [spec((rows, 2 * PAIR), lambda i, s: (0, i))],
        [struct(rows, 2 * pairs * PAIR, dtype=F32)] * 3 + [struct(rows, 2 * rows, dtype=F32)],
        sums,
    )


def wide_back_kernel(
    tile, rows, padded, qkv_ref, grad_ref, out_ref, lse_ref, dqkv_ref, q_t, g_t, k_t, delta,
    dq_t, dk_t, dv_t,
):
    scale = HEAD_DIM**-0.5
    q_t[:, :rows] = qkv_ref[:, :PAIR].T
    g_t[:, :rows] = grad_ref[...].T
    if padded > rows:
        q_t[:, rows:] = jnp.zeros((PAIR, padded - rows), BF16)
        g_t[:, rows:] = jnp.zeros((PAIR, padded - rows), BF16)
        delta[:, rows:] = jnp.zeros((2, padded - rows), F32)
    k_t[...] = qkv_ref[:, PAIR : 2 * PAIR].T
    product = (grad_ref[...].astype(F32) * out_ref[...].astype(F32)).T
    delta[0:1, :rows] = jnp.sum(product[:HEAD_DIM, :], axis=0, keepdims=True)
    delta[1:2, :rows] = jnp.sum(product[HEAD_DIM:, :], axis=0, keepdims=True)
    dk_t[...] = jnp.zeros_like(dk_t)
    dv_t[...] = jnp.zeros_like(dv_t)

    def block(index, carry):
        columns = pl.ds(pl.multiple_of(index * tile, tile), tile)
        empty = jnp.zeros((HEAD_DIM, tile), BF16)
        for head in range(2):
            lanes = slice(head * HEAD_DIM, (head + 1) * HEAD_DIM)
            query = q_t[lanes, columns]
            grad = g_t[lanes, columns]
            query_pad = jnp.concatenate([query, empty] if head == 0 else [empty, query], axis=0)
            grad_pad = jnp.concatenate([grad, empty] if head == 0 else [empty, grad], axis=0)
            scores = contract(qkv_ref[:, PAIR : 2 * PAIR], query_pad, 1, 0)
            grad_probs = contract(qkv_ref[:, 2 * PAIR :], grad_pad, 1, 0)
            weights = jnp.exp2(scores * (scale * LOG2E) - lse_ref[head : head + 1, columns])
            grad_scores = (weights * (grad_probs - delta[head : head + 1, columns])).astype(BF16)
            dv_t[lanes, :] += contract(grad, weights.astype(BF16), 1, 1)
            dq_t[lanes, columns] = contract(k_t[lanes, :], grad_scores, 1, 0)
            dk_t[lanes, :] += contract(query, grad_scores, 1, 1)
        return carry

    lax.fori_loop(0, padded // tile, block, 0)
    dqkv_ref[:, :PAIR] = (dq_t[...].T[:rows, :] * scale).astype(BF16)
    dqkv_ref[:, PAIR : 2 * PAIR] = (dk_t[...].T * scale).astype(BF16)
    dqkv_ref[:, 2 * PAIR :] = dv_t[...].T.astype(BF16)


def wide_back(qkv, grad, out, lse, first_pair, last_pair, tile=256):
    rows, width = qkv.shape
    padded = -(-rows // tile) * tile
    lse = jnp.pad(lse, ((0, 0), (0, 0), (0, padded - lse.shape[2])))
    count = last_pair - first_pair
    return pl.pallas_call(
        functools.partial(wide_back_kernel, tile, rows, padded),
        grid=(count,),
        in_specs=[
            pl.BlockSpec((rows, 3 * PAIR), lambda i: (0, i + first_pair)),
            pl.BlockSpec((rows, PAIR), lambda i: (0, i + first_pair)),
            pl.BlockSpec((rows, PAIR), lambda i: (0, i + first_pair)),
            pl.BlockSpec((None, 2, lse.shape[2]), lambda i: (i + first_pair, 0, 0)),
        ],
        out_specs=pl.BlockSpec((rows, 3 * PAIR), lambda i: (0, i)),
        out_shape=jax.ShapeDtypeStruct((rows, 3 * PAIR * count), BF16),
        scratch_shapes=[
            pltpu.VMEM((PAIR, padded), BF16),
            pltpu.VMEM((PAIR, padded), BF16),
            pltpu.VMEM((PAIR, rows), BF16),
            pltpu.VMEM((2, padded), F32),
            pltpu.VMEM((PAIR, padded), F32),
            pltpu.VMEM((PAIR, rows), F32),
            pltpu.VMEM((PAIR, rows), F32),
        ],
        compiler_params=pltpu.CompilerParams(vmem_limit_bytes=VMEM_LIMIT),
        cost_estimate=pl.CostEstimate(
            flops=160 * rows * rows * PAIR * count,
            bytes_accessed=16 * rows * PAIR * count,
            transcendentals=2 * rows * rows * count,
        ),
        name="wide_back",
    )(qkv, grad, out, lse)


def wide_feed_kernel(
    half_ref, *refs, parts, make, chunk,
):
    xs, refs = refs[:parts], refs[parts:]
    dys, refs = refs[:parts], refs[parts:]
    if not make:
        x_t, refs = refs[0], refs[1:]
    up_ref, bias_ref, down_ref, *refs = refs
    hidden_ref, d_pre_ref, up_send, up_keep, down_send, down_keep, bias_grad_ref, *refs = refs
    if make:
        x_t, refs = refs[0], refs[1:]
    x, dy, sems = refs
    index = pl.program_id(0)
    half = half_ref[0]
    rows, width = x.shape
    block = rows // parts
    own = width // 2
    tile = up_ref.shape[1]

    @pl.when(index == 0)
    def _():
        copies = []
        for i in range(parts):
            part = pl.ds(i * block, block)
            copies.append(pltpu.make_async_copy(xs[i], x.at[part], sems.at[i]))
            copies.append(pltpu.make_async_copy(dys[i], dy.at[part], sems.at[parts + i]))
        for copy in copies:
            copy.start()
        for copy in copies:
            copy.wait()
        if make:
            x_t[...] = x[...].T

    bias_grad = jnp.zeros(bias_grad_ref.shape, F32)
    for start in range(0, rows, chunk):
        part = slice(start, start + chunk)
        pre = contract(x[part, :], up_ref[...], 1, 0) + bias_ref[...]
        d_hidden = contract(dy[part, :], down_ref[...], 1, 1)
        share = 0.5 * (1.0 + lax.erf(pre * 0.7071067811865476))
        hidden_ref[part, :] = (pre * share).astype(BF16)
        slope = share + pre * (jnp.exp(-0.5 * pre * pre) * 0.3989422804014327)
        d_low = (d_hidden * slope).astype(BF16)
        d_pre_ref[part, :] = d_low
        bias_grad = bias_grad + jnp.sum(d_low.astype(F32), axis=0, keepdims=True)
    bias_grad_ref[...] = bias_grad
    columns = pl.ds(pl.multiple_of(index * tile, tile), tile)
    mine = pl.ds(pl.multiple_of(half * own, own), own)
    theirs = pl.ds(pl.multiple_of((1 - half) * own, own), own)
    up_keep[:, columns] = contract(x_t[mine, :], d_pre_ref[...], 1, 0).astype(BF16)
    up_send[:, columns] = contract(x_t[theirs, :], d_pre_ref[...], 1, 0).astype(BF16)
    down_grad = contract(hidden_ref[...], dy[...], 0, 0).astype(BF16)

    @pl.when(index == half)
    def _():
        down_keep[...] = down_grad

    @pl.when(index != half)
    def _():
        down_send[...] = down_grad


def wide_feed(half, xs, dys, x_t, up, bias, down):
    parts = len(xs)
    width = xs[0].shape[1]
    rows = sum(part.shape[0] for part in xs)
    hidden = up.shape[1]
    tile = hidden // 2
    make = x_t is None
    chunk = rows // 2 if rows % 32 == 0 else rows
    anywhere = pl.BlockSpec(memory_space=pl.ANY)
    fixed = lambda shape: pl.BlockSpec(shape, lambda j, s: (0, 0), pipeline_mode=pl.Buffered(1))
    across = lambda size: pl.BlockSpec((size, tile), lambda j, s: (0, j))
    out_specs = [across(rows)] * 2 + [fixed((width // 2, hidden))] * 2
    out_specs += [fixed((tile, width))] * 2 + [across(1)]
    out_shape = [
        jax.ShapeDtypeStruct((rows, hidden), BF16),
        jax.ShapeDtypeStruct((rows, hidden), BF16),
        jax.ShapeDtypeStruct((width // 2, hidden), BF16),
        jax.ShapeDtypeStruct((width // 2, hidden), BF16),
        jax.ShapeDtypeStruct((tile, width), BF16),
        jax.ShapeDtypeStruct((tile, width), BF16),
        jax.ShapeDtypeStruct((1, hidden), F32),
    ]
    if make:
        out_specs.append(fixed((width, rows)))
        out_shape.append(jax.ShapeDtypeStruct((width, rows), BF16))
    return pl.pallas_call(
        functools.partial(wide_feed_kernel, parts=parts, make=make, chunk=chunk),
        grid_spec=pltpu.PrefetchScalarGridSpec(
            num_scalar_prefetch=1,
            grid=(2,),
            in_specs=[anywhere] * (2 * parts)
            + ([] if make else [fixed((width, rows))])
            + [across(width), across(1), pl.BlockSpec((tile, width), lambda j, s: (j, 0))],
            out_specs=out_specs,
            scratch_shapes=[
                pltpu.VMEM((rows, width), BF16),
                pltpu.VMEM((rows, width), BF16),
                pltpu.SemaphoreType.DMA((2 * parts,)),
            ],
        ),
        out_shape=out_shape,
        compiler_params=pltpu.CompilerParams(vmem_limit_bytes=VMEM_LIMIT),
        cost_estimate=pl.CostEstimate(
            flops=8 * rows * width * hidden,
            bytes_accessed=8 * rows * width + 8 * width * hidden,
            transcendentals=2 * rows * hidden,
        ),
        name="wide_feed",
    )(half.reshape(1), *xs, *dys, *(() if make else (x_t,)), up, bias, down)


def norm_parts(values, gain, shift):
    average = jnp.mean(values, axis=-1, keepdims=True)
    centred = values - average
    spread = jnp.mean(centred * centred, axis=-1, keepdims=True)
    inverse = lax.rsqrt(spread + EPS)
    normed = centred * inverse
    return (normed * gain + shift, normed, inverse)


def norm_back(grad, normed, inverse, gain):
    scaled = grad * gain
    first_term = jnp.mean(scaled, axis=-1, keepdims=True)
    second_term = jnp.mean(scaled * normed, axis=-1, keepdims=True)
    result = inverse * (scaled - first_term - normed * second_term)
    return (result, jnp.sum(grad * normed, axis=0), jnp.sum(grad, axis=0))


def pick(values, index, axis):
    return lax.dynamic_index_in_dim(values, index, axis, keepdims=False)


def join(own, other, index):
    return jnp.where(index == 0, jnp.stack([own, other]), jnp.stack([other, own]))


def after(values, *earlier):
    return lax.optimization_barrier((values,) + earlier)[0]


def wide_body(
    rep, grp, tokens, query_weight, key_weight, value_weight, query_bias, value_bias, out_weight,
    out_bias, first_gain, first_shift, second_gain, second_shift, up_weight, up_bias,
    down_weight, down_bias, cotangent,
):
    clips, local, width = tokens.shape
    assert clips == 1
    quarter = grp // 2
    ring = rep // 2
    deep = ring // 2
    core = lax.axis_index("core")
    half = lax.axis_index("half")
    gq = lax.axis_index("gq")
    place = lax.axis_index("rz")
    low = place % 2
    high = place // 2
    own_rows = width // grp
    pairs = own_rows // PAIR
    hidden = up_weight.shape[1]
    set_hidden = hidden // grp
    ranges = max(1, set_hidden // width)
    tile = set_hidden // (2 * ranges)

    there = []
    for b in range(2):
        for h in range(2):
            for q in range(quarter):
                g = h * quarter + q
                source = (b * 2 + h) * quarter + q
                target = ((g % 2) * 2 + b) * quarter + g // 2
                if source != target:
                    there.append((source, target))
    back = [(target, source) for source, target in there]
    block = half * quarter + gq
    stays = (block % 2 == core) & (block // 2 == gq) & (half == core)
    axes = ("core", "half", "gq")
    beside = [(i, i ^ 1) for i in range(ring)]

    def move(values, route):
        return jnp.where(stays, values, lax.ppermute(values, axes, route))

    def swap_half(values):
        return lax.ppermute(values, "half", SWAP)

    def swap_core(values):
        return lax.ppermute(values, "core", SWAP)

    def spread(values):
        if grp == 2:
            return [values, swap_core(values)]
        return [lax.all_gather(values, ("gq", "core"), axis=0, tiled=True)]

    def collect(values):
        if grp == 2:
            other = swap_core(values(slice(local, None)).astype(BF16))
            return values(slice(None, local)) + other.astype(F32)
        return lax.psum_scatter(
            values(slice(None)).astype(BF16), ("gq", "core"), scatter_dimension=0, tiled=True
        ).astype(F32)

    def other_half(pieces):
        mine = pick(jnp.stack(pieces), low, 0)
        first = swap_half(mine)
        second = lax.ppermute(first, "rz", beside)
        return first, jnp.where(low == 0, first, second), jnp.where(low == 0, second, first)

    def by_half(own, other):
        return join(own, other, half).reshape(-1, own.shape[-1])

    def set_columns(values, inner=1):
        parts = values.reshape(values.shape[0], 2, quarter, 2, inner, -1)
        return pick(parts, core, 3).transpose(0, 2, 3, 1, 4)

    def gather_rows(values):
        if quarter > 1:
            values = lax.all_to_all(values, "gq", split_axis=1, concat_axis=0, tiled=True)
        return values.reshape(-1, values.shape[-1])

    def set_entries(values, inner=1):
        parts = values.reshape(2, quarter, 2, inner, -1)
        return pick(pick(parts, core, 2), gq, 1).transpose(1, 0, 2).reshape(inner, 1, -1)

    clip_tokens = move(tokens.reshape(local, width), there)
    vectors = jnp.concatenate(
        [query_bias, value_bias, out_bias, first_gain, first_shift, second_gain, second_shift,
         down_bias, up_bias]
    )
    if quarter > 1:
        vectors = lax.all_gather(vectors, "gq", axis=0)
    vectors = join(vectors, swap_half(vectors), half).reshape(grp, -1)
    (full_qbias, full_vbias, full_obias, gain_one, shift_one, gain_two, shift_two, full_dbias) = [
        vectors[:, i * own_rows : (i + 1) * own_rows].reshape(-1) for i in range(8)
    ]
    bias_sets = set_entries(vectors[:, 8 * own_rows :].reshape(-1), ranges)

    parts = [
        set_columns(w).reshape(own_rows, quarter, pairs, PAIR)
        for w in (query_weight, key_weight, value_weight)
    ]
    own_qkv = gather_rows(jnp.stack(parts, axis=3).reshape(own_rows, quarter, 3 * own_rows))
    own_qkv = own_qkv.reshape(2, -1, 3 * own_rows)
    qkv_x, low_rows, high_rows = other_half([own_qkv[0], own_qkv[1]])
    qkv_weight = by_half(
        own_qkv.reshape(-1, 3 * own_rows), jnp.concatenate([low_rows, high_rows], axis=0)
    )
    own_out = pick(out_weight.reshape(2, -1, width), core, 0)
    out_x, low_rows, high_rows = other_half(
        [after(own_out, qkv_x)[: own_rows // 4], own_out[own_rows // 4 :]]
    )
    out_set = by_half(own_out, jnp.concatenate([low_rows, high_rows], axis=0))

    own_up = set_columns(up_weight, ranges)
    own_down = pick(down_weight.reshape(2, ranges, tile, width), core, 0)
    up_sets, down_sets, stages = [], [], [out_x]
    for j in range(ranges):
        up_part = gather_rows(own_up[:, :, j].reshape(own_rows, quarter, 2 * tile))
        down_part = own_down[j]
        if up_part.shape == down_part.shape:
            stage, other_up, other_down = other_half([after(up_part, stages[-1]), down_part])
        else:
            stage, other_up = swap_half(after(up_part, stages[-1])), None
            other_up, other_down = stage, swap_half(down_part)
        stages.append(stage)
        up_sets.append(by_half(up_part, other_up))
        down_sets.append(by_half(down_part, other_down))
    grad_out = move(after(cotangent.reshape(local, width), stages[1]), there)

    zeros = jnp.zeros((1, own_rows), F32)
    qkv_bias = jnp.stack(
        [
            b.reshape(pairs, PAIR)
            for b in (set_entries(full_qbias), zeros, set_entries(full_vbias))
        ],
        axis=1,
    ).reshape(1, 3 * own_rows)

    inputs = clip_tokens.astype(F32)
    first_norm, first_normed, first_inverse = norm_parts(inputs, gain_one, shift_one)
    first = jnp.concatenate(spread(first_norm.astype(BF16)), axis=0)
    qkv = (contract(first, qkv_weight, 1, 0) + qkv_bias).astype(BF16)
    if pairs > 1:
        kept = attend(qkv, 0, pairs // 2)
        mixed, lse = attend(qkv, pairs // 2, pairs, kept)
    else:
        mixed, lse = attend(qkv, 0, pairs)
    middle = collect(lambda rows: contract(mixed[rows], out_set, 1, 0)) + inputs + full_obias
    second_norm, second_normed, second_inverse = norm_parts(middle, gain_two, shift_two)
    seconds = spread(second_norm.astype(BF16))
    grads_out = spread(grad_out)
    x_t = None
    feeds = []
    for j in range(ranges):
        outs = wide_feed(
            half, seconds, grads_out, x_t, up_sets[j],
            bias_sets[j] if j == 0 else after(bias_sets[j], feeds[-1][6]), down_sets[j],
        )
        x_t = outs[7] if j == 0 else x_t
        feeds.append(outs)

    def reduce_ring(pair):
        send, keep = pair
        total = keep.astype(F32) + lax.ppermute(send, "rz", beside).astype(F32)
        total = total.astype(BF16).reshape(deep, -1, keep.shape[-1])
        shifts = range(1, deep)

        def route(shift):
            return [(i, (i + 2 * shift) % ring) for i in range(ring)]

        pieces = [
            lax.ppermute(pick(total, (high + s) % deep, 0), "rz", route(s)) for s in shifts
        ]
        piece = pick(total, high, 0).astype(F32)
        for other in pieces:
            piece = piece + other.astype(F32)
        piece = piece.astype(BF16)
        gathered = [piece] + [lax.ppermute(piece, "rz", route(s)) for s in shifts]
        whole = jnp.stack(
            [
                functools.reduce(
                    lambda rest, s: jnp.where((high - s) % deep == i, gathered[s], rest),
                    shifts,
                    piece,
                )
                for i in range(deep)
            ]
        ).reshape(keep.shape)
        return whole, lax.ppermute(whole, "rz", beside)

    def reduce_parts(parts):
        stacked = jnp.stack(parts)
        own, other = reduce_ring((pick(stacked, 1 - low, 0), pick(stacked, low, 0)))
        return jnp.where(low == 0, own, other), jnp.where(low == 0, other, own)

    def add_half(keep, send):
        return (keep.astype(F32) + swap_half(send).astype(F32)).astype(BF16)

    def reduce_rows(values):
        size = values.shape[0]
        if size % (16 * ring):
            return lax.psum(values, "rz")
        return jnp.concatenate(reduce_parts([values[: size // 2], values[size // 2 :]]), axis=0)

    def scatter_half(values):
        values = values.reshape(2, -1, values.shape[-1])
        return add_half(pick(values, half, 0), pick(values, 1 - half, 0))

    sums_feed = []
    for outs in feeds:
        up_part, down_part = add_half(outs[3], outs[2]), add_half(outs[5], outs[4])
        if up_part.shape == down_part.shape:
            sums_feed.extend(reduce_parts([up_part, down_part]))
        else:
            sums_feed.extend([reduce_rows(up_part), reduce_rows(down_part)])

    grad_wide = grad_out.astype(F32)
    grad_second = collect(
        lambda rows: functools.reduce(
            jnp.add, [contract(feeds[j][1][rows], up_sets[j], 1, 1) for j in range(ranges)]
        )
    )
    grad_second, grad_gain_two, grad_shift_two = norm_back(
        grad_second, second_normed, second_inverse, gain_two
    )
    grad_middle = grad_wide + grad_second
    grad_middle_low = grad_middle.astype(BF16)
    grad_middle_all = jnp.concatenate(spread(grad_middle_low), axis=0)
    grad_mixed = contract(grad_middle_all, out_set, 1, 1).astype(BF16)
    out_half = reduce_rows(scatter_half(contract(mixed, grad_middle_all, 0, 0).astype(BF16)))
    spans = [(0, pairs // 2), (pairs // 2, pairs)] if pairs > 1 else [(0, pairs)]
    dqkvs, qkv_halves = [], []
    for begin, end in spans:
        gate = lse if not dqkvs else after(lse, qkv_halves[-1])
        dqkvs.append(wide_back(qkv, grad_mixed, mixed, gate, begin, end))
        qkv_halves.append(contract(first, dqkvs[-1], 0, 0).astype(BF16))
    qkv_halves = [reduce_rows(scatter_half(values)) for values in qkv_halves]

    result = collect(
        lambda rows: functools.reduce(
            jnp.add, [contract(feeds[j][0][rows], down_sets[j], 1, 0) for j in range(ranges)]
        )
    )
    result = (middle + result + full_dbias).astype(BF16)
    layer_out = move(result, back).reshape(1, local, width)

    def weight_of(span):
        return qkv_weight[:, span[0] * 3 * PAIR : span[1] * 3 * PAIR]

    grad_first_norm = collect(
        lambda rows: functools.reduce(
            jnp.add,
            [contract(d[rows], weight_of(span), 1, 1) for d, span in zip(dqkvs, spans)],
        )
    )
    grad_first, grad_gain_one, grad_shift_one = norm_back(
        grad_first_norm, first_normed, first_inverse, gain_one
    )
    tokens_grad = move((grad_middle + grad_first).astype(BF16), back).reshape(1, local, width)

    out_weight_grad = join(out_half, swap_core(out_half), core).reshape(-1, width).astype(F32)
    if True:

        def finish_columns(values):
            values = values.reshape(quarter, own_rows, 1, -1)
            values = lax.all_to_all(values, "gq", split_axis=0, concat_axis=2, tiled=True)
            values = values.reshape(own_rows, quarter, -1)
            return join(values, swap_core(values), core).transpose(1, 0, 2, 3)

        def natural_columns(values, inner=1):
            values = values.reshape(own_rows, 2, quarter, inner, 2, -1)
            return values.transpose(0, 4, 2, 1, 3, 5).reshape(own_rows, -1).astype(F32)

        ups = jnp.stack([finish_columns(values) for values in sums_feed[::2]], axis=3)
        up_weight_grad = natural_columns(ups, ranges)
        downs = jnp.stack(sums_feed[1::2])
        down_weight_grad = join(downs, swap_core(downs), core).reshape(-1, width).astype(F32)
        columns = jnp.concatenate([finish_columns(values) for values in qkv_halves], axis=3)
        columns = columns.reshape(own_rows, 2, quarter, pairs, 3, PAIR)
        query_weight_grad, key_weight_grad, value_weight_grad = [
            natural_columns(columns[:, :, :, :, i]) for i in range(3)
        ]

    def place_entries(values, inner=1):
        values = values.reshape(inner, 2, 1, 1, -1).transpose(1, 2, 3, 0, 4)
        shape = (2, quarter, 2) + values.shape[3:]
        zero = jnp.zeros((), core.dtype)
        return lax.dynamic_update_slice(
            jnp.zeros(shape, F32), values, (zero, gq, core, zero, zero)
        ).reshape(grp, -1)

    dqkv_sums = jnp.concatenate([jnp.sum(d.astype(F32), axis=0) for d in dqkvs])
    dqkv_sums = dqkv_sums.reshape(pairs, 3, PAIR)
    sums = [
        place_entries(dqkv_sums[:, 0]),
        place_entries(dqkv_sums[:, 2]),
        jnp.sum(grad_middle_low.astype(F32), axis=0),
        grad_gain_one, grad_shift_one, grad_gain_two, grad_shift_two,
        jnp.sum(grad_wide, axis=0),
        place_entries(jnp.stack([outs[6] for outs in feeds]), ranges),
    ]
    sums = jnp.concatenate([s.reshape(grp, -1) for s in sums], axis=1)
    if grp == 2 and ring & (ring - 1) == 0:
        sums = sums + swap_core(sums)
        sums = pick(sums, half, 0) + swap_half(pick(sums, 1 - half, 0))
        step = 1
        while step < ring:
            sums = sums + lax.ppermute(sums, "rz", [(i, i ^ step) for i in range(ring)])
            step *= 2
    else:
        sums = lax.psum(sums, ("rz", "core", "half", "gq"))
        sums = pick(sums, half * quarter + gq, 0)
    small = [sums[i * own_rows : (i + 1) * own_rows] for i in range(8)]
    return (
        layer_out, tokens_grad, query_weight_grad, key_weight_grad, value_weight_grad,
        small[0], small[1], out_weight_grad, small[2], small[3], small[4], small[5], small[6],
        up_weight_grad, sums[8 * own_rows :], down_weight_grad, small[7],
    )


class Order:
    def __init__(self):
        self.before = ()

    def pin(self, *values):
        pinned = lax.optimization_barrier(values + self.before)[: len(values)]
        self.before = tuple(pinned) + self.before
        return pinned[0] if len(values) == 1 else list(pinned)

    def fence(self, *values):
        self.before = values


class Steps:
    def __init__(self, steps):
        self.steps = steps
        self.waiting = next(steps)


def advance(order, *chains):
    pinned = order.pin(*[values for chain in chains for values in chain.waiting])
    pinned = list(pinned) if isinstance(pinned, (list, tuple)) else [pinned]
    for chain in chains:
        count = len(chain.waiting)
        values, pinned = pinned[:count], pinned[count:]
        chain.waiting = chain.steps.send(values)


def line_steps(order, deep, parts, result):
    place = lax.axis_index("line")
    bits = range((deep - 1).bit_length())

    def exchange(values, bit):
        return lax.ppermute(values, "line", [(i, i ^ (1 << bit)) for i in range(deep)])

    for bit in bits:
        even = (place >> bit) % 2 == 0
        keep, send = order.pin(jnp.where(even, *parts), jnp.where(even, *parts[::-1]))
        (other,) = yield [exchange(send, bit)]
        total = add_low(keep, other)
        size = total.shape[0] // 2
        parts = (total[:size], total[size:])
    for bit in reversed(bits):
        total = order.pin(total)
        (other,) = yield [exchange(total, bit)]
        total = join(total, other, (place >> bit) % 2).reshape(-1, total.shape[-1])
    whole = order.pin(total)
    beside, across = yield [lax.ppermute(whole, "low", SWAP), lax.ppermute(whole, "core", SWAP)]
    crossed = lax.ppermute(beside, "core", SWAP)
    (crossed,) = yield [crossed]
    result.extend([whole, beside, across, crossed])
    yield []


def range_steps(order, deep, parts, result):
    place = lax.axis_index("line")
    bits = range((deep - 1).bit_length())

    def exchange(values, bit):
        return lax.ppermute(values, "line", [(i, i ^ (1 << bit)) for i in range(deep)])

    for bit in bits:
        even = (place >> bit) % 2 == 0
        keep, send = order.pin(jnp.where(even, *parts), jnp.where(even, *parts[::-1]))
        (other,) = yield [exchange(send, bit)]
        total = add_low(keep, other)
        size = total.shape[0] // 2
        parts = (total[:size], total[size:])
    for bit in reversed(bits[1:]):
        total = order.pin(total)
        (other,) = yield [exchange(total, bit)]
        total = join(total, other, (place >> bit) % 2).reshape(-1, total.shape[-1])
    whole = order.pin(total)
    beside, along = yield [lax.ppermute(whole, "low", SWAP), exchange(whole, 0)]
    last, crossed = yield [lax.ppermute(along, "low", SWAP), lax.ppermute(whole, "core", SWAP)]
    rest = yield [lax.ppermute(values, "core", SWAP) for values in (beside, along, last)]
    result.extend([whole, beside, along, last, crossed, *rest])
    yield []


def plane_steps(order, low, deep, send, keep, result, more=()):
    send, keep = order.pin(send, keep)
    other, *more_in = yield [lax.ppermute(send, "half", SWAP), *more[1:]]
    total = add_low(keep, other)
    if more:
        total = jnp.concatenate([total, add_low(more[0], more_in[0])], axis=0)
    size = total.shape[0] // 2
    parts = (total[:size], total[size:])
    even = low == 0
    keep, send = order.pin(jnp.where(even, *parts), jnp.where(even, *parts[::-1]))
    (other,) = yield [lax.ppermute(send, "low", SWAP)]
    total = add_low(keep, other)
    size = total.shape[0] // 2
    yield from line_steps(order, deep, (total[:size], total[size:]), result)


def vector_steps(order, half, deep, entries, result):
    def line(values, bit):
        return lax.ppermute(values, "line", [(i, i ^ (1 << bit)) for i in range(deep)])

    entries = order.pin(entries)
    (other,) = yield [lax.ppermute(entries, "core", SWAP)]
    entries = entries + other
    keep, send = order.pin(pick(entries, half, 0), pick(entries, 1 - half, 0))
    (other,) = yield [lax.ppermute(send, "half", SWAP)]
    total = order.pin(keep + other)
    for bit in range((deep - 1).bit_length()):
        (other,) = yield [line(total, bit)]
        total = order.pin(total + other)
    (other,) = yield [lax.ppermute(total, "low", SWAP)]
    result.append(total + other)
    yield []


def add_low(left, right):
    return (left.astype(F32) + right.astype(F32)).astype(BF16)


def after_all(values, *gates):
    if not gates:
        return tuple(values)
    return lax.optimization_barrier(tuple(values) + gates)[: len(values)]


def pair_body(
    rep, grp, tokens, query_weight, key_weight, value_weight, query_bias, value_bias, out_weight,
    out_bias, first_gain, first_shift, second_gain, second_shift, up_weight, up_bias,
    down_weight, down_bias, cotangent,
):
    clips, local, width = tokens.shape
    assert clips == 1
    ring = rep // 2
    deep = ring // 2
    core, half = lax.axis_index("core"), lax.axis_index("half")
    low, high = lax.axis_index("low"), lax.axis_index("line") % 2
    own_rows = width // 2
    pairs = own_rows // PAIR
    hidden = up_weight.shape[1]
    stays = core == half
    scal = jnp.stack([half, low, core, stays.astype(jnp.int32), high]).astype(jnp.int32)
    cross = [(1, 2), (2, 1)]

    def swap_half(values):
        return lax.ppermute(values, "half", SWAP)

    def swap_core(values):
        return lax.ppermute(values, "core", SWAP)

    def swap_low(values):
        return lax.ppermute(values, "low", SWAP)

    def swap_high(values):
        return lax.ppermute(values, "line", [(i, i ^ 1) for i in range(deep)])

    def cross_over(values):
        return lax.ppermute(values, ("core", "half"), cross)

    tokens, cotangent = tokens.reshape(local, width), cotangent.reshape(local, width)

    tokens_in = cross_over(tokens)
    own_qkv, mine = pack_qkv(scal, (query_weight, key_weight, value_weight))
    qkv_x = swap_half(mine)
    packed = [pack_feed(scal, up_weight, down_weight, j, 2, (1, 4)[j]) for j in range(2)]
    vectors = jnp.concatenate(
        [after(query_bias, mine, *packed), value_bias, out_bias, first_gain, first_shift,
         second_gain, second_shift, down_bias, up_bias]
    )
    order = Order()
    tokens_in, qkv_x, vectors, vectors_in, *packed = order.pin(
        tokens_in, qkv_x, vectors, swap_half(vectors), *packed
    )
    qkv_y = swap_low(qkv_x)
    feed_x = [swap_half(packed[0])]
    vectors = join(vectors, vectors_in, half)
    (full_qbias, full_vbias, full_obias, gain_one, shift_one, gain_two, shift_two, full_dbias) = [
        vectors[:, i * own_rows : (i + 1) * own_rows].reshape(1, width) for i in range(8)
    ]

    def set_entries(values, inner=1):
        return pick(values.reshape(2, 2, inner, -1), core, 1).transpose(1, 0, 2).reshape(inner, -1)

    bias_set = set_entries(vectors[:, 8 * own_rows :], 2).reshape(1, -1)
    quarter = own_rows // 4
    out_mine = lax.dynamic_slice(
        out_weight, (core * (own_rows // 2) + low * quarter, 0 * core), (quarter, width)
    )
    x, first = first_norm(scal, tokens, tokens_in, gain_one, shift_one)
    x, first = order.pin(x, first)
    order.fence(x)
    first, qkv_y, feed_x[0] = order.pin(first, qkv_y, feed_x[0])
    first_in = order.pin(swap_core(first))
    feed_y = [swap_low(feed_x[0])]
    out_x = swap_half(order.pin(out_mine))
    feed_x.append(swap_half(order.pin(packed[1])))
    zeros = jnp.zeros((pairs, PAIR), F32)
    qkv_bias = jnp.stack(
        [set_entries(full_qbias).reshape(pairs, PAIR), zeros,
         set_entries(full_vbias).reshape(pairs, PAIR)],
        axis=1,
    ).reshape(1, 3 * own_rows)
    qkv, qkv_weight, first_all = project(
        scal, (first, first_in), own_qkv, qkv_x, qkv_y, qkv_bias
    )

    qkv, out_x = order.pin(qkv, out_x)
    order.fence(qkv)
    out_y = swap_low(out_x)
    mixed, lse = attend(qkv, 0, pairs - 1)
    lse, out_y, feed_x[1] = order.pin(lse, out_y, feed_x[1])
    feed_y.append(swap_high(feed_x[1]))
    cotangent_in = cross_over(after(cotangent, lse))
    mixed, lse = attend(qkv, pairs - 1, pairs, (mixed, lse))
    mixed = order.pin(mixed)
    out_part, out_set = out_other(scal, mixed, out_weight, out_x, out_y)
    out_part, cotangent_in, *feed_y = order.pin(out_part, cotangent_in, *feed_y)
    out_in = swap_core(out_part)
    grad_out = order.pin(jnp.where(stays, cotangent, cotangent_in))
    grad_out_in = swap_core(grad_out)
    middle, second = second_norm(
        scal, mixed, out_set, x, order.pin(out_in), full_obias, gain_two, shift_two
    )
    middle, second = order.pin(middle, second)
    order.fence(second)
    second_in = swap_core(second)

    second_in = order.pin(second_in)
    (
        out_own, out_part, dx_own, dx_part, up_send, up_keep, down_send, down_keep, low_send,
        low_keep, up_bias_grad,
    ) = feed(
        scal, (second, second_in), (grad_out, grad_out_in), up_weight, down_weight,
        (feed_x[0], feed_y[0], feed_x[1], feed_y[1]), bias_set,
    )
    dx_part, up_send, down_send, low_send, out_part = order.pin(
        dx_part, up_send, down_send, low_send, out_part
    )
    order.fence(dx_part)
    dx_in = swap_core(dx_part)
    up_in, down_in, low_in = swap_half(up_send), swap_half(down_send), swap_low(low_send)
    grad_low, sums_two = second_back(
        scal, dx_own, order.pin(dx_in), middle, grad_out, gain_two
    )
    grad_low = order.pin(grad_low)
    grad_low_in = swap_core(grad_low)
    grad_low_in = order.pin(grad_low_in)
    grad_mixed, out_send, out_keep = mixed_back(scal, (grad_low, grad_low_in), out_set, mixed)
    grad_mixed = order.pin(grad_mixed)

    backs = []

    def back(pair):
        gate = order.pin(lse)
        named = jnp.concatenate([scal, jnp.full((1,), pair, jnp.int32)])
        backs.append(attend_back(named, qkv, grad_mixed, mixed, gate, first_all))
        backs[-1] = order.pin(*backs[-1])
        order.fence(backs[-1][3])

    back(0)
    up_in, down_in, low_in = order.pin(up_in, down_in, low_in)
    up_sum, down_sum = add_low(up_keep, up_in), add_low(down_keep, down_in)
    even = low == 0
    low_mine, low_other = order.pin(
        jnp.where(even, up_sum, down_sum), jnp.where(even, down_sum, up_sum)
    )
    one_in = lax.ppermute(low_other, "low", SWAP)
    range_sum = add_low(low_keep, low_in).reshape(2, own_rows, width)
    half_send, half_keep = order.pin(pick(range_sum, 1 - half, 0), pick(range_sum, half, 0))
    half_in = swap_half(half_send)
    out_half_in = swap_half(order.pin(out_send))

    back(1)
    one_in, half_in = order.pin(one_in, half_in)
    feed_parts, early_parts, late_parts, vector_parts = [], [], [], []
    ranges = Steps(
        range_steps(
            order, deep, (add_low(low_mine, one_in), add_low(half_keep, half_in)), feed_parts
        )
    )
    early = Steps(
        plane_steps(
            order, low, deep,
            jnp.concatenate([backs[0][1], backs[1][1]], axis=0),
            jnp.concatenate([backs[0][2], backs[1][2]], axis=0), early_parts,
            more=(out_keep, out_half_in),
        )
    )

    back(2)
    advance(order, ranges, early)
    out_in = swap_core(order.pin(out_part))

    back(3)
    out_in = order.pin(out_in)
    late = Steps(
        plane_steps(
            order, low, deep,
            jnp.concatenate([backs[2][1], backs[3][1]], axis=0),
            jnp.concatenate([backs[2][2], backs[3][2]], axis=0), late_parts,
        )
    )
    advance(order, ranges, early)
    first_own, first_part = first_grad(
        scal, [order.pin(backs[0][0])] + [b[0] for b in backs[1:]], qkv_weight
    )
    first_own, first_part = order.pin(first_own, first_part)
    order.fence(first_part)
    advance(order, late, early)
    first_part_in = swap_core(order.pin(first_part))
    advance(order, ranges)
    tokens_out, sums_one = first_back(
        scal, first_own, order.pin(first_part_in), x, grad_low, gain_one
    )
    tokens_out, sums_one = order.pin(tokens_out, sums_one)
    order.fence(sums_one)
    layer = order.pin(layer_rows(scal, out_own, out_in, after(middle, sums_one), full_dbias))
    advance(order, early, late, ranges)

    def place_entries(values, inner=1):
        values = values.reshape(inner, 2, 1, -1).transpose(1, 2, 0, 3)
        empty = jnp.zeros_like(values)
        return join(values[:, 0], empty[:, 0], core).transpose(1, 0, 2, 3).reshape(2, -1)

    parts = jnp.concatenate([b[3][0] for b in backs]).reshape(pairs, 3, PAIR)
    entries = [
        place_entries(parts[:, 0]), place_entries(parts[:, 2]), sums_two[3], sums_one[0],
        sums_one[1], sums_two[0], sums_two[1], sums_two[2], place_entries(up_bias_grad, 2),
    ]
    entries = jnp.concatenate([e.reshape(2, -1) for e in entries], axis=1)
    vectors = Steps(vector_steps(order, half, deep, entries, vector_parts))
    advance(order, vectors)
    advance(order, vectors, early, late)
    tokens_in = cross_over(order.pin(tokens_out))
    layer_in = cross_over(layer)
    advance(order, vectors, early, late)
    advance(order, vectors, late)
    advance(order, early, ranges, late)
    advance(order, ranges, vectors, early)
    up_weight_grad, down_weight_grad = order.pin(*finish_feed(scal, feed_parts))
    advance(order, late)
    advance(order, late)
    (entries,) = vector_parts
    query_weight_grad, key_weight_grad, value_weight_grad, out_weight_grad = finish_attention(
        scal, (*early_parts, *late_parts), ((0, 2), (2, 4))
    )
    layer_out = jnp.where(stays, layer, layer_in)
    tokens_grad = jnp.where(stays, tokens_out, tokens_in)
    small = [entries[i * own_rows : (i + 1) * own_rows] for i in range(8)]
    return (
        layer_out.reshape(1, local, width), tokens_grad.reshape(1, local, width),
        query_weight_grad, key_weight_grad, value_weight_grad, small[0], small[1],
        out_weight_grad, small[2], small[3], small[4], small[5], small[6], up_weight_grad,
        entries[8 * own_rows :], down_weight_grad, small[7],
    )


def solution(mesh):
    rep, grp = mesh.shape["rep"], mesh.shape["grp"]
    paired = grp == 2 and rep >= 8 and rep & (rep - 1) == 0
    if paired:
        sizes, names = (rep // 4, 2, 2, 2), ("line", "low", "core", "half")
        reps, groups, body = ("line", "low", "core"), "half", pair_body
    else:
        sizes, names = (rep // 2, 2, 2, grp // 2), ("rz", "core", "half", "gq")
        reps, groups, body = ("rz", "core"), ("half", "gq"), wide_body
    clip, matrix, vector = P(reps, groups, None), P(groups, None), P(groups)
    return jax.shard_map(
        functools.partial(body, rep, grp),
        mesh=Mesh(mesh.devices.reshape(sizes), names),
        in_specs=(
            clip, matrix, matrix, matrix, vector, vector, matrix, vector, vector, vector, vector,
            vector, matrix, vector, matrix, vector, clip,
        ),
        out_specs=(
            clip, clip, matrix, matrix, matrix, vector, vector, matrix, vector, vector, vector,
            vector, vector, matrix, vector, matrix, vector,
        ),
        check_vma=False,
    )
```

```python
import functools

import jax
import jax.numpy as jnp
from jax import lax
from jax.experimental import pallas as pl
from jax.experimental.pallas import tpu as pltpu
from jax.sharding import Mesh
from jax.sharding import PartitionSpec as P

HEAD_DIM = 64
PAIR = 2 * HEAD_DIM
EPS = 1e-06
LOG2E = 1.4426950408889634
F32 = jnp.float32
BF16 = jnp.bfloat16
SWAP = [(0, 1), (1, 0)]
VMEM_LIMIT = 62 << 20


def contract(left, right, left_dim, right_dim):
    return lax.dot_general(
        left, right, (((left_dim,), (right_dim,)), ((), ())), preferred_element_type=F32
    )


def padded_rows(rows, tile):
    full = rows // tile
    return full * tile + -(-(rows - full * tile) // PAIR) * PAIR


def walk(rows, tile, start, finish):
    full = rows // tile
    rest = padded_rows(rows, tile) - full * tile
    start(0, pl.ds(0, tile), tile)

    def step(columns, size, following, following_size):
        start(1, columns, size)
        finish(0, columns, size)
        if following is not None:
            start(0, following, following_size)
        finish(1, columns, size)

    def block(index, carry):
        first = pl.multiple_of(index * tile, tile)
        following = pl.multiple_of(index * tile + tile, tile)
        step(pl.ds(first, tile), tile, pl.ds(following, tile), tile)
        return carry

    lax.fori_loop(0, full - 1, block, 0)
    last = pl.ds(full * tile, rest) if rest else None
    step(pl.ds((full - 1) * tile, tile), tile, last, rest)
    if rest:
        step(last, rest, None, 0)


def one_head(values_t, head, columns, size):
    empty = jnp.zeros((HEAD_DIM, size), BF16)
    values = values_t[head * HEAD_DIM : (head + 1) * HEAD_DIM, columns]
    return jnp.concatenate([values, empty] if head == 0 else [empty, values], axis=0)


def attend_kernel(tile, rows, padded, qkv_ref, out_ref, lse_ref, q_t, v_t, out_t, scores):
    scale = HEAD_DIM**-0.5 * LOG2E
    ones = jnp.ones((16, rows), BF16)
    q_t[:, :rows] = qkv_ref[:, :PAIR].T
    if padded > rows:
        q_t[:, rows:] = jnp.zeros((PAIR, padded - rows), BF16)
    values_t = qkv_ref[:, 2 * PAIR :].T
    step = HEAD_DIM + 16
    for head in range(2):
        v_t[head * step : head * step + HEAD_DIM, :] = values_t[
            head * HEAD_DIM : (head + 1) * HEAD_DIM, :
        ]
        v_t[head * step + HEAD_DIM : (head + 1) * step, :] = ones

    def start(head, columns, size):
        query = one_head(q_t, head, columns, size)
        scores[head, :, :size] = contract(qkv_ref[:, PAIR : 2 * PAIR], query, 1, 0)

    def finish(head, columns, size):
        values = scores[head, :, :size]
        highest = jnp.max(values, axis=0, keepdims=True) * scale
        expon = jnp.exp2(values * scale - highest).astype(BF16)
        mixed = contract(v_t[head * step : (head + 1) * step, :], expon, 1, 0)
        total = mixed[HEAD_DIM : HEAD_DIM + 1, :]
        out_t[head * HEAD_DIM : (head + 1) * HEAD_DIM, columns] = mixed[:HEAD_DIM, :] / total
        lse_ref[head : head + 1, columns] = highest + jnp.log2(total)

    walk(rows, tile, start, finish)
    out_ref[...] = out_t[...].T[:rows, :].astype(BF16)


def attend(qkv, first_pair, last_pair, kept=None, tile=512):
    rows, width = qkv.shape
    pairs = width // (3 * PAIR)
    padded = padded_rows(rows, tile)
    count = last_pair - first_pair
    kernel = functools.partial(attend_kernel, tile, rows, padded)
    anywhere = pl.BlockSpec(memory_space=pl.ANY)
    return pl.pallas_call(
        kernel if kept is None else lambda ref, a, b, *rest: kernel(ref, *rest),
        grid=(count,),
        in_specs=[pl.BlockSpec((rows, 3 * PAIR), lambda i: (0, i + first_pair))]
        + ([] if kept is None else [anywhere] * 2),
        out_specs=[
            pl.BlockSpec((rows, PAIR), lambda i: (0, i + first_pair)),
            pl.BlockSpec((None, 2, padded), lambda i: (i + first_pair, 0, 0)),
        ],
        out_shape=[
            jax.ShapeDtypeStruct((rows, pairs * PAIR), BF16),
            jax.ShapeDtypeStruct((pairs, 2, padded), F32),
        ],
        scratch_shapes=[
            pltpu.VMEM((PAIR, padded), BF16),
            pltpu.VMEM((PAIR + 32, rows), BF16),
            pltpu.VMEM((PAIR, padded), F32),
            pltpu.VMEM((2, rows, tile), F32),
        ],
        input_output_aliases={} if kept is None else {1: 0, 2: 1},
        compiler_params=pltpu.CompilerParams(vmem_limit_bytes=VMEM_LIMIT),
        cost_estimate=pl.CostEstimate(
            flops=64 * rows * rows * PAIR * count,
            bytes_accessed=8 * rows * PAIR * count,
            transcendentals=2 * rows * rows * count,
        ),
        name="attend",
    )(qkv, *(() if kept is None else kept))


def attend_back_kernel(
    tile, rows, padded, s_ref, qkv_ref, grad_ref, out_ref, lse_ref, first_ref, dqkv_ref, send_ref,
    keep_ref, sums_ref, q_t, g_t, k_t, delta, dq_t, dk_t, dv_t, all_t, scores, d_probs,
    rows_in, sem,
):
    scale = HEAD_DIM**-0.5
    fetch = pltpu.make_async_copy(first_ref, rows_in, sem)
    fetch.start()
    q_t[:, :rows] = qkv_ref[:, :PAIR].T
    g_t[:, :rows] = grad_ref[...].T
    if padded > rows:
        q_t[:, rows:] = jnp.zeros((PAIR, padded - rows), BF16)
        g_t[:, rows:] = jnp.zeros((PAIR, padded - rows), BF16)
        delta[:, rows:] = jnp.zeros((2, padded - rows), F32)
    k_t[...] = qkv_ref[:, PAIR : 2 * PAIR].T
    product = (grad_ref[...].astype(F32) * out_ref[...].astype(F32)).T
    delta[0:1, :rows] = jnp.sum(product[:HEAD_DIM, :], axis=0, keepdims=True)
    delta[1:2, :rows] = jnp.sum(product[HEAD_DIM:, :], axis=0, keepdims=True)
    dk_t[...] = jnp.zeros_like(dk_t)
    dv_t[...] = jnp.zeros_like(dv_t)

    def start(head, columns, size):
        query, grad = one_head(q_t, head, columns, size), one_head(g_t, head, columns, size)
        scores[head, :, :size] = contract(qkv_ref[:, PAIR : 2 * PAIR], query, 1, 0)
        d_probs[head, :, :size] = contract(qkv_ref[:, 2 * PAIR :], grad, 1, 0)

    def finish(head, columns, size):
        lanes = slice(head * HEAD_DIM, (head + 1) * HEAD_DIM)
        log_total = lse_ref[head : head + 1, columns]
        weights = jnp.exp2(scores[head, :, :size] * (scale * LOG2E) - log_total)
        inner = delta[head : head + 1, columns]
        d_scores = (weights * (d_probs[head, :, :size] - inner)).astype(BF16)
        dv_t[lanes, :] += contract(g_t[lanes, columns], weights.astype(BF16), 1, 1)
        dq_t[lanes, columns] = contract(k_t[lanes, :], d_scores, 1, 0)
        dk_t[lanes, :] += contract(q_t[lanes, columns], d_scores, 1, 1)

    walk(rows, tile, start, finish)
    all_t[:PAIR, :] = (dq_t[:, :rows] * scale).astype(BF16)
    all_t[PAIR : 2 * PAIR, :] = (dk_t[...] * scale).astype(BF16)
    all_t[2 * PAIR :, :] = dv_t[...].astype(BF16)
    for part in range(3):
        lanes = slice(part * PAIR, (part + 1) * PAIR)
        dqkv_ref[:, lanes] = all_t[lanes, :].T
    sums_ref[...] = contract(jnp.ones((8, rows), BF16), all_t[...], 1, 1)
    own = first_ref.shape[1] // 2
    fetch.wait()
    for h in range(2):
        grad = contract(all_t[...], rows_in[:, h * own : (h + 1) * own], 1, 0).astype(BF16)

        @pl.when(s_ref[0] == h)
        def _():
            keep_ref[...] = grad

        @pl.when(s_ref[0] != h)
        def _():
            send_ref[...] = grad


def attend_back(scal, qkv, grad, out, lse, first, tile=256):
    rows, full = qkv.shape
    width = first.shape[1]
    padded = padded_rows(rows, tile)
    count = 1
    return pl.pallas_call(
        functools.partial(attend_back_kernel, tile, rows, padded),
        grid_spec=pltpu.PrefetchScalarGridSpec(
            num_scalar_prefetch=1,
            grid=(count,),
            in_specs=[
                pl.BlockSpec((rows, 3 * PAIR), lambda i, s: (0, s[5])),
                pl.BlockSpec((rows, PAIR), lambda i, s: (0, s[5])),
                pl.BlockSpec((rows, PAIR), lambda i, s: (0, s[5])),
                pl.BlockSpec((None, 2, lse.shape[2]), lambda i, s: (s[5], 0, 0)),
                pl.BlockSpec(memory_space=pl.ANY),
            ],
            out_specs=[
                pl.BlockSpec((rows, 3 * PAIR), lambda i, s: (0, i)),
                pl.BlockSpec((3 * PAIR, width // 2), lambda i, s: (i, 0)),
                pl.BlockSpec((3 * PAIR, width // 2), lambda i, s: (i, 0)),
                pl.BlockSpec((8, 3 * PAIR), lambda i, s: (0, i)),
            ],
            scratch_shapes=[
                pltpu.VMEM((PAIR, padded), BF16),
                pltpu.VMEM((PAIR, padded), BF16),
                pltpu.VMEM((PAIR, rows), BF16),
                pltpu.VMEM((2, padded), F32),
                pltpu.VMEM((PAIR, padded), F32),
                pltpu.VMEM((PAIR, rows), F32),
                pltpu.VMEM((PAIR, rows), F32),
                pltpu.VMEM((3 * PAIR, rows), BF16),
                pltpu.VMEM((2, rows, tile), F32),
                pltpu.VMEM((2, rows, tile), F32),
                pltpu.VMEM((rows, width), BF16),
                pltpu.SemaphoreType.DMA,
            ],
        ),
        out_shape=[
            jax.ShapeDtypeStruct((rows, 3 * PAIR * count), BF16),
            jax.ShapeDtypeStruct((3 * PAIR * count, width // 2), BF16),
            jax.ShapeDtypeStruct((3 * PAIR * count, width // 2), BF16),
            jax.ShapeDtypeStruct((8, 3 * PAIR * count), F32),
        ],
        compiler_params=pltpu.CompilerParams(vmem_limit_bytes=VMEM_LIMIT),
        cost_estimate=pl.CostEstimate(
            flops=160 * rows * rows * PAIR * count,
            bytes_accessed=16 * rows * PAIR * count,
            transcendentals=2 * rows * rows * count,
        ),
        name="attend_back",
    )(scal, qkv, grad, out, lse, first)


def feed_kernel(
    s_ref, x_own, x_other, dy_own, dy_other, up_ref, down_ref, x_piece, x_beside, z_piece, z_beside,
    bias_ref, out_own, out_other, dx_own, dx_other, up_send, up_keep, down_send, down_keep,
    low_send, low_keep, bias_grad_ref, x, dy, x_t, out_sum, dx_sum, up_full, down_full, hidden,
    d_pre, sems,
):
    index = pl.program_id(0)
    half = s_ref[0]
    rows, width = x.shape
    block = rows // 2
    own = width // 2
    tile = up_ref.shape[1]
    first_range = index < 2
    side = index % 2
    columns = pl.ds(pl.multiple_of(side * tile, tile), tile)
    mine = pl.ds(pl.multiple_of(half * own, own), own)
    theirs = pl.ds(pl.multiple_of((1 - half) * own, own), own)

    @pl.when(index == 0)
    def _():
        copies = []
        for i, ref in enumerate((x_own, x_other)):
            copies.append(pltpu.make_async_copy(ref, x.at[pl.ds(i * block, block)], sems.at[i]))
        for i, ref in enumerate((dy_own, dy_other)):
            copies.append(
                pltpu.make_async_copy(ref, dy.at[pl.ds(i * block, block)], sems.at[2 + i])
            )
        for copy in copies:
            copy.start()
        for copy in copies:
            copy.wait()
        x_t[...] = x[...].T
        out_sum[...] = jnp.zeros_like(out_sum)
        dx_sum[...] = jnp.zeros_like(dx_sum)

    up_full[mine, :] = up_ref[...]

    @pl.when(side == half)
    def _():
        down_full[...] = down_ref[...]

    for chosen, place, piece, beside in (
        (first_range, 1, x_piece, x_beside), (jnp.logical_not(first_range), 4, z_piece, z_beside)
    ):
        even = s_ref[place] == 0

        @pl.when(chosen & even)
        def _():
            up_full[theirs, :] = piece[:, columns]

        @pl.when(chosen & jnp.logical_not(even))
        def _():
            up_full[theirs, :] = beside[:, columns]

        @pl.when(chosen & (side != half) & even)
        def _():
            down_full[...] = beside[...]

        @pl.when(chosen & (side != half) & jnp.logical_not(even))
        def _():
            down_full[...] = piece[...]

    bias_grad = jnp.zeros(bias_grad_ref.shape, F32)
    for start in range(0, rows, block):
        part = slice(start, start + block)
        pre = contract(x[part, :], up_full[...], 1, 0) + bias_ref[...]
        d_hidden = contract(dy[part, :], down_full[...], 1, 1)
        share = 0.5 * (1.0 + lax.erf(pre * 0.7071067811865476))
        hidden[part, :] = (pre * share).astype(BF16)
        slope = share + pre * (jnp.exp(-0.5 * pre * pre) * 0.3989422804014327)
        d_low = (d_hidden * slope).astype(BF16)
        d_pre[part, :] = d_low
        bias_grad = bias_grad + jnp.sum(d_low.astype(F32), axis=0, keepdims=True)
        out_sum[part, :] += contract(hidden[part, :], down_full[...], 1, 0)
        dx_sum[part, :] += contract(d_pre[part, :], up_full[...], 1, 1)
    bias_grad_ref[...] = bias_grad
    down_grad = contract(hidden[...], dy[...], 0, 0).astype(BF16)
    side_rows = pl.ds(pl.multiple_of(side * tile, tile), tile)

    @pl.when(first_range)
    def _():
        up_keep[:, columns] = contract(x_t[mine, :], d_pre[...], 1, 0).astype(BF16)
        up_send[:, columns] = contract(x_t[theirs, :], d_pre[...], 1, 0).astype(BF16)

    @pl.when(first_range & (side == half))
    def _():
        down_keep[...] = down_grad

    @pl.when(first_range & (side != half))
    def _():
        down_send[...] = down_grad

    for even in (True, False):
        up_goal, down_goal = (low_keep, low_send) if even else (low_send, low_keep)

        @pl.when(jnp.logical_not(first_range) & ((s_ref[1] == 0) == even))
        def _():
            up_goal[:, columns] = contract(x_t[...], d_pre[...], 1, 0).astype(BF16)
            down_goal[side_rows, :] = down_grad

    @pl.when(index == pl.num_programs(0) - 1)
    def _():
        out_own[...] = out_sum[:block, :].astype(BF16)
        out_other[...] = out_sum[block:, :].astype(BF16)
        dx_own[...] = dx_sum[:block, :].astype(BF16)
        dx_other[...] = dx_sum[block:, :].astype(BF16)


def feed(scal, seconds, grads, up, down, pieces, bias):
    local, width = seconds[0].shape
    rows = 2 * local
    tile = down.shape[0] // 4
    anywhere = pl.BlockSpec(memory_space=pl.ANY)

    def fixed(*shape):
        return pl.BlockSpec(shape, lambda t, s: (0, 0), pipeline_mode=pl.Buffered(1))

    shapes = [(local, width)] * 4 + [(width // 2, 2 * tile)] * 2 + [(tile, width)] * 2
    shapes += [(width, 2 * tile)] * 2
    across = pl.BlockSpec((1, tile), lambda t, s: (0, t))
    return pl.pallas_call(
        feed_kernel,
        grid_spec=pltpu.PrefetchScalarGridSpec(
            num_scalar_prefetch=1,
            grid=(4,),
            in_specs=[anywhere] * 4
            + [
                pl.BlockSpec(
                    (width // 2, tile), lambda t, s: (0, ((t % 2) * 2 + s[2]) * 2 + t // 2)
                ),
                pl.BlockSpec((tile, width), lambda t, s: (s[2] * 2 + t // 2, 0)),
            ]
            + [fixed(width // 2, 2 * tile)] * 4
            + [across],
            out_specs=[fixed(*shape) for shape in shapes] + [across],
            scratch_shapes=[
                pltpu.VMEM((rows, width), BF16),
                pltpu.VMEM((rows, width), BF16),
                pltpu.VMEM((width, rows), BF16),
                pltpu.VMEM((rows, width), F32),
                pltpu.VMEM((rows, width), F32),
                pltpu.VMEM((width, tile), BF16),
                pltpu.VMEM((tile, width), BF16),
                pltpu.VMEM((rows, tile), BF16),
                pltpu.VMEM((rows, tile), BF16),
                pltpu.SemaphoreType.DMA((4,)),
            ],
        ),
        out_shape=[jax.ShapeDtypeStruct(shape, BF16) for shape in shapes]
        + [jax.ShapeDtypeStruct((1, 4 * tile), F32)],
        compiler_params=pltpu.CompilerParams(vmem_limit_bytes=VMEM_LIMIT),
        cost_estimate=pl.CostEstimate(
            flops=48 * rows * width * tile,
            bytes_accessed=16 * rows * width,
            transcendentals=8 * rows * tile,
        ),
        name="feed",
    )(scal, *seconds, *grads, up, down, *pieces, bias)


def run(kernel, name, scal, grid, in_specs, out_specs, out_shape, args, flops=0, scratch=()):
    moved = sum(a.size * a.dtype.itemsize for a in args)
    return pl.pallas_call(
        kernel,
        grid_spec=pltpu.PrefetchScalarGridSpec(
            num_scalar_prefetch=1,
            grid=grid,
            in_specs=in_specs,
            out_specs=out_specs,
            scratch_shapes=scratch,
        ),
        out_shape=out_shape,
        compiler_params=pltpu.CompilerParams(vmem_limit_bytes=VMEM_LIMIT),
        cost_estimate=pl.CostEstimate(flops=flops, bytes_accessed=2 * moved, transcendentals=0),
        name=name,
    )(scal, *args)


def spec(shape, index):
    return pl.BlockSpec(shape, index)


def held(*shape):
    return pl.BlockSpec(shape, lambda i, s: (0,) * len(shape), pipeline_mode=pl.Buffered(1))


def struct(*shape, dtype=BF16):
    return jax.ShapeDtypeStruct(shape, dtype)


def pack_qkv(scal, weights):
    rows, width = weights[0].shape
    pairs = width // (2 * PAIR)
    per = pairs // 2

    def kernel(s_ref, q_ref, k_ref, v_ref, own_ref, mine_ref):
        for i, ref in enumerate((q_ref, k_ref, v_ref)):
            own_ref[:, i * PAIR : (i + 1) * PAIR] = ref[...]
        start = pl.multiple_of(s_ref[1] * (rows // 2), rows // 2)
        mine_ref[...] = own_ref[pl.ds(start, rows // 2), :]

    block = spec((rows, PAIR), lambda p, s: (0, ((p // per) * 2 + s[2]) * per + p % per))
    return run(
        kernel, "pack_qkv", scal, (pairs,), [block] * 3,
        [
            spec((rows, 3 * PAIR), lambda p, s: (0, p)),
            spec((rows // 2, 3 * PAIR), lambda p, s: (0, p)),
        ],
        [struct(rows, 3 * PAIR * pairs), struct(rows // 2, 3 * PAIR * pairs)],
        weights,
    )


def pack_feed(scal, up, down, j, ranges, bit):
    rows, hidden = up.shape
    tile = hidden // (4 * ranges)
    columns = down.shape[1] // 2

    def kernel(s_ref, up_ref, down_ref, out_ref):
        out_ref[...] = jnp.where(s_ref[bit] == 0, up_ref[...], down_ref[...])

    return run(
        kernel, "pack_feed", scal, (2,),
        [
            spec((rows, tile), lambda t, s: (0, (t * 2 + s[2]) * ranges + j)),
            spec((tile, columns), lambda t, s: (s[2] * ranges + j, t)),
        ],
        spec((rows, tile), lambda t, s: (0, t)), struct(rows, 2 * tile), (up, down),
    )


def normalize(values):
    centred = values - jnp.mean(values, axis=-1, keepdims=True)
    spread = jnp.mean(centred * centred, axis=-1, keepdims=True)
    inverse = lax.rsqrt(spread + EPS)
    return centred * inverse, inverse


def first_norm(scal, tokens, received, gain, shift):
    rows, width = tokens.shape
    step = rows // 2

    def kernel(s_ref, t_ref, r_ref, gain_ref, shift_ref, x_ref, first_ref):
        x = jnp.where(s_ref[3] == 1, t_ref[...], r_ref[...])
        x_ref[...] = x
        normed, _ = normalize(x.astype(F32))
        first_ref[...] = (normed * gain_ref[...] + shift_ref[...]).astype(BF16)

    block = spec((step, width), lambda i, s: (i, 0))
    return run(
        kernel, "first_norm", scal, (2,), [block, block, held(1, width), held(1, width)],
        [block, block], [struct(rows, width)] * 2, (tokens, received, gain, shift),
    )


def project(scal, firsts, own, piece, beside, bias):
    local, width = firsts[0].shape
    rows, total = 2 * local, own.shape[1]
    block = 6 * PAIR
    half_rows, quarter_rows = width // 2, width // 4

    def kernel(
        s_ref, mine_ref, theirs_ref, own_ref, piece_ref, beside_ref, bias_ref, qkv_ref, w_ref,
        all_ref, sems,
    ):
        @pl.when(pl.program_id(0) == 0)
        def _():
            copies = [
                pltpu.make_async_copy(ref, all_ref.at[pl.ds(i * local, local)], sems.at[i])
                for i, ref in enumerate((mine_ref, theirs_ref))
            ]
            for copy in copies:
                copy.start()
            for copy in copies:
                copy.wait()

        half, low = s_ref[0], s_ref[1]
        other = (1 - half) * half_rows
        w_ref[pl.ds(pl.multiple_of(half * half_rows, half_rows), half_rows), :] = own_ref[...]
        start = pl.multiple_of(other + low * quarter_rows, quarter_rows)
        w_ref[pl.ds(start, quarter_rows), :] = piece_ref[...]
        start = pl.multiple_of(other + (1 - low) * quarter_rows, quarter_rows)
        w_ref[pl.ds(start, quarter_rows), :] = beside_ref[...]
        qkv_ref[...] = (contract(all_ref[...], w_ref[...], 1, 0) + bias_ref[...]).astype(BF16)

    def columns(size):
        return spec((size, block), lambda p, s: (0, p))

    anywhere = pl.BlockSpec(memory_space=pl.ANY)
    return run(
        kernel, "project", scal, (total // block,),
        [anywhere] * 2
        + [columns(half_rows), columns(quarter_rows), columns(quarter_rows), columns(1)],
        [columns(rows), columns(width), held(rows, width)],
        [struct(rows, total), struct(width, total), struct(rows, width)],
        (*firsts, own, piece, beside, bias), flops=2 * rows * width * total,
        scratch=[pltpu.SemaphoreType.DMA((2,))],
    )


def out_other(scal, mixed, weight, piece, beside):
    rows, set_width = mixed.shape
    local, width = rows // 2, weight.shape[1]
    block, small = set_width // 2, set_width // 4

    def kernel(s_ref, mixed_ref, own_ref, piece_ref, beside_ref, out_ref, set_ref):
        half, low = s_ref[0], s_ref[1]
        other = (1 - half) * block
        set_ref[pl.ds(pl.multiple_of(half * block, block), block), :] = own_ref[...]
        set_ref[pl.ds(pl.multiple_of(other + low * small, small), small), :] = piece_ref[...]
        start = pl.multiple_of(other + (1 - low) * small, small)
        set_ref[pl.ds(start, small), :] = beside_ref[...]
        out_ref[...] = contract(mixed_ref[...], set_ref[...], 1, 0).astype(BF16)

    return run(
        kernel, "out_other", scal, (1,),
        [
            spec((local, set_width), lambda i, s: (1, 0)),
            spec((block, width), lambda i, s: (s[2], 0)),
            held(small, width), held(small, width),
        ],
        [held(local, width), held(set_width, width)],
        [struct(local, width), struct(set_width, width)],
        (mixed, weight, piece, beside), flops=2 * local * set_width * width,
    )


def second_norm(scal, mixed, out_set, x, received, bias, gain, shift):
    rows, set_width = mixed.shape
    local, width = x.shape
    step = local // 2

    def kernel(
        s_ref, mixed_ref, w_ref, x_ref, r_ref, bias_ref, gain_ref, shift_ref, mid_ref, second_ref
    ):
        middle = contract(mixed_ref[...], w_ref[...], 1, 0) + r_ref[...].astype(F32)
        middle = middle + x_ref[...].astype(F32) + bias_ref[...]
        mid_ref[...] = middle
        normed, _ = normalize(middle)
        second_ref[...] = (normed * gain_ref[...] + shift_ref[...]).astype(BF16)

    block = spec((step, width), lambda i, s: (i, 0))
    return run(
        kernel, "second_norm", scal, (2,),
        [spec((step, set_width), lambda i, s: (i, 0)), held(set_width, width), block, block]
        + [held(1, width)] * 3,
        [block, block], [struct(local, width, dtype=F32), struct(local, width)],
        (mixed, out_set, x, received, bias, gain, shift), flops=2 * local * set_width * width,
    )


def norm_back_rows(grad, normed, inverse, gain):
    scaled = grad * gain
    first_term = jnp.mean(scaled, axis=-1, keepdims=True)
    second_term = jnp.mean(scaled * normed, axis=-1, keepdims=True)
    return inverse * (scaled - first_term - normed * second_term)


def column_sums(refs, values):
    @pl.when(pl.program_id(0) == 0)
    def _():
        refs[...] = jnp.zeros_like(refs)

    for i, value in enumerate(values):
        refs[i : i + 1, :] += jnp.sum(value, axis=0, keepdims=True)


def row_step(rows):
    return rows // 7 if rows % 112 == 0 else rows


def second_back(scal, grad, received, middle, dy, gain):
    local, width = middle.shape
    step = row_step(local)

    def kernel(s_ref, g_ref, r_ref, mid_ref, dy_ref, gain_ref, low_ref, sums_ref):
        grad = g_ref[...].astype(F32) + r_ref[...].astype(F32)
        normed, inverse = normalize(mid_ref[...])
        dy_wide = dy_ref[...].astype(F32)
        low = (dy_wide + norm_back_rows(grad, normed, inverse, gain_ref[...])).astype(BF16)
        low_ref[...] = low
        column_sums(sums_ref, (grad * normed, grad, dy_wide, low.astype(F32)))

    block = spec((step, width), lambda i, s: (i, 0))
    return run(
        kernel, "second_back", scal, (local // step,), [block] * 4 + [held(1, width)],
        [block, held(8, width)], [struct(local, width), struct(8, width, dtype=F32)],
        (grad, received, middle, dy, gain),
    )


def mixed_back(scal, lows, out_set, mixed):
    local, width = lows[0].shape
    rows, set_width = mixed.shape
    block = set_width // 2

    def kernel(
        s_ref, mine_ref, theirs_ref, w_ref, mixed_ref, d_ref, send_ref, keep_ref, low, sems
    ):
        @pl.when(pl.program_id(0) == 0)
        def _():
            copies = [
                pltpu.make_async_copy(ref, low.at[pl.ds(i * local, local)], sems.at[i])
                for i, ref in enumerate((mine_ref, theirs_ref))
            ]
            for copy in copies:
                copy.start()
            for copy in copies:
                copy.wait()

        d_ref[...] = contract(low[...], w_ref[...], 1, 1).astype(BF16)
        grad = contract(mixed_ref[...], low[...], 0, 0).astype(BF16)

        def store(goal):
            for c in range(2):
                for i in range(width // (2 * PAIR)):
                    start = (2 * i + c) * PAIR
                    goal[c * block : (c + 1) * block, i * PAIR : (i + 1) * PAIR] = (
                        grad[:, start : start + PAIR]
                    )

        @pl.when(pl.program_id(0) == s_ref[0])
        def _():
            store(keep_ref)

        @pl.when(pl.program_id(0) != s_ref[0])
        def _():
            store(send_ref)

    anywhere = pl.BlockSpec(memory_space=pl.ANY)
    across = spec((rows, block), lambda t, s: (0, t))
    return run(
        kernel, "mixed_back", scal, (2,),
        [anywhere] * 2 + [spec((block, width), lambda t, s: (t, 0)), across],
        [across, held(2 * block, width // 2), held(2 * block, width // 2)],
        [struct(rows, set_width)] + [struct(2 * block, width // 2)] * 2,
        (*lows, out_set, mixed), flops=4 * rows * set_width * width,
        scratch=[pltpu.VMEM((rows, width), BF16), pltpu.SemaphoreType.DMA((2,))],
    )


def first_grad(scal, dqkvs, weights):
    rows = dqkvs[0].shape[0]
    width = weights.shape[0]
    local = rows // 2
    count = len(dqkvs)
    step = width // 4

    def kernel(s_ref, *refs):
        left = jnp.concatenate([refs[j][...] for j in range(count)], axis=1)
        total = contract(left, refs[count][...], 1, 1)
        refs[-2][...] = total[:local].astype(BF16)
        refs[-1][...] = total[local:].astype(BF16)

    across = spec((local, step), lambda i, s: (0, i))
    return run(
        kernel, "first_grad", scal, (4,),
        [held(*a.shape) for a in dqkvs] + [spec((step, weights.shape[1]), lambda i, s: (i, 0))],
        [across, across], [struct(local, width)] * 2, (*dqkvs, weights),
        flops=sum(2 * rows * a.shape[1] * width for a in dqkvs),
    )


def first_back(scal, grad, received, x, wide, gain):
    local, width = x.shape
    step = row_step(local)

    def kernel(s_ref, g_ref, r_ref, x_ref, wide_ref, gain_ref, out_ref, sums_ref):
        grad = g_ref[...].astype(F32) + r_ref[...].astype(F32)
        normed, inverse = normalize(x_ref[...].astype(F32))
        total = wide_ref[...].astype(F32) + norm_back_rows(grad, normed, inverse, gain_ref[...])
        out_ref[...] = total.astype(BF16)
        column_sums(sums_ref, (grad * normed, grad))

    block = spec((step, width), lambda i, s: (i, 0))
    return run(
        kernel, "first_back", scal, (local // step,), [block] * 4 + [held(1, width)],
        [block, held(8, width)], [struct(local, width), struct(8, width, dtype=F32)],
        (grad, received, x, wide, gain),
    )


def layer_rows(scal, own, received, middle, bias):
    local, width = middle.shape
    step = row_step(local)

    def kernel(s_ref, o_ref, r_ref, mid_ref, bias_ref, out_ref):
        total = mid_ref[...] + o_ref[...].astype(F32) + r_ref[...].astype(F32) + bias_ref[...]
        out_ref[...] = total.astype(BF16)

    block = spec((step, width), lambda i, s: (i, 0))
    return run(
        kernel, "layer_rows", scal, (local // step,), [block] * 3 + [held(1, width)],
        block, struct(local, width), (own, received, middle, bias),
    )


def finish_feed_kernel(s_ref, *refs, tile):
    up_out, down_out = refs[8:]
    first = s_ref[2] == 0
    even = s_ref[1] == 0
    low_range = s_ref[4] == 0
    cores = []
    for refs_of in (refs[:4], refs[4:8]):
        whole, beside, along, last = [ref[...] for ref in refs_of]
        ranges = []
        for j in range(2):
            mine = jnp.where(low_range == (j == 0), whole, along)
            theirs = jnp.where(low_range == (j == 0), beside, last)
            ranges.append((jnp.where(even, mine, theirs), jnp.where(even, theirs, mine)))
        cores.append(ranges)
    for c in range(2):
        for j in range(2):
            up, down = [
                jnp.where(first == (c == 0), cores[0][j][kind], cores[1][j][kind]).astype(F32)
                for kind in range(2)
            ]
            down_out[c, j] = down
            for h in range(2):
                start = ((h * 2 + c) * 2 + j) * tile
                up_out[:, start : start + tile] = up[:, h * tile : (h + 1) * tile]


def finish_feed(scal, sums):
    rows, width = sums[0].shape
    steps = 4
    block = spec((rows // steps, width), lambda i, s: (i, 0))
    up, down = run(
        functools.partial(finish_feed_kernel, tile=rows), "finish_feed", scal, (steps,),
        [block] * 8,
        [
            spec((rows // steps, 4 * width), lambda i, s: (i, 0)),
            spec((2, 2, rows // steps, width), lambda i, s: (0, 0, i, 0)),
        ],
        [struct(rows, 4 * width, dtype=F32), struct(2, 2, rows, width, dtype=F32)],
        sums,
    )
    return up, down.reshape(4 * rows, width)


def finish_attention_kernel(s_ref, *refs, pairs, spans):
    q_out, k_out, v_out, out_out = refs[-4:]
    first, even = s_ref[2] == 0, s_ref[1] == 0
    half_pairs = pairs // 2
    for g, (begin, end) in enumerate(spans):
        mine, beside, mine_across, beside_across = [ref[...] for ref in refs[4 * g : 4 * g + 4]]
        own = jnp.concatenate(
            [jnp.where(even, mine, beside), jnp.where(even, beside, mine)], axis=0
        )
        other = jnp.concatenate(
            [
                jnp.where(even, mine_across, beside_across),
                jnp.where(even, beside_across, mine_across),
            ],
            axis=0,
        )
        for c in range(2):
            total = jnp.where(first == (c == 0), own, other).astype(F32)
            wide = total[: (end - begin) * 3 * PAIR].T
            for q in range(end - begin):
                pair = begin + q
                h, p = pair // half_pairs, pair % half_pairs
                goal = ((h * 2 + c) * half_pairs + p) * PAIR
                for i, out in enumerate((q_out, k_out, v_out)):
                    start = (q * 3 + i) * PAIR
                    out[:, goal : goal + PAIR] = wide[:, start : start + PAIR]
            if g == 0:
                rest = total[(end - begin) * 3 * PAIR :]
                rows = rest.shape[0] // 2
                out_out[c * rows : (c + 1) * rows, :PAIR] = rest[:rows]
                out_out[c * rows : (c + 1) * rows, PAIR:] = rest[rows:]


def finish_attention(scal, sums, spans):
    rows = sums[0].shape[1]
    pairs = spans[-1][1]
    steps = rows // PAIR
    return run(
        functools.partial(finish_attention_kernel, pairs=pairs, spans=spans), "finish_attention",
        scal, (steps,),
        [spec((values.shape[0], PAIR), lambda i, s: (0, i)) for values in sums],
        [spec((PAIR, 2 * pairs * PAIR), lambda i, s: (i, 0))] * 3
        + [spec((rows, 2 * PAIR), lambda i, s: (0, i))],
        [struct(rows, 2 * pairs * PAIR, dtype=F32)] * 3 + [struct(rows, 2 * rows, dtype=F32)],
        sums,
    )


def wide_back_kernel(
    tile, rows, padded, qkv_ref, grad_ref, out_ref, lse_ref, dqkv_ref, q_t, g_t, k_t, delta,
    dq_t, dk_t, dv_t,
):
    scale = HEAD_DIM**-0.5
    q_t[:, :rows] = qkv_ref[:, :PAIR].T
    g_t[:, :rows] = grad_ref[...].T
    if padded > rows:
        q_t[:, rows:] = jnp.zeros((PAIR, padded - rows), BF16)
        g_t[:, rows:] = jnp.zeros((PAIR, padded - rows), BF16)
        delta[:, rows:] = jnp.zeros((2, padded - rows), F32)
    k_t[...] = qkv_ref[:, PAIR : 2 * PAIR].T
    product = (grad_ref[...].astype(F32) * out_ref[...].astype(F32)).T
    delta[0:1, :rows] = jnp.sum(product[:HEAD_DIM, :], axis=0, keepdims=True)
    delta[1:2, :rows] = jnp.sum(product[HEAD_DIM:, :], axis=0, keepdims=True)
    dk_t[...] = jnp.zeros_like(dk_t)
    dv_t[...] = jnp.zeros_like(dv_t)

    def block(index, carry):
        columns = pl.ds(pl.multiple_of(index * tile, tile), tile)
        empty = jnp.zeros((HEAD_DIM, tile), BF16)
        for head in range(2):
            lanes = slice(head * HEAD_DIM, (head + 1) * HEAD_DIM)
            query = q_t[lanes, columns]
            grad = g_t[lanes, columns]
            query_pad = jnp.concatenate([query, empty] if head == 0 else [empty, query], axis=0)
            grad_pad = jnp.concatenate([grad, empty] if head == 0 else [empty, grad], axis=0)
            scores = contract(qkv_ref[:, PAIR : 2 * PAIR], query_pad, 1, 0)
            grad_probs = contract(qkv_ref[:, 2 * PAIR :], grad_pad, 1, 0)
            weights = jnp.exp2(scores * (scale * LOG2E) - lse_ref[head : head + 1, columns])
            grad_scores = (weights * (grad_probs - delta[head : head + 1, columns])).astype(BF16)
            dv_t[lanes, :] += contract(grad, weights.astype(BF16), 1, 1)
            dq_t[lanes, columns] = contract(k_t[lanes, :], grad_scores, 1, 0)
            dk_t[lanes, :] += contract(query, grad_scores, 1, 1)
        return carry

    lax.fori_loop(0, padded // tile, block, 0)
    dqkv_ref[:, :PAIR] = (dq_t[...].T[:rows, :] * scale).astype(BF16)
    dqkv_ref[:, PAIR : 2 * PAIR] = (dk_t[...].T * scale).astype(BF16)
    dqkv_ref[:, 2 * PAIR :] = dv_t[...].T.astype(BF16)


def wide_back(qkv, grad, out, lse, first_pair, last_pair, tile=256):
    rows, width = qkv.shape
    padded = -(-rows // tile) * tile
    lse = jnp.pad(lse, ((0, 0), (0, 0), (0, padded - lse.shape[2])))
    count = last_pair - first_pair
    return pl.pallas_call(
        functools.partial(wide_back_kernel, tile, rows, padded),
        grid=(count,),
        in_specs=[
            pl.BlockSpec((rows, 3 * PAIR), lambda i: (0, i + first_pair)),
            pl.BlockSpec((rows, PAIR), lambda i: (0, i + first_pair)),
            pl.BlockSpec((rows, PAIR), lambda i: (0, i + first_pair)),
            pl.BlockSpec((None, 2, lse.shape[2]), lambda i: (i + first_pair, 0, 0)),
        ],
        out_specs=pl.BlockSpec((rows, 3 * PAIR), lambda i: (0, i)),
        out_shape=jax.ShapeDtypeStruct((rows, 3 * PAIR * count), BF16),
        scratch_shapes=[
            pltpu.VMEM((PAIR, padded), BF16),
            pltpu.VMEM((PAIR, padded), BF16),
            pltpu.VMEM((PAIR, rows), BF16),
            pltpu.VMEM((2, padded), F32),
            pltpu.VMEM((PAIR, padded), F32),
            pltpu.VMEM((PAIR, rows), F32),
            pltpu.VMEM((PAIR, rows), F32),
        ],
        compiler_params=pltpu.CompilerParams(vmem_limit_bytes=VMEM_LIMIT),
        cost_estimate=pl.CostEstimate(
            flops=160 * rows * rows * PAIR * count,
            bytes_accessed=16 * rows * PAIR * count,
            transcendentals=2 * rows * rows * count,
        ),
        name="wide_back",
    )(qkv, grad, out, lse)


def wide_feed_kernel(
    half_ref, *refs, parts, make, chunk,
):
    xs, refs = refs[:parts], refs[parts:]
    dys, refs = refs[:parts], refs[parts:]
    if not make:
        x_t, refs = refs[0], refs[1:]
    up_ref, bias_ref, down_ref, *refs = refs
    hidden_ref, d_pre_ref, up_send, up_keep, down_send, down_keep, bias_grad_ref, *refs = refs
    if make:
        x_t, refs = refs[0], refs[1:]
    x, dy, sems = refs
    index = pl.program_id(0)
    half = half_ref[0]
    rows, width = x.shape
    block = rows // parts
    own = width // 2
    tile = up_ref.shape[1]

    @pl.when(index == 0)
    def _():
        copies = []
        for i in range(parts):
            part = pl.ds(i * block, block)
            copies.append(pltpu.make_async_copy(xs[i], x.at[part], sems.at[i]))
            copies.append(pltpu.make_async_copy(dys[i], dy.at[part], sems.at[parts + i]))
        for copy in copies:
            copy.start()
        for copy in copies:
            copy.wait()
        if make:
            x_t[...] = x[...].T

    bias_grad = jnp.zeros(bias_grad_ref.shape, F32)
    for start in range(0, rows, chunk):
        part = slice(start, start + chunk)
        pre = contract(x[part, :], up_ref[...], 1, 0) + bias_ref[...]
        d_hidden = contract(dy[part, :], down_ref[...], 1, 1)
        share = 0.5 * (1.0 + lax.erf(pre * 0.7071067811865476))
        hidden_ref[part, :] = (pre * share).astype(BF16)
        slope = share + pre * (jnp.exp(-0.5 * pre * pre) * 0.3989422804014327)
        d_low = (d_hidden * slope).astype(BF16)
        d_pre_ref[part, :] = d_low
        bias_grad = bias_grad + jnp.sum(d_low.astype(F32), axis=0, keepdims=True)
    bias_grad_ref[...] = bias_grad
    columns = pl.ds(pl.multiple_of(index * tile, tile), tile)
    mine = pl.ds(pl.multiple_of(half * own, own), own)
    theirs = pl.ds(pl.multiple_of((1 - half) * own, own), own)
    up_keep[:, columns] = contract(x_t[mine, :], d_pre_ref[...], 1, 0).astype(BF16)
    up_send[:, columns] = contract(x_t[theirs, :], d_pre_ref[...], 1, 0).astype(BF16)
    down_grad = contract(hidden_ref[...], dy[...], 0, 0).astype(BF16)

    @pl.when(index == half)
    def _():
        down_keep[...] = down_grad

    @pl.when(index != half)
    def _():
        down_send[...] = down_grad


def wide_feed(half, xs, dys, x_t, up, bias, down):
    parts = len(xs)
    width = xs[0].shape[1]
    rows = sum(part.shape[0] for part in xs)
    hidden = up.shape[1]
    tile = hidden // 2
    make = x_t is None
    chunk = rows // 2 if rows % 32 == 0 else rows
    anywhere = pl.BlockSpec(memory_space=pl.ANY)
    fixed = lambda shape: pl.BlockSpec(shape, lambda j, s: (0, 0), pipeline_mode=pl.Buffered(1))
    across = lambda size: pl.BlockSpec((size, tile), lambda j, s: (0, j))
    out_specs = [across(rows)] * 2 + [fixed((width // 2, hidden))] * 2
    out_specs += [fixed((tile, width))] * 2 + [across(1)]
    out_shape = [
        jax.ShapeDtypeStruct((rows, hidden), BF16),
        jax.ShapeDtypeStruct((rows, hidden), BF16),
        jax.ShapeDtypeStruct((width // 2, hidden), BF16),
        jax.ShapeDtypeStruct((width // 2, hidden), BF16),
        jax.ShapeDtypeStruct((tile, width), BF16),
        jax.ShapeDtypeStruct((tile, width), BF16),
        jax.ShapeDtypeStruct((1, hidden), F32),
    ]
    if make:
        out_specs.append(fixed((width, rows)))
        out_shape.append(jax.ShapeDtypeStruct((width, rows), BF16))
    return pl.pallas_call(
        functools.partial(wide_feed_kernel, parts=parts, make=make, chunk=chunk),
        grid_spec=pltpu.PrefetchScalarGridSpec(
            num_scalar_prefetch=1,
            grid=(2,),
            in_specs=[anywhere] * (2 * parts)
            + ([] if make else [fixed((width, rows))])
            + [across(width), across(1), pl.BlockSpec((tile, width), lambda j, s: (j, 0))],
            out_specs=out_specs,
            scratch_shapes=[
                pltpu.VMEM((rows, width), BF16),
                pltpu.VMEM((rows, width), BF16),
                pltpu.SemaphoreType.DMA((2 * parts,)),
            ],
        ),
        out_shape=out_shape,
        compiler_params=pltpu.CompilerParams(vmem_limit_bytes=VMEM_LIMIT),
        cost_estimate=pl.CostEstimate(
            flops=8 * rows * width * hidden,
            bytes_accessed=8 * rows * width + 8 * width * hidden,
            transcendentals=2 * rows * hidden,
        ),
        name="wide_feed",
    )(half.reshape(1), *xs, *dys, *(() if make else (x_t,)), up, bias, down)


def norm_parts(values, gain, shift):
    average = jnp.mean(values, axis=-1, keepdims=True)
    centred = values - average
    spread = jnp.mean(centred * centred, axis=-1, keepdims=True)
    inverse = lax.rsqrt(spread + EPS)
    normed = centred * inverse
    return (normed * gain + shift, normed, inverse)


def norm_back(grad, normed, inverse, gain):
    scaled = grad * gain
    first_term = jnp.mean(scaled, axis=-1, keepdims=True)
    second_term = jnp.mean(scaled * normed, axis=-1, keepdims=True)
    result = inverse * (scaled - first_term - normed * second_term)
    return (result, jnp.sum(grad * normed, axis=0), jnp.sum(grad, axis=0))


def pick(values, index, axis):
    return lax.dynamic_index_in_dim(values, index, axis, keepdims=False)


def join(own, other, index):
    return jnp.where(index == 0, jnp.stack([own, other]), jnp.stack([other, own]))


def after(values, *earlier):
    return lax.optimization_barrier((values,) + earlier)[0]


def wide_body(
    rep, grp, tokens, query_weight, key_weight, value_weight, query_bias, value_bias, out_weight,
    out_bias, first_gain, first_shift, second_gain, second_shift, up_weight, up_bias,
    down_weight, down_bias, cotangent,
):
    clips, local, width = tokens.shape
    assert clips == 1
    quarter = grp // 2
    ring = rep // 2
    deep = ring // 2
    core = lax.axis_index("core")
    half = lax.axis_index("half")
    gq = lax.axis_index("gq")
    place = lax.axis_index("rz")
    low = place % 2
    high = place // 2
    own_rows = width // grp
    pairs = own_rows // PAIR
    hidden = up_weight.shape[1]
    set_hidden = hidden // grp
    ranges = max(1, set_hidden // width)
    tile = set_hidden // (2 * ranges)

    there = []
    for b in range(2):
        for h in range(2):
            for q in range(quarter):
                g = h * quarter + q
                source = (b * 2 + h) * quarter + q
                target = ((g % 2) * 2 + b) * quarter + g // 2
                if source != target:
                    there.append((source, target))
    back = [(target, source) for source, target in there]
    block = half * quarter + gq
    stays = (block % 2 == core) & (block // 2 == gq) & (half == core)
    axes = ("core", "half", "gq")
    beside = [(i, i ^ 1) for i in range(ring)]

    def move(values, route):
        return jnp.where(stays, values, lax.ppermute(values, axes, route))

    def swap_half(values):
        return lax.ppermute(values, "half", SWAP)

    def swap_core(values):
        return lax.ppermute(values, "core", SWAP)

    def spread(values):
        if grp == 2:
            return [values, swap_core(values)]
        return [lax.all_gather(values, ("gq", "core"), axis=0, tiled=True)]

    def collect(values):
        if grp == 2:
            other = swap_core(values(slice(local, None)).astype(BF16))
            return values(slice(None, local)) + other.astype(F32)
        return lax.psum_scatter(
            values(slice(None)).astype(BF16), ("gq", "core"), scatter_dimension=0, tiled=True
        ).astype(F32)

    def other_half(pieces):
        mine = pick(jnp.stack(pieces), low, 0)
        first = swap_half(mine)
        second = lax.ppermute(first, "rz", beside)
        return first, jnp.where(low == 0, first, second), jnp.where(low == 0, second, first)

    def by_half(own, other):
        return join(own, other, half).reshape(-1, own.shape[-1])

    def set_columns(values, inner=1):
        parts = values.reshape(values.shape[0], 2, quarter, 2, inner, -1)
        return pick(parts, core, 3).transpose(0, 2, 3, 1, 4)

    def gather_rows(values):
        if quarter > 1:
            values = lax.all_to_all(values, "gq", split_axis=1, concat_axis=0, tiled=True)
        return values.reshape(-1, values.shape[-1])

    def set_entries(values, inner=1):
        parts = values.reshape(2, quarter, 2, inner, -1)
        return pick(pick(parts, core, 2), gq, 1).transpose(1, 0, 2).reshape(inner, 1, -1)

    clip_tokens = move(tokens.reshape(local, width), there)
    vectors = jnp.concatenate(
        [query_bias, value_bias, out_bias, first_gain, first_shift, second_gain, second_shift,
         down_bias, up_bias]
    )
    if quarter > 1:
        vectors = lax.all_gather(vectors, "gq", axis=0)
    vectors = join(vectors, swap_half(vectors), half).reshape(grp, -1)
    (full_qbias, full_vbias, full_obias, gain_one, shift_one, gain_two, shift_two, full_dbias) = [
        vectors[:, i * own_rows : (i + 1) * own_rows].reshape(-1) for i in range(8)
    ]
    bias_sets = set_entries(vectors[:, 8 * own_rows :].reshape(-1), ranges)

    parts = [
        set_columns(w).reshape(own_rows, quarter, pairs, PAIR)
        for w in (query_weight, key_weight, value_weight)
    ]
    own_qkv = gather_rows(jnp.stack(parts, axis=3).reshape(own_rows, quarter, 3 * own_rows))
    own_qkv = own_qkv.reshape(2, -1, 3 * own_rows)
    qkv_x, low_rows, high_rows = other_half([own_qkv[0], own_qkv[1]])
    qkv_weight = by_half(
        own_qkv.reshape(-1, 3 * own_rows), jnp.concatenate([low_rows, high_rows], axis=0)
    )
    own_out = pick(out_weight.reshape(2, -1, width), core, 0)
    out_x, low_rows, high_rows = other_half(
        [after(own_out, qkv_x)[: own_rows // 4], own_out[own_rows // 4 :]]
    )
    out_set = by_half(own_out, jnp.concatenate([low_rows, high_rows], axis=0))

    own_up = set_columns(up_weight, ranges)
    own_down = pick(down_weight.reshape(2, ranges, tile, width), core, 0)
    up_sets, down_sets, stages = [], [], [out_x]
    for j in range(ranges):
        up_part = gather_rows(own_up[:, :, j].reshape(own_rows, quarter, 2 * tile))
        down_part = own_down[j]
        if up_part.shape == down_part.shape:
            stage, other_up, other_down = other_half([after(up_part, stages[-1]), down_part])
        else:
            stage, other_up = swap_half(after(up_part, stages[-1])), None
            other_up, other_down = stage, swap_half(down_part)
        stages.append(stage)
        up_sets.append(by_half(up_part, other_up))
        down_sets.append(by_half(down_part, other_down))
    grad_out = move(after(cotangent.reshape(local, width), stages[1]), there)

    zeros = jnp.zeros((1, own_rows), F32)
    qkv_bias = jnp.stack(
        [
            b.reshape(pairs, PAIR)
            for b in (set_entries(full_qbias), zeros, set_entries(full_vbias))
        ],
        axis=1,
    ).reshape(1, 3 * own_rows)

    inputs = clip_tokens.astype(F32)
    first_norm, first_normed, first_inverse = norm_parts(inputs, gain_one, shift_one)
    first = jnp.concatenate(spread(first_norm.astype(BF16)), axis=0)
    qkv = (contract(first, qkv_weight, 1, 0) + qkv_bias).astype(BF16)
    if pairs > 1:
        kept = attend(qkv, 0, pairs // 2)
        mixed, lse = attend(qkv, pairs // 2, pairs, kept)
    else:
        mixed, lse = attend(qkv, 0, pairs)
    middle = collect(lambda rows: contract(mixed[rows], out_set, 1, 0)) + inputs + full_obias
    second_norm, second_normed, second_inverse = norm_parts(middle, gain_two, shift_two)
    seconds = spread(second_norm.astype(BF16))
    grads_out = spread(grad_out)
    x_t = None
    feeds = []
    for j in range(ranges):
        outs = wide_feed(
            half, seconds, grads_out, x_t, up_sets[j],
            bias_sets[j] if j == 0 else after(bias_sets[j], feeds[-1][6]), down_sets[j],
        )
        x_t = outs[7] if j == 0 else x_t
        feeds.append(outs)

    def reduce_ring(pair):
        send, keep = pair
        total = keep.astype(F32) + lax.ppermute(send, "rz", beside).astype(F32)
        total = total.astype(BF16).reshape(deep, -1, keep.shape[-1])
        shifts = range(1, deep)

        def route(shift):
            return [(i, (i + 2 * shift) % ring) for i in range(ring)]

        pieces = [
            lax.ppermute(pick(total, (high + s) % deep, 0), "rz", route(s)) for s in shifts
        ]
        piece = pick(total, high, 0).astype(F32)
        for other in pieces:
            piece = piece + other.astype(F32)
        piece = piece.astype(BF16)
        gathered = [piece] + [lax.ppermute(piece, "rz", route(s)) for s in shifts]
        whole = jnp.stack(
            [
                functools.reduce(
                    lambda rest, s: jnp.where((high - s) % deep == i, gathered[s], rest),
                    shifts,
                    piece,
                )
                for i in range(deep)
            ]
        ).reshape(keep.shape)
        return whole, lax.ppermute(whole, "rz", beside)

    def reduce_parts(parts):
        stacked = jnp.stack(parts)
        own, other = reduce_ring((pick(stacked, 1 - low, 0), pick(stacked, low, 0)))
        return jnp.where(low == 0, own, other), jnp.where(low == 0, other, own)

    def add_half(keep, send):
        return (keep.astype(F32) + swap_half(send).astype(F32)).astype(BF16)

    def reduce_rows(values):
        size = values.shape[0]
        if size % (16 * ring):
            return lax.psum(values, "rz")
        return jnp.concatenate(reduce_parts([values[: size // 2], values[size // 2 :]]), axis=0)

    def scatter_half(values):
        values = values.reshape(2, -1, values.shape[-1])
        return add_half(pick(values, half, 0), pick(values, 1 - half, 0))

    sums_feed = []
    for outs in feeds:
        up_part, down_part = add_half(outs[3], outs[2]), add_half(outs[5], outs[4])
        if up_part.shape == down_part.shape:
            sums_feed.extend(reduce_parts([up_part, down_part]))
        else:
            sums_feed.extend([reduce_rows(up_part), reduce_rows(down_part)])

    grad_wide = grad_out.astype(F32)
    grad_second = collect(
        lambda rows: functools.reduce(
            jnp.add, [contract(feeds[j][1][rows], up_sets[j], 1, 1) for j in range(ranges)]
        )
    )
    grad_second, grad_gain_two, grad_shift_two = norm_back(
        grad_second, second_normed, second_inverse, gain_two
    )
    grad_middle = grad_wide + grad_second
    grad_middle_low = grad_middle.astype(BF16)
    grad_middle_all = jnp.concatenate(spread(grad_middle_low), axis=0)
    grad_mixed = contract(grad_middle_all, out_set, 1, 1).astype(BF16)
    out_half = reduce_rows(scatter_half(contract(mixed, grad_middle_all, 0, 0).astype(BF16)))
    spans = [(0, pairs // 2), (pairs // 2, pairs)] if pairs > 1 else [(0, pairs)]
    dqkvs, qkv_halves = [], []
    for begin, end in spans:
        gate = lse if not dqkvs else after(lse, qkv_halves[-1])
        dqkvs.append(wide_back(qkv, grad_mixed, mixed, gate, begin, end))
        qkv_halves.append(contract(first, dqkvs[-1], 0, 0).astype(BF16))
    qkv_halves = [reduce_rows(scatter_half(values)) for values in qkv_halves]

    result = collect(
        lambda rows: functools.reduce(
            jnp.add, [contract(feeds[j][0][rows], down_sets[j], 1, 0) for j in range(ranges)]
        )
    )
    result = (middle + result + full_dbias).astype(BF16)
    layer_out = move(result, back).reshape(1, local, width)

    def weight_of(span):
        return qkv_weight[:, span[0] * 3 * PAIR : span[1] * 3 * PAIR]

    grad_first_norm = collect(
        lambda rows: functools.reduce(
            jnp.add,
            [contract(d[rows], weight_of(span), 1, 1) for d, span in zip(dqkvs, spans)],
        )
    )
    grad_first, grad_gain_one, grad_shift_one = norm_back(
        grad_first_norm, first_normed, first_inverse, gain_one
    )
    tokens_grad = move((grad_middle + grad_first).astype(BF16), back).reshape(1, local, width)

    out_weight_grad = join(out_half, swap_core(out_half), core).reshape(-1, width).astype(F32)
    if True:

        def finish_columns(values):
            values = values.reshape(quarter, own_rows, 1, -1)
            values = lax.all_to_all(values, "gq", split_axis=0, concat_axis=2, tiled=True)
            values = values.reshape(own_rows, quarter, -1)
            return join(values, swap_core(values), core).transpose(1, 0, 2, 3)

        def natural_columns(values, inner=1):
            values = values.reshape(own_rows, 2, quarter, inner, 2, -1)
            return values.transpose(0, 4, 2, 1, 3, 5).reshape(own_rows, -1).astype(F32)

        ups = jnp.stack([finish_columns(values) for values in sums_feed[::2]], axis=3)
        up_weight_grad = natural_columns(ups, ranges)
        downs = jnp.stack(sums_feed[1::2])
        down_weight_grad = join(downs, swap_core(downs), core).reshape(-1, width).astype(F32)
        columns = jnp.concatenate([finish_columns(values) for values in qkv_halves], axis=3)
        columns = columns.reshape(own_rows, 2, quarter, pairs, 3, PAIR)
        query_weight_grad, key_weight_grad, value_weight_grad = [
            natural_columns(columns[:, :, :, :, i]) for i in range(3)
        ]

    def place_entries(values, inner=1):
        values = values.reshape(inner, 2, 1, 1, -1).transpose(1, 2, 3, 0, 4)
        shape = (2, quarter, 2) + values.shape[3:]
        zero = jnp.zeros((), core.dtype)
        return lax.dynamic_update_slice(
            jnp.zeros(shape, F32), values, (zero, gq, core, zero, zero)
        ).reshape(grp, -1)

    dqkv_sums = jnp.concatenate([jnp.sum(d.astype(F32), axis=0) for d in dqkvs])
    dqkv_sums = dqkv_sums.reshape(pairs, 3, PAIR)
    sums = [
        place_entries(dqkv_sums[:, 0]),
        place_entries(dqkv_sums[:, 2]),
        jnp.sum(grad_middle_low.astype(F32), axis=0),
        grad_gain_one, grad_shift_one, grad_gain_two, grad_shift_two,
        jnp.sum(grad_wide, axis=0),
        place_entries(jnp.stack([outs[6] for outs in feeds]), ranges),
    ]
    sums = jnp.concatenate([s.reshape(grp, -1) for s in sums], axis=1)
    if grp == 2 and ring & (ring - 1) == 0:
        sums = sums + swap_core(sums)
        sums = pick(sums, half, 0) + swap_half(pick(sums, 1 - half, 0))
        step = 1
        while step < ring:
            sums = sums + lax.ppermute(sums, "rz", [(i, i ^ step) for i in range(ring)])
            step *= 2
    else:
        sums = lax.psum(sums, ("rz", "core", "half", "gq"))
        sums = pick(sums, half * quarter + gq, 0)
    small = [sums[i * own_rows : (i + 1) * own_rows] for i in range(8)]
    return (
        layer_out, tokens_grad, query_weight_grad, key_weight_grad, value_weight_grad,
        small[0], small[1], out_weight_grad, small[2], small[3], small[4], small[5], small[6],
        up_weight_grad, sums[8 * own_rows :], down_weight_grad, small[7],
    )


class Order:
    def __init__(self):
        self.before = ()

    def pin(self, *values):
        pinned = lax.optimization_barrier(values + self.before)[: len(values)]
        self.before = tuple(pinned) + self.before
        return pinned[0] if len(values) == 1 else list(pinned)

    def fence(self, *values):
        self.before = values


class Steps:
    def __init__(self, steps):
        self.steps = steps
        self.waiting = next(steps)


def advance(order, *chains):
    pinned = order.pin(*[values for chain in chains for values in chain.waiting])
    pinned = list(pinned) if isinstance(pinned, (list, tuple)) else [pinned]
    for chain in chains:
        count = len(chain.waiting)
        values, pinned = pinned[:count], pinned[count:]
        chain.waiting = chain.steps.send(values)


def line_steps(order, deep, parts, result):
    place = lax.axis_index("line")
    bits = range((deep - 1).bit_length())

    def exchange(values, bit):
        return lax.ppermute(values, "line", [(i, i ^ (1 << bit)) for i in range(deep)])

    for bit in bits:
        even = (place >> bit) % 2 == 0
        keep, send = order.pin(jnp.where(even, *parts), jnp.where(even, *parts[::-1]))
        (other,) = yield [exchange(send, bit)]
        total = add_low(keep, other)
        size = total.shape[0] // 2
        parts = (total[:size], total[size:])
    for bit in reversed(bits):
        total = order.pin(total)
        (other,) = yield [exchange(total, bit)]
        total = join(total, other, (place >> bit) % 2).reshape(-1, total.shape[-1])
    whole = order.pin(total)
    beside, across = yield [lax.ppermute(whole, "low", SWAP), lax.ppermute(whole, "core", SWAP)]
    crossed = lax.ppermute(beside, "core", SWAP)
    (crossed,) = yield [crossed]
    result.extend([whole, beside, across, crossed])
    yield []


def range_steps(order, deep, parts, result):
    place = lax.axis_index("line")
    bits = range((deep - 1).bit_length())

    def exchange(values, bit):
        return lax.ppermute(values, "line", [(i, i ^ (1 << bit)) for i in range(deep)])

    for bit in bits:
        even = (place >> bit) % 2 == 0
        keep, send = order.pin(jnp.where(even, *parts), jnp.where(even, *parts[::-1]))
        (other,) = yield [exchange(send, bit)]
        total = add_low(keep, other)
        size = total.shape[0] // 2
        parts = (total[:size], total[size:])
    for bit in reversed(bits[1:]):
        total = order.pin(total)
        (other,) = yield [exchange(total, bit)]
        total = join(total, other, (place >> bit) % 2).reshape(-1, total.shape[-1])
    whole = order.pin(total)
    beside, along = yield [lax.ppermute(whole, "low", SWAP), exchange(whole, 0)]
    last, crossed = yield [lax.ppermute(along, "low", SWAP), lax.ppermute(whole, "core", SWAP)]
    rest = yield [lax.ppermute(values, "core", SWAP) for values in (beside, along, last)]
    result.extend([whole, beside, along, last, crossed, *rest])
    yield []


def plane_steps(order, low, deep, send, keep, result, more=()):
    send, keep = order.pin(send, keep)
    other, *more_in = yield [lax.ppermute(send, "half", SWAP), *more[1:]]
    total = add_low(keep, other)
    if more:
        total = jnp.concatenate([total, add_low(more[0], more_in[0])], axis=0)
    size = total.shape[0] // 2
    parts = (total[:size], total[size:])
    even = low == 0
    keep, send = order.pin(jnp.where(even, *parts), jnp.where(even, *parts[::-1]))
    (other,) = yield [lax.ppermute(send, "low", SWAP)]
    total = add_low(keep, other)
    size = total.shape[0] // 2
    yield from line_steps(order, deep, (total[:size], total[size:]), result)


def vector_steps(order, half, deep, entries, result):
    def line(values, bit):
        return lax.ppermute(values, "line", [(i, i ^ (1 << bit)) for i in range(deep)])

    entries = order.pin(entries)
    (other,) = yield [lax.ppermute(entries, "core", SWAP)]
    entries = entries + other
    keep, send = order.pin(pick(entries, half, 0), pick(entries, 1 - half, 0))
    (other,) = yield [lax.ppermute(send, "half", SWAP)]
    total = order.pin(keep + other)
    for bit in range((deep - 1).bit_length()):
        (other,) = yield [line(total, bit)]
        total = order.pin(total + other)
    (other,) = yield [lax.ppermute(total, "low", SWAP)]
    result.append(total + other)
    yield []


def add_low(left, right):
    return (left.astype(F32) + right.astype(F32)).astype(BF16)


def after_all(values, *gates):
    if not gates:
        return tuple(values)
    return lax.optimization_barrier(tuple(values) + gates)[: len(values)]


def pair_body(
    rep, grp, tokens, query_weight, key_weight, value_weight, query_bias, value_bias, out_weight,
    out_bias, first_gain, first_shift, second_gain, second_shift, up_weight, up_bias,
    down_weight, down_bias, cotangent,
):
    clips, local, width = tokens.shape
    assert clips == 1
    ring = rep // 2
    deep = ring // 2
    core, half = lax.axis_index("core"), lax.axis_index("half")
    low, high = lax.axis_index("low"), lax.axis_index("line") % 2
    own_rows = width // 2
    pairs = own_rows // PAIR
    hidden = up_weight.shape[1]
    stays = core == half
    scal = jnp.stack([half, low, core, stays.astype(jnp.int32), high]).astype(jnp.int32)
    cross = [(1, 2), (2, 1)]

    def swap_half(values):
        return lax.ppermute(values, "half", SWAP)

    def swap_core(values):
        return lax.ppermute(values, "core", SWAP)

    def swap_low(values):
        return lax.ppermute(values, "low", SWAP)

    def swap_high(values):
        return lax.ppermute(values, "line", [(i, i ^ 1) for i in range(deep)])

    def cross_over(values):
        return lax.ppermute(values, ("core", "half"), cross)

    tokens, cotangent = tokens.reshape(local, width), cotangent.reshape(local, width)

    tokens_in = cross_over(tokens)
    own_qkv, mine = pack_qkv(scal, (query_weight, key_weight, value_weight))
    qkv_x = swap_half(mine)
    packed = [pack_feed(scal, up_weight, down_weight, j, 2, (1, 4)[j]) for j in range(2)]
    vectors = jnp.concatenate(
        [after(query_bias, mine, *packed), value_bias, out_bias, first_gain, first_shift,
         second_gain, second_shift, down_bias, up_bias]
    )
    order = Order()
    tokens_in, qkv_x, vectors, vectors_in, *packed = order.pin(
        tokens_in, qkv_x, vectors, swap_half(vectors), *packed
    )
    qkv_y = swap_low(qkv_x)
    feed_x = [swap_half(packed[0])]
    vectors = join(vectors, vectors_in, half)
    (full_qbias, full_vbias, full_obias, gain_one, shift_one, gain_two, shift_two, full_dbias) = [
        vectors[:, i * own_rows : (i + 1) * own_rows].reshape(1, width) for i in range(8)
    ]

    def set_entries(values, inner=1):
        return pick(values.reshape(2, 2, inner, -1), core, 1).transpose(1, 0, 2).reshape(inner, -1)

    bias_set = set_entries(vectors[:, 8 * own_rows :], 2).reshape(1, -1)
    quarter = own_rows // 4
    out_mine = lax.dynamic_slice(
        out_weight, (core * (own_rows // 2) + low * quarter, 0 * core), (quarter, width)
    )
    x, first = first_norm(scal, tokens, tokens_in, gain_one, shift_one)
    x, first = order.pin(x, first)
    order.fence(x)
    first, qkv_y, feed_x[0] = order.pin(first, qkv_y, feed_x[0])
    first_in = order.pin(swap_core(first))
    feed_y = [swap_low(feed_x[0])]
    out_x = swap_half(order.pin(out_mine))
    feed_x.append(swap_half(order.pin(packed[1])))
    zeros = jnp.zeros((pairs, PAIR), F32)
    qkv_bias = jnp.stack(
        [set_entries(full_qbias).reshape(pairs, PAIR), zeros,
         set_entries(full_vbias).reshape(pairs, PAIR)],
        axis=1,
    ).reshape(1, 3 * own_rows)
    qkv, qkv_weight, first_all = project(
        scal, (first, first_in), own_qkv, qkv_x, qkv_y, qkv_bias
    )

    qkv, out_x = order.pin(qkv, out_x)
    order.fence(qkv)
    out_y = swap_low(out_x)
    mixed, lse = attend(qkv, 0, pairs - 1)
    lse, out_y, feed_x[1] = order.pin(lse, out_y, feed_x[1])
    feed_y.append(swap_high(feed_x[1]))
    cotangent_in = cross_over(after(cotangent, lse))
    mixed, lse = attend(qkv, pairs - 1, pairs, (mixed, lse))
    mixed = order.pin(mixed)
    out_part, out_set = out_other(scal, mixed, out_weight, out_x, out_y)
    out_part, cotangent_in, *feed_y = order.pin(out_part, cotangent_in, *feed_y)
    out_in = swap_core(out_part)
    grad_out = order.pin(jnp.where(stays, cotangent, cotangent_in))
    grad_out_in = swap_core(grad_out)
    middle, second = second_norm(
        scal, mixed, out_set, x, order.pin(out_in), full_obias, gain_two, shift_two
    )
    middle, second = order.pin(middle, second)
    order.fence(second)
    second_in = swap_core(second)

    second_in = order.pin(second_in)
    (
        out_own, out_part, dx_own, dx_part, up_send, up_keep, down_send, down_keep, low_send,
        low_keep, up_bias_grad,
    ) = feed(
        scal, (second, second_in), (grad_out, grad_out_in), up_weight, down_weight,
        (feed_x[0], feed_y[0], feed_x[1], feed_y[1]), bias_set,
    )
    dx_part, up_send, down_send, low_send, out_part = order.pin(
        dx_part, up_send, down_send, low_send, out_part
    )
    order.fence(dx_part)
    dx_in = swap_core(dx_part)
    up_in, down_in, low_in = swap_half(up_send), swap_half(down_send), swap_low(low_send)
    grad_low, sums_two = second_back(
        scal, dx_own, order.pin(dx_in), middle, grad_out, gain_two
    )
    grad_low = order.pin(grad_low)
    grad_low_in = swap_core(grad_low)
    grad_low_in = order.pin(grad_low_in)
    grad_mixed, out_send, out_keep = mixed_back(scal, (grad_low, grad_low_in), out_set, mixed)
    grad_mixed = order.pin(grad_mixed)

    backs = []

    def back(pair):
        gate = order.pin(lse)
        named = jnp.concatenate([scal, jnp.full((1,), pair, jnp.int32)])
        backs.append(attend_back(named, qkv, grad_mixed, mixed, gate, first_all))
        backs[-1] = order.pin(*backs[-1])
        order.fence(backs[-1][3])

    back(0)
    up_in, down_in, low_in = order.pin(up_in, down_in, low_in)
    up_sum, down_sum = add_low(up_keep, up_in), add_low(down_keep, down_in)
    even = low == 0
    low_mine, low_other = order.pin(
        jnp.where(even, up_sum, down_sum), jnp.where(even, down_sum, up_sum)
    )
    one_in = lax.ppermute(low_other, "low", SWAP)
    range_sum = add_low(low_keep, low_in).reshape(2, own_rows, width)
    half_send, half_keep = order.pin(pick(range_sum, 1 - half, 0), pick(range_sum, half, 0))
    half_in = swap_half(half_send)
    out_half_in = swap_half(order.pin(out_send))

    back(1)
    one_in, half_in = order.pin(one_in, half_in)
    feed_parts, early_parts, late_parts, vector_parts = [], [], [], []
    ranges = Steps(
        range_steps(
            order, deep, (add_low(low_mine, one_in), add_low(half_keep, half_in)), feed_parts
        )
    )
    early = Steps(
        plane_steps(
            order, low, deep,
            jnp.concatenate([backs[0][1], backs[1][1]], axis=0),
            jnp.concatenate([backs[0][2], backs[1][2]], axis=0), early_parts,
            more=(out_keep, out_half_in),
        )
    )

    back(2)
    advance(order, ranges, early)
    out_in = swap_core(order.pin(out_part))

    back(3)
    out_in = order.pin(out_in)
    late = Steps(
        plane_steps(
            order, low, deep,
            jnp.concatenate([backs[2][1], backs[3][1]], axis=0),
            jnp.concatenate([backs[2][2], backs[3][2]], axis=0), late_parts,
        )
    )
    advance(order, ranges, early)
    first_own, first_part = first_grad(
        scal, [order.pin(backs[0][0])] + [b[0] for b in backs[1:]], qkv_weight
    )
    first_own, first_part = order.pin(first_own, first_part)
    order.fence(first_part)
    advance(order, late, early)
    first_part_in = swap_core(order.pin(first_part))
    advance(order, ranges)
    tokens_out, sums_one = first_back(
        scal, first_own, order.pin(first_part_in), x, grad_low, gain_one
    )
    tokens_out, sums_one = order.pin(tokens_out, sums_one)
    order.fence(sums_one)
    layer = order.pin(layer_rows(scal, out_own, out_in, after(middle, sums_one), full_dbias))
    advance(order, early, late, ranges)

    def place_entries(values, inner=1):
        values = values.reshape(inner, 2, 1, -1).transpose(1, 2, 0, 3)
        empty = jnp.zeros_like(values)
        return join(values[:, 0], empty[:, 0], core).transpose(1, 0, 2, 3).reshape(2, -1)

    parts = jnp.concatenate([b[3][0] for b in backs]).reshape(pairs, 3, PAIR)
    entries = [
        place_entries(parts[:, 0]), place_entries(parts[:, 2]), sums_two[3], sums_one[0],
        sums_one[1], sums_two[0], sums_two[1], sums_two[2], place_entries(up_bias_grad, 2),
    ]
    entries = jnp.concatenate([e.reshape(2, -1) for e in entries], axis=1)
    vectors = Steps(vector_steps(order, half, deep, entries, vector_parts))
    advance(order, vectors)
    advance(order, vectors, early, late)
    tokens_in = cross_over(order.pin(tokens_out))
    layer_in = cross_over(layer)
    advance(order, vectors, early, late)
    advance(order, vectors, late)
    advance(order, early, ranges, late)
    advance(order, ranges, vectors, early)
    up_weight_grad, down_weight_grad = order.pin(*finish_feed(scal, feed_parts))
    advance(order, late)
    advance(order, late)
    (entries,) = vector_parts
    query_weight_grad, key_weight_grad, value_weight_grad, out_weight_grad = finish_attention(
        scal, (*early_parts, *late_parts), ((0, 2), (2, 4))
    )
    layer_out = jnp.where(stays, layer, layer_in)
    tokens_grad = jnp.where(stays, tokens_out, tokens_in)
    small = [entries[i * own_rows : (i + 1) * own_rows] for i in range(8)]
    return (
        layer_out.reshape(1, local, width), tokens_grad.reshape(1, local, width),
        query_weight_grad, key_weight_grad, value_weight_grad, small[0], small[1],
        out_weight_grad, small[2], small[3], small[4], small[5], small[6], up_weight_grad,
        entries[8 * own_rows :], down_weight_grad, small[7],
    )


def solution(mesh):
    rep, grp = mesh.shape["rep"], mesh.shape["grp"]
    paired = grp == 2 and rep >= 8 and rep & (rep - 1) == 0
    if paired:
        sizes, names = (rep // 4, 2, 2, 2), ("line", "low", "core", "half")
        reps, groups, body = ("line", "low", "core"), "half", pair_body
    else:
        sizes, names = (rep // 2, 2, 2, grp // 2), ("rz", "core", "half", "gq")
        reps, groups, body = ("rz", "core"), ("half", "gq"), wide_body
    clip, matrix, vector = P(reps, groups, None), P(groups, None), P(groups)
    return jax.shard_map(
        functools.partial(body, rep, grp),
        mesh=Mesh(mesh.devices.reshape(sizes), names),
        in_specs=(
            clip, matrix, matrix, matrix, vector, vector, matrix, vector, vector, vector, vector,
            vector, matrix, vector, matrix, vector, clip,
        ),
        out_specs=(
            clip, clip, matrix, matrix, matrix, vector, vector, matrix, vector, vector, vector,
            vector, vector, matrix, vector, matrix, vector,
        ),
        check_vma=False,
    )
```
